32 devices in a mesh: fsdp: 8 (over z, x), tensor: 4 (over y, core).
Axes of the slice: x: 2, y: 2, z: 4, core: 2. Of those that a mesh axis runs over, the one named last changes fastest.
Arguments:
- layer_in: bfloat16 [4096, 512], P(('fsdp', 'tensor')), may hold values from -6 to 6
- grad_out: bfloat16 [4096, 512], P(('fsdp', 'tensor')), may hold values from -6 to 6
- ln_scale: bfloat16 [512], P('fsdp'), may hold values from 0.099609375 to 1.8984375
- ln_bias: bfloat16 [512], P('fsdp'), may hold values from -3 to 3
- decay_rate: float32 [384], P('tensor'), may hold values from 0.02 to 0.5
- lam_im: float32 [384], P('tensor'), may hold values from -20 to 20
- log_dt: float32 [384], P('tensor'), may hold values from -6.9 to -2.3
- in_re: bfloat16 [384, 512], P('tensor', 'fsdp'), may hold values from -0.25 to 0.25
- in_im: bfloat16 [384, 512], P('tensor', 'fsdp'), may hold values from -0.25 to 0.25
- out_re: bfloat16 [384, 512], P('tensor', 'fsdp'), may hold values from -0.29882812 to 0.29882812
- out_im: bfloat16 [384, 512], P('tensor', 'fsdp'), may hold values from -0.29882812 to 0.29882812
- skip: bfloat16 [512], P('fsdp'), may hold values from -3 to 3
- glu_weight: bfloat16 [512, 512], P(None, 'fsdp'), may hold values from -0.25 to 0.25
- glu_bias: bfloat16 [512], P('fsdp'), may hold values from -4 to 4
- seq_lengths: int32 [4], replicated, may hold values from 1 to 2048, 4096 in all
Outputs:
- layer_out: bfloat16 [4096, 512], P(('fsdp', 'tensor'))
- grad_in: float32 [4096, 512], P(('fsdp', 'tensor'))
- grad_ln_scale: float32 [512], replicated
- grad_ln_bias: float32 [512], replicated
- grad_decay: float32 [384], replicated
- grad_lam_im: float32 [384], replicated
- grad_log_dt: float32 [384], replicated
- grad_in_re: float32 [384, 512], P('tensor', 'fsdp')
- grad_in_im: float32 [384, 512], P('tensor', 'fsdp')
- grad_out_re: float32 [384, 512], P('tensor', 'fsdp')
- grad_out_im: float32 [384, 512], P('tensor', 'fsdp')
- grad_skip: float32 [512], replicated
- grad_glu_weight: float32 [512, 512], P('tensor', 'fsdp')
- grad_glu_bias: float32 [512], P(('tensor', 'fsdp'))
- rms: float32 [2], replicated
The draws below stay inside these ranges and needn't reach their ends.
Inputs may be any that keep to these rules, and one draw needn't show every extreme that they name: `seq_lengths`: the lengths sum to 4096 and the largest is exactly 2048.
All inputs are finite; a program needn't handle non-finite values.
Results may differ from the reference program's by a relative error of at most 0.012.
Values may be sent and summed in bfloat16 or wider, within the bound.
No kernel may reach another device: no remote copies, remote signals or barrier semaphores. Data moves between devices by JAX's collectives and lax.ppermute only.
A program may use at most 128 MiB of HBM per device.

```python
import math
import jax
import jax.numpy as jnp
import numpy as np
from jax import lax

H = 512
P_SIZE = 384
TOKENS = 4096
LMAX = 2048
NSEQ = 4


def levels(key, shape, split, least, largest):
    level, own = 1.0, jax.random.fold_in(key, 6)
    for dim, blocks in split:
        draws = jnp.exp(jax.random.uniform(jax.random.fold_in(own, dim), (blocks,), jnp.float32, least / len(split), largest / len(split)))
        level = level * jnp.repeat(draws, shape[dim] // blocks).reshape([-1 if axis == dim else 1 for axis in range(len(shape))])
    return level


def profile(amount, total, bound, lean):
    portions = [(1 << 20) // math.isqrt(grade ** lean) + 1 for grade in range(2, amount + 1)]
    rest, holding = total - bound - (amount - 1), [1] * (amount - 1)
    while rest > 0:
        candidates = [i for i in range(amount - 1) if holding[i] < bound]
        whole, budget = sum([portions[i] for i in candidates]), rest
        for i in candidates:
            more = min(bound - holding[i], max(1, budget * portions[i] // whole), rest)
            holding[i] = holding[i] + more
            rest = rest - more
    return np.array([bound] + holding)


def ragged(own_key, number_of, total, most, skew):
    if number_of == 2:
        one = jax.random.randint(own_key, (), max(1, total - most), min(most, total - 1) + 1)
        return jnp.stack([one, total - one])
    tallies = jnp.asarray(profile(number_of, total, most, skew), jnp.int32)
    pairs = (number_of - 1) // 2
    source_of, sink = tallies[1:1 + 2 * pairs:2], tallies[2:2 + 2 * pairs:2]
    room = jnp.minimum(source_of - 1, most - sink)
    passed = jax.random.randint(jax.random.fold_in(own_key, 1), (pairs,), 0, 1 << 20) % (room + 1)
    tallies = tallies.at[1:1 + 2 * pairs:2].set(source_of - passed).at[2:2 + 2 * pairs:2].set(sink + passed)
    return tallies[jax.random.permutation(jax.random.fold_in(own_key, 2), number_of)]


def gaussian(stream_key, extent, scale, most, cuts=(), kind=jnp.bfloat16):
    values = jax.random.normal(stream_key, extent, jnp.float32) * scale
    if len(cuts) > 0:
        values = levels(stream_key, extent, cuts, -0.22, 0.18) * values
    return jnp.clip(values, min=-most, max=most).astype(kind)


def setup_inputs(seed: int = 0) -> dict:
    splits = jax.random.split(jax.random.key(seed), 16)
    return {
        "layer_in": gaussian(splits[0], (TOKENS, H), 1.0, 6.0, ((0, 32),)),
        "grad_out": gaussian(splits[1], (TOKENS, H), 1.0, 6.0, ((0, 32),)),
        "ln_scale": jnp.clip(1.0 + 0.18 * jax.random.normal(splits[2], (H,), jnp.float32), 0.099609375, 1.8984375).astype(jnp.bfloat16),
        "ln_bias": gaussian(splits[3], (H,), 0.5, 3.0, ((0, 8),)),
        "decay_rate": jnp.clip(jnp.exp(math.log(0.5) - 3.218876 * jax.random.uniform(splits[4], (P_SIZE,), jnp.float32) ** levels(splits[4], (P_SIZE,), ((0, 4),), -0.2, 0.2)), 0.02, 0.5),
        "lam_im": jnp.clip(jax.random.uniform(splits[5], (P_SIZE,), jnp.float32, -20.0, 20.0) * levels(splits[5], (P_SIZE,), ((0, 4),), -0.4, 0.0), -20.0, 20.0),
        "log_dt": jnp.clip(-6.9 + 4.6000001430511475 * jax.random.uniform(splits[6], (P_SIZE,), jnp.float32) ** levels(splits[6], (P_SIZE,), ((0, 4),), -0.2, 0.2), -6.9, -2.3),
        "in_re": gaussian(splits[7], (P_SIZE, H), H ** -0.5, 0.25, ((0, 4), (1, 8))),
        "in_im": gaussian(splits[8], (P_SIZE, H), H ** -0.5, 0.25, ((0, 4), (1, 8))),
        "out_re": gaussian(splits[9], (P_SIZE, H), 0.05, 0.29882812, ((0, 4), (1, 8))),
        "out_im": gaussian(splits[10], (P_SIZE, H), 0.05, 0.29882812, ((0, 4), (1, 8))),
        "skip": gaussian(splits[11], (H,), 0.5, 3.0, ((0, 8),)),
        "glu_weight": gaussian(splits[12], (H, H), H ** -0.5, 0.25, ((1, 8),)),
        "glu_bias": gaussian(splits[13], (H,), 1.0, 4.0, ((0, 8),)),
        "seq_lengths": ragged(splits[14], NSEQ, TOKENS, LMAX, 2).astype(jnp.int32),
    }


@jax.custom_vjp
def low(v):
    return lax.optimization_barrier(v.astype(jnp.bfloat16)).astype(jnp.float32)

@jax.custom_vjp
def low_back(v):
    return v

def low_keep(v):
    return (low(v), None)

def low_pass(kept, grad):
    return (grad,)

def back_keep(v):
    return (v, None)

def back_low(kept, grad):
    return (low(grad),)
low.defvjp(low_keep, low_pass)
low_back.defvjp(back_keep, back_low)

def complex_mul(left_re, left_im, right_re, right_im):
    return (left_re * right_re - left_im * right_im, left_re * right_im + left_im * right_re)

def combine(former, latter):
    mul_re, mul_im = complex_mul(former[0], former[1], latter[0], latter[1])
    add_re, add_im = complex_mul(latter[0], latter[1], former[2], former[3])
    return (mul_re, mul_im, add_re + latter[2], add_im + latter[3])

def discretize(decay_rate, lam_im, log_dt):
    step_size = jnp.exp(log_dt)
    lam_re = -decay_rate
    magnitude = jnp.exp(lam_re * step_size)
    phase = lam_im * step_size
    abar_re = magnitude * jnp.cos(phase)
    abar_im = magnitude * jnp.sin(phase)
    half_sin = jnp.sin(0.5 * phase)
    less_re = jnp.expm1(lam_re * step_size) * jnp.cos(phase) - 2.0 * half_sin * half_sin
    denom = lam_re * lam_re + lam_im * lam_im
    coef_re = (less_re * lam_re + abar_im * lam_im) / denom
    coef_im = (abar_im * lam_re - less_re * lam_im) / denom
    return (abar_re, abar_im, coef_re, coef_im)

def chain(decay_re, decay_im, drive_re, drive_im):
    total, width = decay_re.shape
    block_len = min(4096, total)

    def one_block(carry, items):
        cum_re, cum_im, loc_re, loc_im = lax.associative_scan(combine, items, axis=0)
        state_re = loc_re + cum_re * carry[0] - cum_im * carry[1]
        state_im = loc_im + cum_re * carry[1] + cum_im * carry[0]
        return ((state_re[-1], state_im[-1]), (state_re, state_im))
    start = (jnp.zeros((width,), jnp.float32), jnp.zeros((width,), jnp.float32))
    items = tuple((member.reshape(total // block_len, block_len, width) for member in (decay_re, decay_im, drive_re, drive_im)))
    unused, states = lax.scan(jax.checkpoint(one_block), start, items)
    return (states[0].reshape(total, width), states[1].reshape(total, width))

def forward(keep, resid, scale, norm_offset, decay_rate, lam_im, log_dt, in_re, in_im, out_re, out_im, skip, glu_weight, glu_bias):
    highest = lax.Precision.HIGHEST
    centered_input = resid - lax.optimization_barrier(jnp.mean(resid, axis=1, keepdims=True))
    inverse_deviation = lax.rsqrt(lax.optimization_barrier(jnp.mean(centered_input * centered_input, axis=1, keepdims=True)) + 1e-05)
    normalized_rows = low(centered_input * inverse_deviation * scale + norm_offset)
    abar_re, abar_im, coef_re, coef_im = discretize(decay_rate, lam_im, log_dt)
    proj_re = low_back(jnp.dot(normalized_rows, in_re.T, precision=highest))
    proj_im = low_back(jnp.dot(normalized_rows, in_im.T, precision=highest))
    drive_re = coef_re * proj_re - coef_im * proj_im
    drive_im = coef_re * proj_im + coef_im * proj_re
    decay_re = keep[:, None] * abar_re
    decay_im = keep[:, None] * abar_im
    state_re, state_im = chain(decay_re, decay_im, drive_re, drive_im)
    readout = 2.0 * (jnp.dot(low(state_re), out_re, precision=highest) - jnp.dot(low(state_im), out_im, precision=highest))
    mixed = low_back(readout) + skip * normalized_rows
    act = low(jax.nn.gelu(mixed, approximate=False))
    logit = low_back(jnp.dot(act, glu_weight.T, precision=highest) + glu_bias)
    branch = low(act * jax.nn.sigmoid(logit))
    return (resid + branch, branch)

def reference(layer_in, grad_out, ln_scale, ln_bias, decay_rate, lam_im, log_dt, in_re, in_im, out_re, out_im, skip, glu_weight, glu_bias, seq_lengths):
    total = layer_in.shape[0]
    offsets = (jnp.cumsum(seq_lengths) - seq_lengths).astype(jnp.int32)
    positions = jnp.arange(total, dtype=jnp.int32)
    starts = jnp.any(positions[:, None] == offsets[None, :], axis=1)
    keep = jnp.where(starts, 0.0, 1.0).astype(jnp.float32)
    params = tuple((member.astype(jnp.float32) for member in (layer_in, ln_scale, ln_bias, decay_rate, lam_im, log_dt, in_re, in_im, out_re, out_im, skip, glu_weight, glu_bias)))

    def wrapped(*values):
        return forward(keep, *values)
    result, pull, branch = jax.vjp(wrapped, *params, has_aux=True)
    grads = pull(grad_out.astype(jnp.float32))
    resid = params[0]
    rms = jnp.stack([jnp.sqrt(jnp.mean(resid * resid)), jnp.sqrt(jnp.mean(branch * branch))])
    return (result.astype(jnp.bfloat16), grads[0], grads[1], grads[2], grads[3], grads[4], grads[5], grads[6], grads[7], grads[8], grads[9], grads[10], grads[11], grads[12], rms)
```

```python
import functools

import jax
import jax.numpy as jnp
from jax import lax
from jax.experimental import pallas as pl
from jax.experimental.pallas import tpu as pltpu
from jax.sharding import Mesh
from jax.sharding import PartitionSpec as P

F32 = jnp.float32
BF16 = jnp.bfloat16
AXES = ("fsdp", "ty", "tc")
VM = pl.BlockSpec(memory_space=pltpu.VMEM)
SM = pl.BlockSpec(memory_space=pltpu.SMEM)

GROUPS = 8


def sds(shape, dtype=F32):
    return jax.ShapeDtypeStruct(shape, dtype)


def low_half(shape):
    return lax.broadcasted_iota(jnp.int32, shape, len(shape) - 1) < 64


def lane_iota(shape):
    return lax.broadcasted_iota(jnp.int32, shape, len(shape) - 1)


def dot(a, b, dims):
    return lax.dot_general(a, b, (dims, ((), ())), preferred_element_type=F32)


NT = ((1,), (1,))
NN = ((1,), (0,))
TN = ((0,), (0,))


def spread(x):
    lo = low_half((x.shape[0], 128))
    upper, lower = [], []
    for c in range(x.shape[1] // 128):
        xc = x[:, 128 * c : 128 * c + 128]
        turned = pltpu.roll(xc, 64, 1)
        upper += [jnp.where(lo, xc, 0.0).astype(BF16), jnp.where(lo, turned, 0.0).astype(BF16)]
        lower += [jnp.where(lo, 0.0, turned).astype(BF16), jnp.where(lo, 0.0, xc).astype(BF16)]
    return jnp.concatenate(
        [jnp.concatenate(upper, axis=1), jnp.concatenate(lower, axis=1)], axis=0
    )


def folded(pq):
    rows = pq.shape[0] // 2
    lo = low_half((rows, 128))
    out = []
    for c in range(pq.shape[1] // 256):
        p0, p1 = pq[:rows, 256 * c : 256 * c + 128], pq[:rows, 256 * c + 128 : 256 * c + 256]
        q0, q1 = pq[rows:, 256 * c : 256 * c + 128], pq[rows:, 256 * c + 128 : 256 * c + 256]
        out.append(jnp.where(lo, p0 + pltpu.roll(q0, 64, 1), pltpu.roll(p1, 64, 1) + q1))
    return jnp.concatenate(out, axis=1)


def weights(refs, start, count):
    return jnp.concatenate(
        [
            jnp.concatenate([ref[f, start : start + count, :] for ref in refs], axis=0)
            for f in range(GROUPS)
        ],
        axis=1,
    )


def feature_rows(ref, row):
    lo = low_half((8, 128))
    first, second = [], []
    for c in range(GROUPS // 2):
        a = jnp.broadcast_to(ref[2 * c, row : row + 1, :].astype(F32), (8, 128))
        b = jnp.broadcast_to(ref[2 * c + 1, row : row + 1, :].astype(F32), (8, 128))
        first.append(jnp.where(lo, a, pltpu.roll(b, 64, 1)))
        second.append(jnp.where(lo, pltpu.roll(a, 64, 1), b))
    return jnp.concatenate(first, axis=1)[:1], jnp.concatenate(second, axis=1)[:1]


def rows_to_lanes(rows):
    turned = [rows, pltpu.roll(rows, 96, 1), pltpu.roll(rows, 64, 1), pltpu.roll(rows, 32, 1)]
    lane = lane_iota((1, 128))
    return [
        jnp.where(lane < 96, rows[0:1], turned[1][1:2]),
        jnp.where(lane < 64, turned[1][1:2], turned[2][2:3]),
        jnp.where(lane < 32, turned[2][2:3], turned[3][3:4]),
    ]


def lanes_to_rows(chunks):
    wide = [jnp.broadcast_to(chunk, (8, 128)) for chunk in chunks]
    lane = lane_iota((8, 128))
    r1 = jnp.where(lane < 32, pltpu.roll(wide[0], 32, 1), pltpu.roll(wide[1], 32, 1))
    r2 = jnp.where(lane < 64, pltpu.roll(wide[1], 64, 1), pltpu.roll(wide[2], 64, 1))
    r3 = pltpu.roll(wide[2], 96, 1)
    return [jnp.where(lane < 96, r, 0.0)[:1] for r in (wide[0], r1, r2, r3)]


def cmul(a, b):
    return a[0] * b[0] - a[1] * b[1], a[0] * b[1] + a[1] * b[0]


def tensor_pos():
    return lax.axis_index("ty") * 2 + lax.axis_index("tc")


def block_pos():
    return lax.axis_index("fsdp") * 4 + tensor_pos()


def offsets_of(seq_ref):
    out, total = [], 0
    for n in range(seq_ref.shape[0]):
        out.append(total)
        total = total + seq_ref[n]
    return out


def starts_until(offsets, base, rows):
    at = lax.broadcasted_iota(jnp.int32, (rows, 128), 0) + base
    count = jnp.zeros((rows, 128), F32)
    for off in offsets:
        count = count + jnp.where((at >= off) & (off >= base), 1.0, 0.0)
    return count


def no_start(offsets, base, rows):
    hit = False
    for off in offsets:
        hit = hit | ((off >= base) & (off < base + rows))
    return jnp.where(hit, 0.0, 1.0)


def expm1(x):
    series = x * (1 + x / 2 * (1 + x / 3 * (1 + x / 4 * (1 + x / 5 * (1 + x / 6 * (1 + x / 7))))))
    return jnp.where(jnp.abs(x) < 0.25, series, jnp.exp(x) - 1.0)


def discretize(decay_rate, lam_im, log_dt):
    step_size = jnp.exp(log_dt)
    lam_re = -decay_rate
    magnitude = jnp.exp(lam_re * step_size)
    phase = lam_im * step_size
    abar_re = magnitude * jnp.cos(phase)
    abar_im = magnitude * jnp.sin(phase)
    half_sin = jnp.sin(0.5 * phase)
    less_re = expm1(lam_re * step_size) * jnp.cos(phase) - 2.0 * half_sin * half_sin
    denom = lam_re * lam_re + lam_im * lam_im
    coef_re = (less_re * lam_re + abar_im * lam_im) / denom
    coef_im = (abar_im * lam_re - less_re * lam_im) / denom
    return abar_re, abar_im, coef_re, coef_im, step_size


def pack_kernel(re_ref, im_ref, ore_ref, oim_ref, glu_ref, sc_ref, lb_ref, sk_ref, gb_ref, de_ref, la_ref, dt_ref, out_ref):
    tens = tensor_pos()
    first = pl.multiple_of(tens * 64, 64)
    pieces = [
        jnp.concatenate([re_ref[...], im_ref[...]], axis=1),
        jnp.concatenate([ore_ref[...], oim_ref[...]], axis=1),
        jnp.concatenate([glu_ref[pl.ds(first, 64), :], glu_ref[pl.ds(first + 256, 64), :]], axis=1),
    ]
    vec = [
        jnp.concatenate([sc_ref[...], lb_ref[...]], axis=1).astype(F32),
        jnp.concatenate([sk_ref[...], gb_ref[...]], axis=1).astype(F32),
    ]
    for ref in (de_ref, la_ref, dt_ref):
        value = jnp.concatenate([ref[...], jnp.zeros((1, 32), F32)], axis=1)
        for _ in range(3):
            part = value.astype(BF16).astype(F32)
            value = value - part
            vec.append(part)
    vec.append(jnp.zeros((16 - len(vec), 128), F32))
    pieces.append(jnp.concatenate(vec, axis=0).astype(BF16))
    packet = jnp.concatenate(pieces, axis=0)
    for f in range(GROUPS):
        out_ref[f] = packet


def params_of(refs, vec_row):
    lane = lane_iota((8, 128))
    out = []
    for k, safe in enumerate((1.0, 0.0, 0.0)):
        rows = []
        for ref in refs:
            part = ref[0, vec_row : vec_row + 16, :].astype(F32)
            rows.append((part[2 + 3 * k : 3 + 3 * k] + part[3 + 3 * k : 4 + 3 * k]) + part[4 + 3 * k : 5 + 3 * k])
        value = jnp.concatenate(rows + [jnp.full((4, 128), safe, F32)], axis=0)
        out.append(jnp.where(lane < 96, value, safe))
    return out


def block_of(chunks_re, chunks_im, scratch, tens):
    for half, chunks in ((0, chunks_re), (4, chunks_im)):
        for i, row in enumerate(lanes_to_rows(chunks)):
            scratch[pl.ds(half + (tens ^ i), 1), :] = row


def chunks_from(scratch, half, tens):
    rows = jnp.concatenate([scratch[pl.ds(half + (tens ^ i), 1), :] for i in range(4)] + [jnp.zeros((4, 128), F32)], axis=0)
    return rows_to_lanes(rows)


VEC = 256


def first_kernel(blocks, x_ref, seq_ref, g0, g1, g2, g3, xhat_ref, inv_ref, normed_ref, v_ref, lane_ref, row_ref, send_ref, scratch):
    refs = (g0, g1, g2, g3)
    tens = tensor_pos()
    rows = x_ref.shape[0]
    width = x_ref.shape[1]
    x = x_ref[...].astype(F32)
    centered = x - jnp.sum(x, axis=1, keepdims=True) / width
    inverse = lax.rsqrt(jnp.sum(centered * centered, axis=1, keepdims=True) / width + 1e-05)
    xhat = centered * inverse
    xhat_ref[...] = xhat
    inv_ref[...] = jnp.broadcast_to(inverse, (rows, 128))
    scale, bias = feature_rows(g0, VEC)
    normed = (xhat * scale + bias).astype(BF16)
    normed_ref[...] = normed
    v_ref[...] = dot(spread(normed.astype(F32)), weights(refs, 0, 96), NT)

    decay, lam, log_dt = params_of(refs, VEC)
    abar_re, abar_im, coef_re, coef_im, step_size = discretize(decay, lam, log_dt)
    power = (abar_re, abar_im)
    per_row = [decay, lam, step_size, abar_re, abar_im, coef_re, coef_im]
    for _ in range(7):
        power = cmul(power, power)
    for half in (0, 1):
        for i in range(4):
            scratch[pl.ds(half * 4 + (tens ^ i), 1), :] = power[half][i : i + 1]
    for k, value in enumerate(per_row):
        row_ref[k] = value
    row_ref[len(per_row)] = scratch[...]
    abar = (rows_to_lanes(abar_re), rows_to_lanes(abar_im))
    coef = (rows_to_lanes(coef_re), rows_to_lanes(coef_im))
    for k, chunks in enumerate((*abar, *coef)):
        for c in range(3):
            lane_ref[k : k + 1, 128 * c : 128 * c + 128] = chunks[c]

    offsets = offsets_of(seq_ref)
    count = starts_until(offsets, block_pos() * rows, rows)
    open_tail = jnp.where(count == count[rows - 1 : rows], 1.0, 0.0)
    last = ([], [])
    for c in range(3):
        a = (abar[0][c], abar[1][c])
        eight, tail = eighth_powers(a, 7)
        b = (coef[0][c], coef[1][c])
        acc = (jnp.zeros((8, 128), F32), jnp.zeros((8, 128), F32))
        for blk in range(rows // 8):
            here = slice(8 * blk, 8 * blk + 8)
            v = (v_ref[here, 128 * c : 128 * c + 128], v_ref[rows + 8 * blk : rows + 8 * blk + 8, 128 * c : 128 * c + 128])
            drive = cmul(b, v)
            moved = cmul(eight, acc)
            acc = (moved[0] + drive[0] * open_tail[here], moved[1] + drive[1] * open_tail[here])
        total = cmul(tail, acc)
        last[0].append(jnp.sum(total[0], axis=0, keepdims=True))
        last[1].append(jnp.sum(total[1], axis=0, keepdims=True))
    block_of(last[0], last[1], scratch, tens)
    packet = scratch[...]
    for d in range(blocks):
        send_ref[d] = packet


def eighth_powers(a, top):
    sub = lax.broadcasted_iota(jnp.int32, (8, 128), 0)
    exponent = (7 - sub) if top == 7 else sub + 1
    a = (jnp.broadcast_to(a[0], (8, 128)), jnp.broadcast_to(a[1], (8, 128)))
    tile = (jnp.ones((8, 128), F32), jnp.zeros((8, 128), F32))
    for bit in range(4):
        if bit == 3:
            eight = a
        taken = (exponent & (1 << bit)) != 0
        more = cmul(tile, a)
        tile = (jnp.where(taken, more[0], tile[0]), jnp.where(taken, more[1], tile[1]))
        a = cmul(a, a)
    return eight, tile


def scan_chunk(value, a, count, reverse):
    rows = count.shape[0]
    at = lax.broadcasted_iota(jnp.int32, (rows, 128), 0)
    step = 1
    while step < rows:
        shift = rows - step if reverse else step
        other = pltpu.roll(count, shift, 0)
        inside = (at < rows - step) if reverse else (at >= step)
        linked = inside & (other == count)
        moved = (pltpu.roll(value[0], shift, 0), pltpu.roll(value[1], shift, 0))
        more = cmul(a, moved)
        value = (value[0] + jnp.where(linked, more[0], 0.0), value[1] + jnp.where(linked, more[1], 0.0))
        a = cmul(a, a)
        step *= 2
    return value


def carried(recv_ref, row_ref, offsets, rows, reverse, scratch, tens):
    blocks = recv_ref.shape[0]
    power = row_ref[7]
    pre, pim = power[0:4], power[4:8]
    if reverse:
        pim = -pim
    place = block_pos()

    def turn(k, state):
        j = blocks - 1 - k if reverse else k
        link = no_start(offsets, j * rows, rows)
        got = recv_ref[j]
        new = cmul((pre * link, pim * link), state)
        return new[0] + got[0:4], new[1] + got[4:8]

    zero = jnp.zeros((4, 128), F32)
    out = lax.fori_loop(0, blocks - 1 - place if reverse else place, turn, (zero, zero))
    scratch[0:4, :] = out[0]
    scratch[4:8, :] = out[1]
    return chunks_from(scratch, 0, tens), chunks_from(scratch, 4, tens)


def column_sum(value):
    return jnp.sum(value, axis=0, keepdims=True)


def second_kernel(
    blocks, recv_ref, seq_ref, x_ref, up_ref, normed_ref, v_ref, lane_ref, row_ref, g0, g1, g2, g3,
    out_ref, state_ref, dstate_ref, enter_ref, dmixed_ref, part_ref, keep_ref, away_ref, send_ref,
    scratch, gate_ref, dgate_ref,
):
    refs = (g0, g1, g2, g3)
    tens = tensor_pos()
    rows, width = x_ref.shape
    offsets = offsets_of(seq_ref)
    base = block_pos() * rows
    count = starts_until(offsets, base, rows)
    for i, ref in enumerate(refs):
        for f in range(GROUPS):
            gate_ref[f, tens ^ i] = ref[f, 192:256, :]
    enter = carried(recv_ref, row_ref, offsets, rows, False, scratch, tens)
    keep_first = no_start(offsets, base, 1)
    top = lax.broadcasted_iota(jnp.int32, (rows, 128), 0) == 0
    for c in range(3):
        lanes = slice(128 * c, 128 * c + 128)
        a = (lane_ref[0:1, lanes], lane_ref[1:2, lanes])
        b = (lane_ref[2:3, lanes], lane_ref[3:4, lanes])
        drive = cmul(b, (v_ref[:rows, lanes], v_ref[rows:, lanes]))
        came = cmul((a[0] * keep_first, a[1] * keep_first), (enter[0][c], enter[1][c]))
        drive = (drive[0] + jnp.where(top, came[0], 0.0), drive[1] + jnp.where(top, came[1], 0.0))
        state = scan_chunk(drive, a, count, False)
        state_ref[:rows, lanes] = state[0]
        state_ref[rows:, lanes] = state[1]
        enter_ref[0:1, lanes] = enter[0][c]
        enter_ref[1:2, lanes] = enter[1][c]
    twice = jnp.concatenate([state_ref[:rows].astype(BF16) * 2, state_ref[rows:].astype(BF16) * -2], axis=0)
    readout = weights(refs, 96, 96)
    skip, gate_bias = feature_rows(g0, VEC + 1)
    normed = normed_ref[...].astype(F32)
    mixed = folded(dot(twice, readout, NN)) + skip * normed
    cdf = 0.5 * (1.0 + lax.erf(mixed * 0.7071067811865476))
    act = (mixed * cdf).astype(BF16).astype(F32)
    spread_act = spread(act)
    w_gate = jnp.concatenate([gate_ref[f].reshape(256, 128) for f in range(GROUPS)], axis=1)
    logit = dot(spread_act, w_gate, NT)
    logit = jnp.concatenate([logit[:rows], logit[rows:]], axis=1) + gate_bias
    gate = 1.0 / (1.0 + jnp.exp(-logit))
    branch = (act * gate).astype(BF16).astype(F32)
    x = x_ref[...].astype(F32)
    out_ref[...] = (x + branch).astype(BF16)
    up = up_ref[...].astype(F32)
    dlogit = (up * act * gate * (1.0 - gate)).astype(BF16)
    halves = jnp.concatenate([dlogit[:, :256], dlogit[:, 256:]], axis=0)
    d_act = folded(dot(halves, w_gate, NN)) + up * gate
    slope = cdf + mixed * jnp.exp(-0.5 * mixed * mixed) * 0.3989422804014327
    d_mixed = d_act * slope
    dmixed_ref[...] = d_mixed
    dlogit_f = dlogit.astype(F32)
    squares_x, squares_b = x * x, branch * branch
    part = [column_sum(d_mixed * normed), column_sum(dlogit_f), column_sum(squares_x), column_sum(squares_b)]
    for k, value in enumerate(part):
        part_ref[k : k + 1, :] = value
    spread_dy = spread(d_mixed.astype(BF16).astype(F32))
    d_state = dot(spread_dy, readout, NT)
    dstate_ref[:rows] = d_state[:rows] * 2.0
    dstate_ref[rows:] = d_state[rows:] * -2.0
    head = jnp.where(count == 0.0, 1.0, 0.0)
    first = ([], [])
    for c in range(3):
        lanes = slice(128 * c, 128 * c + 128)
        a = (lane_ref[0:1, lanes], -lane_ref[1:2, lanes])
        eight, tail = eighth_powers(a, 0)
        acc = (jnp.zeros((8, 128), F32), jnp.zeros((8, 128), F32))
        for blk in range(rows // 8 - 1, -1, -1):
            here = slice(8 * blk, 8 * blk + 8)
            moved = cmul(eight, acc)
            acc = (
                moved[0] + dstate_ref[here, lanes] * head[here],
                moved[1] + dstate_ref[rows + 8 * blk : rows + 8 * blk + 8, lanes] * head[here],
            )
        total = cmul(tail, acc)
        first[0].append(column_sum(total[0]))
        first[1].append(column_sum(total[1]))
    block_of(first[0], first[1], scratch, tens)
    packet = scratch[...]
    for d in range(blocks):
        send_ref[d] = packet
    d_c = dot(twice, spread_dy, TN).astype(BF16)
    lo = low_half((rows, 128))
    first_units, last_units = [], []
    for c in range(2):
        left = dlogit_f[:, 256 * c : 256 * c + 128]
        right = dlogit_f[:, 256 * c + 128 : 256 * c + 256]
        first_units.append(jnp.where(lo, left, pltpu.roll(right, 64, 1)))
        last_units.append(jnp.where(lo, pltpu.roll(left, 64, 1), right))
    units = jnp.concatenate([jnp.concatenate(first_units, axis=1), jnp.concatenate(last_units, axis=1)], axis=0)
    d_gate = dot(units.astype(BF16), spread_act, TN).astype(BF16)
    for k in range(4):
        for f in range(GROUPS):
            dgate_ref[k, f] = d_gate[64 * k : 64 * k + 64, 128 * f : 128 * f + 128]
    for i in range(4):
        target = away_ref if i % 2 else keep_ref
        for f in range(GROUPS):
            target[i // 2, f, 0:96, :] = d_c[96 * i : 96 * i + 96, 128 * f : 128 * f + 128]
            target[i // 2, f, 96:160, :] = dgate_ref[tens ^ i, f]


def split_rows(value):
    upper = value.astype(BF16)
    return jnp.concatenate([upper, (value - upper.astype(F32)).astype(BF16)], axis=0)


def third_kernel(
    recv_ref, seq_ref, up_ref, normed_ref, xhat_ref, inv_ref, v_ref, lane_ref, row_ref, state_ref, dstate_ref, enter_ref, dmixed_ref,
    part_ref, g0, g1, g2, g3, gin_ref, keep_ref, away_ref, vec_ref, scratch, dv_ref,
):
    refs = (g0, g1, g2, g3)
    tens = tensor_pos()
    rows, width = up_ref.shape
    offsets = offsets_of(seq_ref)
    base = block_pos() * rows
    count = starts_until(offsets, base, rows)
    later = carried(recv_ref, row_ref, offsets, rows, True, scratch, tens)
    at = lax.broadcasted_iota(jnp.int32, (rows, 128), 0)
    before = jnp.where(at == 0, 0.0, pltpu.roll(count, 1, 0))
    keep = jnp.where(count == before, 1.0, 0.0)
    sums = ([], [], [], [])
    for c in range(3):
        lanes = slice(128 * c, 128 * c + 128)
        a = (lane_ref[0:1, lanes], -lane_ref[1:2, lanes])
        bottom = at == rows - 1
        start = (
            dstate_ref[:rows, lanes] + jnp.where(bottom, later[0][c], 0.0),
            dstate_ref[rows:, lanes] + jnp.where(bottom, later[1][c], 0.0),
        )
        adj = scan_chunk(start, a, count, True)
        prev = (
            jnp.where(at == 0, enter_ref[0:1, lanes], pltpu.roll(state_ref[:rows, lanes], 1, 0)) * keep,
            jnp.where(at == 0, enter_ref[1:2, lanes], pltpu.roll(state_ref[rows:, lanes], 1, 0)) * keep,
        )
        v = (v_ref[:rows, lanes], v_ref[rows:, lanes])
        sums[0].append(column_sum(adj[0] * prev[0] + adj[1] * prev[1]))
        sums[1].append(column_sum(adj[1] * prev[0] - adj[0] * prev[1]))
        sums[2].append(column_sum(adj[0] * v[0] + adj[1] * v[1]))
        sums[3].append(column_sum(adj[1] * v[0] - adj[0] * v[1]))
        dv = cmul((lane_ref[2:3, lanes], -lane_ref[3:4, lanes]), adj)
        dv_ref[:rows, lanes] = dv[0].astype(BF16)
        dv_ref[rows:, lanes] = dv[1].astype(BF16)
    dv = dv_ref[...]
    normed = normed_ref[...].astype(F32)
    d_b = dot(dv, spread(normed), TN).astype(BF16)
    for i in range(4):
        for f in range(GROUPS):
            block = d_b[96 * i : 96 * i + 96, 128 * f : 128 * f + 128]
            if i % 2:
                away_ref[(i // 2) * GROUPS + f] = block
            else:
                keep_ref[i // 2, f] = block
    skip, unused = feature_rows(g0, VEC + 1)
    scale, unused = feature_rows(g0, VEC)
    d_normed = folded(dot(dv, weights(refs, 0, 96), NN)) + dmixed_ref[...] * skip
    xhat = xhat_ref[...]
    d_xhat = d_normed * scale
    mean = jnp.sum(d_xhat, axis=1, keepdims=True) / width
    mean_hat = jnp.sum(d_xhat * xhat, axis=1, keepdims=True) / width
    gin_ref[...] = up_ref[...].astype(F32) + inv_ref[:, 0:1] * (d_xhat - mean - xhat * mean_hat)

    vector = [column_sum(d_normed * xhat), column_sum(d_normed), part_ref[0:1, :], part_ref[1:2, :]]
    for k, value in enumerate(vector):
        for c in range(4):
            vec_ref[4 * k + c : 4 * k + c + 1, :] = value[:, 128 * c : 128 * c + 128]
    g = [jnp.concatenate(lanes_to_rows(chunks) + [jnp.zeros((4, 128), F32)], axis=0) for chunks in sums]
    decay, lam, step, abar_re, abar_im, coef_re, coef_im = (row_ref[k] for k in range(7))
    d_abar, d_coef = (g[0], g[1]), (g[2], g[3])
    denom = decay * decay + lam * lam
    numer = (step * abar_re - coef_re, step * abar_im - coef_im)
    ratio = cmul(numer, (-decay / denom, -lam / denom))
    to_lam_a = cmul((step * abar_re, -step * abar_im), d_abar)
    to_lam_c = cmul((ratio[0], -ratio[1]), d_coef)
    g_decay = -(to_lam_a[0] + to_lam_c[0])
    g_lam = to_lam_a[1] + to_lam_c[1]
    slope = cmul((-decay, lam), (abar_re, abar_im))
    g_step = (slope[0] * d_abar[0] + slope[1] * d_abar[1] + abar_re * d_coef[0] + abar_im * d_coef[1]) * step
    for k, value in enumerate((g_decay, g_lam, g_step)):
        for i in range(4):
            vec_ref[pl.ds(16 + 4 * k + (tens ^ i), 1), :] = value[i : i + 1]
    for k in range(2):
        squares = part_ref[2 + k : 3 + k, :]
        total = squares[:, 0:128]
        for c in range(1, 4):
            total = total + squares[:, 128 * c : 128 * c + 128]
        vec_ref[28 + k : 29 + k, :] = total
    vec_ref[30:32, :] = jnp.zeros((2, 128), F32)
    away_ref[2 * GROUPS, 0:64, :] = split_rows(vec_ref[...])
    away_ref[2 * GROUPS, 64:96, :] = jnp.zeros((32, 128), BF16)


def added(a, b):
    return (a.astype(F32) + b.astype(F32)).astype(BF16)


def core_cw_kernel(keep_ref, got_ref, stay_ref, away_ref):
    for f in range(GROUPS):
        stay_ref[f] = added(keep_ref[0, f], got_ref[0, f])
        away_ref[f] = added(keep_ref[1, f], got_ref[1, f])


def joined(packet):
    return packet[0:32].astype(F32) + packet[32:64].astype(F32)


def core_b_kernel(keep_ref, vec_ref, got_ref, stay_ref, total_ref, away_ref):
    for f in range(GROUPS):
        stay_ref[f] = added(keep_ref[0, f], got_ref[f])
        away_ref[f] = added(keep_ref[1, f], got_ref[GROUPS + f])
    total = vec_ref[...] + joined(got_ref[2 * GROUPS, 0:64, :])
    total_ref[...] = total
    away_ref[GROUPS, 0:64, :] = split_rows(total)
    away_ref[GROUPS, 64:96, :] = jnp.zeros((32, 128), BF16)


def last_add_kernel(cw_ref, gotcw_ref, b_ref, vec_ref, gotb_ref, out_ref):
    total = split_rows(vec_ref[...] + joined(gotb_ref[GROUPS, 0:64, :]))
    for f in range(GROUPS):
        out_ref[f, 0:96, :] = added(b_ref[f], gotb_ref[f])
        out_ref[f, 96:256, :] = added(cw_ref[f], gotcw_ref[f])
        out_ref[f, 256:320, :] = total


def finish_vectors(vec, count_all, scale_ref, bias_ref, skip_ref, gbias_ref, decay_ref, lam_ref, step_ref, rms_ref, vec_ref):
    for k, ref in enumerate((scale_ref, bias_ref, skip_ref)):
        for c in range(4):
            ref[:, 128 * c : 128 * c + 128] = vec[4 * k + c : 4 * k + c + 1]
    for k, ref in enumerate((decay_ref, lam_ref, step_ref)):
        for c, chunk in enumerate(rows_to_lanes(vec[16 + 4 * k : 20 + 4 * k])):
            ref[:, 128 * c : 128 * c + 128] = chunk
    total = jnp.sum(vec[28:30], axis=1, keepdims=True)
    lane = lane_iota((1, 2))
    rms_ref[...] = jnp.sqrt(jnp.where(lane == 0, total[0:1], total[1:2]) / count_all)


def finish_kernel(
    count_all, got_ref, dre_ref, dim_ref, ore_ref, oim_ref, glu_ref, gbias_ref,
    scale_ref, bias_ref, skip_ref, decay_ref, lam_ref, step_ref, rms_ref, vec_ref,
):
    def total(start, count):
        value = got_ref[0, start : start + count, :].astype(F32)
        for f in range(1, GROUPS):
            value = value + got_ref[f, start : start + count, :].astype(F32)
        return value

    for start, low_ref, high_ref in ((0, dre_ref, dim_ref), (96, ore_ref, oim_ref)):
        value = total(start, 96)
        low_ref[...] = value[:, 0:64]
        high_ref[...] = pltpu.roll(value, 64, 1)[:, 0:64]
    value = total(192, 64)
    glu_ref[0:64, :] = value[:, 0:64]
    glu_ref[64:128, :] = pltpu.roll(value, 64, 1)[:, 0:64]
    vec = joined(got_ref[0, 256:320, :])
    for f in range(1, GROUPS):
        vec = vec + joined(got_ref[f, 256:320, :])
    vec_ref[...] = vec
    finish_vectors(vec, count_all, scale_ref, bias_ref, skip_ref, None, decay_ref, lam_ref, step_ref, rms_ref, None)
    place = tensor_pos() * GROUPS + lax.axis_index("fsdp")
    row = jnp.broadcast_to(vec_ref[pl.ds(12 + place // 8, 1), :], (8, 128))
    gbias_ref[...] = pltpu.roll(row, 128 - 16 * (place % 8), 1)[0:1, 0:16]


def call(kernel, outs, args, scratch=(), specs=None, limit=24):
    return pl.pallas_call(
        kernel,
        out_shape=outs,
        in_specs=specs or [VM] * len(args),
        out_specs=jax.tree.map(lambda _: VM, outs),
        scratch_shapes=list(scratch),
        compiler_params=pltpu.CompilerParams(vmem_limit_bytes=limit << 20),
    )(*args)


def swap(value, axis):
    return lax.ppermute(value, axis, [(0, 1), (1, 0)])


def on_device(
    layer_in, grad_out, ln_scale, ln_bias, decay_rate, lam_im, log_dt, in_re, in_im, out_re, out_im, skip, glu_weight, glu_bias, seq_lengths
):
    rows, width = layer_in.shape
    fsdp = lax.axis_size("fsdp")
    blocks = fsdp * 4
    count_all = float(rows * blocks * width)
    fast = fsdp == GROUPS
    if fast:
        row = lambda v: v.reshape(1, -1)
        sent = call(
            pack_kernel,
            sds((GROUPS, 272, 128), BF16),
            (in_re, in_im, out_re, out_im, glu_weight, row(ln_scale), row(ln_bias), row(skip), row(glu_bias),
             row(decay_rate), row(lam_im), row(log_dt)),
        )
        g0 = lax.all_to_all(sent, "fsdp", 0, 0, tiled=True)
        g2 = swap(g0, "ty")
        g1 = swap(g0, "tc")
        g3 = swap(g2, "tc")
    else:
        g0, g1, g2, g3 = gathered(ln_scale, ln_bias, decay_rate, lam_im, log_dt, in_re, in_im, out_re, out_im, skip, glu_weight, glu_bias)

    xhat, inverse, normed, v, lane, row_prm, carry = call(
        functools.partial(first_kernel, blocks),
        (sds((rows, width)), sds((rows, 128)), sds((rows, width), BF16), sds((2 * rows, 384)), sds((8, 384)), sds((8, 8, 128)), sds((blocks, 8, 128))),
        (layer_in, seq_lengths, g0, g1, g2, g3),
        [pltpu.VMEM((8, 128), F32)],
        [VM, SM, VM, VM, VM, VM],
    )
    came = lax.all_to_all(carry, AXES, 0, 0, tiled=True)
    layer_out, state, d_state, enter, d_mixed, part, keep_cw, away_cw, carry = call(
        functools.partial(second_kernel, blocks),
        (sds((rows, width), BF16), sds((2 * rows, 384)), sds((2 * rows, 384)), sds((8, 384)), sds((rows, width)), sds((8, width)),
         sds((2, GROUPS, 160, 128), BF16), sds((2, GROUPS, 160, 128), BF16), sds((blocks, 8, 128))),
        (came, seq_lengths, layer_in, grad_out, normed, v, lane, row_prm, g0, g1, g2, g3),
        [pltpu.VMEM((8, 128), F32), pltpu.VMEM((GROUPS, 4, 64, 128), BF16), pltpu.VMEM((4, GROUPS, 64, 128), BF16)],
        [VM, SM] + [VM] * 10,
    )
    came = lax.all_to_all(carry, AXES, 0, 0, tiled=True)
    grad_in, keep_b, away_b, vec = call(
        third_kernel,
        (sds((rows, width)), sds((2, GROUPS, 96, 128), BF16), sds((2 * GROUPS + 1, 96, 128), BF16), sds((32, 128))),
        (came, seq_lengths, grad_out, normed, xhat, inverse, v, lane, row_prm, state, d_state, enter, d_mixed, part, g0, g1, g2, g3),
        [pltpu.VMEM((8, 128), F32), pltpu.VMEM((2 * rows, 384), BF16)],
        [VM, SM] + [VM] * 16,
    )
    if not fast:
        return reduced(layer_out, grad_in, keep_cw, away_cw, keep_b, away_b, vec, count_all, fsdp, width)
    got_cw = swap(away_cw, "tc")
    stay_cw, away_cw = call(
        core_cw_kernel, (sds((GROUPS, 160, 128), BF16), sds((GROUPS, 160, 128), BF16)), (keep_cw, got_cw)
    )
    got_cw = swap(away_cw, "ty")
    got_b = swap(away_b, "tc")
    stay_b, vec, away_b = call(
        core_b_kernel, (sds((GROUPS, 96, 128), BF16), sds((32, 128)), sds((GROUPS + 1, 96, 128), BF16)), (keep_b, vec, got_b)
    )
    got_b = swap(away_b, "ty")
    sent = call(last_add_kernel, sds((GROUPS, 320, 128), BF16), (stay_cw, got_cw, stay_b, vec, got_b))
    got = lax.all_to_all(sent, "fsdp", 0, 0, tiled=True)
    d_re, d_im, d_ore, d_oim, d_glu, d_gbias, d_scale, d_bias, d_skip, g_decay, g_lam, g_step, rms = call(
        functools.partial(finish_kernel, count_all),
        (*[sds((96, 64))] * 4, sds((128, 64)), sds((1, 16)), *[sds((1, 512))] * 3, *[sds((1, 384))] * 3, sds((1, 2))),
        (got,),
        [pltpu.VMEM((32, 128), F32)],
    )
    flat = lambda value: value.reshape(-1)
    return (
        layer_out, grad_in, flat(d_scale), flat(d_bias), flat(g_decay), flat(g_lam), flat(g_step), d_re, d_im, d_ore, d_oim,
        flat(d_skip), d_glu, flat(d_gbias), flat(rms),
    )


def gathered(ln_scale, ln_bias, decay_rate, lam_im, log_dt, in_re, in_im, out_re, out_im, skip, glu_weight, glu_bias):
    tens = tensor_pos()
    full = lambda value, axis: lax.all_gather(value, "fsdp", axis=axis, tiled=True)

    def pair(first, second):
        halves = jnp.stack([first.reshape(-1, GROUPS, 64), second.reshape(-1, GROUPS, 64)], axis=2)
        return halves.reshape(-1, GROUPS, 128).swapaxes(0, 1)

    gate = full(glu_weight, 1)
    units = lambda start: lax.dynamic_slice_in_dim(gate, start, 64, 0)
    vectors = [pair(full(ln_scale, 0)[None], full(ln_bias, 0)[None]), pair(full(skip, 0)[None], full(glu_bias, 0)[None])]
    for value in (decay_rate, lam_im, log_dt):
        value = jnp.pad(value, (0, 32))
        for _ in range(3):
            piece = lax.reduce_precision(value, 8, 7)
            value = value - piece
            vectors.append(jnp.broadcast_to(piece.astype(BF16)[None, None], (GROUPS, 1, 128)))
    vectors.append(jnp.zeros((GROUPS, 5, 128), BF16))
    packet = jnp.concatenate(
        [pair(full(in_re, 1), full(in_im, 1)), pair(full(out_re, 1), full(out_im, 1)), pair(units(tens * 64), units(tens * 64 + 256)), *vectors],
        axis=1,
    )
    everyone = lax.all_gather(packet, ("ty", "tc"), axis=0)
    return [lax.dynamic_index_in_dim(everyone, tens ^ i, 0, keepdims=False) for i in range(4)]


def reduced(layer_out, grad_in, keep_cw, away_cw, keep_b, away_b, vec, count_all, fsdp, width):
    tens = tensor_pos()
    blocks_b = away_b[: 2 * GROUPS].reshape(2, GROUPS, 96, 128)

    def natural(keep, away, first, second):
        four = jnp.stack([keep[0], away[0], keep[1], away[1]]).astype(F32)
        four = jnp.concatenate([lax.dynamic_index_in_dim(four, tens ^ i, 0) for i in range(4)], axis=0)
        halves = four.reshape(4, GROUPS, -1, 2, 64).transpose(3, 0, 2, 1, 4)
        halves = halves.reshape(2, 4, halves.shape[2], width)
        if not first:
            return halves.transpose(1, 0, 2, 3).reshape(-1, width)
        return halves[0].reshape(-1, width), halves[1].reshape(-1, width)

    def scattered(value):
        value = lax.psum_scatter(value, ("ty", "tc"), scatter_dimension=0, tiled=True)
        return lax.psum_scatter(value, "fsdp", scatter_dimension=1, tiled=True)

    d_re, d_im = natural(keep_b, blocks_b, True, True)
    d_ore, d_oim = natural(keep_cw[:, :, :96], away_cw[:, :, :96], True, True)
    d_glu = natural(keep_cw[:, :, 96:], away_cw[:, :, 96:], False, False)
    vec = lax.psum(vec, AXES)
    states = lambda k: vec[16 + 4 * k : 20 + 4 * k, :96].reshape(-1)
    own = width // (4 * fsdp)
    place = tens * fsdp + lax.axis_index("fsdp")
    d_gbias = lax.dynamic_slice_in_dim(vec[12:16].reshape(-1), place * own, own, 0)
    rms = jnp.sqrt(jnp.sum(vec[28:30], axis=1) / count_all)
    return (
        layer_out, grad_in, vec[0:4].reshape(-1), vec[4:8].reshape(-1), states(0), states(1), states(2), scattered(d_re), scattered(d_im),
        scattered(d_ore), scattered(d_oim), vec[8:12].reshape(-1), scattered(d_glu), d_gbias, rms,
    )


def solution(mesh):
    tensor = ("ty", "tc")
    split = Mesh(mesh.devices.reshape(mesh.shape["fsdp"], mesh.shape["tensor"] // 2, 2), AXES)
    tokens, matrix = P(AXES, None), P(tensor, "fsdp")
    return jax.shard_map(
        on_device,
        mesh=split,
        in_specs=(
            tokens, tokens, P("fsdp"), P("fsdp"), P(tensor), P(tensor), P(tensor), matrix, matrix, matrix, matrix,
            P("fsdp"), P(None, "fsdp"), P("fsdp"), P(),
        ),
        out_specs=(
            tokens, tokens, P(), P(), P(), P(), P(), matrix, matrix, matrix, matrix, P(), matrix, P((*tensor, "fsdp")), P(),
        ),
        check_vma=False,
    )
```

```python
import functools

import jax
import jax.numpy as jnp
from jax import lax
from jax.experimental import pallas as pl
from jax.experimental.pallas import tpu as pltpu
from jax.sharding import Mesh
from jax.sharding import PartitionSpec as P

F32 = jnp.float32
BF16 = jnp.bfloat16
FSDP = ("fz", "fx")
TENSOR = ("ty", "tc")
AXES = (*FSDP, *TENSOR)
HBM = pl.BlockSpec(memory_space=pltpu.HBM)
VM = pl.BlockSpec(memory_space=pltpu.VMEM)
SM = pl.BlockSpec(memory_space=pltpu.SMEM)

GROUPS = 8
VEC = 96


def sds(shape, dtype=F32):
    return jax.ShapeDtypeStruct(shape, dtype)


def low_half(shape):
    return lax.broadcasted_iota(jnp.int32, shape, len(shape) - 1) < 64


def lane_iota(shape):
    return lax.broadcasted_iota(jnp.int32, shape, len(shape) - 1)


def dot(a, b, dims):
    return lax.dot_general(a, b, (dims, ((), ())), preferred_element_type=F32)


NT = ((1,), (1,))
NN = ((1,), (0,))
TN = ((0,), (0,))


def spread(x):
    lo = low_half((x.shape[0], 128))
    upper, lower = [], []
    for c in range(x.shape[1] // 128):
        xc = x[:, 128 * c : 128 * c + 128]
        turned = pltpu.roll(xc, 64, 1)
        upper += [jnp.where(lo, xc, 0.0).astype(BF16), jnp.where(lo, turned, 0.0).astype(BF16)]
        lower += [jnp.where(lo, 0.0, turned).astype(BF16), jnp.where(lo, 0.0, xc).astype(BF16)]
    return jnp.concatenate(
        [jnp.concatenate(upper, axis=1), jnp.concatenate(lower, axis=1)], axis=0
    )


def folded(pq):
    rows = pq.shape[0] // 2
    lo = low_half((rows, 128))
    out = []
    for c in range(pq.shape[1] // 256):
        p0, p1 = pq[:rows, 256 * c : 256 * c + 128], pq[:rows, 256 * c + 128 : 256 * c + 256]
        q0, q1 = pq[rows:, 256 * c : 256 * c + 128], pq[rows:, 256 * c + 128 : 256 * c + 256]
        out.append(jnp.where(lo, p0 + pltpu.roll(q0, 64, 1), pltpu.roll(p1, 64, 1) + q1))
    return jnp.concatenate(out, axis=1)


def slot_pos(k):
    return (k % 2) * 2 + (lax.axis_index("tc") ^ (k // 2))


def piece(refs, k, f, start, count):
    return refs[k // 2][f % 2, k % 2, f // 2, start : start + count, :]


def weights(get):
    return jnp.concatenate([jnp.concatenate([get(k, f) for k in range(4)], axis=0) for f in range(GROUPS)], axis=1)


def feature_rows(refs, row):
    lo = low_half((8, 128))
    first, second = [], []
    for c in range(GROUPS // 2):
        a = jnp.broadcast_to(piece(refs, 0, 2 * c, row, 1).astype(F32), (8, 128))
        b = jnp.broadcast_to(piece(refs, 0, 2 * c + 1, row, 1).astype(F32), (8, 128))
        first.append(jnp.where(lo, a, pltpu.roll(b, 64, 1)))
        second.append(jnp.where(lo, pltpu.roll(a, 64, 1), b))
    return jnp.concatenate(first, axis=1)[:1], jnp.concatenate(second, axis=1)[:1]


def rows_to_lanes(rows):
    turned = [rows, pltpu.roll(rows, 96, 1), pltpu.roll(rows, 64, 1), pltpu.roll(rows, 32, 1)]
    lane = lane_iota((1, 128))
    return [
        jnp.where(lane < 96, rows[0:1], turned[1][1:2]),
        jnp.where(lane < 64, turned[1][1:2], turned[2][2:3]),
        jnp.where(lane < 32, turned[2][2:3], turned[3][3:4]),
    ]


def lanes_to_rows(chunks):
    wide = [jnp.broadcast_to(chunk, (8, 128)) for chunk in chunks]
    lane = lane_iota((8, 128))
    r1 = jnp.where(lane < 32, pltpu.roll(wide[0], 32, 1), pltpu.roll(wide[1], 32, 1))
    r2 = jnp.where(lane < 64, pltpu.roll(wide[1], 64, 1), pltpu.roll(wide[2], 64, 1))
    r3 = pltpu.roll(wide[2], 96, 1)
    return [jnp.where(lane < 96, r, 0.0)[:1] for r in (wide[0], r1, r2, r3)]


def cmul(a, b):
    return a[0] * b[0] - a[1] * b[1], a[0] * b[1] + a[1] * b[0]


def tensor_pos():
    return lax.axis_index("ty") * 2 + lax.axis_index("tc")


def fsdp_pos():
    return lax.axis_index("fz") * 2 + lax.axis_index("fx")


def block_pos():
    return fsdp_pos() * 4 + tensor_pos()


def offsets_of(start_ref):
    return [start_ref[n : n + 1, :] for n in range(start_ref.shape[0])]


def starts_until(offsets, base, rows):
    at = (lax.broadcasted_iota(jnp.int32, (rows, 128), 0) + base).astype(F32)
    count = jnp.zeros((rows, 128), F32)
    for off in offsets:
        count = count + jnp.where((at >= off) & (off >= at[0:1]), 1.0, 0.0)
    return count


def no_start(offsets, base, rows):
    link = jnp.ones((1, 128), F32)
    first = (jnp.zeros((1, 128), jnp.int32) + base).astype(F32)
    for off in offsets:
        link = jnp.where((off >= first) & (off < first + rows), 0.0, link)
    return link


def expm1(x):
    series = x * (1 + x / 2 * (1 + x / 3 * (1 + x / 4 * (1 + x / 5 * (1 + x / 6 * (1 + x / 7))))))
    return jnp.where(jnp.abs(x) < 0.25, series, jnp.exp(x) - 1.0)


def discretize(decay_rate, lam_im, log_dt):
    step_size = jnp.exp(log_dt)
    lam_re = -decay_rate
    magnitude = jnp.exp(lam_re * step_size)
    phase = lam_im * step_size
    abar_re = magnitude * jnp.cos(phase)
    abar_im = magnitude * jnp.sin(phase)
    half_sin = jnp.sin(0.5 * phase)
    less_re = expm1(lam_re * step_size) * jnp.cos(phase) - 2.0 * half_sin * half_sin
    denom = lam_re * lam_re + lam_im * lam_im
    coef_re = (less_re * lam_re + abar_im * lam_im) / denom
    coef_im = (abar_im * lam_re - less_re * lam_im) / denom
    return abar_re, abar_im, coef_re, coef_im, step_size


def pack_kernel(*refs):
    *inputs, out_ref, square, four, glu_ref, halves, params, lengths, sems = refs
    seq_hbm, matrices, glu_hbm, features, states = inputs[0], inputs[1:5], inputs[5], inputs[6:10], inputs[10:13]
    units = pl.multiple_of(tensor_pos() * 128, 128)
    pairs = [(ref, four.at[k]) for k, ref in enumerate(matrices)]
    pairs += [(glu_hbm.at[:, pl.ds(units, 128)], glu_ref), (seq_hbm, lengths)]
    pairs += [(ref, halves.at[k]) for k, ref in enumerate(features)]
    pairs += [(ref, params.at[k]) for k, ref in enumerate(states)]
    copies = [pltpu.make_async_copy(source, target, sems.at[k]) for k, (source, target) in enumerate(pairs)]
    for copy in copies:
        copy.start()
    square[:, 96:128] = jnp.zeros((128, 32), F32)
    for copy in copies:
        copy.wait()
    vec = [
        jnp.concatenate([halves[0], halves[1]], axis=1).astype(F32),
        jnp.concatenate([halves[2], halves[3]], axis=1).astype(F32),
    ]
    for k in range(3):
        value = jnp.concatenate([params[k], jnp.zeros((1, 32), F32)], axis=1)
        for _ in range(3):
            part = value.astype(BF16).astype(F32)
            value = value - part
            vec.append(part)
    lane = lane_iota((1, 128))
    upper, lower, total = jnp.zeros((1, 128), jnp.int32), jnp.zeros((1, 128), jnp.int32), 0
    for n in range(lengths.shape[0]):
        upper = jnp.where(lane == n, total >> 8, upper)
        lower = jnp.where(lane == n, total & 255, lower)
        total = total + lengths[n]
    vec += [upper.astype(F32), lower.astype(F32)]
    vec.append(jnp.zeros((16 - len(vec), 128), F32))
    vec = jnp.concatenate(vec, axis=0).astype(BF16)
    pieces = []
    for k in (0, 2):
        square[0:64, 0:96] = four[k].astype(F32)
        square[64:128, 0:96] = four[k + 1].astype(F32)
        pieces.append(square[...].T[0:96].astype(BF16))
    packet = jnp.concatenate([pieces[0], vec, pieces[1], glu_ref[...]], axis=0)
    for z in range(GROUPS // 2):
        out_ref[z] = packet


def params_of(refs, vec_row):
    lane = lane_iota((8, 128))
    out = []
    for k, safe in enumerate((1.0, 0.0, 0.0)):
        rows = []
        for k4 in range(4):
            part = piece(refs, k4, 0, vec_row, 16).astype(F32)
            rows.append((part[2 + 3 * k : 3 + 3 * k] + part[3 + 3 * k : 4 + 3 * k]) + part[4 + 3 * k : 5 + 3 * k])
        value = jnp.concatenate(rows + [jnp.full((4, 128), safe, F32)], axis=0)
        out.append(jnp.where(lane < 96, value, safe))
    return out


def block_of(chunks_re, chunks_im, scratch):
    for half, chunks in ((0, chunks_re), (4, chunks_im)):
        for k, row in enumerate(lanes_to_rows(chunks)):
            scratch[pl.ds(half + slot_pos(k), 1), :] = row


def chunks_from(scratch, half):
    rows = [scratch[pl.ds(half + slot_pos(k), 1), :] for k in range(4)]
    return rows_to_lanes(jnp.concatenate([*rows, jnp.zeros((4, 128), F32)], axis=0))


def norm_kernel(x_ref, g_ref, xhat_ref, inv_ref, normed_ref, wide_ref, feat_ref, start_ref):
    rows, width = x_ref.shape
    x = x_ref[...].astype(F32)
    centered = x - jnp.sum(x, axis=1, keepdims=True) / width
    inverse = lax.rsqrt(jnp.sum(centered * centered, axis=1, keepdims=True) / width + 1e-05)
    xhat = centered * inverse
    xhat_ref[...] = xhat
    inv_ref[...] = jnp.broadcast_to(inverse, (rows, 128))
    scale, bias = feature_rows((g_ref,), VEC)
    feat_ref[0:1] = scale
    feat_ref[1:2], feat_ref[2:3] = feature_rows((g_ref,), VEC + 1)
    normed = (xhat * scale + bias).astype(BF16)
    normed_ref[...] = normed
    wide_ref[...] = spread(normed.astype(F32))
    upper, lower = (piece((g_ref,), 0, 0, VEC + 11 + k, 1).astype(F32) for k in range(2))
    starts = upper * 256.0 + lower
    for n in range(start_ref.shape[0]):
        start_ref[n : n + 1, :] = jnp.broadcast_to(starts[:, n : n + 1], (1, 128))


def first_kernel(blocks, wide_ref, start_ref, g0, g1, v_ref, lane_ref, row_ref, send_ref, scratch):
    refs = (g0, g1)
    rows = wide_ref.shape[0] // 2
    v_ref[...] = dot(wide_ref[...], weights(lambda k, f: piece(refs, k, f, 0, 96)), NT)

    decay, lam, log_dt = params_of(refs, VEC)
    abar_re, abar_im, coef_re, coef_im, step_size = discretize(decay, lam, log_dt)
    power = (abar_re, abar_im)
    per_row = [decay, lam, step_size, abar_re, abar_im, coef_re, coef_im]
    for _ in range(7):
        power = cmul(power, power)
    for half in (0, 1):
        for k in range(4):
            scratch[pl.ds(half * 4 + slot_pos(k), 1), :] = power[half][k : k + 1]
    for k, value in enumerate(per_row):
        row_ref[k] = value
    row_ref[len(per_row)] = scratch[...]
    abar = (rows_to_lanes(abar_re), rows_to_lanes(abar_im))
    coef = (rows_to_lanes(coef_re), rows_to_lanes(coef_im))
    for k, chunks in enumerate((*abar, *coef)):
        for c in range(3):
            lane_ref[k : k + 1, 128 * c : 128 * c + 128] = chunks[c]

    offsets = offsets_of(start_ref)
    count = starts_until(offsets, block_pos() * rows, rows)
    open_tail = jnp.where(count == count[rows - 1 : rows], 1.0, 0.0)
    last = ([], [])
    for c in range(3):
        lanes = slice(128 * c, 128 * c + 128)
        a = (abar[0][c], abar[1][c])
        eight, tail = eighth_powers(a, 7)
        b = (coef[0][c], coef[1][c])
        acc = (jnp.zeros((8, 128), F32), jnp.zeros((8, 128), F32))
        for blk in range(rows // 8):
            here = slice(8 * blk, 8 * blk + 8)
            there = slice(rows + 8 * blk, rows + 8 * blk + 8)
            drive = cmul(b, (v_ref[here, lanes], v_ref[there, lanes]))
            moved = cmul(eight, acc)
            acc = (moved[0] + drive[0] * open_tail[here], moved[1] + drive[1] * open_tail[here])
        total = cmul(tail, acc)
        last[0].append(column_sum(total[0]))
        last[1].append(column_sum(total[1]))
    block_of(last[0], last[1], scratch)
    packet = scratch[...]
    for d in range(blocks):
        send_ref[d] = packet


def local_scan_kernel(start_ref, v_ref, lane_ref, local_ref, power_ref):
    rows = v_ref.shape[0] // 2
    count = starts_until(offsets_of(start_ref), block_pos() * rows, rows)
    for c in range(3):
        lanes = slice(128 * c, 128 * c + 128)
        a = (lane_ref[0:1, lanes], lane_ref[1:2, lanes])
        b = (lane_ref[2:3, lanes], lane_ref[3:4, lanes])
        state = scan_chunk(cmul(b, (v_ref[:rows, lanes], v_ref[rows:, lanes])), a, count, False)
        local_ref[:rows, lanes] = state[0]
        local_ref[rows:, lanes] = state[1]
        eight, power = eighth_powers(a, 0)
        for blk in range(rows // 8):
            power_ref[8 * blk : 8 * blk + 8, lanes] = power[0]
            power_ref[rows + 8 * blk : rows + 8 * blk + 8, lanes] = power[1]
            if blk < rows // 8 - 1:
                power = cmul(power, eight)


def eighth_powers(a, top):
    sub = lax.broadcasted_iota(jnp.int32, (8, 128), 0)
    exponent = (7 - sub) if top == 7 else sub + 1
    a = (jnp.broadcast_to(a[0], (8, 128)), jnp.broadcast_to(a[1], (8, 128)))
    tile = (jnp.ones((8, 128), F32), jnp.zeros((8, 128), F32))
    for bit in range(4):
        if bit == 3:
            eight = a
        taken = (exponent & (1 << bit)) != 0
        more = cmul(tile, a)
        tile = (jnp.where(taken, more[0], tile[0]), jnp.where(taken, more[1], tile[1]))
        a = cmul(a, a)
    return eight, tile


def scan_chunk(value, a, count, reverse):
    rows = count.shape[0]
    at = lax.broadcasted_iota(jnp.int32, (rows, 128), 0)
    step = 1
    while step < rows:
        shift = rows - step if reverse else step
        other = pltpu.roll(count, shift, 0)
        inside = (at < rows - step) if reverse else (at >= step)
        linked = inside & (other == count)
        moved = (pltpu.roll(value[0], shift, 0), pltpu.roll(value[1], shift, 0))
        more = cmul(a, moved)
        value = (value[0] + jnp.where(linked, more[0], 0.0), value[1] + jnp.where(linked, more[1], 0.0))
        a = cmul(a, a)
        step *= 2
    return value


def carried(recv_ref, row_ref, offsets, rows, reverse, scratch):
    blocks = recv_ref.shape[0]
    power = row_ref[7]
    pre, pim = power[0:4], power[4:8]
    if reverse:
        pim = -pim
    place = block_pos()

    def turn(k, state):
        j = blocks - 1 - k if reverse else k
        link = no_start(offsets, j * rows, rows)
        got = recv_ref[j]
        new = cmul((pre * link, pim * link), state)
        return new[0] + got[0:4], new[1] + got[4:8]

    zero = jnp.zeros((4, 128), F32)
    out = lax.fori_loop(0, blocks - 1 - place if reverse else place, turn, (zero, zero))
    scratch[0:4, :] = out[0]
    scratch[4:8, :] = out[1]
    return chunks_from(scratch, 0), chunks_from(scratch, 4)


def column_sum(value):
    return jnp.sum(value, axis=0, keepdims=True)


def second_kernel(
    blocks, recv_ref, start_ref, x_ref, up_ref, normed_ref, lane_ref, row_ref, feat_ref, local_ref, power_ref, g0, g1, g2, g3,
    out_ref, state_ref, twice_ref, dstate_ref, enter_ref, dmixed_ref, act_ref, dlogit_ref, part_ref, send_ref,
    scratch, gate_ref, c_ref,
):
    rows, width = x_ref.shape
    x_pos, y_pos = lax.axis_index("fx"), lax.axis_index("ty")
    offsets = offsets_of(start_ref)
    base = block_pos() * rows
    count = starts_until(offsets, base, rows)
    for i, ref in enumerate((g0, g1, g2, g3)):
        y = y_pos ^ (i % 2)
        tens = y * 2 + (lax.axis_index("tc") ^ (i // 2))
        lanes = pl.ds(pl.multiple_of(tens * 128, 128), 128)
        for j in range(2):
            for z in range(GROUPS // 2):
                f = z * 2 + (x_pos ^ j)
                c_ref[f, (i // 2) * 2 + y] = ref[j, z, 0:96, :]
                gate_ref[pl.ds(pl.multiple_of(f * 64, 64), 64), lanes] = ref[j, z, 96:160, :]
    enter = carried(recv_ref, row_ref, offsets, rows, False, scratch)
    head = jnp.where(count == 0.0, 1.0, 0.0)
    for c in range(3):
        lanes = slice(128 * c, 128 * c + 128)
        power = (power_ref[:rows, lanes] * head, power_ref[rows:, lanes] * head)
        came = cmul(power, (enter[0][c], enter[1][c]))
        state = (local_ref[:rows, lanes] + came[0], local_ref[rows:, lanes] + came[1])
        state_ref[:rows, lanes] = state[0]
        state_ref[rows:, lanes] = state[1]
        twice_ref[:rows, lanes] = state[0].astype(BF16) * 2
        twice_ref[rows:, lanes] = state[1].astype(BF16) * -2
        enter_ref[0:1, lanes] = enter[0][c]
        enter_ref[1:2, lanes] = enter[1][c]
    readout = weights(lambda k, f: c_ref[f, k])
    scale, skip, gate_bias = (feat_ref[k : k + 1] for k in range(3))
    normed = normed_ref[...].astype(F32)
    mixed = folded(dot(twice_ref[...], readout, NN)) + skip * normed
    cdf = 0.5 * (1.0 + lax.erf(mixed * 0.7071067811865476))
    act_low = (mixed * cdf).astype(BF16)
    act_ref[...] = act_low
    act = act_low.astype(F32)
    w_gate = gate_ref[...]
    logit = dot(act_low, w_gate, NN) + gate_bias
    gate = 1.0 / (1.0 + jnp.exp(-logit))
    branch = (act * gate).astype(BF16).astype(F32)
    x = x_ref[...].astype(F32)
    out_ref[...] = (x + branch).astype(BF16)
    up = up_ref[...].astype(F32)
    dlogit = (up * act * gate * (1.0 - gate)).astype(BF16)
    dlogit_ref[...] = dlogit
    d_act = dot(dlogit, w_gate, NT) + up * gate
    slope = cdf + mixed * jnp.exp(-0.5 * mixed * mixed) * 0.3989422804014327
    d_mixed = d_act * slope
    dmixed_ref[...] = d_mixed
    part = [column_sum(d_mixed * normed), column_sum(dlogit.astype(F32)), column_sum(x * x), column_sum(branch * branch)]
    for k, value in enumerate(part):
        part_ref[k : k + 1, :] = value
    d_state = dot(spread(d_mixed.astype(BF16).astype(F32)), readout, NT)
    dstate_ref[:rows] = d_state[:rows] * 2.0
    dstate_ref[rows:] = d_state[rows:] * -2.0
    first = ([], [])
    for c in range(3):
        lanes = slice(128 * c, 128 * c + 128)
        a = (lane_ref[0:1, lanes], -lane_ref[1:2, lanes])
        eight, tail = eighth_powers(a, 0)
        acc = (jnp.zeros((8, 128), F32), jnp.zeros((8, 128), F32))
        for blk in range(rows // 8 - 1, -1, -1):
            here = slice(8 * blk, 8 * blk + 8)
            there = slice(rows + 8 * blk, rows + 8 * blk + 8)
            moved = cmul(eight, acc)
            acc = (moved[0] + dstate_ref[here, lanes] * head[here], moved[1] + dstate_ref[there, lanes] * head[here])
        total = cmul(tail, acc)
        first[0].append(column_sum(total[0]))
        first[1].append(column_sum(total[1]))
    block_of(first[0], first[1], scratch)
    packet = scratch[...]
    for d in range(blocks):
        send_ref[d] = packet


def readout_grad_kernel(twice_ref, dmixed_ref, act_ref, dlogit_ref, keep_ref, away_ref, dgate_ref):
    dy = dmixed_ref[...].astype(BF16).astype(F32)
    d_c = dot(twice_ref[...], spread(dy), TN).astype(BF16)
    dgate_ref[...] = dot(act_ref[...], dlogit_ref[...], TN).astype(BF16)
    for k in range(4):
        target = away_ref if k // 2 else keep_ref
        lanes = pl.ds(pl.multiple_of(slot_pos(k) * 128, 128), 128)
        for f in range(GROUPS):
            target[k % 2, f, 0:96, :] = d_c[96 * k : 96 * k + 96, 128 * f : 128 * f + 128]
            target[k % 2, f, 96:160, :] = dgate_ref[64 * f : 64 * f + 64, lanes]


def back_scan_kernel(start_ref, lane_ref, dstate_ref, local_ref):
    rows = dstate_ref.shape[0] // 2
    count = starts_until(offsets_of(start_ref), block_pos() * rows, rows)
    for c in range(3):
        lanes = slice(128 * c, 128 * c + 128)
        a = (lane_ref[0:1, lanes], -lane_ref[1:2, lanes])
        adj = scan_chunk((dstate_ref[:rows, lanes], dstate_ref[rows:, lanes]), a, count, True)
        local_ref[:rows, lanes] = adj[0]
        local_ref[rows:, lanes] = adj[1]


def split_rows(value):
    upper = value.astype(BF16)
    return jnp.concatenate([upper, (value - upper.astype(F32)).astype(BF16)], axis=0)


def third_kernel(
    recv_ref, start_ref, up_ref, wide_ref, xhat_ref, inv_ref, v_ref, lane_ref, row_ref, feat_ref, state_ref, local_ref, enter_ref,
    dmixed_ref, part_ref, g0, g1, gin_ref, keep_ref, away_ref, vec_ref, scratch, dv_ref,
):
    refs = (g0, g1)
    rows, width = up_ref.shape
    offsets = offsets_of(start_ref)
    base = block_pos() * rows
    count = starts_until(offsets, base, rows)
    later = carried(recv_ref, row_ref, offsets, rows, True, scratch)
    at = lax.broadcasted_iota(jnp.int32, (rows, 128), 0)
    before = jnp.where(at == 0, 0.0, pltpu.roll(count, 1, 0))
    keep = jnp.where(count == before, 1.0, 0.0)
    tail = jnp.where(count == count[rows - 1 : rows], 1.0, 0.0)
    sums = ([], [], [], [])
    for c in range(3):
        lanes = slice(128 * c, 128 * c + 128)
        a = (lane_ref[0:1, lanes], -lane_ref[1:2, lanes])
        eight, power = eighth_powers(a, 7)
        came = cmul(power, (later[0][c], later[1][c]))
        parts = ([], [])
        for blk in range(rows // 8 - 1, -1, -1):
            here = slice(8 * blk, 8 * blk + 8)
            there = slice(rows + 8 * blk, rows + 8 * blk + 8)
            parts[0].insert(0, local_ref[here, lanes] + came[0] * tail[here])
            parts[1].insert(0, local_ref[there, lanes] + came[1] * tail[here])
            came = cmul(came, eight)
        adj = (jnp.concatenate(parts[0], axis=0), jnp.concatenate(parts[1], axis=0))
        prev = (
            jnp.where(at == 0, enter_ref[0:1, lanes], pltpu.roll(state_ref[:rows, lanes], 1, 0)) * keep,
            jnp.where(at == 0, enter_ref[1:2, lanes], pltpu.roll(state_ref[rows:, lanes], 1, 0)) * keep,
        )
        v = (v_ref[:rows, lanes], v_ref[rows:, lanes])
        sums[0].append(column_sum(adj[0] * prev[0] + adj[1] * prev[1]))
        sums[1].append(column_sum(adj[1] * prev[0] - adj[0] * prev[1]))
        sums[2].append(column_sum(adj[0] * v[0] + adj[1] * v[1]))
        sums[3].append(column_sum(adj[1] * v[0] - adj[0] * v[1]))
        dv = cmul((lane_ref[2:3, lanes], -lane_ref[3:4, lanes]), adj)
        dv_ref[:rows, lanes] = dv[0].astype(BF16)
        dv_ref[rows:, lanes] = dv[1].astype(BF16)
    dv = dv_ref[...]
    d_b = dot(dv, wide_ref[...], TN).astype(BF16)
    for k in range(4):
        for f in range(GROUPS):
            block = d_b[96 * k : 96 * k + 96, 128 * f : 128 * f + 128]
            if k // 2:
                away_ref[(k % 2) * GROUPS + f] = block
            else:
                keep_ref[k % 2, f] = block
    scale, skip = feat_ref[0:1], feat_ref[1:2]
    d_normed = folded(dot(dv, weights(lambda k, f: piece(refs, k, f, 0, 96)), NN)) + dmixed_ref[...] * skip
    xhat = xhat_ref[...]
    d_xhat = d_normed * scale
    mean = jnp.sum(d_xhat, axis=1, keepdims=True) / width
    mean_hat = jnp.sum(d_xhat * xhat, axis=1, keepdims=True) / width
    gin_ref[...] = up_ref[...].astype(F32) + inv_ref[:, 0:1] * (d_xhat - mean - xhat * mean_hat)

    vector = [column_sum(d_normed * xhat), column_sum(d_normed), part_ref[0:1, :], part_ref[1:2, :]]
    for k, value in enumerate(vector):
        for c in range(4):
            vec_ref[4 * k + c : 4 * k + c + 1, :] = value[:, 128 * c : 128 * c + 128]
    g = [jnp.concatenate(lanes_to_rows(chunks) + [jnp.zeros((4, 128), F32)], axis=0) for chunks in sums]
    decay, lam, step, abar_re, abar_im, coef_re, coef_im = (row_ref[k] for k in range(7))
    d_abar, d_coef = (g[0], g[1]), (g[2], g[3])
    denom = decay * decay + lam * lam
    numer = (step * abar_re - coef_re, step * abar_im - coef_im)
    ratio = cmul(numer, (-decay / denom, -lam / denom))
    to_lam_a = cmul((step * abar_re, -step * abar_im), d_abar)
    to_lam_c = cmul((ratio[0], -ratio[1]), d_coef)
    g_decay = -(to_lam_a[0] + to_lam_c[0])
    g_lam = to_lam_a[1] + to_lam_c[1]
    slope = cmul((-decay, lam), (abar_re, abar_im))
    g_step = (slope[0] * d_abar[0] + slope[1] * d_abar[1] + abar_re * d_coef[0] + abar_im * d_coef[1]) * step
    for k, value in enumerate((g_decay, g_lam, g_step)):
        for i in range(4):
            vec_ref[pl.ds(16 + 4 * k + slot_pos(i), 1), :] = value[i : i + 1]
    for k in range(2):
        squares = part_ref[2 + k : 3 + k, :]
        total = squares[:, 0:128]
        for c in range(1, 4):
            total = total + squares[:, 128 * c : 128 * c + 128]
        vec_ref[28 + k : 29 + k, :] = total
    vec_ref[30:32, :] = jnp.zeros((2, 128), F32)
    away_ref[2 * GROUPS, 0:64, :] = split_rows(vec_ref[...])
    away_ref[2 * GROUPS, 64:96, :] = jnp.zeros((32, 128), BF16)


def added(a, b):
    return (a.astype(F32) + b.astype(F32)).astype(BF16)


def core_cw_kernel(keep_ref, got_ref, stay_ref, leave_ref):
    y = lax.axis_index("ty")
    for f in range(GROUPS):
        stay_ref[f] = added(keep_ref[y, f], got_ref[y, f])
        leave_ref[f] = added(keep_ref[1 - y, f], got_ref[1 - y, f])


def y_cw_kernel(keep_ref, got_ref, stay_ref, leave_ref):
    x = lax.axis_index("fx")
    for z in range(GROUPS // 2):
        stay_ref[z] = added(keep_ref[2 * z + x], got_ref[2 * z + x])
        leave_ref[z] = added(keep_ref[2 * z + 1 - x], got_ref[2 * z + 1 - x])


def joined(packet):
    return packet[0:32].astype(F32) + packet[32:64].astype(F32)


def core_b_kernel(keep_ref, vec_ref, got_ref, out_ref):
    total = split_rows(vec_ref[...] + joined(got_ref[2 * GROUPS, 0:64, :]))
    for x in range(2):
        for y in range(2):
            for z in range(GROUPS // 2):
                f = 2 * z + x
                out_ref[2 * x + y, 96 * z : 96 * z + 96, :] = added(keep_ref[y, f], got_ref[y * GROUPS + f])
            out_ref[2 * x + y, 384:448, :] = total


def last_add_kernel(cw_ref, gotcw_ref, gotb_ref, out_ref):
    vec = joined(gotb_ref[0, 384:448, :])
    for n in range(1, 4):
        vec = vec + joined(gotb_ref[n, 384:448, :])
    vec = split_rows(vec)
    for z in range(GROUPS // 2):
        here = slice(96 * z, 96 * z + 96)
        value = gotb_ref[0, here, :].astype(F32)
        for n in range(1, 4):
            value = value + gotb_ref[n, here, :].astype(F32)
        out_ref[z, 0:96, :] = value.astype(BF16)
        out_ref[z, 96:256, :] = added(cw_ref[z], gotcw_ref[z])
        out_ref[z, 256:320, :] = vec


def finish_vectors(vec, count_all, scale_ref, bias_ref, skip_ref, gbias_ref, decay_ref, lam_ref, step_ref, rms_ref, vec_ref):
    for k, ref in enumerate((scale_ref, bias_ref, skip_ref)):
        for c in range(4):
            ref[:, 128 * c : 128 * c + 128] = vec[4 * k + c : 4 * k + c + 1]
    for k, ref in enumerate((decay_ref, lam_ref, step_ref)):
        for c, chunk in enumerate(rows_to_lanes(vec[16 + 4 * k : 20 + 4 * k])):
            ref[128 * c : 128 * c + 128] = chunk.reshape(128)
    total = jnp.sum(vec[28:30], axis=1, keepdims=True)
    lane = lane_iota((1, 2))
    rms_ref[...] = jnp.sqrt(jnp.where(lane == 0, total[0:1], total[1:2]) / count_all)


def finish_kernel(
    count_all, got_ref, dre_ref, dim_ref, ore_ref, oim_ref, glu_ref, gbias_ref,
    scale_ref, bias_ref, skip_ref, decay_ref, lam_ref, step_ref, rms_ref, vec_ref, square,
):
    def total(start, count):
        value = got_ref[0, start : start + count, :].astype(F32)
        for z in range(1, GROUPS // 2):
            value = value + got_ref[z, start : start + count, :].astype(F32)
        return value

    for start, first_ref, second_ref in ((0, dre_ref, dim_ref), (96, ore_ref, oim_ref)):
        square[0:96, :] = total(start, 96)
        square[96:128, :] = jnp.zeros((32, 128), F32)
        turned = square[...].T
        first_ref[...] = turned[0:64, 0:96]
        second_ref[...] = turned[64:128, 0:96]
    glu_ref[...] = total(192, 64)
    vec = joined(got_ref[0, 256:320, :])
    for z in range(1, GROUPS // 2):
        vec = vec + joined(got_ref[z, 256:320, :])
    vec_ref[...] = vec
    finish_vectors(vec, count_all, scale_ref, bias_ref, skip_ref, None, decay_ref, lam_ref, step_ref, rms_ref, None)
    place = tensor_pos() * GROUPS + fsdp_pos()
    row = jnp.broadcast_to(vec_ref[pl.ds(12 + place // 8, 1), :], (8, 128))
    gbias_ref[...] = pltpu.roll(row, 128 - 16 * (place % 8), 1)[0:1, 0:16]


TAKES = {
    "pack": 1.5, "norm": 0.3, "first": 1.8, "local_scan": 1.3, "second": 3.0, "readout_grad": 0.7, "back_scan": 1.2, "third": 2.9,
    "finish": 0.7,
}


def call(kernel, outs, args, scratch=(), specs=None, limit=24):
    name = getattr(kernel, "func", kernel).__name__.removesuffix("_kernel")
    return pl.pallas_call(
        kernel,
        out_shape=outs,
        in_specs=specs or [VM] * len(args),
        out_specs=jax.tree.map(lambda _: VM, outs),
        scratch_shapes=list(scratch),
        compiler_params=pltpu.CompilerParams(vmem_limit_bytes=limit << 20),
        cost_estimate=pl.CostEstimate(flops=0, transcendentals=0, bytes_accessed=int(TAKES.get(name, 0.1) * 3.6e6)),
        name=name,
    )(*args)


def tied(value, other):
    return lax.optimization_barrier((value, other))[0]


def swap(value, axis):
    return lax.ppermute(value, axis, [(0, 1), (1, 0)])


def on_device(
    layer_in, grad_out, ln_scale, ln_bias, decay_rate, lam_im, log_dt, in_re, in_im, out_re, out_im, skip, glu_weight, glu_bias, seq_lengths
):
    rows, width = layer_in.shape
    fsdp = lax.axis_size(FSDP)
    blocks = fsdp * 4
    count_all = float(rows * blocks * width)
    fast = fsdp == GROUPS
    if fast:
        row = lambda v: v.reshape(1, -1)
        sent = call(
            pack_kernel,
            sds((GROUPS // 2, 272, 128), BF16),
            (seq_lengths, in_re.T, in_im.T, out_re.T, out_im.T, glu_weight.T, row(ln_scale), row(ln_bias), row(skip), row(glu_bias),
             row(decay_rate), row(lam_im), row(log_dt)),
            [pltpu.VMEM((128, 128), F32), pltpu.VMEM((4, 64, 96), BF16), pltpu.VMEM((64, 128), BF16), pltpu.VMEM((4, 1, 64), BF16),
             pltpu.VMEM((3, 1, 96), F32), pltpu.SMEM(seq_lengths.shape, jnp.int32), pltpu.SemaphoreType.DMA((13,))],
            [HBM] * 13,
            60,
        )
        mine = lax.all_to_all(sent, "fz", 0, 0, tiled=True)
        own_b, own_cw = lax.optimization_barrier((mine[:, :112], mine[:, 112:]))
        side_cw = swap(own_cw, "fx")
        own_b = lax.all_gather(own_b, ("fx", "ty"), axis=0)
        own_b, side_cw = lax.optimization_barrier((own_b, side_cw))
        own_b = own_b.reshape(2, 2, GROUPS // 2, 112, 128)
        g = (own_b, swap(own_b, "tc"))
        own_cw = jnp.stack([own_cw, side_cw])
        far_cw = swap(own_cw, "ty")
    else:
        g, g_cw = gathered(
            ln_scale, ln_bias, decay_rate, lam_im, log_dt, in_re, in_im, out_re, out_im, skip, glu_weight, glu_bias, seq_lengths
        )

    xhat, inverse, normed, wide, feat, starts = call(
        norm_kernel,
        (sds((rows, width)), sds((rows, 128)), sds((rows, width), BF16), sds((2 * rows, 2 * width), BF16), sds((8, width)),
         sds((seq_lengths.shape[0], 128))),
        (layer_in, g[0]),
    )
    v, lane, row_prm, carry = call(
        functools.partial(first_kernel, blocks),
        (sds((2 * rows, 384)), sds((8, 384)), sds((8, 8, 128)), sds((blocks, 8, 128))),
        (wide, starts, *g),
        [pltpu.VMEM((8, 128), F32)],
    )
    came = lax.all_to_all(carry, AXES, 0, 0, tiled=True)
    if fast:
        own_cw, far_cw = tied((own_cw, far_cw), came)
        g_cw = (own_cw, far_cw, swap(own_cw, "tc"), swap(far_cw, "tc"))
    local, power = call(
        local_scan_kernel, (sds((2 * rows, 384)), sds((2 * rows, 384))), (starts, tied(v, came), lane)
    )
    layer_out, state, twice, d_state, enter, d_mixed, act, dlogit, part, carry = call(
        functools.partial(second_kernel, blocks),
        (sds((rows, width), BF16), sds((2 * rows, 384)), sds((2 * rows, 384), BF16), sds((2 * rows, 384)), sds((8, 384)), sds((rows, width)),
         sds((rows, width), BF16), sds((rows, width), BF16), sds((8, width)), sds((blocks, 8, 128))),
        (came, starts, layer_in, grad_out, normed, lane, row_prm, feat, local, power, *g_cw),
        [pltpu.VMEM((8, 128), F32), pltpu.VMEM((width, width), BF16), pltpu.VMEM((GROUPS, 4, 96, 128), BF16)],
    )
    keep_cw, away_cw = call(
        readout_grad_kernel,
        (sds((2, GROUPS, 160, 128), BF16), sds((2, GROUPS, 160, 128), BF16)),
        (twice, d_mixed, act, dlogit),
        [pltpu.VMEM((width, width), BF16)],
    )
    local = call(back_scan_kernel, sds((2 * rows, 384)), (starts, lane, d_state))
    if fast:
        got_cw, local = lax.optimization_barrier((swap(away_cw, "tc"), local))
        stay_cw, leave_cw = call(core_cw_kernel, [sds((GROUPS, 160, 128), BF16)] * 2, (keep_cw, got_cw))
        far_cw = swap(leave_cw, "ty")
        carry = tied(carry, leave_cw)
    came = lax.all_to_all(carry, AXES, 0, 0, tiled=True)
    if fast:
        came, far_cw, stay_cw = lax.optimization_barrier((came, far_cw, stay_cw))
        stay_cw, leave_cw = call(y_cw_kernel, [sds((GROUPS // 2, 160, 128), BF16)] * 2, (stay_cw, far_cw))
        far_cw = swap(leave_cw, "fx")
        came = tied(came, leave_cw)
    grad_in, keep_b, away_b, vec = call(
        third_kernel,
        (sds((rows, width)), sds((2, GROUPS, 96, 128), BF16), sds((2 * GROUPS + 1, 96, 128), BF16), sds((32, 128))),
        (came, starts, grad_out, wide, xhat, inverse, v, lane, row_prm, feat, state, local, enter, d_mixed, part, *g),
        [pltpu.VMEM((8, 128), F32), pltpu.VMEM((2 * rows, 384), BF16)],
    )
    if not fast:
        return reduced(layer_out, grad_in, keep_cw, away_cw, keep_b, away_b, vec, count_all, fsdp, width)
    away_b, far_cw = lax.optimization_barrier((away_b, far_cw))
    got_b = swap(away_b, "tc")
    sent = call(core_b_kernel, sds((4, 448, 128), BF16), (keep_b, vec, got_b))
    got_b = lax.all_to_all(sent, ("fx", "ty"), 0, 0, tiled=True)
    sent = call(last_add_kernel, sds((GROUPS // 2, 320, 128), BF16), (stay_cw, far_cw, got_b))
    got = lax.all_to_all(sent, "fz", 0, 0, tiled=True)
    d_re, d_im, d_ore, d_oim, d_glu, d_gbias, d_scale, d_bias, d_skip, g_decay, g_lam, g_step, rms = call(
        functools.partial(finish_kernel, count_all),
        (*[sds((64, 96))] * 4, sds((64, 128)), sds((1, 16)), *[sds((1, 512))] * 3, *[sds((384,))] * 3, sds((1, 2))),
        (got,),
        [pltpu.VMEM((32, 128), F32), pltpu.VMEM((128, 128), F32)],
    )
    flat = lambda value: value.reshape(-1)
    return (
        layer_out, grad_in, flat(d_scale), flat(d_bias), g_decay, g_lam, g_step, d_re.T, d_im.T, d_ore.T, d_oim.T,
        flat(d_skip), d_glu.T, flat(d_gbias), flat(rms),
    )


def gathered(ln_scale, ln_bias, decay_rate, lam_im, log_dt, in_re, in_im, out_re, out_im, skip, glu_weight, glu_bias, seq_lengths):
    tens = tensor_pos()
    full = lambda value, axis: lax.all_gather(value, FSDP, axis=axis, tiled=True)

    def pair(first, second):
        halves = jnp.stack([first.reshape(-1, GROUPS, 64), second.reshape(-1, GROUPS, 64)], axis=2)
        return halves.reshape(-1, GROUPS, 128).swapaxes(0, 1)

    gate = lax.dynamic_slice_in_dim(full(glu_weight, 1), tens * 128, 128, 0).T.reshape(GROUPS, 64, 128)
    vectors = [pair(full(ln_scale, 0)[None], full(ln_bias, 0)[None]), pair(full(skip, 0)[None], full(glu_bias, 0)[None])]
    for value in (decay_rate, lam_im, log_dt):
        value = jnp.pad(value, (0, 32))
        for _ in range(3):
            piece = lax.reduce_precision(value, 8, 7)
            value = value - piece
            vectors.append(jnp.broadcast_to(piece.astype(BF16)[None, None], (GROUPS, 1, 128)))
    starts = jnp.cumsum(seq_lengths) - seq_lengths
    for value in (starts >> 8, starts & 255):
        value = jnp.pad(value, (0, 128 - value.shape[0])).astype(BF16)
        vectors.append(jnp.broadcast_to(value[None, None], (GROUPS, 1, 128)))
    vectors.append(jnp.zeros((GROUPS, 3, 128), BF16))
    packet = jnp.concatenate(
        [pair(full(in_re, 1), full(in_im, 1)), *vectors, pair(full(out_re, 1), full(out_im, 1)), gate],
        axis=1,
    )
    everyone = lax.all_gather(packet, TENSOR, axis=0).reshape(2, 2, GROUPS // 2, 2, 272, 128)
    x, y, core = (lax.axis_index(axis) for axis in ("fx", "ty", "tc"))
    of_core = lambda c: lax.dynamic_index_in_dim(everyone, c, 1, keepdims=False)
    g = [of_core(core ^ i).transpose(2, 0, 1, 3, 4)[:, :, :, :112] for i in range(2)]
    g_cw = []
    for i in range(4):
        picked = lax.dynamic_index_in_dim(of_core(core ^ (i // 2)), y ^ (i % 2), 0, keepdims=False)
        g_cw.append(jnp.stack([lax.dynamic_index_in_dim(picked, x ^ j, 1, keepdims=False)[:, 112:] for j in range(2)]))
    return g, g_cw


def reduced(layer_out, grad_in, keep_cw, away_cw, keep_b, away_b, vec, count_all, fsdp, width):
    tens, core = tensor_pos(), lax.axis_index("tc")
    blocks_b = away_b[: 2 * GROUPS].reshape(2, GROUPS, 96, 128)

    def canonical(keep, away):
        both = jnp.stack([keep, away]).astype(F32)
        both = jnp.concatenate([lax.dynamic_index_in_dim(both, core ^ i, 0) for i in range(2)], axis=0)
        return both.swapaxes(0, 1).reshape(4, *keep.shape[1:])

    def natural(keep, away):
        halves = canonical(keep, away).reshape(4, GROUPS, -1, 2, 64).transpose(3, 0, 2, 1, 4)
        return halves[0].reshape(-1, width), halves[1].reshape(-1, width)

    def scattered(value):
        value = lax.psum_scatter(value, TENSOR, scatter_dimension=0, tiled=True)
        return lax.psum_scatter(value, FSDP, scatter_dimension=1, tiled=True)

    d_re, d_im = natural(keep_b, blocks_b)
    d_ore, d_oim = natural(keep_cw[:, :, :96], away_cw[:, :, :96])
    d_glu = canonical(keep_cw[:, :, 96:], away_cw[:, :, 96:]).reshape(4, width, 128).swapaxes(1, 2).reshape(-1, width)
    vec = lax.psum(vec, AXES)
    states = lambda k: vec[16 + 4 * k : 20 + 4 * k, :96].reshape(-1)
    own = width // (4 * fsdp)
    place = tens * fsdp + fsdp_pos()
    d_gbias = lax.dynamic_slice_in_dim(vec[12:16].reshape(-1), place * own, own, 0)
    rms = jnp.sqrt(jnp.sum(vec[28:30], axis=1) / count_all)
    return (
        layer_out, grad_in, vec[0:4].reshape(-1), vec[4:8].reshape(-1), states(0), states(1), states(2), scattered(d_re), scattered(d_im),
        scattered(d_ore), scattered(d_oim), vec[8:12].reshape(-1), scattered(d_glu), d_gbias, rms,
    )


def solution(mesh):
    shape = (mesh.shape["fsdp"] // 2, 2, mesh.shape["tensor"] // 2, 2)
    split = Mesh(mesh.devices.reshape(shape), AXES)
    tokens, matrix = P(AXES, None), P(TENSOR, FSDP)
    return jax.shard_map(
        on_device,
        mesh=split,
        in_specs=(
            tokens, tokens, P(FSDP), P(FSDP), P(TENSOR), P(TENSOR), P(TENSOR), matrix, matrix, matrix, matrix,
            P(FSDP), P(None, FSDP), P(FSDP), P(),
        ),
        out_specs=(
            tokens, tokens, P(), P(), P(), P(), P(), matrix, matrix, matrix, matrix, P(), matrix, P((*TENSOR, *FSDP)), P(),
        ),
        check_vma=False,
    )
```

```python
import functools

import jax
import jax.numpy as jnp
from jax import lax
from jax.experimental import pallas as pl
from jax.experimental.pallas import tpu as pltpu
from jax.sharding import Mesh
from jax.sharding import PartitionSpec as P

F32 = jnp.float32
BF16 = jnp.bfloat16
FSDP = ("fz", "fx")
TENSOR = ("ty", "tc")
AXES = (*FSDP, *TENSOR)
HBM = pl.BlockSpec(memory_space=pltpu.HBM)
VM = pl.BlockSpec(memory_space=pltpu.VMEM)
SM = pl.BlockSpec(memory_space=pltpu.SMEM)

GROUPS = 8
VEC = 96


def sds(shape, dtype=F32):
    return jax.ShapeDtypeStruct(shape, dtype)


def low_half(shape):
    return lax.broadcasted_iota(jnp.int32, shape, len(shape) - 1) < 64


def lane_iota(shape):
    return lax.broadcasted_iota(jnp.int32, shape, len(shape) - 1)


def dot(a, b, dims):
    return lax.dot_general(a, b, (dims, ((), ())), preferred_element_type=F32)


NT = ((1,), (1,))
NN = ((1,), (0,))
TN = ((0,), (0,))


def flipped():
    return lax.axis_index("fx") == 1


def spread(x):
    lo = low_half((x.shape[0], 128))
    flip = flipped()
    upper, lower = [], []
    for c in range(x.shape[1] // 128):
        xc = x[:, 128 * c : 128 * c + 128]
        turned = pltpu.roll(xc, 64, 1)
        xc, turned = jnp.where(flip, turned, xc), jnp.where(flip, xc, turned)
        upper += [jnp.where(lo, xc, 0.0).astype(BF16), jnp.where(lo, turned, 0.0).astype(BF16)]
        lower += [jnp.where(lo, 0.0, turned).astype(BF16), jnp.where(lo, 0.0, xc).astype(BF16)]
    return jnp.concatenate(
        [jnp.concatenate(upper, axis=1), jnp.concatenate(lower, axis=1)], axis=0
    )


def folded(pq):
    rows = pq.shape[0] // 2
    lo = low_half((rows, 128))
    flip = flipped()
    out = []
    for c in range(pq.shape[1] // 256):
        p0, p1 = pq[:rows, 256 * c : 256 * c + 128], pq[:rows, 256 * c + 128 : 256 * c + 256]
        q0, q1 = pq[rows:, 256 * c : 256 * c + 128], pq[rows:, 256 * c + 128 : 256 * c + 256]
        even = jnp.where(lo, p0, q1) + jnp.where(lo, pltpu.roll(q0, 64, 1), pltpu.roll(p1, 64, 1))
        out.append(jnp.where(flip, pltpu.roll(even, 64, 1), even))
    return jnp.concatenate(out, axis=1)


def slot_pos(k):
    return tensor_pos() ^ ((k % 2) * 2 + k // 2)


def piece(refs, k, f, start, count):
    return refs[k // 2][f % 2, k % 2, f // 2, start : start + count, :]


def weights(get):
    return jnp.concatenate([jnp.concatenate([get(k, f) for k in range(4)], axis=0) for f in range(GROUPS)], axis=1)


def feature_rows(refs, row):
    lo = low_half((8, 128))
    flip = flipped()
    first, second = [], []
    for c in range(GROUPS // 2):
        a = jnp.broadcast_to(piece(refs, 0, 2 * c, row, 1).astype(F32), (8, 128))
        b = jnp.broadcast_to(piece(refs, 0, 2 * c + 1, row, 1).astype(F32), (8, 128))
        a, b = jnp.where(flip, b, a), jnp.where(flip, a, b)
        first.append(jnp.where(lo, a, pltpu.roll(b, 64, 1)))
        second.append(jnp.where(lo, pltpu.roll(a, 64, 1), b))
    return jnp.concatenate(first, axis=1)[:1], jnp.concatenate(second, axis=1)[:1]


def rows_to_lanes(rows):
    turned = [rows, pltpu.roll(rows, 96, 1), pltpu.roll(rows, 64, 1), pltpu.roll(rows, 32, 1)]
    lane = lane_iota((1, 128))
    return [
        jnp.where(lane < 96, rows[0:1], turned[1][1:2]),
        jnp.where(lane < 64, turned[1][1:2], turned[2][2:3]),
        jnp.where(lane < 32, turned[2][2:3], turned[3][3:4]),
    ]


def lanes_to_rows(chunks):
    wide = [jnp.broadcast_to(chunk, (8, 128)) for chunk in chunks]
    lane = lane_iota((8, 128))
    r1 = jnp.where(lane < 32, pltpu.roll(wide[0], 32, 1), pltpu.roll(wide[1], 32, 1))
    r2 = jnp.where(lane < 64, pltpu.roll(wide[1], 64, 1), pltpu.roll(wide[2], 64, 1))
    r3 = pltpu.roll(wide[2], 96, 1)
    return [jnp.where(lane < 96, r, 0.0)[:1] for r in (wide[0], r1, r2, r3)]


def cmul(a, b):
    return a[0] * b[0] - a[1] * b[1], a[0] * b[1] + a[1] * b[0]


def tensor_pos():
    return lax.axis_index("ty") * 2 + lax.axis_index("tc")


def fsdp_pos():
    return lax.axis_index("fz") * 2 + lax.axis_index("fx")


def block_pos():
    return fsdp_pos() * 4 + tensor_pos()


def offsets_of(start_ref):
    return [start_ref[n : n + 1, :] for n in range(start_ref.shape[0])]


def starts_until(offsets, base, rows):
    at = (lax.broadcasted_iota(jnp.int32, (rows, 128), 0) + base).astype(F32)
    count = jnp.zeros((rows, 128), F32)
    for off in offsets:
        count = count + jnp.where((at >= off) & (off >= at[0:1]), 1.0, 0.0)
    return count


def no_start(offsets, base, rows):
    link = jnp.ones((1, 128), F32)
    first = (jnp.zeros((1, 128), jnp.int32) + base).astype(F32)
    for off in offsets:
        link = jnp.where((off >= first) & (off < first + rows), 0.0, link)
    return link


def expm1(x):
    series = x * (1 + x / 2 * (1 + x / 3 * (1 + x / 4 * (1 + x / 5 * (1 + x / 6 * (1 + x / 7))))))
    return jnp.where(jnp.abs(x) < 0.25, series, jnp.exp(x) - 1.0)


def discretize(decay_rate, lam_im, log_dt):
    step_size = jnp.exp(log_dt)
    lam_re = -decay_rate
    magnitude = jnp.exp(lam_re * step_size)
    phase = lam_im * step_size
    abar_re = magnitude * jnp.cos(phase)
    abar_im = magnitude * jnp.sin(phase)
    half_sin = jnp.sin(0.5 * phase)
    less_re = expm1(lam_re * step_size) * jnp.cos(phase) - 2.0 * half_sin * half_sin
    denom = lam_re * lam_re + lam_im * lam_im
    coef_re = (less_re * lam_re + abar_im * lam_im) / denom
    coef_im = (abar_im * lam_re - less_re * lam_im) / denom
    return abar_re, abar_im, coef_re, coef_im, step_size


def pack_kernel(*refs):
    *inputs, out_ref, square, four, glu_ref, halves, params, lengths, sems = refs
    seq_hbm, matrices, glu_hbm, features, states = inputs[0], inputs[1:5], inputs[5], inputs[6:10], inputs[10:13]
    units = pl.multiple_of(tensor_pos() * 128, 128)
    pairs = [(ref, four.at[k]) for k, ref in enumerate(matrices)]
    pairs += [(glu_hbm.at[:, pl.ds(units, 128)], glu_ref), (seq_hbm, lengths)]
    pairs += [(ref, halves.at[k]) for k, ref in enumerate(features)]
    pairs += [(ref, params.at[k]) for k, ref in enumerate(states)]
    copies = [pltpu.make_async_copy(source, target, sems.at[k]) for k, (source, target) in enumerate(pairs)]
    for copy in copies:
        copy.start()
    square[:, 96:128] = jnp.zeros((128, 32), F32)
    for copy in copies:
        copy.wait()
    vec = [
        jnp.concatenate([halves[0], halves[1]], axis=1).astype(F32),
        jnp.concatenate([halves[2], halves[3]], axis=1).astype(F32),
    ]
    for k in range(3):
        value = jnp.concatenate([params[k], jnp.zeros((1, 32), F32)], axis=1)
        for _ in range(3):
            part = value.astype(BF16).astype(F32)
            value = value - part
            vec.append(part)
    lane = lane_iota((1, 128))
    upper, lower, total = jnp.zeros((1, 128), jnp.int32), jnp.zeros((1, 128), jnp.int32), 0
    for n in range(lengths.shape[0]):
        upper = jnp.where(lane == n, total >> 8, upper)
        lower = jnp.where(lane == n, total & 255, lower)
        total = total + lengths[n]
    vec += [upper.astype(F32), lower.astype(F32)]
    vec.append(jnp.zeros((16 - len(vec), 128), F32))
    vec = jnp.concatenate(vec, axis=0).astype(BF16)
    pieces = []
    for k in (0, 2):
        square[0:64, 0:96] = four[k].astype(F32)
        square[64:128, 0:96] = four[k + 1].astype(F32)
        pieces.append(square[...].T[0:96].astype(BF16))
    packet = jnp.concatenate([pieces[0], vec, pieces[1], glu_ref[...]], axis=0)
    for z in range(GROUPS // 2):
        out_ref[z] = packet


def params_of(refs, vec_row):
    lane = lane_iota((8, 128))
    out = []
    for k, safe in enumerate((1.0, 0.0, 0.0)):
        rows = []
        for k4 in range(4):
            part = piece(refs, k4, 0, vec_row, 16).astype(F32)
            rows.append((part[2 + 3 * k : 3 + 3 * k] + part[3 + 3 * k : 4 + 3 * k]) + part[4 + 3 * k : 5 + 3 * k])
        value = jnp.concatenate(rows + [jnp.full((4, 128), safe, F32)], axis=0)
        out.append(jnp.where(lane < 96, value, safe))
    return out


def block_of(chunks_re, chunks_im, scratch):
    for half, chunks in ((0, chunks_re), (4, chunks_im)):
        for k, row in enumerate(lanes_to_rows(chunks)):
            scratch[pl.ds(half + slot_pos(k), 1), :] = row


def chunks_from(scratch, half):
    rows = [scratch[pl.ds(half + slot_pos(k), 1), :] for k in range(4)]
    return rows_to_lanes(jnp.concatenate([*rows, jnp.zeros((4, 128), F32)], axis=0))


def standardize_kernel(x_ref, xhat_ref, inv_ref):
    rows, width = x_ref.shape
    x = x_ref[...].astype(F32)
    centered = x - jnp.sum(x, axis=1, keepdims=True) / width
    inverse = lax.rsqrt(jnp.sum(centered * centered, axis=1, keepdims=True) / width + 1e-05)
    xhat_ref[...] = centered * inverse
    inv_ref[...] = jnp.broadcast_to(inverse, (rows, 128))


def norm_kernel(xhat_ref, g_ref, normed_ref, wide_ref, feat_ref, start_ref):
    scale, bias = feature_rows((g_ref,), VEC)
    feat_ref[0:1] = scale
    feat_ref[1:2], feat_ref[2:3] = feature_rows((g_ref,), VEC + 1)
    normed = (xhat_ref[...] * scale + bias).astype(BF16)
    normed_ref[...] = normed
    wide_ref[...] = spread(normed.astype(F32))
    upper, lower = (piece((g_ref,), 0, 0, VEC + 11 + k, 1).astype(F32) for k in range(2))
    starts = upper * 256.0 + lower
    for n in range(start_ref.shape[0]):
        start_ref[n : n + 1, :] = jnp.broadcast_to(starts[:, n : n + 1], (1, 128))


def first_kernel(blocks, wide_ref, start_ref, g0, g1, v_ref, lane_ref, row_ref, send_ref, scratch):
    refs = (g0, g1)
    rows = wide_ref.shape[0] // 2
    v_ref[...] = dot(wide_ref[...], weights(lambda k, f: piece(refs, k, f, 0, 96)), NT)

    decay, lam, log_dt = params_of(refs, VEC)
    abar_re, abar_im, coef_re, coef_im, step_size = discretize(decay, lam, log_dt)
    power = (abar_re, abar_im)
    per_row = [decay, lam, step_size, abar_re, abar_im, coef_re, coef_im]
    for _ in range(7):
        power = cmul(power, power)
    for half in (0, 1):
        for k in range(4):
            scratch[pl.ds(half * 4 + slot_pos(k), 1), :] = power[half][k : k + 1]
    for k, value in enumerate(per_row):
        row_ref[k] = value
    row_ref[len(per_row)] = scratch[...]
    abar = (rows_to_lanes(abar_re), rows_to_lanes(abar_im))
    coef = (rows_to_lanes(coef_re), rows_to_lanes(coef_im))
    for k, chunks in enumerate((*abar, *coef)):
        for c in range(3):
            lane_ref[k : k + 1, 128 * c : 128 * c + 128] = chunks[c]

    offsets = offsets_of(start_ref)
    count = starts_until(offsets, block_pos() * rows, rows)
    open_tail = jnp.where(count == count[rows - 1 : rows], 1.0, 0.0)
    last = ([], [])
    for c in range(3):
        lanes = slice(128 * c, 128 * c + 128)
        a = (abar[0][c], abar[1][c])
        eight, tail = eighth_powers(a, 7)
        b = (coef[0][c], coef[1][c])
        acc = (jnp.zeros((8, 128), F32), jnp.zeros((8, 128), F32))
        for blk in range(rows // 8):
            here = slice(8 * blk, 8 * blk + 8)
            there = slice(rows + 8 * blk, rows + 8 * blk + 8)
            drive = cmul(b, (v_ref[here, lanes], v_ref[there, lanes]))
            moved = cmul(eight, acc)
            acc = (moved[0] + drive[0] * open_tail[here], moved[1] + drive[1] * open_tail[here])
        total = cmul(tail, acc)
        last[0].append(column_sum(total[0]))
        last[1].append(column_sum(total[1]))
    block_of(last[0], last[1], scratch)
    packet = scratch[...]
    for d in range(blocks):
        send_ref[d] = packet


def states_kernel(recv_ref, start_ref, v_ref, lane_ref, row_ref, state_ref, twice_ref, enter_ref, scratch):
    rows = v_ref.shape[0] // 2
    offsets = offsets_of(start_ref)
    base = block_pos() * rows
    count = starts_until(offsets, base, rows)
    enter = carried(recv_ref, row_ref, offsets, rows, False, scratch)
    keep_first = no_start(offsets, base, 1)
    top = lax.broadcasted_iota(jnp.int32, (rows, 128), 0) == 0
    for c in range(3):
        lanes = slice(128 * c, 128 * c + 128)
        a = (lane_ref[0:1, lanes], lane_ref[1:2, lanes])
        b = (lane_ref[2:3, lanes], lane_ref[3:4, lanes])
        drive = cmul(b, (v_ref[:rows, lanes], v_ref[rows:, lanes]))
        came = cmul((a[0] * keep_first, a[1] * keep_first), (enter[0][c], enter[1][c]))
        drive = (drive[0] + jnp.where(top, came[0], 0.0), drive[1] + jnp.where(top, came[1], 0.0))
        state = scan_chunk(drive, a, count, False)
        state_ref[:rows, lanes] = state[0]
        state_ref[rows:, lanes] = state[1]
        twice_ref[:rows, lanes] = state[0].astype(BF16) * 2
        twice_ref[rows:, lanes] = state[1].astype(BF16) * -2
        enter_ref[0:1, lanes] = enter[0][c]
        enter_ref[1:2, lanes] = enter[1][c]


def eighth_powers(a, top):
    sub = lax.broadcasted_iota(jnp.int32, (8, 128), 0)
    exponent = (7 - sub) if top == 7 else sub + 1
    a = (jnp.broadcast_to(a[0], (8, 128)), jnp.broadcast_to(a[1], (8, 128)))
    tile = (jnp.ones((8, 128), F32), jnp.zeros((8, 128), F32))
    for bit in range(4):
        if bit == 3:
            eight = a
        taken = (exponent & (1 << bit)) != 0
        more = cmul(tile, a)
        tile = (jnp.where(taken, more[0], tile[0]), jnp.where(taken, more[1], tile[1]))
        a = cmul(a, a)
    return eight, tile


def scan_chunk(value, a, count, reverse):
    rows = count.shape[0]
    at = lax.broadcasted_iota(jnp.int32, (rows, 128), 0)
    step = 1
    while step < rows:
        shift = rows - step if reverse else step
        other = pltpu.roll(count, shift, 0)
        inside = (at < rows - step) if reverse else (at >= step)
        linked = inside & (other == count)
        moved = (pltpu.roll(value[0], shift, 0), pltpu.roll(value[1], shift, 0))
        more = cmul(a, moved)
        value = (value[0] + jnp.where(linked, more[0], 0.0), value[1] + jnp.where(linked, more[1], 0.0))
        a = cmul(a, a)
        step *= 2
    return value


def carried(recv_ref, row_ref, offsets, rows, reverse, scratch):
    blocks = recv_ref.shape[0]
    power = row_ref[7]
    pre, pim = power[0:4], power[4:8]
    if reverse:
        pim = -pim
    place = block_pos()

    def turn(k, state):
        j = blocks - 1 - k if reverse else k
        link = no_start(offsets, j * rows, rows)
        got = recv_ref[j]
        new = cmul((pre * link, pim * link), state)
        return new[0] + got[0:4], new[1] + got[4:8]

    zero = jnp.zeros((4, 128), F32)
    out = lax.fori_loop(0, blocks - 1 - place if reverse else place, turn, (zero, zero))
    scratch[0:4, :] = out[0]
    scratch[4:8, :] = out[1]
    return chunks_from(scratch, 0), chunks_from(scratch, 4)


def column_sum(value):
    return jnp.sum(value, axis=0, keepdims=True)


def second_kernel(
    blocks, twice_ref, start_ref, up_ref, normed_ref, lane_ref, feat_ref, g0, g1, g2, g3,
    branch_ref, dstate_ref, dmixed_ref, act_ref, dlogit_ref, send_ref, scratch, gate_ref,
):
    rows, width = up_ref.shape
    offsets = offsets_of(start_ref)
    count = starts_until(offsets, block_pos() * rows, rows)
    slots = (g0, g1, g2, g3)
    for k in range(4):
        lanes = pl.ds(pl.multiple_of(slot_pos(k) * 128, 128), 128)
        for f in range(GROUPS):
            place = (f // 2) * 2 + (lax.axis_index("fx") ^ (f % 2))
            gate_ref[pl.ds(pl.multiple_of(place * 64, 64), 64), lanes] = slots[k][f % 2, f // 2, 96:160, :]
    head = jnp.where(count == 0.0, 1.0, 0.0)
    readout = weights(lambda k, f: slots[k][f % 2, f // 2, 0:96, :])
    scale, skip, gate_bias = (feat_ref[k : k + 1] for k in range(3))
    normed = normed_ref[...].astype(F32)
    mixed = folded(dot(twice_ref[...], readout, NN)) + skip * normed
    cdf = 0.5 * (1.0 + lax.erf(mixed * 0.7071067811865476))
    act_low = (mixed * cdf).astype(BF16)
    act_ref[...] = act_low
    act = act_low.astype(F32)
    w_gate = gate_ref[...]
    logit = dot(act_low, w_gate, NN) + gate_bias
    gate = 1.0 / (1.0 + jnp.exp(-logit))
    branch_ref[...] = (act * gate).astype(BF16)
    up = up_ref[...].astype(F32)
    dlogit = (up * act * gate * (1.0 - gate)).astype(BF16)
    dlogit_ref[...] = dlogit
    d_act = dot(dlogit, w_gate, NT) + up * gate
    slope = cdf + mixed * jnp.exp(-0.5 * mixed * mixed) * 0.3989422804014327
    d_mixed = d_act * slope
    dmixed_ref[...] = d_mixed
    d_state = dot(spread(d_mixed.astype(BF16).astype(F32)), readout, NT)
    dstate_ref[:rows] = d_state[:rows] * 2.0
    dstate_ref[rows:] = d_state[rows:] * -2.0
    first = ([], [])
    for c in range(3):
        lanes = slice(128 * c, 128 * c + 128)
        a = (lane_ref[0:1, lanes], -lane_ref[1:2, lanes])
        eight, tail = eighth_powers(a, 0)
        acc = (jnp.zeros((8, 128), F32), jnp.zeros((8, 128), F32))
        for blk in range(rows // 8 - 1, -1, -1):
            here = slice(8 * blk, 8 * blk + 8)
            there = slice(rows + 8 * blk, rows + 8 * blk + 8)
            moved = cmul(eight, acc)
            acc = (moved[0] + dstate_ref[here, lanes] * head[here], moved[1] + dstate_ref[there, lanes] * head[here])
        total = cmul(tail, acc)
        first[0].append(column_sum(total[0]))
        first[1].append(column_sum(total[1]))
    block_of(first[0], first[1], scratch)
    packet = scratch[...]
    for d in range(blocks):
        send_ref[d] = packet


def sums_kernel(x_ref, branch_ref, normed_ref, dmixed_ref, dlogit_ref, out_ref, part_ref):
    x = x_ref[...].astype(F32)
    branch = branch_ref[...].astype(F32)
    out_ref[...] = (x + branch).astype(BF16)
    skip = column_sum(dmixed_ref[...] * normed_ref[...].astype(F32))
    for k, value in enumerate((skip, column_sum(dlogit_ref[...].astype(F32)), column_sum(x * x), column_sum(branch * branch))):
        part_ref[k : k + 1, :] = value


def readout_grad_kernel(twice_ref, dmixed_ref, act_ref, dlogit_ref, keep_ref, away_ref, dgate_ref):
    dy = dmixed_ref[...].astype(BF16).astype(F32)
    d_c = dot(twice_ref[...], spread(dy), TN).astype(BF16)
    dgate_ref[...] = dot(act_ref[...], dlogit_ref[...], TN).astype(BF16)
    for k in range(4):
        target = away_ref if k // 2 else keep_ref
        lanes = pl.ds(pl.multiple_of(slot_pos(k) * 128, 128), 128)
        for f in range(GROUPS):
            target[k % 2, f, 0:96, :] = d_c[96 * k : 96 * k + 96, 128 * f : 128 * f + 128]
            rows = pl.ds(pl.multiple_of(((f // 2) * 2 + (lax.axis_index("fx") ^ (f % 2))) * 64, 64), 64)
            target[k % 2, f, 96:160, :] = dgate_ref[rows, lanes]


def back_scan_kernel(start_ref, lane_ref, dstate_ref, local_ref):
    rows = dstate_ref.shape[0] // 2
    count = starts_until(offsets_of(start_ref), block_pos() * rows, rows)
    for c in range(3):
        lanes = slice(128 * c, 128 * c + 128)
        a = (lane_ref[0:1, lanes], -lane_ref[1:2, lanes])
        adj = scan_chunk((dstate_ref[:rows, lanes], dstate_ref[rows:, lanes]), a, count, True)
        local_ref[:rows, lanes] = adj[0]
        local_ref[rows:, lanes] = adj[1]


def split_rows(value):
    upper = value.astype(BF16)
    return jnp.concatenate([upper, (value - upper.astype(F32)).astype(BF16)], axis=0)


def third_kernel(
    recv_ref, start_ref, up_ref, wide_ref, xhat_ref, inv_ref, v_ref, lane_ref, row_ref, feat_ref, state_ref, local_ref, enter_ref,
    dmixed_ref, part_ref, g0, g1, gin_ref, keep_ref, away_ref, scratch, dv_ref, vec_ref,
):
    refs = (g0, g1)
    rows, width = up_ref.shape
    offsets = offsets_of(start_ref)
    base = block_pos() * rows
    count = starts_until(offsets, base, rows)
    later = carried(recv_ref, row_ref, offsets, rows, True, scratch)
    at = lax.broadcasted_iota(jnp.int32, (rows, 128), 0)
    before = jnp.where(at == 0, 0.0, pltpu.roll(count, 1, 0))
    keep = jnp.where(count == before, 1.0, 0.0)
    tail = jnp.where(count == count[rows - 1 : rows], 1.0, 0.0)
    sums = ([], [], [], [])
    for c in range(3):
        lanes = slice(128 * c, 128 * c + 128)
        a = (lane_ref[0:1, lanes], -lane_ref[1:2, lanes])
        eight, power = eighth_powers(a, 7)
        came = cmul(power, (later[0][c], later[1][c]))
        parts = ([], [])
        for blk in range(rows // 8 - 1, -1, -1):
            here = slice(8 * blk, 8 * blk + 8)
            there = slice(rows + 8 * blk, rows + 8 * blk + 8)
            parts[0].insert(0, local_ref[here, lanes] + came[0] * tail[here])
            parts[1].insert(0, local_ref[there, lanes] + came[1] * tail[here])
            came = cmul(came, eight)
        adj = (jnp.concatenate(parts[0], axis=0), jnp.concatenate(parts[1], axis=0))
        prev = (
            jnp.where(at == 0, enter_ref[0:1, lanes], pltpu.roll(state_ref[:rows, lanes], 1, 0)) * keep,
            jnp.where(at == 0, enter_ref[1:2, lanes], pltpu.roll(state_ref[rows:, lanes], 1, 0)) * keep,
        )
        v = (v_ref[:rows, lanes], v_ref[rows:, lanes])
        sums[0].append(column_sum(adj[0] * prev[0] + adj[1] * prev[1]))
        sums[1].append(column_sum(adj[1] * prev[0] - adj[0] * prev[1]))
        sums[2].append(column_sum(adj[0] * v[0] + adj[1] * v[1]))
        sums[3].append(column_sum(adj[1] * v[0] - adj[0] * v[1]))
        dv = cmul((lane_ref[2:3, lanes], -lane_ref[3:4, lanes]), adj)
        dv_ref[:rows, lanes] = dv[0].astype(BF16)
        dv_ref[rows:, lanes] = dv[1].astype(BF16)
    dv = dv_ref[...]
    d_b = dot(dv, wide_ref[...], TN).astype(BF16)
    for k in range(4):
        for f in range(GROUPS):
            block = d_b[96 * k : 96 * k + 96, 128 * f : 128 * f + 128]
            target = away_ref if k // 2 else keep_ref
            target[(k % 2) * GROUPS + f] = block
    scale, skip = feat_ref[0:1], feat_ref[1:2]
    d_normed = folded(dot(dv, weights(lambda k, f: piece(refs, k, f, 0, 96)), NN)) + dmixed_ref[...] * skip
    xhat = xhat_ref[...]
    d_xhat = d_normed * scale
    mean = jnp.sum(d_xhat, axis=1, keepdims=True) / width
    mean_hat = jnp.sum(d_xhat * xhat, axis=1, keepdims=True) / width
    gin_ref[...] = up_ref[...].astype(F32) + inv_ref[:, 0:1] * (d_xhat - mean - xhat * mean_hat)

    vector = [column_sum(d_normed * xhat), column_sum(d_normed), part_ref[0:1, :], part_ref[1:2, :]]
    for k, value in enumerate(vector):
        for c in range(4):
            vec_ref[4 * k + c : 4 * k + c + 1, :] = value[:, 128 * c : 128 * c + 128]
    g = [jnp.concatenate(lanes_to_rows(chunks) + [jnp.zeros((4, 128), F32)], axis=0) for chunks in sums]
    decay, lam, step, abar_re, abar_im, coef_re, coef_im = (row_ref[k] for k in range(7))
    d_abar, d_coef = (g[0], g[1]), (g[2], g[3])
    denom = decay * decay + lam * lam
    numer = (step * abar_re - coef_re, step * abar_im - coef_im)
    ratio = cmul(numer, (-decay / denom, -lam / denom))
    to_lam_a = cmul((step * abar_re, -step * abar_im), d_abar)
    to_lam_c = cmul((ratio[0], -ratio[1]), d_coef)
    g_decay = -(to_lam_a[0] + to_lam_c[0])
    g_lam = to_lam_a[1] + to_lam_c[1]
    slope = cmul((-decay, lam), (abar_re, abar_im))
    g_step = (slope[0] * d_abar[0] + slope[1] * d_abar[1] + abar_re * d_coef[0] + abar_im * d_coef[1]) * step
    for k, value in enumerate((g_decay, g_lam, g_step)):
        for i in range(4):
            vec_ref[pl.ds(16 + 4 * k + slot_pos(i), 1), :] = value[i : i + 1]
    for k in range(2):
        squares = part_ref[2 + k : 3 + k, :]
        total = squares[:, 0:128]
        for c in range(1, 4):
            total = total + squares[:, 128 * c : 128 * c + 128]
        vec_ref[28 + k : 29 + k, :] = total
    vec_ref[30:32, :] = jnp.zeros((2, 128), F32)
    for ref in (keep_ref, away_ref):
        ref[2 * GROUPS, 0:64, :] = split_rows(vec_ref[...])
        ref[2 * GROUPS, 64:96, :] = jnp.zeros((32, 128), BF16)


def added(a, b):
    return (a.astype(F32) + b.astype(F32)).astype(BF16)


def core_cw_kernel(keep_ref, got_ref, stay_ref, leave_ref):
    for f in range(GROUPS):
        stay_ref[f] = added(keep_ref[0, f], got_ref[0, f])
        leave_ref[f] = added(keep_ref[1, f], got_ref[1, f])


def joined(packet):
    return packet[0:32].astype(F32) + packet[32:64].astype(F32)


def core_b_kernel(keep_ref, got_ref, stay_ref, y_ref, x_ref, xy_ref):
    total = split_rows(joined(keep_ref[2 * GROUPS, 0:64, :]) + joined(got_ref[2 * GROUPS, 0:64, :]))
    for ref, m, j in ((stay_ref, 0, 0), (y_ref, 1, 0), (x_ref, 0, 1), (xy_ref, 1, 1)):
        for z in range(GROUPS // 2):
            block = m * GROUPS + 2 * z + j
            ref[96 * z : 96 * z + 96, :] = added(keep_ref[block], got_ref[block])
        ref[384:448, :] = total


def y_cw_kernel(keep_ref, got_ref, stay_ref, leave_ref):
    for z in range(GROUPS // 2):
        f, other = 2 * z, 2 * z + 1
        stay_ref[z] = added(keep_ref[f], got_ref[f])
        leave_ref[z] = added(keep_ref[other], got_ref[other])


def plane_add_kernel(cw_ref, gotcw_ref, stay_ref, y_ref, x_ref, xy_ref, out_ref):
    def total(read):
        return (read(stay_ref) + read(y_ref)) + (read(x_ref) + read(xy_ref))

    vec = split_rows(total(lambda ref: joined(ref[384:448, :])))
    for z in range(GROUPS // 2):
        here = slice(96 * z, 96 * z + 96)
        out_ref[z, 0:96, :] = total(lambda ref, here=here: ref[here, :].astype(F32)).astype(BF16)
        out_ref[z, 96:256, :] = added(cw_ref[z], gotcw_ref[z])
        out_ref[z, 256:320, :] = vec


def finish_vectors(vec, count_all, scale_ref, bias_ref, skip_ref, gbias_ref, decay_ref, lam_ref, step_ref, rms_ref, vec_ref):
    for k, ref in enumerate((scale_ref, bias_ref, skip_ref)):
        for c in range(4):
            ref[:, 128 * c : 128 * c + 128] = vec[4 * k + c : 4 * k + c + 1]
    for k, ref in enumerate((decay_ref, lam_ref, step_ref)):
        for c, chunk in enumerate(rows_to_lanes(vec[16 + 4 * k : 20 + 4 * k])):
            ref[128 * c : 128 * c + 128] = chunk.reshape(128)
    total = jnp.sum(vec[28:30], axis=1, keepdims=True)
    lane = lane_iota((1, 2))
    rms_ref[...] = jnp.sqrt(jnp.where(lane == 0, total[0:1], total[1:2]) / count_all)


def finish_kernel(
    count_all, got_ref, dre_ref, dim_ref, ore_ref, oim_ref, glu_ref, gbias_ref,
    scale_ref, bias_ref, skip_ref, decay_ref, lam_ref, step_ref, rms_ref, vec_ref, square,
):
    def total(start, count):
        value = got_ref[0, start : start + count, :].astype(F32)
        for z in range(1, GROUPS // 2):
            value = value + got_ref[z, start : start + count, :].astype(F32)
        return value

    for start, first_ref, second_ref in ((0, dre_ref, dim_ref), (96, ore_ref, oim_ref)):
        square[0:96, :] = total(start, 96)
        square[96:128, :] = jnp.zeros((32, 128), F32)
        turned = square[...].T
        first_ref[...] = turned[0:64, 0:96]
        second_ref[...] = turned[64:128, 0:96]
    glu_ref[...] = total(192, 64)
    vec = joined(got_ref[0, 256:320, :])
    for z in range(1, GROUPS // 2):
        vec = vec + joined(got_ref[z, 256:320, :])
    vec_ref[...] = vec
    finish_vectors(vec, count_all, scale_ref, bias_ref, skip_ref, None, decay_ref, lam_ref, step_ref, rms_ref, None)
    place = tensor_pos() * GROUPS + fsdp_pos()
    row = jnp.broadcast_to(vec_ref[pl.ds(12 + place // 8, 1), :], (8, 128))
    gbias_ref[...] = pltpu.roll(row, 128 - 16 * (place % 8), 1)[0:1, 0:16]


TAKES = {
    "pack": 1.5, "standardize": 0.2, "norm": 0.2, "first": 1.3, "states": 1.2, "second": 1.9, "readout_grad": 0.7, "back_scan": 0.7,
    "sums": 0.3, "third": 2.1, "finish": 0.7,
}


def call(kernel, outs, args, scratch=(), specs=None, limit=24):
    name = getattr(kernel, "func", kernel).__name__.removesuffix("_kernel")
    return pl.pallas_call(
        kernel,
        out_shape=outs,
        in_specs=specs or [VM] * len(args),
        out_specs=jax.tree.map(lambda _: VM, outs),
        scratch_shapes=list(scratch),
        compiler_params=pltpu.CompilerParams(vmem_limit_bytes=limit << 20),
        cost_estimate=pl.CostEstimate(flops=0, transcendentals=0, bytes_accessed=int(TAKES.get(name, 0.1) * 3.6e6)),
        name=name,
    )(*args)


def tied(value, other):
    return lax.optimization_barrier((value, other))[0]


def swap(value, axis):
    return lax.ppermute(value, axis, [(0, 1), (1, 0)])


def across(value):
    return lax.ppermute(value, ("fx", "ty"), [(n, 3 - n) for n in range(4)])


def on_device(
    layer_in, grad_out, ln_scale, ln_bias, decay_rate, lam_im, log_dt, in_re, in_im, out_re, out_im, skip, glu_weight, glu_bias, seq_lengths
):
    rows, width = layer_in.shape
    fsdp = lax.axis_size(FSDP)
    blocks = fsdp * 4
    count_all = float(rows * blocks * width)
    fast = fsdp == GROUPS
    if fast:
        row = lambda v: v.reshape(1, -1)
        sent = call(
            pack_kernel,
            sds((GROUPS // 2, 272, 128), BF16),
            (seq_lengths, in_re.T, in_im.T, out_re.T, out_im.T, glu_weight.T, row(ln_scale), row(ln_bias), row(skip), row(glu_bias),
             row(decay_rate), row(lam_im), row(log_dt)),
            [pltpu.VMEM((128, 128), F32), pltpu.VMEM((4, 64, 96), BF16), pltpu.VMEM((64, 128), BF16), pltpu.VMEM((4, 1, 64), BF16),
             pltpu.VMEM((3, 1, 96), F32), pltpu.SMEM(seq_lengths.shape, jnp.int32), pltpu.SemaphoreType.DMA((13,))],
            [HBM] * 13,
            60,
        )
        mine = lax.all_to_all(sent, "fz", 0, 0, tiled=True)
        own_b, own_cw = lax.optimization_barrier((mine[:, :112], mine[:, 112:]))
        plane_b = [own_b, swap(own_b, "ty"), swap(own_b, "fx"), across(own_b)]
        plane_b, side_cw = lax.optimization_barrier((plane_b, swap(own_cw, "fx")))
        side_cw = jnp.stack([own_cw, side_cw])
        far_cw = swap(side_cw, "ty")
        own_b = jnp.stack(plane_b).reshape(2, 2, GROUPS // 2, 112, 128)
        g = (own_b, swap(own_b, "tc"))
    else:
        g, g_cw = gathered(
            ln_scale, ln_bias, decay_rate, lam_im, log_dt, in_re, in_im, out_re, out_im, skip, glu_weight, glu_bias, seq_lengths
        )

    xhat, inverse = call(standardize_kernel, (sds((rows, width)), sds((rows, 128))), (layer_in,))
    normed, wide, feat, starts = call(
        norm_kernel,
        (sds((rows, width), BF16), sds((2 * rows, 2 * width), BF16), sds((8, width)),
         sds((seq_lengths.shape[0], 128))),
        (xhat, g[0]),
    )
    v, lane, row_prm, carry = call(
        functools.partial(first_kernel, blocks),
        (sds((2 * rows, 384)), sds((8, 384)), sds((8, 8, 128)), sds((blocks, 8, 128))),
        (wide, starts, *g),
        [pltpu.VMEM((8, 128), F32)],
    )
    came = lax.all_to_all(carry, AXES, 0, 0, tiled=True)
    if fast:
        side_cw, far_cw = tied((side_cw, far_cw), came)
        g_cw = (side_cw, far_cw, swap(side_cw, "tc"), swap(far_cw, "tc"))
    state, twice, enter = call(
        states_kernel,
        (sds((2 * rows, 384)), sds((2 * rows, 384), BF16), sds((8, 384))),
        (came, starts, v, lane, row_prm),
        [pltpu.VMEM((8, 128), F32)],
    )
    branch, d_state, d_mixed, act, dlogit, carry = call(
        functools.partial(second_kernel, blocks),
        (sds((rows, width), BF16), sds((2 * rows, 384)), sds((rows, width)), sds((rows, width), BF16), sds((rows, width), BF16),
         sds((blocks, 8, 128))),
        (twice, starts, grad_out, normed, lane, feat, *g_cw),
        [pltpu.VMEM((8, 128), F32), pltpu.VMEM((width, width), BF16)],
    )
    keep_cw, away_cw = call(
        readout_grad_kernel,
        (sds((2, GROUPS, 160, 128), BF16), sds((2, GROUPS, 160, 128), BF16)),
        (twice, d_mixed, act, dlogit),
        [pltpu.VMEM((width, width), BF16)],
    )
    local = call(back_scan_kernel, sds((2 * rows, 384)), (starts, lane, d_state))
    layer_out, part = call(
        sums_kernel, (sds((rows, width), BF16), sds((8, width))), (layer_in, branch, normed, d_mixed, dlogit)
    )
    if fast:
        got_cw, local, part = lax.optimization_barrier((swap(away_cw, "tc"), local, part))
        stay_cw, leave_cw = call(core_cw_kernel, [sds((GROUPS, 160, 128), BF16)] * 2, (keep_cw, got_cw))
        far_cw = swap(leave_cw, "ty")
        carry = tied(carry, leave_cw)
    came = lax.all_to_all(carry, AXES, 0, 0, tiled=True)
    if fast:
        came, far_cw, stay_cw = lax.optimization_barrier((came, far_cw, stay_cw))
        stay_cw, leave_cw = call(y_cw_kernel, [sds((GROUPS // 2, 160, 128), BF16)] * 2, (stay_cw, far_cw))
        far_cw = swap(leave_cw, "fx")
        came = tied(came, leave_cw)
    grad_in, keep_b, away_b = call(
        third_kernel,
        (sds((rows, width)), sds((2 * GROUPS + 1, 96, 128), BF16), sds((2 * GROUPS + 1, 96, 128), BF16)),
        (came, starts, grad_out, wide, xhat, inverse, v, lane, row_prm, feat, state, local, enter, d_mixed, part, *g),
        [pltpu.VMEM((8, 128), F32), pltpu.VMEM((2 * rows, 384), BF16), pltpu.VMEM((32, 128), F32)],
    )
    if not fast:
        return reduced(layer_out, grad_in, keep_cw, away_cw, keep_b, away_b, count_all, fsdp, width)
    stay_b, y_b, x_b, xy_b = call(core_b_kernel, [sds((448, 128), BF16)] * 4, (keep_b, swap(away_b, "tc")))
    sent = call(
        plane_add_kernel,
        sds((GROUPS // 2, 320, 128), BF16),
        (stay_cw, far_cw, stay_b, swap(y_b, "ty"), swap(x_b, "fx"), across(xy_b)),
    )
    got = lax.all_to_all(sent, "fz", 0, 0, tiled=True)
    d_re, d_im, d_ore, d_oim, d_glu, d_gbias, d_scale, d_bias, d_skip, g_decay, g_lam, g_step, rms = call(
        functools.partial(finish_kernel, count_all),
        (*[sds((64, 96))] * 4, sds((64, 128)), sds((1, 16)), *[sds((1, 512))] * 3, *[sds((384,))] * 3, sds((1, 2))),
        (got,),
        [pltpu.VMEM((32, 128), F32), pltpu.VMEM((128, 128), F32)],
    )
    flat = lambda value: value.reshape(-1)
    return (
        layer_out, grad_in, flat(d_scale), flat(d_bias), g_decay, g_lam, g_step, d_re.T, d_im.T, d_ore.T, d_oim.T,
        flat(d_skip), d_glu.T, flat(d_gbias), flat(rms),
    )


def gathered(ln_scale, ln_bias, decay_rate, lam_im, log_dt, in_re, in_im, out_re, out_im, skip, glu_weight, glu_bias, seq_lengths):
    tens = tensor_pos()
    full = lambda value, axis: lax.all_gather(value, FSDP, axis=axis, tiled=True)

    def pair(first, second):
        halves = jnp.stack([first.reshape(-1, GROUPS, 64), second.reshape(-1, GROUPS, 64)], axis=2)
        return halves.reshape(-1, GROUPS, 128).swapaxes(0, 1)

    gate = lax.dynamic_slice_in_dim(full(glu_weight, 1), tens * 128, 128, 0).T.reshape(GROUPS, 64, 128)
    vectors = [pair(full(ln_scale, 0)[None], full(ln_bias, 0)[None]), pair(full(skip, 0)[None], full(glu_bias, 0)[None])]
    for value in (decay_rate, lam_im, log_dt):
        value = jnp.pad(value, (0, 32))
        for _ in range(3):
            piece = lax.reduce_precision(value, 8, 7)
            value = value - piece
            vectors.append(jnp.broadcast_to(piece.astype(BF16)[None, None], (GROUPS, 1, 128)))
    starts = jnp.cumsum(seq_lengths) - seq_lengths
    for value in (starts >> 8, starts & 255):
        value = jnp.pad(value, (0, 128 - value.shape[0])).astype(BF16)
        vectors.append(jnp.broadcast_to(value[None, None], (GROUPS, 1, 128)))
    vectors.append(jnp.zeros((GROUPS, 3, 128), BF16))
    packet = jnp.concatenate(
        [pair(full(in_re, 1), full(in_im, 1)), *vectors, pair(full(out_re, 1), full(out_im, 1)), gate],
        axis=1,
    )
    everyone = lax.all_gather(packet, TENSOR, axis=0).reshape(2, 2, GROUPS // 2, 2, 272, 128)
    x, y, core = (lax.axis_index(axis) for axis in ("fx", "ty", "tc"))
    own_x = lambda value, axis: jnp.stack([lax.dynamic_index_in_dim(value, x ^ j, axis, keepdims=False) for j in range(2)])
    g, g_cw = [], []
    for i in range(2):
        both = lax.dynamic_index_in_dim(everyone, core ^ i, 1, keepdims=False)
        slots = [own_x(lax.dynamic_index_in_dim(both, y ^ m, 0, keepdims=False), 1) for m in range(2)]
        g.append(jnp.stack(slots, axis=1)[:, :, :, :112])
        g_cw += [slot[:, :, 112:] for slot in slots]
    return g, g_cw


def reduced(layer_out, grad_in, keep_cw, away_cw, keep_b, away_b, count_all, fsdp, width):
    tens = tensor_pos()
    x, y, core = (lax.axis_index(axis) for axis in ("fx", "ty", "tc"))
    vec = joined(keep_b[2 * GROUPS, :64])
    keep_b, away_b = (value[: 2 * GROUPS].reshape(2, GROUPS, 96, 128) for value in (keep_b, away_b))

    def ordered(value, own, axis):
        return jnp.concatenate([lax.dynamic_index_in_dim(value, own ^ n, axis) for n in range(2)], axis=axis)

    def canonical(keep, away):
        both = jnp.stack([keep, away]).astype(F32)
        both = both.reshape(2, 2, GROUPS // 2, 2, *keep.shape[2:])
        both = ordered(ordered(ordered(both, core, 0), y, 1), x, 3)
        return both.swapaxes(0, 1).reshape(4, *keep.shape[1:])

    def natural(keep, away):
        halves = canonical(keep, away).reshape(4, GROUPS, -1, 2, 64).transpose(3, 0, 2, 1, 4)
        return halves[0].reshape(-1, width), halves[1].reshape(-1, width)

    def scattered(value):
        value = lax.psum_scatter(value, TENSOR, scatter_dimension=0, tiled=True)
        return lax.psum_scatter(value, FSDP, scatter_dimension=1, tiled=True)

    d_re, d_im = natural(keep_b, away_b)
    d_ore, d_oim = natural(keep_cw[:, :, :96], away_cw[:, :, :96])
    d_glu = canonical(keep_cw[:, :, 96:], away_cw[:, :, 96:]).reshape(4, width, 128).swapaxes(1, 2).reshape(-1, width)
    vec = lax.psum(vec, AXES)
    states = lambda k: vec[16 + 4 * k : 20 + 4 * k, :96].reshape(-1)
    own = width // (4 * fsdp)
    place = tens * fsdp + fsdp_pos()
    d_gbias = lax.dynamic_slice_in_dim(vec[12:16].reshape(-1), place * own, own, 0)
    rms = jnp.sqrt(jnp.sum(vec[28:30], axis=1) / count_all)
    return (
        layer_out, grad_in, vec[0:4].reshape(-1), vec[4:8].reshape(-1), states(0), states(1), states(2), scattered(d_re), scattered(d_im),
        scattered(d_ore), scattered(d_oim), vec[8:12].reshape(-1), scattered(d_glu), d_gbias, rms,
    )


def solution(mesh):
    shape = (mesh.shape["fsdp"] // 2, 2, mesh.shape["tensor"] // 2, 2)
    split = Mesh(mesh.devices.reshape(shape), AXES)
    tokens, matrix = P(AXES, None), P(TENSOR, FSDP)
    return jax.shard_map(
        on_device,
        mesh=split,
        in_specs=(
            tokens, tokens, P(FSDP), P(FSDP), P(TENSOR), P(TENSOR), P(TENSOR), matrix, matrix, matrix, matrix,
            P(FSDP), P(None, FSDP), P(FSDP), P(),
        ),
        out_specs=(
            tokens, tokens, P(), P(), P(), P(), P(), matrix, matrix, matrix, matrix, P(), matrix, P((*TENSOR, *FSDP)), P(),
        ),
        check_vma=False,
    )
```

```python
import functools

import jax
import jax.numpy as jnp
from jax import lax
from jax.experimental import pallas as pl
from jax.experimental.pallas import tpu as pltpu
from jax.sharding import Mesh
from jax.sharding import PartitionSpec as P

F32 = jnp.float32
BF16 = jnp.bfloat16
FSDP = ("fz", "fx")
TENSOR = ("ty", "tc")
AXES = (*FSDP, *TENSOR)
HBM = pl.BlockSpec(memory_space=pltpu.HBM)
VM = pl.BlockSpec(memory_space=pltpu.VMEM)
SM = pl.BlockSpec(memory_space=pltpu.SMEM)

GROUPS = 8
VEC = 96


def sds(shape, dtype=F32):
    return jax.ShapeDtypeStruct(shape, dtype)


def low_half(shape):
    return lax.broadcasted_iota(jnp.int32, shape, len(shape) - 1) < 64


def lane_iota(shape):
    return lax.broadcasted_iota(jnp.int32, shape, len(shape) - 1)


def dot(a, b, dims):
    return lax.dot_general(a, b, (dims, ((), ())), preferred_element_type=F32)


NT = ((1,), (1,))
NN = ((1,), (0,))
TN = ((0,), (0,))


def flipped():
    return lax.axis_index("fx") == 1


def spread(x):
    lo = low_half((x.shape[0], 128))
    flip = flipped()
    upper, lower = [], []
    for c in range(x.shape[1] // 128):
        xc = x[:, 128 * c : 128 * c + 128]
        turned = pltpu.roll(xc, 64, 1)
        xc, turned = jnp.where(flip, turned, xc), jnp.where(flip, xc, turned)
        upper += [jnp.where(lo, xc, 0.0).astype(BF16), jnp.where(lo, turned, 0.0).astype(BF16)]
        lower += [jnp.where(lo, 0.0, turned).astype(BF16), jnp.where(lo, 0.0, xc).astype(BF16)]
    return jnp.concatenate(
        [jnp.concatenate(upper, axis=1), jnp.concatenate(lower, axis=1)], axis=0
    )


def folded(lhs, parts):
    rows = lhs.shape[0] // 2
    lo = low_half((rows, 128))
    flip = flipped()
    out = []
    for part in parts:
        pq = dot(lhs, part, NN)
        p0, p1, q0, q1 = pq[:rows, :128], pq[:rows, 128:], pq[rows:, :128], pq[rows:, 128:]
        even = jnp.where(lo, p0, q1) + jnp.where(lo, pltpu.roll(q0, 64, 1), pltpu.roll(p1, 64, 1))
        out.append(jnp.where(flip, pltpu.roll(even, 64, 1), even))
    return jnp.concatenate(out, axis=1)


def slot_pos(m, core):
    return (lax.axis_index("ty") ^ m) * 2 + (lax.axis_index("tc") ^ core)


def own_rows(rows):
    return pl.ds(pl.multiple_of(lax.axis_index("tc") * rows, rows), rows)


def other_rows(rows):
    return pl.ds(pl.multiple_of((1 - lax.axis_index("tc")) * rows, rows), rows)


def piece(ref, m, f, start, count):
    return ref[f % 2, m, f // 2, start : start + count, :]


def weights(get):
    none = jnp.zeros((32, 128), BF16)
    block = lambda f: jnp.concatenate([get(0, f), none, get(1, f), none], axis=0)
    return [jnp.concatenate([block(f), block(f + 1)], axis=1) for f in range(0, GROUPS, 2)]


def feature_rows(ref, row):
    lo = low_half((8, 128))
    flip = flipped()
    first, second = [], []
    for c in range(GROUPS // 2):
        a = jnp.broadcast_to(piece(ref, 0, 2 * c, row, 1).astype(F32), (8, 128))
        b = jnp.broadcast_to(piece(ref, 0, 2 * c + 1, row, 1).astype(F32), (8, 128))
        a, b = jnp.where(flip, b, a), jnp.where(flip, a, b)
        first.append(jnp.where(lo, a, pltpu.roll(b, 64, 1)))
        second.append(jnp.where(lo, pltpu.roll(a, 64, 1), b))
    return jnp.concatenate(first, axis=1)[:1], jnp.concatenate(second, axis=1)[:1]


def cmul(a, b):
    return a[0] * b[0] - a[1] * b[1], a[0] * b[1] + a[1] * b[0]


def tensor_pos():
    return lax.axis_index("ty") * 2 + lax.axis_index("tc")


def fsdp_pos():
    return lax.axis_index("fz") * 2 + lax.axis_index("fx")


def pair_pos():
    return fsdp_pos() * 2 + lax.axis_index("ty")


def offsets_of(start_ref):
    return [start_ref[n : n + 1, :] for n in range(start_ref.shape[0])]


def starts_until(offsets, base, rows):
    at = (lax.broadcasted_iota(jnp.int32, (rows, 128), 0) + base).astype(F32)
    count = jnp.zeros((rows, 128), F32)
    for off in offsets:
        count = count + jnp.where((at >= off) & (off >= at[0:1]), 1.0, 0.0)
    return count


def no_start(offsets, base, rows):
    link = jnp.ones((1, 128), F32)
    first = (jnp.zeros((1, 128), jnp.int32) + base).astype(F32)
    for off in offsets:
        link = jnp.where((off >= first) & (off < first + rows), 0.0, link)
    return link


def expm1(x):
    series = x * (1 + x / 2 * (1 + x / 3 * (1 + x / 4 * (1 + x / 5 * (1 + x / 6 * (1 + x / 7))))))
    return jnp.where(jnp.abs(x) < 0.25, series, jnp.exp(x) - 1.0)


def discretize(decay_rate, lam_im, log_dt):
    step_size = jnp.exp(log_dt)
    lam_re = -decay_rate
    magnitude = jnp.exp(lam_re * step_size)
    phase = lam_im * step_size
    abar_re = magnitude * jnp.cos(phase)
    abar_im = magnitude * jnp.sin(phase)
    half_sin = jnp.sin(0.5 * phase)
    less_re = expm1(lam_re * step_size) * jnp.cos(phase) - 2.0 * half_sin * half_sin
    denom = lam_re * lam_re + lam_im * lam_im
    coef_re = (less_re * lam_re + abar_im * lam_im) / denom
    coef_im = (abar_im * lam_re - less_re * lam_im) / denom
    return abar_re, abar_im, coef_re, coef_im, step_size


def pack_kernel(*refs):
    *inputs, out_ref, square, four, glu_ref, halves, params, lengths, sems = refs
    seq_hbm, matrices, glu_hbm, features, states = inputs[0], inputs[1:5], inputs[5], inputs[6:10], inputs[10:13]
    units = pl.multiple_of(tensor_pos() * 128, 128)
    pairs = [(ref, four.at[k]) for k, ref in enumerate(matrices)]
    pairs += [(glu_hbm.at[:, pl.ds(units, 128)], glu_ref), (seq_hbm, lengths)]
    pairs += [(ref, halves.at[k]) for k, ref in enumerate(features)]
    pairs += [(ref, params.at[k]) for k, ref in enumerate(states)]
    copies = [pltpu.make_async_copy(source, target, sems.at[k]) for k, (source, target) in enumerate(pairs)]
    for copy in copies:
        copy.start()
    square[:, 96:128] = jnp.zeros((128, 32), F32)
    for copy in copies:
        copy.wait()
    vec = [
        jnp.concatenate([halves[0], halves[1]], axis=1).astype(F32),
        jnp.concatenate([halves[2], halves[3]], axis=1).astype(F32),
    ]
    for k in range(3):
        value = jnp.concatenate([params[k], jnp.zeros((1, 32), F32)], axis=1)
        for _ in range(3):
            part = value.astype(BF16).astype(F32)
            value = value - part
            vec.append(part)
    lane = lane_iota((1, 128))
    upper, lower, total = jnp.zeros((1, 128), jnp.int32), jnp.zeros((1, 128), jnp.int32), 0
    for n in range(lengths.shape[0]):
        upper = jnp.where(lane == n, total >> 8, upper)
        lower = jnp.where(lane == n, total & 255, lower)
        total = total + lengths[n]
    vec += [upper.astype(F32), lower.astype(F32)]
    vec.append(jnp.zeros((16 - len(vec), 128), F32))
    vec = jnp.concatenate(vec, axis=0).astype(BF16)
    pieces = []
    for k in (0, 2):
        square[0:64, 0:96] = four[k].astype(F32)
        square[64:128, 0:96] = four[k + 1].astype(F32)
        pieces.append(square[...].T[0:96].astype(BF16))
    packet = jnp.concatenate([pieces[0], vec, pieces[1], glu_ref[...]], axis=0)
    for z in range(GROUPS // 2):
        out_ref[z] = packet


def params_of(ref, vec_row):
    lane = lane_iota((8, 128))
    out = []
    for k, safe in enumerate((1.0, 0.0, 0.0)):
        rows = []
        for m in range(2):
            part = piece(ref, m, 0, vec_row, 16).astype(F32)
            rows.append((part[2 + 3 * k : 3 + 3 * k] + part[3 + 3 * k : 4 + 3 * k]) + part[4 + 3 * k : 5 + 3 * k])
        value = jnp.concatenate(rows + [jnp.full((6, 128), safe, F32)], axis=0)
        out.append(jnp.where(lane < 96, value, safe))
    return out


def carry_block(re_rows, im_rows, scratch):
    for m in range(2):
        y = lax.axis_index("ty") ^ m
        scratch[pl.ds(y, 1), :] = re_rows[m]
        scratch[pl.ds(2 + y, 1), :] = im_rows[m]


def standardize_kernel(x_ref, other_ref, xhat_ref, inv_ref):
    rows, width = x_ref.shape
    for ref, where, own in ((x_ref, own_rows(rows), True), (other_ref, other_rows(rows), False)):
        x = ref[...].astype(F32)
        centered = x - jnp.sum(x, axis=1, keepdims=True) / width
        inverse = lax.rsqrt(jnp.sum(centered * centered, axis=1, keepdims=True) / width + 1e-05)
        xhat_ref[where, :] = centered * inverse
        if own:
            inv_ref[...] = jnp.broadcast_to(inverse, (rows, 128))


def norm_kernel(xhat_ref, g_ref, normed_ref, wide_ref, feat_ref, start_ref):
    scale, bias = feature_rows(g_ref, VEC)
    feat_ref[0:1] = scale
    feat_ref[1:2], feat_ref[2:3] = feature_rows(g_ref, VEC + 1)
    normed = (xhat_ref[...] * scale + bias).astype(BF16)
    normed_ref[...] = normed
    wide_ref[...] = spread(normed.astype(F32))
    upper, lower = (piece(g_ref, 0, 0, VEC + 11 + k, 1).astype(F32) for k in range(2))
    starts = upper * 256.0 + lower
    for n in range(start_ref.shape[0]):
        start_ref[n : n + 1, :] = jnp.broadcast_to(starts[:, n : n + 1], (1, 128))


def first_kernel(pairs, wide_ref, start_ref, g_ref, v_ref, lane_ref, row_ref, send_ref, scratch):
    rows = wide_ref.shape[0] // 2
    b_all = jnp.concatenate(weights(lambda m, f: piece(g_ref, m, f, 0, 96)), axis=1)
    v_ref[...] = dot(wide_ref[...], b_all, NT)

    decay, lam, log_dt = params_of(g_ref, VEC)
    abar_re, abar_im, coef_re, coef_im, step_size = discretize(decay, lam, log_dt)
    power = (abar_re, abar_im)
    for _ in range(8):
        power = cmul(power, power)
    scratch[...] = jnp.zeros((8, 128), F32)
    carry_block([power[0][m : m + 1] for m in range(2)], [power[1][m : m + 1] for m in range(2)], scratch)
    for k, value in enumerate((decay, lam, step_size, abar_re, abar_im, coef_re, coef_im, scratch[...])):
        row_ref[k] = value
    for k, value in enumerate((abar_re, abar_im, coef_re, coef_im)):
        for m in range(2):
            lane_ref[k : k + 1, 128 * m : 128 * m + 128] = value[m : m + 1]

    count = starts_until(offsets_of(start_ref), pair_pos() * rows, rows)
    open_tail = jnp.where(count == count[rows - 1 : rows], 1.0, 0.0)
    last = ([], [])
    for m in range(2):
        lanes = slice(128 * m, 128 * m + 128)
        eight, tail = eighth_powers((abar_re[m : m + 1], abar_im[m : m + 1]), 7)
        b = (coef_re[m : m + 1], coef_im[m : m + 1])
        acc = (jnp.zeros((8, 128), F32), jnp.zeros((8, 128), F32))
        for blk in range(rows // 8):
            here = slice(8 * blk, 8 * blk + 8)
            there = slice(rows + 8 * blk, rows + 8 * blk + 8)
            drive = cmul(b, (v_ref[here, lanes], v_ref[there, lanes]))
            moved = cmul(eight, acc)
            acc = (moved[0] + drive[0] * open_tail[here], moved[1] + drive[1] * open_tail[here])
        total = cmul(tail, acc)
        last[0].append(column_sum(total[0]))
        last[1].append(column_sum(total[1]))
    carry_block(last[0], last[1], scratch)
    packet = scratch[...]
    for d in range(pairs):
        send_ref[d] = packet


def eighth_powers(a, top):
    sub = lax.broadcasted_iota(jnp.int32, (8, 128), 0)
    exponent = (7 - sub) if top == 7 else sub + 1
    a = (jnp.broadcast_to(a[0], (8, 128)), jnp.broadcast_to(a[1], (8, 128)))
    tile = (jnp.ones((8, 128), F32), jnp.zeros((8, 128), F32))
    for bit in range(4):
        if bit == 3:
            eight = a
        taken = (exponent & (1 << bit)) != 0
        more = cmul(tile, a)
        tile = (jnp.where(taken, more[0], tile[0]), jnp.where(taken, more[1], tile[1]))
        a = cmul(a, a)
    return eight, tile


def scan_chunk(value, a, count, reverse):
    rows = count.shape[0]
    at = lax.broadcasted_iota(jnp.int32, (rows, 128), 0)
    step = 1
    while step < rows:
        shift = rows - step if reverse else step
        other = pltpu.roll(count, shift, 0)
        inside = (at < rows - step) if reverse else (at >= step)
        linked = inside & (other == count)
        moved = (pltpu.roll(value[0], shift, 0), pltpu.roll(value[1], shift, 0))
        more = cmul(a, moved)
        value = (value[0] + jnp.where(linked, more[0], 0.0), value[1] + jnp.where(linked, more[1], 0.0))
        a = cmul(a, a)
        step *= 2
    return value


def carried(recv_ref, row_ref, offsets, rows, reverse, scratch):
    pairs = recv_ref.shape[0]
    power = row_ref[7]
    pre, pim = power[0:2], power[2:4]
    if reverse:
        pim = -pim
    place = pair_pos()

    def turn(k, state):
        j = pairs - 1 - k if reverse else k
        link = no_start(offsets, j * rows, rows)
        got = recv_ref[j]
        new = cmul((pre * link, pim * link), state)
        return new[0] + got[0:2], new[1] + got[2:4]

    zero = jnp.zeros((2, 128), F32)
    out = lax.fori_loop(0, pairs - 1 - place if reverse else place, turn, (zero, zero))
    scratch[0:2, :] = out[0]
    scratch[2:4, :] = out[1]
    own = [lax.axis_index("ty") ^ m for m in range(2)]
    return [scratch[pl.ds(y, 1), :] for y in own], [scratch[pl.ds(2 + y, 1), :] for y in own]


def column_sum(value):
    return jnp.sum(value, axis=0, keepdims=True)


def states_kernel(recv_ref, start_ref, v_ref, lane_ref, row_ref, state_ref, twice_ref, enter_ref, scratch):
    rows = v_ref.shape[0] // 2
    half = rows // 2
    offsets = offsets_of(start_ref)
    base = pair_pos() * rows
    count = starts_until(offsets, base, rows)
    enter = carried(recv_ref, row_ref, offsets, rows, False, scratch)
    top = lax.broadcasted_iota(jnp.int32, (half, 128), 0) == 0
    links = (no_start(offsets, base, 1), jnp.where(count[half : half + 1] == count[half - 1 : half], 1.0, 0.0))
    for m in range(2):
        lanes = slice(128 * m, 128 * m + 128)
        a = (lane_ref[0:1, lanes], lane_ref[1:2, lanes])
        b = (lane_ref[2:3, lanes], lane_ref[3:4, lanes])
        before = (enter[0][m], enter[1][m])
        enter_ref[0:1, lanes] = before[0]
        enter_ref[1:2, lanes] = before[1]
        for h in range(2):
            here = slice(half * h, half * h + half)
            there = slice(rows + half * h, rows + half * h + half)
            drive = cmul(b, (v_ref[here, lanes], v_ref[there, lanes]))
            came = cmul((a[0] * links[h], a[1] * links[h]), before)
            drive = (drive[0] + jnp.where(top, came[0], 0.0), drive[1] + jnp.where(top, came[1], 0.0))
            state = scan_chunk(drive, a, count[here], False)
            before = (state[0][half - 1 : half], state[1][half - 1 : half])
            state_ref[here, lanes] = state[0]
            state_ref[there, lanes] = state[1]
            twice_ref[here, lanes] = state[0].astype(BF16) * 2
            twice_ref[there, lanes] = state[1].astype(BF16) * -2


def readout_kernel(twice_ref, c0_ref, c1_ref, own_ref, away_ref, scratch):
    rows = own_ref.shape[0]
    slots = (c0_ref, c1_ref)
    scratch[...] = folded(twice_ref[...], weights(lambda m, f: slots[m][f % 2, f // 2, 0:96, :]))
    own_ref[...] = scratch[own_rows(rows), :]
    away_ref[...] = scratch[other_rows(rows), :]


def second_kernel(
    own_ref, got_ref, up_ref, normed_ref, feat_ref, g0, g1, g2, g3,
    branch_ref, dmixed_ref, dlogit_ref, mine_ref, away_ref, gate_ref, all_ref,
):
    rows, width = up_ref.shape
    for core, slots in enumerate(((g0, g1), (g2, g3))):
        for m in range(2):
            lanes = pl.ds(pl.multiple_of(slot_pos(m, core) * 128, 128), 128)
            for f in range(GROUPS):
                place = (f // 2) * 2 + (lax.axis_index("fx") ^ (f % 2))
                gate_ref[pl.ds(pl.multiple_of(place * 64, 64), 64), lanes] = slots[m][f % 2, f // 2, 96:160, :]
    skip, gate_bias = feat_ref[1:2], feat_ref[2:3]
    normed = normed_ref[own_rows(rows), :].astype(F32)
    mixed = (own_ref[...] + got_ref[...]) + skip * normed
    cdf = 0.5 * (1.0 + lax.erf(mixed * 0.7071067811865476))
    act_low = (mixed * cdf).astype(BF16)
    act = act_low.astype(F32)
    w_gate = gate_ref[...]
    logit = dot(act_low, w_gate, NN) + gate_bias
    gate = 1.0 / (1.0 + jnp.exp(-logit))
    branch_ref[...] = (act * gate).astype(BF16)
    up = up_ref[...].astype(F32)
    dlogit = (up * act * gate * (1.0 - gate)).astype(BF16)
    dlogit_ref[...] = dlogit
    all_ref[...] = dlogit
    d_act = dot(dlogit, w_gate, NT) + up * gate
    slope = cdf + mixed * jnp.exp(-0.5 * mixed * mixed) * 0.3989422804014327
    d_mixed = d_act * slope
    dmixed_ref[...] = d_mixed
    for core, ref in enumerate((mine_ref, away_ref)):
        ref[:, 0:width] = d_mixed.astype(BF16)
        ref[:, width : 2 * width] = act_low
        for m in range(2):
            lanes = pl.ds(pl.multiple_of(slot_pos(m, core) * 128, 128), 128)
            ref[:, 2 * width + 128 * m : 2 * width + 128 * m + 128] = all_ref[:, lanes]


def sums_kernel(x_ref, branch_ref, normed_ref, dmixed_ref, dlogit_ref, out_ref, part_ref):
    x = x_ref[...].astype(F32)
    branch = branch_ref[...].astype(F32)
    out_ref[...] = (x + branch).astype(BF16)
    skip = column_sum(dmixed_ref[...] * normed_ref[own_rows(x_ref.shape[0]), :].astype(F32))
    for k, value in enumerate((skip, column_sum(dlogit_ref[...].astype(F32)), column_sum(x * x), column_sum(branch * branch))):
        part_ref[k : k + 1, :] = value


def back_kernel(
    pairs, mine_ref, got_ref, twice_ref, start_ref, lane_ref, c0_ref, c1_ref,
    dstate_ref, send_ref, stay_ref, leave_ref, dy_ref, dgate_ref, scratch,
):
    rows, width = dy_ref.shape
    half = rows // 2
    dy_ref[own_rows(half), :] = mine_ref[:, 0:width]
    dy_ref[other_rows(half), :] = got_ref[:, 0:width]
    slots = (c0_ref, c1_ref)
    c_all = jnp.concatenate(weights(lambda m, f: slots[m][f % 2, f // 2, 0:96, :]), axis=1)
    spread_dy = spread(dy_ref[...].astype(F32))
    d_state = dot(spread_dy, c_all, NT)
    dstate_ref[:rows] = d_state[:rows] * 2.0
    dstate_ref[rows:] = d_state[rows:] * -2.0
    count = starts_until(offsets_of(start_ref), pair_pos() * rows, rows)
    head = jnp.where(count == 0.0, 1.0, 0.0)
    first = ([], [])
    for m in range(2):
        lanes = slice(128 * m, 128 * m + 128)
        eight, tail = eighth_powers((lane_ref[0:1, lanes], -lane_ref[1:2, lanes]), 0)
        acc = (jnp.zeros((8, 128), F32), jnp.zeros((8, 128), F32))
        for blk in range(rows // 8 - 1, -1, -1):
            here = slice(8 * blk, 8 * blk + 8)
            there = slice(rows + 8 * blk, rows + 8 * blk + 8)
            moved = cmul(eight, acc)
            acc = (moved[0] + dstate_ref[here, lanes] * head[here], moved[1] + dstate_ref[there, lanes] * head[here])
        total = cmul(tail, acc)
        first[0].append(column_sum(total[0]))
        first[1].append(column_sum(total[1]))
    scratch[...] = jnp.zeros((8, 128), F32)
    carry_block(first[0], first[1], scratch)
    packet = scratch[...]
    for d in range(pairs):
        send_ref[d] = packet
    d_c = dot(twice_ref[...], spread_dy, TN).astype(BF16)
    act = slice(width, 2 * width)
    units = slice(2 * width, 2 * width + 256)
    d_gate = dot(mine_ref[:, act], mine_ref[:, units], TN) + dot(got_ref[:, act], got_ref[:, units], TN)
    dgate_ref[...] = d_gate.astype(BF16)
    for m, ref in enumerate((stay_ref, leave_ref)):
        for f in range(GROUPS):
            ref[f, 0:96, :] = d_c[128 * m : 128 * m + 96, 128 * f : 128 * f + 128]
            place = pl.ds(pl.multiple_of(((f // 2) * 2 + (lax.axis_index("fx") ^ (f % 2))) * 64, 64), 64)
            ref[f, 96:160, :] = dgate_ref[place, 128 * m : 128 * m + 128]


def split_rows(value):
    upper = value.astype(BF16)
    return jnp.concatenate([upper, (value - upper.astype(F32)).astype(BF16)], axis=0)


def third_kernel(
    recv_ref, start_ref, wide_ref, xhat_ref, v_ref, lane_ref, row_ref, feat_ref, state_ref, dstate_ref, enter_ref, dmixed_ref,
    part_ref, g_ref, stay_ref, y_ref, x_ref, xy_ref, dn_ref, dnaway_ref, scratch, dv_ref, all_ref, vec_ref,
):
    rows, width = xhat_ref.shape
    half = rows // 2
    offsets = offsets_of(start_ref)
    base = pair_pos() * rows
    count = starts_until(offsets, base, rows)
    later = carried(recv_ref, row_ref, offsets, rows, True, scratch)
    at = lax.broadcasted_iota(jnp.int32, (half, 128), 0)
    top, bottom = at == 0, at == half - 1
    before = jnp.where(lax.broadcasted_iota(jnp.int32, (rows, 128), 0) == 0, 0.0, pltpu.roll(count, 1, 0))
    keep = jnp.where(count == before, 1.0, 0.0)
    sums = ([], [], [], [])
    for m in range(2):
        lanes = slice(128 * m, 128 * m + 128)
        a = (lane_ref[0:1, lanes], -lane_ref[1:2, lanes])
        b = (lane_ref[2:3, lanes], -lane_ref[3:4, lanes])
        came = (later[0][m], later[1][m])
        totals = None
        for h in (1, 0):
            here = slice(half * h, half * h + half)
            there = slice(rows + half * h, rows + half * h + half)
            start = (
                dstate_ref[here, lanes] + jnp.where(bottom, came[0], 0.0),
                dstate_ref[there, lanes] + jnp.where(bottom, came[1], 0.0),
            )
            adj = scan_chunk(start, a, count[here], True)
            if h:
                link = keep[half : half + 1]
                came = cmul((a[0] * link, a[1] * link), (adj[0][0:1], adj[1][0:1]))
                edge = (state_ref[half - 1 : half, lanes], state_ref[rows + half - 1 : rows + half, lanes])
            else:
                edge = (enter_ref[0:1, lanes], enter_ref[1:2, lanes])
            prev = (
                jnp.where(top, edge[0], pltpu.roll(state_ref[here, lanes], 1, 0)) * keep[here],
                jnp.where(top, edge[1], pltpu.roll(state_ref[there, lanes], 1, 0)) * keep[here],
            )
            v = (v_ref[here, lanes], v_ref[there, lanes])
            new = [
                column_sum(adj[0] * prev[0] + adj[1] * prev[1]),
                column_sum(adj[1] * prev[0] - adj[0] * prev[1]),
                column_sum(adj[0] * v[0] + adj[1] * v[1]),
                column_sum(adj[1] * v[0] - adj[0] * v[1]),
            ]
            totals = new if totals is None else [p + q for p, q in zip(totals, new)]
            dv = cmul(b, adj)
            dv_ref[here, lanes] = dv[0].astype(BF16)
            dv_ref[there, lanes] = dv[1].astype(BF16)
        for k in range(4):
            sums[k].append(totals[k])
    dv = dv_ref[...]
    d_b = dot(dv, wide_ref[...], TN).astype(BF16)
    for ref, m, j in ((stay_ref, 0, 0), (y_ref, 1, 0), (x_ref, 0, 1), (xy_ref, 1, 1)):
        for z in range(GROUPS // 2):
            f = 2 * z + j
            ref[96 * z : 96 * z + 96, :] = d_b[128 * m : 128 * m + 96, 128 * f : 128 * f + 128]
    all_ref[...] = folded(dv, weights(lambda m, f: piece(g_ref, m, f, 0, 96)))
    dnaway_ref[...] = all_ref[other_rows(half), :]
    own = all_ref[own_rows(half), :] + dmixed_ref[...] * feat_ref[1:2]
    dn_ref[...] = own
    all_ref[own_rows(half), :] = own
    d_normed = all_ref[...]
    vector = [column_sum(d_normed * xhat_ref[...]), column_sum(d_normed), part_ref[0:1, :], part_ref[1:2, :]]
    for k, value in enumerate(vector):
        for c in range(4):
            vec_ref[4 * k + c : 4 * k + c + 1, :] = value[:, 128 * c : 128 * c + 128]
    g = [jnp.concatenate(pair + [jnp.zeros((6, 128), F32)], axis=0) for pair in sums]
    decay, lam, step, abar_re, abar_im, coef_re, coef_im = (row_ref[k] for k in range(7))
    d_abar, d_coef = (g[0], g[1]), (g[2], g[3])
    denom = decay * decay + lam * lam
    numer = (step * abar_re - coef_re, step * abar_im - coef_im)
    ratio = cmul(numer, (-decay / denom, -lam / denom))
    to_lam_a = cmul((step * abar_re, -step * abar_im), d_abar)
    to_lam_c = cmul((ratio[0], -ratio[1]), d_coef)
    g_decay = -(to_lam_a[0] + to_lam_c[0])
    g_lam = to_lam_a[1] + to_lam_c[1]
    slope = cmul((-decay, lam), (abar_re, abar_im))
    g_step = (slope[0] * d_abar[0] + slope[1] * d_abar[1] + abar_re * d_coef[0] + abar_im * d_coef[1]) * step
    vec_ref[16:32, :] = jnp.zeros((16, 128), F32)
    for k, value in enumerate((g_decay, g_lam, g_step)):
        for m in range(2):
            vec_ref[pl.ds(16 + 4 * k + slot_pos(m, 0), 1), :] = value[m : m + 1]
    for k in range(2):
        squares = part_ref[2 + k : 3 + k, :]
        total = squares[:, 0:128]
        for c in range(1, 4):
            total = total + squares[:, 128 * c : 128 * c + 128]
        vec_ref[28 + k : 29 + k, :] = total
    vec_ref[30:32, :] = jnp.zeros((2, 128), F32)
    vec = split_rows(vec_ref[...])
    for ref in (stay_ref, y_ref, x_ref, xy_ref):
        ref[384:448, :] = vec


def input_grad_kernel(dn_ref, got_ref, up_ref, xhat_ref, inv_ref, feat_ref, gin_ref):
    rows, width = up_ref.shape
    xhat = xhat_ref[own_rows(rows), :]
    d_xhat = (dn_ref[...] + got_ref[...]) * feat_ref[0:1]
    mean = jnp.sum(d_xhat, axis=1, keepdims=True) / width
    mean_hat = jnp.sum(d_xhat * xhat, axis=1, keepdims=True) / width
    gin_ref[...] = up_ref[...].astype(F32) + inv_ref[:, 0:1] * (d_xhat - mean - xhat * mean_hat)


def added(a, b):
    return (a.astype(F32) + b.astype(F32)).astype(BF16)


def joined(packet):
    return packet[0:32].astype(F32) + packet[32:64].astype(F32)


def y_cw_kernel(keep_ref, got_ref, stay_ref, leave_ref):
    for z in range(GROUPS // 2):
        f, other = 2 * z, 2 * z + 1
        stay_ref[z] = added(keep_ref[f], got_ref[f])
        leave_ref[z] = added(keep_ref[other], got_ref[other])


def plane_add_kernel(cw_ref, gotcw_ref, stay_ref, y_ref, x_ref, xy_ref, out_ref):
    def total(read):
        return (read(stay_ref) + read(y_ref)) + (read(x_ref) + read(xy_ref))

    vec = split_rows(total(lambda ref: joined(ref[384:448, :])))
    for z in range(GROUPS // 2):
        here = slice(96 * z, 96 * z + 96)
        out_ref[z, 0:96, :] = total(lambda ref, here=here: ref[here, :].astype(F32)).astype(BF16)
        out_ref[z, 96:256, :] = added(cw_ref[z], gotcw_ref[z])
        out_ref[z, 256:320, :] = vec


def vectors_kernel(got_ref, vec_ref):
    vec = joined(got_ref[0, 256:320, :])
    for z in range(1, GROUPS // 2):
        vec = vec + joined(got_ref[z, 256:320, :])
    vec_ref[...] = vec


def rows_to_lanes(rows):
    turned = [rows, pltpu.roll(rows, 96, 1), pltpu.roll(rows, 64, 1), pltpu.roll(rows, 32, 1)]
    lane = lane_iota((1, 128))
    return [
        jnp.where(lane < 96, rows[0:1], turned[1][1:2]),
        jnp.where(lane < 64, turned[1][1:2], turned[2][2:3]),
        jnp.where(lane < 32, turned[2][2:3], turned[3][3:4]),
    ]


def matrices_kernel(got_ref, dre_ref, dim_ref, ore_ref, oim_ref, glu_ref, square):
    def total(start, count):
        value = got_ref[0, start : start + count, :].astype(F32)
        for z in range(1, GROUPS // 2):
            value = value + got_ref[z, start : start + count, :].astype(F32)
        return value

    for start, first_ref, second_ref in ((0, dre_ref, dim_ref), (96, ore_ref, oim_ref)):
        square[0:96, :] = total(start, 96)
        square[96:128, :] = jnp.zeros((32, 128), F32)
        turned = square[...].T
        first_ref[...] = turned[0:64, 0:96]
        second_ref[...] = turned[64:128, 0:96]
    glu_ref[...] = total(192, 64)


def finish_kernel(
    count_all, own_ref, other_ref, gbias_ref, scale_ref, bias_ref, skip_ref, decay_ref, lam_ref, step_ref, rms_ref, vec_ref
):
    vec = own_ref[...] + other_ref[...]
    vec_ref[...] = vec
    for k, ref in enumerate((scale_ref, bias_ref, skip_ref)):
        for c in range(4):
            ref[:, 128 * c : 128 * c + 128] = vec[4 * k + c : 4 * k + c + 1]
    for k, ref in enumerate((decay_ref, lam_ref, step_ref)):
        for c, chunk in enumerate(rows_to_lanes(vec[16 + 4 * k : 20 + 4 * k])):
            ref[128 * c : 128 * c + 128] = chunk.reshape(128)
    total = jnp.sum(vec[28:30], axis=1, keepdims=True)
    lane = lane_iota((1, 2))
    rms_ref[...] = jnp.sqrt(jnp.where(lane == 0, total[0:1], total[1:2]) / count_all)
    place = tensor_pos() * GROUPS + fsdp_pos()
    row = jnp.broadcast_to(vec_ref[pl.ds(12 + place // 8, 1), :], (8, 128))
    gbias_ref[...] = pltpu.roll(row, 128 - 16 * (place % 8), 1)[0:1, 0:16]


TAKES = {
    "pack": 1.5, "standardize": 0.4, "norm": 0.4, "first": 1.4, "states": 1.5, "readout": 0.5, "second": 1.2, "sums": 0.7, "back": 1.6,
    "third": 2.4, "input_grad": 0.5, "matrices": 0.5, "finish": 0.4,
}


def call(kernel, outs, args, scratch=(), specs=None, limit=24):
    name = getattr(kernel, "func", kernel).__name__.removesuffix("_kernel")
    return pl.pallas_call(
        kernel,
        out_shape=outs,
        in_specs=specs or [VM] * len(args),
        out_specs=jax.tree.map(lambda _: VM, outs),
        scratch_shapes=list(scratch),
        compiler_params=pltpu.CompilerParams(vmem_limit_bytes=limit << 20),
        cost_estimate=pl.CostEstimate(flops=0, transcendentals=0, bytes_accessed=int(TAKES.get(name, 0.1) * 3.6e6)),
        name=name,
    )(*args)


def tied(value, other):
    return lax.optimization_barrier((value, other))[0]


def swap(value, axis):
    return lax.ppermute(value, axis, [(0, 1), (1, 0)])


def across(value):
    return lax.ppermute(value, ("fx", "ty"), [(n, 3 - n) for n in range(4)])


def on_device(
    layer_in, grad_out, ln_scale, ln_bias, decay_rate, lam_im, log_dt, in_re, in_im, out_re, out_im, skip, glu_weight, glu_bias, seq_lengths
):
    rows, width = layer_in.shape
    fsdp = lax.axis_size(FSDP)
    pairs, pair = fsdp * 2, 2 * rows
    count_all = float(rows * pairs * 2 * width)
    fast = fsdp == GROUPS
    same_core = (*FSDP, "ty")
    if fast:
        row = lambda v: v.reshape(1, -1)
        sent = call(
            pack_kernel,
            sds((GROUPS // 2, 272, 128), BF16),
            (seq_lengths, in_re.T, in_im.T, out_re.T, out_im.T, glu_weight.T, row(ln_scale), row(ln_bias), row(skip), row(glu_bias),
             row(decay_rate), row(lam_im), row(log_dt)),
            [pltpu.VMEM((128, 128), F32), pltpu.VMEM((4, 64, 96), BF16), pltpu.VMEM((64, 128), BF16), pltpu.VMEM((4, 1, 64), BF16),
             pltpu.VMEM((3, 1, 96), F32), pltpu.SMEM(seq_lengths.shape, jnp.int32), pltpu.SemaphoreType.DMA((13,))],
            [HBM] * 13,
            60,
        )
        mine = lax.all_to_all(sent, "fz", 0, 0, tiled=True)
        own_b, own_cw = lax.optimization_barrier((mine[:, :112], mine[:, 112:]))
        plane_b = [own_b, swap(own_b, "ty"), swap(own_b, "fx"), across(own_b)]
        plane_b, side_cw = lax.optimization_barrier((plane_b, swap(own_cw, "fx")))
        side_cw = jnp.stack([own_cw, side_cw])
        far_cw = swap(side_cw, "ty")
        g = jnp.stack(plane_b).reshape(2, 2, GROUPS // 2, 112, 128)
    else:
        g, g_cw = gathered(
            ln_scale, ln_bias, decay_rate, lam_im, log_dt, in_re, in_im, out_re, out_im, skip, glu_weight, glu_bias, seq_lengths
        )

    xhat, inverse = call(standardize_kernel, (sds((pair, width)), sds((rows, 128))), (layer_in, swap(layer_in, "tc")))
    normed, wide, feat, starts = call(
        norm_kernel,
        (sds((pair, width), BF16), sds((2 * pair, 2 * width), BF16), sds((8, width)), sds((seq_lengths.shape[0], 128))),
        (xhat, g),
    )
    v, lane, row_prm, carry = call(
        functools.partial(first_kernel, pairs),
        (sds((2 * pair, 256)), sds((8, 256)), sds((8, 8, 128)), sds((pairs, 8, 128))),
        (wide, starts, g),
        [pltpu.VMEM((8, 128), F32)],
    )
    came = lax.all_to_all(carry, same_core, 0, 0, tiled=True)
    if fast:
        g_cw = tied((side_cw, far_cw), came)
    state, twice, enter = call(
        states_kernel,
        (sds((2 * pair, 256)), sds((2 * pair, 256), BF16), sds((8, 256))),
        (came, starts, v, lane, row_prm),
        [pltpu.VMEM((8, 128), F32)],
    )
    if fast:
        far = tied(g_cw, twice)
        g_cw = (*g_cw, swap(far[0], "tc"), swap(far[1], "tc"))
    own, away = call(
        readout_kernel, (sds((rows, width)), sds((rows, width))), (twice, *g_cw[:2]), [pltpu.VMEM((pair, width), F32)]
    )
    branch, d_mixed, dlogit, kept, away = call(
        second_kernel,
        (sds((rows, width), BF16), sds((rows, width)), sds((rows, width), BF16), *[sds((rows, 2 * width + 256), BF16)] * 2),
        (own, swap(away, "tc"), grad_out, normed, feat, *g_cw),
        [pltpu.VMEM((width, width), BF16), pltpu.VMEM((rows, width), BF16)],
    )
    got = swap(away, "tc")
    layer_out, part = call(
        sums_kernel, (sds((rows, width), BF16), sds((8, width))), (layer_in, branch, normed, d_mixed, dlogit)
    )
    got, part = lax.optimization_barrier((got, part))
    d_state, carry, stay_cw, leave_cw = call(
        functools.partial(back_kernel, pairs),
        (sds((2 * pair, 256)), sds((pairs, 8, 128)), sds((GROUPS, 160, 128), BF16), sds((GROUPS, 160, 128), BF16)),
        (kept, got, twice, starts, lane, *g_cw[:2]),
        [pltpu.VMEM((pair, width), BF16), pltpu.VMEM((width, 256), BF16), pltpu.VMEM((8, 128), F32)],
    )
    if fast:
        far_cw = swap(leave_cw, "ty")
    came = lax.all_to_all(carry, same_core, 0, 0, tiled=True)
    if fast:
        came, far_cw, stay_cw = lax.optimization_barrier((came, far_cw, stay_cw))
        stay_cw, leave_cw = call(y_cw_kernel, [sds((GROUPS // 2, 160, 128), BF16)] * 2, (stay_cw, far_cw))
        far_cw = swap(leave_cw, "fx")
        came = tied(came, leave_cw)
    stay_b, y_b, x_b, xy_b, d_normed, away = call(
        third_kernel,
        (*[sds((448, 128), BF16)] * 4, sds((rows, width)), sds((rows, width))),
        (came, starts, wide, xhat, v, lane, row_prm, feat, state, d_state, enter, d_mixed, part, g),
        [pltpu.VMEM((8, 128), F32), pltpu.VMEM((2 * pair, 256), BF16), pltpu.VMEM((pair, width), F32), pltpu.VMEM((32, 128), F32)],
    )
    input_grad = lambda away: call(
        input_grad_kernel, sds((rows, width)), (d_normed, swap(away, "tc"), grad_out, xhat, inverse, feat)
    )
    if not fast:
        grad_in = input_grad(away)
        return reduced(layer_out, grad_in, stay_cw, leave_cw, (stay_b, y_b, x_b, xy_b), count_all, fsdp, width)
    sent = call(
        plane_add_kernel,
        sds((GROUPS // 2, 320, 128), BF16),
        (stay_cw, far_cw, stay_b, swap(y_b, "ty"), swap(x_b, "fx"), across(xy_b)),
    )
    got = lax.all_to_all(sent, "fz", 0, 0, tiled=True)
    grad_in = input_grad(tied(away, got))
    vec = call(vectors_kernel, sds((32, 128)), (got,))
    other = swap(vec, "tc")
    d_re, d_im, d_ore, d_oim, d_glu = call(
        matrices_kernel, (*[sds((64, 96))] * 4, sds((64, 128))), (got,), [pltpu.VMEM((128, 128), F32)]
    )
    d_gbias, d_scale, d_bias, d_skip, g_decay, g_lam, g_step, rms = call(
        functools.partial(finish_kernel, count_all),
        (sds((1, 16)), *[sds((1, 512))] * 3, *[sds((384,))] * 3, sds((1, 2))),
        (vec, other),
        [pltpu.VMEM((32, 128), F32)],
    )
    flat = lambda value: value.reshape(-1)
    return (
        layer_out, grad_in, flat(d_scale), flat(d_bias), g_decay, g_lam, g_step, d_re.T, d_im.T, d_ore.T, d_oim.T,
        flat(d_skip), d_glu.T, flat(d_gbias), flat(rms),
    )


def gathered(ln_scale, ln_bias, decay_rate, lam_im, log_dt, in_re, in_im, out_re, out_im, skip, glu_weight, glu_bias, seq_lengths):
    tens = tensor_pos()
    full = lambda value, axis: lax.all_gather(value, FSDP, axis=axis, tiled=True)

    def pair(first, second):
        halves = jnp.stack([first.reshape(-1, GROUPS, 64), second.reshape(-1, GROUPS, 64)], axis=2)
        return halves.reshape(-1, GROUPS, 128).swapaxes(0, 1)

    gate = lax.dynamic_slice_in_dim(full(glu_weight, 1), tens * 128, 128, 0).T.reshape(GROUPS, 64, 128)
    vectors = [pair(full(ln_scale, 0)[None], full(ln_bias, 0)[None]), pair(full(skip, 0)[None], full(glu_bias, 0)[None])]
    for value in (decay_rate, lam_im, log_dt):
        value = jnp.pad(value, (0, 32))
        for _ in range(3):
            piece = lax.reduce_precision(value, 8, 7)
            value = value - piece
            vectors.append(jnp.broadcast_to(piece.astype(BF16)[None, None], (GROUPS, 1, 128)))
    starts = jnp.cumsum(seq_lengths) - seq_lengths
    for value in (starts >> 8, starts & 255):
        value = jnp.pad(value, (0, 128 - value.shape[0])).astype(BF16)
        vectors.append(jnp.broadcast_to(value[None, None], (GROUPS, 1, 128)))
    vectors.append(jnp.zeros((GROUPS, 3, 128), BF16))
    packet = jnp.concatenate(
        [pair(full(in_re, 1), full(in_im, 1)), *vectors, pair(full(out_re, 1), full(out_im, 1)), gate],
        axis=1,
    )
    everyone = lax.all_gather(packet, TENSOR, axis=0).reshape(2, 2, GROUPS // 2, 2, 272, 128)
    x, y, core = (lax.axis_index(axis) for axis in ("fx", "ty", "tc"))
    own_x = lambda value, axis: jnp.stack([lax.dynamic_index_in_dim(value, x ^ j, axis, keepdims=False) for j in range(2)])
    g_cw = []
    for i in range(2):
        both = lax.dynamic_index_in_dim(everyone, core ^ i, 1, keepdims=False)
        slots = [own_x(lax.dynamic_index_in_dim(both, y ^ m, 0, keepdims=False), 1) for m in range(2)]
        g_cw += [slot[:, :, 112:] for slot in slots]
        if i == 0:
            g = jnp.stack(slots, axis=1)[:, :, :, :112]
    return g, g_cw


def reduced(layer_out, grad_in, stay_cw, leave_cw, plane_b, count_all, fsdp, width):
    tens = tensor_pos()
    x = lax.axis_index("fx")

    def canonical(slots):
        out = jnp.zeros((4, GROUPS, *slots[0].shape[2:]), F32)
        for m, slot in enumerate(slots):
            parts = [lax.dynamic_index_in_dim(slot.astype(F32), x ^ n, 1) for n in range(2)]
            block = jnp.concatenate(parts, axis=1).reshape(1, GROUPS, *slot.shape[2:])
            out = lax.dynamic_update_slice_in_dim(out, block, slot_pos(m, 0), 0)
        return out

    def natural(slots):
        halves = canonical(slots).reshape(4, GROUPS, -1, 2, 64).transpose(3, 0, 2, 1, 4)
        return halves[0].reshape(-1, width), halves[1].reshape(-1, width)

    def scattered(value):
        value = lax.psum_scatter(value, TENSOR, scatter_dimension=0, tiled=True)
        return lax.psum_scatter(value, FSDP, scatter_dimension=1, tiled=True)

    blocks = [value[:384].reshape(GROUPS // 2, 96, 128) for value in plane_b]
    d_re, d_im = natural([jnp.stack([blocks[m], blocks[2 + m]], axis=1) for m in range(2)])
    cw = [value.reshape(GROUPS // 2, 2, 160, 128) for value in (stay_cw, leave_cw)]
    d_ore, d_oim = natural([value[:, :, :96] for value in cw])
    d_glu = canonical([value[:, :, 96:] for value in cw]).reshape(4, width, 128).swapaxes(1, 2).reshape(-1, width)
    vec = lax.psum(joined(plane_b[0][384:448]), AXES)
    states = lambda k: vec[16 + 4 * k : 20 + 4 * k, :96].reshape(-1)
    own = width // (4 * fsdp)
    place = tens * fsdp + fsdp_pos()
    d_gbias = lax.dynamic_slice_in_dim(vec[12:16].reshape(-1), place * own, own, 0)
    rms = jnp.sqrt(jnp.sum(vec[28:30], axis=1) / count_all)
    return (
        layer_out, grad_in, vec[0:4].reshape(-1), vec[4:8].reshape(-1), states(0), states(1), states(2), scattered(d_re), scattered(d_im),
        scattered(d_ore), scattered(d_oim), vec[8:12].reshape(-1), scattered(d_glu), d_gbias, rms,
    )


def solution(mesh):
    shape = (mesh.shape["fsdp"] // 2, 2, mesh.shape["tensor"] // 2, 2)
    split = Mesh(mesh.devices.reshape(shape), AXES)
    tokens, matrix = P(AXES, None), P(TENSOR, FSDP)
    return jax.shard_map(
        on_device,
        mesh=split,
        in_specs=(
            tokens, tokens, P(FSDP), P(FSDP), P(TENSOR), P(TENSOR), P(TENSOR), matrix, matrix, matrix, matrix,
            P(FSDP), P(None, FSDP), P(FSDP), P(),
        ),
        out_specs=(
            tokens, tokens, P(), P(), P(), P(), P(), matrix, matrix, matrix, matrix, P(), matrix, P((*TENSOR, *FSDP)), P(),
        ),
        check_vma=False,
    )
```

```python
import functools

import jax
import jax.numpy as jnp
from jax import lax
from jax.experimental import pallas as pl
from jax.experimental.pallas import tpu as pltpu
from jax.sharding import Mesh
from jax.sharding import PartitionSpec as P

F32 = jnp.float32
BF16 = jnp.bfloat16
FSDP = ("fz", "fx")
TENSOR = ("ty", "tc")
AXES = (*FSDP, *TENSOR)
HBM = pl.BlockSpec(memory_space=pltpu.HBM)
VM = pl.BlockSpec(memory_space=pltpu.VMEM)
SM = pl.BlockSpec(memory_space=pltpu.SMEM)

GROUPS = 8
VEC = 96


def sds(shape, dtype=F32):
    return jax.ShapeDtypeStruct(shape, dtype)


def low_half(shape):
    return lax.broadcasted_iota(jnp.int32, shape, len(shape) - 1) < 64


def lane_iota(shape):
    return lax.broadcasted_iota(jnp.int32, shape, len(shape) - 1)


def dot(a, b, dims):
    return lax.dot_general(a, b, (dims, ((), ())), preferred_element_type=F32)


NT = ((1,), (1,))
NN = ((1,), (0,))
TN = ((0,), (0,))


def flipped():
    return lax.axis_index("fx") == 1


def part_lanes(part, m):
    return slice(256 * part + 128 * m, 256 * part + 128 * m + 128)


def slot_pos(m, core):
    return (lax.axis_index("ty") ^ m) * 2 + (lax.axis_index("tc") ^ core)


def own_rows(rows):
    return pl.ds(pl.multiple_of(lax.axis_index("tc") * rows, rows), rows)


def other_rows(rows):
    return pl.ds(pl.multiple_of((1 - lax.axis_index("tc")) * rows, rows), rows)


def piece(ref, m, f, start, count):
    return ref[f % 2, m, f // 2, start : start + count, :]


def natural(get, ref):
    lo = low_half((96, 128))
    for m in range(2):
        for part in range(2):
            lanes = part_lanes(part, m)
            ref[lanes.start + 96 : lanes.stop, :] = jnp.zeros((32, 512), BF16)
        for z in range(GROUPS // 2):
            even, odd = get(m, z, 0).astype(F32), get(m, z, 1).astype(F32)
            here = slice(128 * z, 128 * z + 128)
            ref[128 * m : 128 * m + 96, here] = jnp.where(lo, even, pltpu.roll(odd, 64, 1)).astype(BF16)
            ref[256 + 128 * m : 256 + 128 * m + 96, here] = jnp.where(lo, pltpu.roll(even, 64, 1), odd).astype(BF16)


def packets(value, m, z):
    lo = low_half((96, 128))
    here = slice(128 * z, 128 * z + 128)
    re, im = value[128 * m : 128 * m + 96, here], value[256 + 128 * m : 256 + 128 * m + 96, here]
    return jnp.where(lo, re, pltpu.roll(im, 64, 1)), jnp.where(lo, pltpu.roll(re, 64, 1), im)


def feature_rows(ref, row):
    lo = low_half((8, 128))
    flip = flipped()
    first, second = [], []
    for c in range(GROUPS // 2):
        a = jnp.broadcast_to(piece(ref, 0, 2 * c, row, 1).astype(F32), (8, 128))
        b = jnp.broadcast_to(piece(ref, 0, 2 * c + 1, row, 1).astype(F32), (8, 128))
        a, b = jnp.where(flip, b, a), jnp.where(flip, a, b)
        first.append(jnp.where(lo, a, pltpu.roll(b, 64, 1)))
        second.append(jnp.where(lo, pltpu.roll(a, 64, 1), b))
    return jnp.concatenate(first, axis=1)[:1], jnp.concatenate(second, axis=1)[:1]


def cmul(a, b):
    return a[0] * b[0] - a[1] * b[1], a[0] * b[1] + a[1] * b[0]


def tensor_pos():
    return lax.axis_index("ty") * 2 + lax.axis_index("tc")


def fsdp_pos():
    return lax.axis_index("fz") * 2 + lax.axis_index("fx")


def pair_pos():
    return fsdp_pos() * 2 + lax.axis_index("ty")


def offsets_of(start_ref):
    return [start_ref[n : n + 1, :] for n in range(start_ref.shape[0])]


def starts_until(offsets, base, rows):
    at = (lax.broadcasted_iota(jnp.int32, (rows, 128), 0) + base).astype(F32)
    count = jnp.zeros((rows, 128), F32)
    for off in offsets:
        count = count + jnp.where((at >= off) & (off >= at[0:1]), 1.0, 0.0)
    return count


def no_start(offsets, base, rows):
    link = jnp.ones((1, 128), F32)
    first = (jnp.zeros((1, 128), jnp.int32) + base).astype(F32)
    for off in offsets:
        link = jnp.where((off >= first) & (off < first + rows), 0.0, link)
    return link


def expm1(x):
    series = x * (1 + x / 2 * (1 + x / 3 * (1 + x / 4 * (1 + x / 5 * (1 + x / 6 * (1 + x / 7))))))
    return jnp.where(jnp.abs(x) < 0.25, series, jnp.exp(x) - 1.0)


def discretize(decay_rate, lam_im, log_dt):
    step_size = jnp.exp(log_dt)
    lam_re = -decay_rate
    magnitude = jnp.exp(lam_re * step_size)
    phase = lam_im * step_size
    abar_re = magnitude * jnp.cos(phase)
    abar_im = magnitude * jnp.sin(phase)
    half_sin = jnp.sin(0.5 * phase)
    less_re = expm1(lam_re * step_size) * jnp.cos(phase) - 2.0 * half_sin * half_sin
    denom = lam_re * lam_re + lam_im * lam_im
    coef_re = (less_re * lam_re + abar_im * lam_im) / denom
    coef_im = (abar_im * lam_re - less_re * lam_im) / denom
    return abar_re, abar_im, coef_re, coef_im, step_size


def pack_kernel(*refs):
    *inputs, out_ref, square, four, glu_ref, halves, params, lengths, sems = refs
    seq_hbm, matrices, glu_hbm, features, states = inputs[0], inputs[1:5], inputs[5], inputs[6:10], inputs[10:13]
    units = pl.multiple_of(tensor_pos() * 128, 128)
    pairs = [(ref, four.at[k]) for k, ref in enumerate(matrices)]
    pairs += [(glu_hbm.at[:, pl.ds(units, 128)], glu_ref), (seq_hbm, lengths)]
    pairs += [(ref, halves.at[k]) for k, ref in enumerate(features)]
    pairs += [(ref, params.at[k]) for k, ref in enumerate(states)]
    copies = [pltpu.make_async_copy(source, target, sems.at[k]) for k, (source, target) in enumerate(pairs)]
    for copy in copies:
        copy.start()
    square[:, 96:128] = jnp.zeros((128, 32), F32)
    for copy in copies:
        copy.wait()
    vec = [
        jnp.concatenate([halves[0], halves[1]], axis=1).astype(F32),
        jnp.concatenate([halves[2], halves[3]], axis=1).astype(F32),
    ]
    for k in range(3):
        value = jnp.concatenate([params[k], jnp.zeros((1, 32), F32)], axis=1)
        for _ in range(3):
            part = value.astype(BF16).astype(F32)
            value = value - part
            vec.append(part)
    lane = lane_iota((1, 128))
    upper, lower, total = jnp.zeros((1, 128), jnp.int32), jnp.zeros((1, 128), jnp.int32), 0
    for n in range(lengths.shape[0]):
        upper = jnp.where(lane == n, total >> 8, upper)
        lower = jnp.where(lane == n, total & 255, lower)
        total = total + lengths[n]
    vec += [upper.astype(F32), lower.astype(F32)]
    vec.append(jnp.zeros((16 - len(vec), 128), F32))
    vec = jnp.concatenate(vec, axis=0).astype(BF16)
    pieces = []
    for k in (0, 2):
        square[0:64, 0:96] = four[k].astype(F32)
        square[64:128, 0:96] = four[k + 1].astype(F32)
        pieces.append(square[...].T[0:96].astype(BF16))
    packet = jnp.concatenate([pieces[0], vec, pieces[1], glu_ref[...]], axis=0)
    for z in range(GROUPS // 2):
        out_ref[z] = packet


def params_of(ref, vec_row):
    lane = lane_iota((8, 128))
    out = []
    for k, safe in enumerate((1.0, 0.0, 0.0)):
        rows = []
        for m in range(2):
            part = piece(ref, m, 0, vec_row, 16).astype(F32)
            rows.append((part[2 + 3 * k : 3 + 3 * k] + part[3 + 3 * k : 4 + 3 * k]) + part[4 + 3 * k : 5 + 3 * k])
        value = jnp.concatenate(rows + [jnp.full((6, 128), safe, F32)], axis=0)
        out.append(jnp.where(lane < 96, value, safe))
    return out


def carry_block(re_rows, im_rows, scratch):
    for m in range(2):
        y = lax.axis_index("ty") ^ m
        scratch[pl.ds(y, 1), :] = re_rows[m]
        scratch[pl.ds(2 + y, 1), :] = im_rows[m]


def standardize_kernel(x_ref, other_ref, xhat_ref, inv_ref):
    rows, width = x_ref.shape
    for ref, where, own in ((x_ref, own_rows(rows), True), (other_ref, other_rows(rows), False)):
        x = ref[...].astype(F32)
        centered = x - jnp.sum(x, axis=1, keepdims=True) / width
        inverse = lax.rsqrt(jnp.sum(centered * centered, axis=1, keepdims=True) / width + 1e-05)
        xhat_ref[where, :] = centered * inverse
        if own:
            inv_ref[...] = jnp.broadcast_to(inverse, (rows, 128))


def norm_kernel(xhat_ref, g_ref, normed_ref, feat_ref, start_ref):
    scale, bias = feature_rows(g_ref, VEC)
    feat_ref[0:1] = scale
    feat_ref[1:2], feat_ref[2:3] = feature_rows(g_ref, VEC + 1)
    normed = (xhat_ref[...] * scale + bias).astype(BF16)
    normed_ref[...] = normed
    upper, lower = (piece(g_ref, 0, 0, VEC + 11 + k, 1).astype(F32) for k in range(2))
    starts = upper * 256.0 + lower
    for n in range(start_ref.shape[0]):
        start_ref[n : n + 1, :] = jnp.broadcast_to(starts[:, n : n + 1], (1, 128))


def first_kernel(pairs, normed_ref, start_ref, g_ref, b_ref, v_ref, lane_ref, row_ref, send_ref, scratch):
    rows = normed_ref.shape[0]
    natural(lambda m, z, x: g_ref[lax.axis_index("fx") ^ x, m, z, 0:96, :], b_ref)
    v_ref[...] = dot(normed_ref[...], b_ref[...], NT)

    decay, lam, log_dt = params_of(g_ref, VEC)
    abar_re, abar_im, coef_re, coef_im, step_size = discretize(decay, lam, log_dt)
    power = (abar_re, abar_im)
    for _ in range(8):
        power = cmul(power, power)
    scratch[...] = jnp.zeros((8, 128), F32)
    carry_block([power[0][m : m + 1] for m in range(2)], [power[1][m : m + 1] for m in range(2)], scratch)
    for k, value in enumerate((decay, lam, step_size, abar_re, abar_im, coef_re, coef_im, scratch[...])):
        row_ref[k] = value
    for k, value in enumerate((abar_re, abar_im, coef_re, coef_im)):
        for m in range(2):
            lane_ref[k : k + 1, 128 * m : 128 * m + 128] = value[m : m + 1]

    count = starts_until(offsets_of(start_ref), pair_pos() * rows, rows)
    open_tail = jnp.where(count == count[rows - 1 : rows], 1.0, 0.0)
    last = ([], [])
    for m in range(2):
        eight, tail = eighth_powers((abar_re[m : m + 1], abar_im[m : m + 1]), lambda sub: 7 - sub)
        b = (coef_re[m : m + 1], coef_im[m : m + 1])
        acc = (jnp.zeros((8, 128), F32), jnp.zeros((8, 128), F32))
        for blk in range(rows // 8):
            here = slice(8 * blk, 8 * blk + 8)
            drive = cmul(b, (v_ref[here, part_lanes(0, m)], v_ref[here, part_lanes(1, m)]))
            moved = cmul(eight, acc)
            acc = (moved[0] + drive[0] * open_tail[here], moved[1] + drive[1] * open_tail[here])
        total = cmul(tail, acc)
        last[0].append(column_sum(total[0]))
        last[1].append(column_sum(total[1]))
    carry_block(last[0], last[1], scratch)
    packet = scratch[...]
    for d in range(pairs):
        send_ref[d] = packet


def eighth_powers(a, exponent_of):
    exponent = exponent_of(lax.broadcasted_iota(jnp.int32, (8, 128), 0))
    a = (jnp.broadcast_to(a[0], (8, 128)), jnp.broadcast_to(a[1], (8, 128)))
    tile = (jnp.ones((8, 128), F32), jnp.zeros((8, 128), F32))
    for bit in range(4):
        if bit == 3:
            eight = a
        taken = (exponent & (1 << bit)) != 0
        more = cmul(tile, a)
        tile = (jnp.where(taken, more[0], tile[0]), jnp.where(taken, more[1], tile[1]))
        a = cmul(a, a)
    return eight, tile


def all_rows(row):
    return jnp.broadcast_to(row, (8, 128))


def scan(read, powers, carry, count, reverse, emit):
    groups = count.shape[0] // 8
    sub = lax.broadcasted_iota(jnp.int32, (8, 128), 0)
    steps, eights, tiles = [], [], []
    for a in powers:
        squared = cmul(a, a)
        steps.append((a, squared, cmul(squared, squared)))
        eight, tile = eighth_powers(a, (lambda sub: 8 - sub) if reverse else (lambda sub: sub + 1))
        eights.append(eight)
        tiles.append(tile)
    carry = [(all_rows(c[0]), all_rows(c[1])) for c in carry]
    edge = 0 if reverse else 7
    seen = all_rows(count[8 * groups - 1 :]) if reverse else jnp.zeros((8, 128), F32)
    for b in range(groups - 1, -1, -1) if reverse else range(groups):
        here = count[8 * b : 8 * b + 8]
        links = []
        for k in (1, 2, 4):
            other = pltpu.roll(here, 8 - k if reverse else k, 0)
            links.append(((sub < 8 - k) if reverse else (sub >= k)) & (other == here))
        came = here == seen
        last = all_rows(here[edge : edge + 1])
        through = last == seen
        seen = last
        for m in range(2):
            value = read(b, m)
            for k, link, a in zip((1, 2, 4), links, steps[m]):
                shift = 8 - k if reverse else k
                more = cmul(a, (pltpu.roll(value[0], shift, 0), pltpu.roll(value[1], shift, 0)))
                value = (value[0] + jnp.where(link, more[0], 0.0), value[1] + jnp.where(link, more[1], 0.0))
            more = cmul(tiles[m], carry[m])
            done = (value[0] + jnp.where(came, more[0], 0.0), value[1] + jnp.where(came, more[1], 0.0))
            more = cmul(eights[m], carry[m])
            carry[m] = (
                all_rows(value[0][edge : edge + 1]) + jnp.where(through, more[0], 0.0),
                all_rows(value[1][edge : edge + 1]) + jnp.where(through, more[1], 0.0),
            )
            emit(b, m, done)


def carried(recv_ref, row_ref, offsets, rows, reverse, scratch):
    pairs = recv_ref.shape[0]
    power = row_ref[7]
    pre, pim = power[0:2], power[2:4]
    if reverse:
        pim = -pim
    place = pair_pos()

    def turn(k, state):
        j = pairs - 1 - k if reverse else k
        link = no_start(offsets, j * rows, rows)
        got = recv_ref[j]
        new = cmul((pre * link, pim * link), state)
        return new[0] + got[0:2], new[1] + got[2:4]

    zero = jnp.zeros((2, 128), F32)
    out = lax.fori_loop(0, pairs - 1 - place if reverse else place, turn, (zero, zero))
    scratch[0:2, :] = out[0]
    scratch[2:4, :] = out[1]
    own = [lax.axis_index("ty") ^ m for m in range(2)]
    return [scratch[pl.ds(y, 1), :] for y in own], [scratch[pl.ds(2 + y, 1), :] for y in own]


def column_sum(value):
    return jnp.sum(value, axis=0, keepdims=True)


def states_kernel(
    recv_ref, start_ref, v_ref, lane_ref, row_ref, cw_ref, state_ref, twice_ref, enter_ref, c_ref, scratch
):
    rows = v_ref.shape[0]
    offsets = offsets_of(start_ref)
    count = starts_until(offsets, pair_pos() * rows, rows)
    enter = carried(recv_ref, row_ref, offsets, rows, False, scratch)
    for part in range(2):
        for m in range(2):
            enter_ref[0:1, part_lanes(part, m)] = enter[part][m]
    powers = [(lane_ref[0:1, 128 * m : 128 * m + 128], lane_ref[1:2, 128 * m : 128 * m + 128]) for m in range(2)]

    def read(b, m):
        here, lanes = slice(8 * b, 8 * b + 8), slice(128 * m, 128 * m + 128)
        return cmul((lane_ref[2:3, lanes], lane_ref[3:4, lanes]), (v_ref[here, part_lanes(0, m)], v_ref[here, part_lanes(1, m)]))

    def emit(b, m, value):
        for part in range(2):
            state_ref[8 * b : 8 * b + 8, part_lanes(part, m)] = value[part]

    scan(read, powers, [(enter[0][m], enter[1][m]) for m in range(2)], count, False, emit)
    twice_ref[:, 0:256] = state_ref[:, 0:256].astype(BF16) * 2
    twice_ref[:, 256:512] = state_ref[:, 256:512].astype(BF16) * -2
    natural(lambda m, z, x: cw_ref[lax.axis_index("fx") ^ x, m, z, 0:96, :], c_ref)


def readout_kernel(twice_ref, c_ref, own_ref, away_ref, scratch):
    rows = own_ref.shape[0]
    scratch[...] = dot(twice_ref[...], c_ref[...], NN)
    own_ref[...] = scratch[own_rows(rows), :]
    away_ref[...] = scratch[other_rows(rows), :]


def second_kernel(
    own_ref, got_ref, up_ref, normed_ref, feat_ref, cw_ref, othercw_ref,
    branch_ref, dmixed_ref, dlogit_ref, mine_ref, away_ref, gate_ref, all_ref,
):
    rows, width = up_ref.shape
    for core, ref in enumerate((cw_ref, othercw_ref)):
        for m in range(2):
            lanes = pl.ds(pl.multiple_of(slot_pos(m, core) * 128, 128), 128)
            for f in range(GROUPS):
                place = (f // 2) * 2 + (lax.axis_index("fx") ^ (f % 2))
                gate_ref[pl.ds(pl.multiple_of(place * 64, 64), 64), lanes] = piece(ref, m, f, 96, 64)
    skip, gate_bias = feat_ref[1:2], feat_ref[2:3]
    normed = normed_ref[own_rows(rows), :].astype(F32)
    mixed = (own_ref[...] + got_ref[...]) + skip * normed
    cdf = 0.5 * (1.0 + lax.erf(mixed * 0.7071067811865476))
    act_low = (mixed * cdf).astype(BF16)
    act = act_low.astype(F32)
    w_gate = gate_ref[...]
    logit = dot(act_low, w_gate, NN) + gate_bias
    gate = 1.0 / (1.0 + jnp.exp(-logit))
    branch_ref[...] = (act * gate).astype(BF16)
    up = up_ref[...].astype(F32)
    dlogit = (up * act * gate * (1.0 - gate)).astype(BF16)
    dlogit_ref[...] = dlogit
    all_ref[...] = dlogit
    d_act = dot(dlogit, w_gate, NT) + up * gate
    slope = cdf + mixed * jnp.exp(-0.5 * mixed * mixed) * 0.3989422804014327
    d_mixed = d_act * slope
    dmixed_ref[...] = d_mixed
    for core, ref in enumerate((mine_ref, away_ref)):
        ref[:, 0:width] = d_mixed.astype(BF16)
        ref[:, width : 2 * width] = act_low
        for m in range(2):
            lanes = pl.ds(pl.multiple_of(slot_pos(m, core) * 128, 128), 128)
            ref[:, 2 * width + 128 * m : 2 * width + 128 * m + 128] = all_ref[:, lanes]


def sums_kernel(x_ref, branch_ref, normed_ref, dmixed_ref, dlogit_ref, out_ref, part_ref):
    x = x_ref[...].astype(F32)
    branch = branch_ref[...].astype(F32)
    out_ref[...] = (x + branch).astype(BF16)
    skip = column_sum(dmixed_ref[...] * normed_ref[own_rows(x_ref.shape[0]), :].astype(F32))
    for k, value in enumerate((skip, column_sum(dlogit_ref[...].astype(F32)), column_sum(x * x), column_sum(branch * branch))):
        part_ref[k : k + 1, :] = value


def back_kernel(
    pairs, mine_ref, got_ref, twice_ref, start_ref, lane_ref, c_ref,
    dstate_ref, send_ref, stay_ref, leave_ref, dy_ref, dgate_ref, scratch, all_ref,
):
    rows, width = dy_ref.shape
    half = rows // 2
    dy_ref[own_rows(half), :] = mine_ref[:, 0:width]
    dy_ref[other_rows(half), :] = got_ref[:, 0:width]
    d_state = dot(dy_ref[...], c_ref[...], NT)
    dstate_ref[:, 0:256] = d_state[:, 0:256] * 2.0
    dstate_ref[:, 256:512] = d_state[:, 256:512] * -2.0
    count = starts_until(offsets_of(start_ref), pair_pos() * rows, rows)
    head = jnp.where(count == 0.0, 1.0, 0.0)
    first = ([], [])
    for m in range(2):
        lanes = slice(128 * m, 128 * m + 128)
        eight, tail = eighth_powers((lane_ref[0:1, lanes], -lane_ref[1:2, lanes]), lambda sub: sub + 1)
        acc = (jnp.zeros((8, 128), F32), jnp.zeros((8, 128), F32))
        for blk in range(rows // 8 - 1, -1, -1):
            here = slice(8 * blk, 8 * blk + 8)
            moved = cmul(eight, acc)
            acc = (
                moved[0] + dstate_ref[here, part_lanes(0, m)] * head[here],
                moved[1] + dstate_ref[here, part_lanes(1, m)] * head[here],
            )
        total = cmul(tail, acc)
        first[0].append(column_sum(total[0]))
        first[1].append(column_sum(total[1]))
    scratch[...] = jnp.zeros((8, 128), F32)
    carry_block(first[0], first[1], scratch)
    packet = scratch[...]
    for d in range(pairs):
        send_ref[d] = packet
    d_c = dot(twice_ref[...], dy_ref[...], TN)
    act = slice(width, 2 * width)
    units = slice(2 * width, 2 * width + 256)
    d_gate = dot(mine_ref[:, act], mine_ref[:, units], TN) + dot(got_ref[:, act], got_ref[:, units], TN)
    dgate_ref[...] = d_gate.astype(BF16)
    for m in range(2):
        for z in range(GROUPS // 2):
            for x, packet in enumerate(packets(d_c, m, z)):
                j = lax.axis_index("fx") ^ x
                all_ref[j, m, z, 0:96, :] = packet.astype(BF16)
                all_ref[j, m, z, 96:160, :] = dgate_ref[128 * z + 64 * x : 128 * z + 64 * x + 64, 128 * m : 128 * m + 128]
    stay_ref[...] = all_ref[0]
    leave_ref[...] = all_ref[1]


def split_rows(value):
    upper = value.astype(BF16)
    return jnp.concatenate([upper, (value - upper.astype(F32)).astype(BF16)], axis=0)


def third_kernel(
    recv_ref, start_ref, normed_ref, xhat_ref, v_ref, lane_ref, row_ref, feat_ref, state_ref, dstate_ref, enter_ref, dmixed_ref,
    part_ref, b_ref, stay_ref, y_ref, x_ref, xy_ref, dn_ref, dnaway_ref, scratch, dv_ref, all_ref, vec_ref,
):
    rows, width = xhat_ref.shape
    half = rows // 2
    offsets = offsets_of(start_ref)
    count = starts_until(offsets, pair_pos() * rows, rows)
    later = carried(recv_ref, row_ref, offsets, rows, True, scratch)
    sub = lax.broadcasted_iota(jnp.int32, (8, 128), 0)
    none = jnp.zeros((1, 128), F32)
    totals = [[jnp.zeros((8, 128), F32) for _ in range(4)] for _ in range(2)]
    powers = [(lane_ref[0:1, 128 * m : 128 * m + 128], -lane_ref[1:2, 128 * m : 128 * m + 128]) for m in range(2)]

    def read(b, m):
        value = [dstate_ref[8 * b : 8 * b + 8, part_lanes(part, m)] for part in range(2)]
        if b == rows // 8 - 1:
            value = [value[part] + jnp.where(sub == 7, later[part][m], 0.0) for part in range(2)]
        return tuple(value)

    def emit(b, m, adj):
        here, lanes = slice(8 * b, 8 * b + 8), slice(128 * m, 128 * m + 128)
        seen = count[8 * b - 1 : 8 * b] if b else none
        keep = count[here] == jnp.where(sub == 0, seen, pltpu.roll(count[here], 1, 0))
        prev = []
        for part in range(2):
            edge = state_ref[8 * b - 1 : 8 * b, part_lanes(part, m)] if b else enter_ref[0:1, part_lanes(part, m)]
            moved = jnp.where(sub == 0, edge, pltpu.roll(state_ref[here, part_lanes(part, m)], 1, 0))
            prev.append(jnp.where(keep, moved, 0.0))
        v = (v_ref[here, part_lanes(0, m)], v_ref[here, part_lanes(1, m)])
        for k, (p, q) in enumerate((prev, v)):
            totals[m][2 * k] = totals[m][2 * k] + (adj[0] * p + adj[1] * q)
            totals[m][2 * k + 1] = totals[m][2 * k + 1] + (adj[1] * p - adj[0] * q)
        dv = cmul((lane_ref[2:3, lanes], -lane_ref[3:4, lanes]), adj)
        for part in range(2):
            dvf_ref[here, part_lanes(part, m)] = dv[part]

    dvf_ref = all_ref
    scan(read, powers, [(none, none), (none, none)], count, True, emit)
    sums = [[column_sum(totals[m][k]) for m in range(2)] for k in range(4)]
    dv_ref[...] = dvf_ref[...].astype(BF16)
    dv = dv_ref[...]
    d_b = dot(dv, normed_ref[...], TN)
    flip = flipped()
    for m, (near, side) in enumerate(((stay_ref, x_ref), (y_ref, xy_ref))):
        for z in range(GROUPS // 2):
            even, odd = packets(d_b, m, z)
            here = slice(96 * z, 96 * z + 96)
            near[here, :] = jnp.where(flip, odd, even).astype(BF16)
            side[here, :] = jnp.where(flip, even, odd).astype(BF16)
    all_ref[...] = dot(dv, b_ref[...], NN)
    dnaway_ref[...] = all_ref[other_rows(half), :]
    own = all_ref[own_rows(half), :] + dmixed_ref[...] * feat_ref[1:2]
    dn_ref[...] = own
    all_ref[own_rows(half), :] = own
    d_normed = all_ref[...]
    vector = [column_sum(d_normed * xhat_ref[...]), column_sum(d_normed), part_ref[0:1, :], part_ref[1:2, :]]
    for k, value in enumerate(vector):
        for c in range(4):
            vec_ref[4 * k + c : 4 * k + c + 1, :] = value[:, 128 * c : 128 * c + 128]
    g = [jnp.concatenate(pair + [jnp.zeros((6, 128), F32)], axis=0) for pair in sums]
    decay, lam, step, abar_re, abar_im, coef_re, coef_im = (row_ref[k] for k in range(7))
    d_abar, d_coef = (g[0], g[1]), (g[2], g[3])
    denom = decay * decay + lam * lam
    numer = (step * abar_re - coef_re, step * abar_im - coef_im)
    ratio = cmul(numer, (-decay / denom, -lam / denom))
    to_lam_a = cmul((step * abar_re, -step * abar_im), d_abar)
    to_lam_c = cmul((ratio[0], -ratio[1]), d_coef)
    g_decay = -(to_lam_a[0] + to_lam_c[0])
    g_lam = to_lam_a[1] + to_lam_c[1]
    slope = cmul((-decay, lam), (abar_re, abar_im))
    g_step = (slope[0] * d_abar[0] + slope[1] * d_abar[1] + abar_re * d_coef[0] + abar_im * d_coef[1]) * step
    vec_ref[16:32, :] = jnp.zeros((16, 128), F32)
    for k, value in enumerate((g_decay, g_lam, g_step)):
        for m in range(2):
            vec_ref[pl.ds(16 + 4 * k + slot_pos(m, 0), 1), :] = value[m : m + 1]
    for k in range(2):
        squares = part_ref[2 + k : 3 + k, :]
        total = squares[:, 0:128]
        for c in range(1, 4):
            total = total + squares[:, 128 * c : 128 * c + 128]
        vec_ref[28 + k : 29 + k, :] = total
    vec_ref[30:32, :] = jnp.zeros((2, 128), F32)
    vec = split_rows(vec_ref[...])
    for ref in (stay_ref, y_ref, x_ref, xy_ref):
        ref[384:448, :] = vec


def input_grad(dn_ref, got_ref, up_ref, xhat_ref, inv_ref, feat_ref, gin_ref):
    rows, width = up_ref.shape
    xhat = xhat_ref[own_rows(rows), :]
    d_xhat = (dn_ref[...] + got_ref[...]) * feat_ref[0:1]
    mean = jnp.sum(d_xhat, axis=1, keepdims=True) / width
    mean_hat = jnp.sum(d_xhat * xhat, axis=1, keepdims=True) / width
    gin_ref[...] = up_ref[...].astype(F32) + inv_ref[:, 0:1] * (d_xhat - mean - xhat * mean_hat)


def input_grad_kernel(*refs):
    input_grad(*refs)


def added(a, b):
    return (a.astype(F32) + b.astype(F32)).astype(BF16)


def joined(packet):
    return packet[0:32].astype(F32) + packet[32:64].astype(F32)


def middle_kernel(keep_ref, got_ref, stay_ref, leave_ref):
    stay_ref[...] = added(keep_ref[0], got_ref[0])
    leave_ref[...] = added(keep_ref[1], got_ref[1])


def plane_add_kernel(cw_ref, gotcw_ref, stay_ref, y_ref, x_ref, xy_ref, out_ref):
    def total(read):
        return (read(stay_ref) + read(y_ref)) + (read(x_ref) + read(xy_ref))

    vec = split_rows(total(lambda ref: joined(ref[384:448, :])))
    for z in range(GROUPS // 2):
        here = slice(96 * z, 96 * z + 96)
        out_ref[z, 0:96, :] = total(lambda ref, here=here: ref[here, :].astype(F32)).astype(BF16)
        out_ref[z, 96:256, :] = added(cw_ref[z], gotcw_ref[z])
        out_ref[z, 256:320, :] = vec


def vectors_kernel(got_ref, vec_ref):
    vec = joined(got_ref[0, 256:320, :])
    for z in range(1, GROUPS // 2):
        vec = vec + joined(got_ref[z, 256:320, :])
    vec_ref[...] = vec


def rows_to_lanes(rows):
    turned = [rows, pltpu.roll(rows, 96, 1), pltpu.roll(rows, 64, 1), pltpu.roll(rows, 32, 1)]
    lane = lane_iota((1, 128))
    return [
        jnp.where(lane < 96, rows[0:1], turned[1][1:2]),
        jnp.where(lane < 64, turned[1][1:2], turned[2][2:3]),
        jnp.where(lane < 32, turned[2][2:3], turned[3][3:4]),
    ]


def matrices_kernel(got_ref, dre_ref, dim_ref, ore_ref, oim_ref, glu_ref, square):
    def total(start, count):
        value = got_ref[0, start : start + count, :].astype(F32)
        for z in range(1, GROUPS // 2):
            value = value + got_ref[z, start : start + count, :].astype(F32)
        return value

    for start, first_ref, second_ref in ((0, dre_ref, dim_ref), (96, ore_ref, oim_ref)):
        square[0:96, :] = total(start, 96)
        square[96:128, :] = jnp.zeros((32, 128), F32)
        turned = square[...].T
        first_ref[...] = turned[0:64, 0:96]
        second_ref[...] = turned[64:128, 0:96]
    glu_ref[...] = total(192, 64)


def finish_kernel(
    count_all, own_ref, other_ref, dn_ref, got_ref, up_ref, xhat_ref, inv_ref, feat_ref,
    gin_ref, gbias_ref, scale_ref, bias_ref, skip_ref, decay_ref, lam_ref, step_ref, rms_ref, vec_ref,
):
    input_grad(dn_ref, got_ref, up_ref, xhat_ref, inv_ref, feat_ref, gin_ref)
    vec = own_ref[...] + other_ref[...]
    vec_ref[...] = vec
    for k, ref in enumerate((scale_ref, bias_ref, skip_ref)):
        for c in range(4):
            ref[:, 128 * c : 128 * c + 128] = vec[4 * k + c : 4 * k + c + 1]
    for k, ref in enumerate((decay_ref, lam_ref, step_ref)):
        for c, chunk in enumerate(rows_to_lanes(vec[16 + 4 * k : 20 + 4 * k])):
            ref[128 * c : 128 * c + 128] = chunk.reshape(128)
    total = jnp.sum(vec[28:30], axis=1, keepdims=True)
    lane = lane_iota((1, 2))
    rms_ref[...] = jnp.sqrt(jnp.where(lane == 0, total[0:1], total[1:2]) / count_all)
    place = tensor_pos() * GROUPS + fsdp_pos()
    row = jnp.broadcast_to(vec_ref[pl.ds(12 + place // 8, 1), :], (8, 128))
    gbias_ref[...] = pltpu.roll(row, 128 - 16 * (place % 8), 1)[0:1, 0:16]


TAKES = {
    "pack": 1.5, "standardize": 0.4, "norm": 0.4, "first": 0.6, "states": 0.9, "readout": 0.4, "second": 0.7, "sums": 0.7, "back": 0.8,
    "third": 1.5, "input_grad": 0.5, "matrices": 0.5, "finish": 0.4,
}


def call(kernel, outs, args, scratch=(), specs=None, limit=24):
    name = getattr(kernel, "func", kernel).__name__.removesuffix("_kernel")
    return pl.pallas_call(
        kernel,
        out_shape=outs,
        in_specs=specs or [VM] * len(args),
        out_specs=jax.tree.map(lambda _: VM, outs),
        scratch_shapes=list(scratch),
        compiler_params=pltpu.CompilerParams(vmem_limit_bytes=limit << 20),
        cost_estimate=pl.CostEstimate(flops=0, transcendentals=0, bytes_accessed=int(TAKES.get(name, 0.1) * 3.6e6)),
        name=name,
    )(*args)


def tied(value, other):
    return lax.optimization_barrier((value, other))[0]


def swap(value, axis):
    return lax.ppermute(value, axis, [(0, 1), (1, 0)])


def across(value):
    return lax.ppermute(value, ("fx", "ty"), [(n, 3 - n) for n in range(4)])


def on_device(
    layer_in, grad_out, ln_scale, ln_bias, decay_rate, lam_im, log_dt, in_re, in_im, out_re, out_im, skip, glu_weight, glu_bias, seq_lengths
):
    rows, width = layer_in.shape
    fsdp = lax.axis_size(FSDP)
    pairs, pair = fsdp * 2, 2 * rows
    count_all = float(rows * pairs * 2 * width)
    fast = fsdp == GROUPS
    same_core = (*FSDP, "ty")
    if fast:
        row = lambda v: v.reshape(1, -1)
        sent = call(
            pack_kernel,
            sds((GROUPS // 2, 272, 128), BF16),
            (seq_lengths, in_re.T, in_im.T, out_re.T, out_im.T, glu_weight.T, row(ln_scale), row(ln_bias), row(skip), row(glu_bias),
             row(decay_rate), row(lam_im), row(log_dt)),
            [pltpu.VMEM((128, 128), F32), pltpu.VMEM((4, 64, 96), BF16), pltpu.VMEM((64, 128), BF16), pltpu.VMEM((4, 1, 64), BF16),
             pltpu.VMEM((3, 1, 96), F32), pltpu.SMEM(seq_lengths.shape, jnp.int32), pltpu.SemaphoreType.DMA((13,))],
            [HBM] * 13,
            60,
        )
        mine = lax.all_to_all(sent, "fz", 0, 0, tiled=True)
        own_b, own_cw = lax.optimization_barrier((mine[:, :112], mine[:, 112:]))
        plane_b = [own_b, swap(own_b, "ty"), swap(own_b, "fx"), across(own_b)]
        xhat, inverse = call(standardize_kernel, (sds((pair, width)), sds((rows, 128))), (layer_in, swap(layer_in, "tc")))
        plane_b, side_cw, xhat = lax.optimization_barrier((plane_b, swap(own_cw, "ty"), xhat))
        side_cw = jnp.stack([own_cw, side_cw])
        far_cw = swap(side_cw, "fx")
        g = jnp.stack(plane_b).reshape(2, 2, GROUPS // 2, 112, 128)
    else:
        xhat, inverse = call(standardize_kernel, (sds((pair, width)), sds((rows, 128))), (layer_in, swap(layer_in, "tc")))
        g, cw, other_cw = gathered(
            ln_scale, ln_bias, decay_rate, lam_im, log_dt, in_re, in_im, out_re, out_im, skip, glu_weight, glu_bias, seq_lengths
        )

    normed, feat, starts = call(
        norm_kernel,
        (sds((pair, width), BF16), sds((8, width)), sds((seq_lengths.shape[0], 128))),
        (xhat, g),
    )
    b_all, v, lane, row_prm, carry = call(
        functools.partial(first_kernel, pairs),
        (sds((512, width), BF16), sds((pair, 512)), sds((8, 256)), sds((8, 8, 128)), sds((pairs, 8, 128))),
        (normed, starts, g),
        [pltpu.VMEM((8, 128), F32)],
    )
    came = lax.all_to_all(carry, same_core, 0, 0, tiled=True)
    if fast:
        cw = jnp.stack(tied((side_cw, far_cw), came))
    state, twice, enter, c_all = call(
        states_kernel,
        (sds((pair, 512)), sds((pair, 512), BF16), sds((8, 512)), sds((512, width), BF16)),
        (came, starts, v, lane, row_prm, cw),
        [pltpu.VMEM((8, 128), F32)],
    )
    if fast:
        other_cw = swap(tied(cw, twice), "tc")
    own, away = call(
        readout_kernel, (sds((rows, width)), sds((rows, width))), (twice, c_all), [pltpu.VMEM((pair, width), F32)]
    )
    branch, d_mixed, dlogit, kept, away = call(
        second_kernel,
        (sds((rows, width), BF16), sds((rows, width)), sds((rows, width), BF16), *[sds((rows, 2 * width + 256), BF16)] * 2),
        (own, swap(away, "tc"), grad_out, normed, feat, cw, other_cw),
        [pltpu.VMEM((width, width), BF16), pltpu.VMEM((rows, width), BF16)],
    )
    got = swap(away, "tc")
    layer_out, part = call(
        sums_kernel, (sds((rows, width), BF16), sds((8, width))), (layer_in, branch, normed, d_mixed, dlogit)
    )
    got, part = lax.optimization_barrier((got, part))
    d_state, carry, stay_cw, leave_cw = call(
        functools.partial(back_kernel, pairs),
        (sds((pair, 512)), sds((pairs, 8, 128)), *[sds((2, GROUPS // 2, 160, 128), BF16)] * 2),
        (kept, got, twice, starts, lane, c_all),
        [pltpu.VMEM((pair, width), BF16), pltpu.VMEM((width, 256), BF16), pltpu.VMEM((8, 128), F32),
         pltpu.VMEM((2, 2, GROUPS // 2, 160, 128), BF16)],
    )
    if fast:
        far_cw = swap(leave_cw, "fx")
    came = lax.all_to_all(carry, same_core, 0, 0, tiled=True)
    if fast:
        came, far_cw, stay_cw = lax.optimization_barrier((came, far_cw, stay_cw))
        stay_cw, leave_cw = call(middle_kernel, [sds((GROUPS // 2, 160, 128), BF16)] * 2, (stay_cw, far_cw))
        far_cw = swap(leave_cw, "ty")
        came = tied(came, leave_cw)
    stay_b, y_b, x_b, xy_b, d_normed, away = call(
        third_kernel,
        (*[sds((448, 128), BF16)] * 4, sds((rows, width)), sds((rows, width))),
        (came, starts, normed, xhat, v, lane, row_prm, feat, state, d_state, enter, d_mixed, part, b_all),
        [pltpu.VMEM((8, 128), F32), pltpu.VMEM((pair, 512), BF16), pltpu.VMEM((pair, width), F32), pltpu.VMEM((32, 128), F32)],
    )
    if not fast:
        grad_in = call(
            input_grad_kernel, sds((rows, width)), (d_normed, swap(away, "tc"), grad_out, xhat, inverse, feat)
        )
        return reduced(layer_out, grad_in, stay_cw, leave_cw, (stay_b, y_b, x_b, xy_b), count_all, fsdp, width)
    sent = call(
        plane_add_kernel,
        sds((GROUPS // 2, 320, 128), BF16),
        (stay_cw, far_cw, stay_b, swap(y_b, "ty"), swap(x_b, "fx"), across(xy_b)),
    )
    got = lax.all_to_all(sent, "fz", 0, 0, tiled=True)
    away = swap(tied(away, got), "tc")
    vec = call(vectors_kernel, sds((32, 128)), (got,))
    other = swap(vec, "tc")
    d_re, d_im, d_ore, d_oim, d_glu = call(
        matrices_kernel, (*[sds((64, 96))] * 4, sds((64, 128))), (got,), [pltpu.VMEM((128, 128), F32)]
    )
    grad_in, d_gbias, d_scale, d_bias, d_skip, g_decay, g_lam, g_step, rms = call(
        functools.partial(finish_kernel, count_all),
        (sds((rows, width)), sds((1, 16)), *[sds((1, 512))] * 3, *[sds((384,))] * 3, sds((1, 2))),
        (vec, other, d_normed, away, grad_out, xhat, inverse, feat),
        [pltpu.VMEM((32, 128), F32)],
    )
    flat = lambda value: value.reshape(-1)
    return (
        layer_out, grad_in, flat(d_scale), flat(d_bias), g_decay, g_lam, g_step, d_re.T, d_im.T, d_ore.T, d_oim.T,
        flat(d_skip), d_glu.T, flat(d_gbias), flat(rms),
    )


def gathered(ln_scale, ln_bias, decay_rate, lam_im, log_dt, in_re, in_im, out_re, out_im, skip, glu_weight, glu_bias, seq_lengths):
    tens = tensor_pos()
    full = lambda value, axis: lax.all_gather(value, FSDP, axis=axis, tiled=True)

    def pair(first, second):
        halves = jnp.stack([first.reshape(-1, GROUPS, 64), second.reshape(-1, GROUPS, 64)], axis=2)
        return halves.reshape(-1, GROUPS, 128).swapaxes(0, 1)

    gate = lax.dynamic_slice_in_dim(full(glu_weight, 1), tens * 128, 128, 0).T.reshape(GROUPS, 64, 128)
    vectors = [pair(full(ln_scale, 0)[None], full(ln_bias, 0)[None]), pair(full(skip, 0)[None], full(glu_bias, 0)[None])]
    for value in (decay_rate, lam_im, log_dt):
        value = jnp.pad(value, (0, 32))
        for _ in range(3):
            piece = lax.reduce_precision(value, 8, 7)
            value = value - piece
            vectors.append(jnp.broadcast_to(piece.astype(BF16)[None, None], (GROUPS, 1, 128)))
    starts = jnp.cumsum(seq_lengths) - seq_lengths
    for value in (starts >> 8, starts & 255):
        value = jnp.pad(value, (0, 128 - value.shape[0])).astype(BF16)
        vectors.append(jnp.broadcast_to(value[None, None], (GROUPS, 1, 128)))
    vectors.append(jnp.zeros((GROUPS, 3, 128), BF16))
    packet = jnp.concatenate(
        [pair(full(in_re, 1), full(in_im, 1)), *vectors, pair(full(out_re, 1), full(out_im, 1)), gate],
        axis=1,
    )
    everyone = lax.all_gather(packet, TENSOR, axis=0).reshape(2, 2, GROUPS // 2, 2, 272, 128)
    x, y, core = (lax.axis_index(axis) for axis in ("fx", "ty", "tc"))
    own_x = lambda value, axis: jnp.stack([lax.dynamic_index_in_dim(value, x ^ j, axis, keepdims=False) for j in range(2)])
    for i in range(2):
        both = lax.dynamic_index_in_dim(everyone, core ^ i, 1, keepdims=False)
        slots = [own_x(lax.dynamic_index_in_dim(both, y ^ m, 0, keepdims=False), 1) for m in range(2)]
        slots = jnp.stack(slots, axis=1)
        if i == 0:
            g, cw = slots[:, :, :, :112], slots[:, :, :, 112:]
    return g, cw, slots[:, :, :, 112:]


def reduced(layer_out, grad_in, stay_cw, leave_cw, plane_b, count_all, fsdp, width):
    tens = tensor_pos()
    x = lax.axis_index("fx")

    def canonical(slots):
        out = jnp.zeros((4, GROUPS, *slots[0].shape[2:]), F32)
        for m, slot in enumerate(slots):
            parts = [lax.dynamic_index_in_dim(slot.astype(F32), x ^ n, 1) for n in range(2)]
            block = jnp.concatenate(parts, axis=1).reshape(1, GROUPS, *slot.shape[2:])
            out = lax.dynamic_update_slice_in_dim(out, block, slot_pos(m, 0), 0)
        return out

    def natural(slots):
        halves = canonical(slots).reshape(4, GROUPS, -1, 2, 64).transpose(3, 0, 2, 1, 4)
        return halves[0].reshape(-1, width), halves[1].reshape(-1, width)

    def scattered(value):
        value = lax.psum_scatter(value, TENSOR, scatter_dimension=0, tiled=True)
        return lax.psum_scatter(value, FSDP, scatter_dimension=1, tiled=True)

    blocks = [value[:384].reshape(GROUPS // 2, 96, 128) for value in plane_b]
    d_re, d_im = natural([jnp.stack([blocks[m], blocks[2 + m]], axis=1) for m in range(2)])
    cw = jnp.stack([stay_cw, leave_cw]).transpose(1, 2, 0, 3, 4)
    d_ore, d_oim = natural([value[:, :, :96] for value in cw])
    d_glu = canonical([value[:, :, 96:] for value in cw]).reshape(4, width, 128).swapaxes(1, 2).reshape(-1, width)
    vec = lax.psum(joined(plane_b[0][384:448]), AXES)
    states = lambda k: vec[16 + 4 * k : 20 + 4 * k, :96].reshape(-1)
    own = width // (4 * fsdp)
    place = tens * fsdp + fsdp_pos()
    d_gbias = lax.dynamic_slice_in_dim(vec[12:16].reshape(-1), place * own, own, 0)
    rms = jnp.sqrt(jnp.sum(vec[28:30], axis=1) / count_all)
    return (
        layer_out, grad_in, vec[0:4].reshape(-1), vec[4:8].reshape(-1), states(0), states(1), states(2), scattered(d_re), scattered(d_im),
        scattered(d_ore), scattered(d_oim), vec[8:12].reshape(-1), scattered(d_glu), d_gbias, rms,
    )


def solution(mesh):
    shape = (mesh.shape["fsdp"] // 2, 2, mesh.shape["tensor"] // 2, 2)
    split = Mesh(mesh.devices.reshape(shape), AXES)
    tokens, matrix = P(AXES, None), P(TENSOR, FSDP)
    return jax.shard_map(
        on_device,
        mesh=split,
        in_specs=(
            tokens, tokens, P(FSDP), P(FSDP), P(TENSOR), P(TENSOR), P(TENSOR), matrix, matrix, matrix, matrix,
            P(FSDP), P(None, FSDP), P(FSDP), P(),
        ),
        out_specs=(
            tokens, tokens, P(), P(), P(), P(), P(), matrix, matrix, matrix, matrix, P(), matrix, P((*TENSOR, *FSDP)), P(),
        ),
        check_vma=False,
    )
```

```python
import functools

import jax
import jax.numpy as jnp
from jax import lax
from jax.experimental import pallas as pl
from jax.experimental.pallas import tpu as pltpu
from jax.sharding import Mesh
from jax.sharding import PartitionSpec as P

F32 = jnp.float32
BF16 = jnp.bfloat16
FSDP = ("fz", "fx")
TENSOR = ("ty", "tc")
AXES = (*FSDP, *TENSOR)
HBM = pl.BlockSpec(memory_space=pltpu.HBM)
VM = pl.BlockSpec(memory_space=pltpu.VMEM)
SM = pl.BlockSpec(memory_space=pltpu.SMEM)

GROUPS = 8
VEC = 96


def sds(shape, dtype=F32):
    return jax.ShapeDtypeStruct(shape, dtype)


def low_half(shape):
    return lax.broadcasted_iota(jnp.int32, shape, len(shape) - 1) < 64


def lane_iota(shape):
    return lax.broadcasted_iota(jnp.int32, shape, len(shape) - 1)


def dot(a, b, dims):
    return lax.dot_general(a, b, (dims, ((), ())), preferred_element_type=F32)


NT = ((1,), (1,))
NN = ((1,), (0,))
TN = ((0,), (0,))


def flipped():
    return lax.axis_index("fx") == 1


def part_lanes(part, m):
    return slice(256 * part + 128 * m, 256 * part + 128 * m + 128)


def slot_pos(m, core):
    return (lax.axis_index("ty") ^ m) * 2 + (lax.axis_index("tc") ^ core)


def own_rows(rows):
    return pl.ds(pl.multiple_of(lax.axis_index("tc") * rows, rows), rows)


def other_rows(rows):
    return pl.ds(pl.multiple_of((1 - lax.axis_index("tc")) * rows, rows), rows)


def piece(ref, m, f, start, count):
    return ref[f % 2, m, f // 2, start : start + count, :]


def natural(get, ref):
    lo = low_half((96, 128))
    for m in range(2):
        for part in range(2):
            lanes = part_lanes(part, m)
            ref[lanes.start + 96 : lanes.stop, :] = jnp.zeros((32, 512), BF16)
        for z in range(GROUPS // 2):
            even, odd = get(m, z, 0).astype(F32), get(m, z, 1).astype(F32)
            here = slice(128 * z, 128 * z + 128)
            ref[128 * m : 128 * m + 96, here] = jnp.where(lo, even, pltpu.roll(odd, 64, 1)).astype(BF16)
            ref[256 + 128 * m : 256 + 128 * m + 96, here] = jnp.where(lo, pltpu.roll(even, 64, 1), odd).astype(BF16)


def packets(value, m, z):
    lo = low_half((96, 128))
    here = slice(128 * z, 128 * z + 128)
    re, im = value[128 * m : 128 * m + 96, here], value[256 + 128 * m : 256 + 128 * m + 96, here]
    return jnp.where(lo, re, pltpu.roll(im, 64, 1)), jnp.where(lo, pltpu.roll(re, 64, 1), im)


def feature_rows(ref, row):
    lo = low_half((8, 128))
    flip = flipped()
    first, second = [], []
    for c in range(GROUPS // 2):
        a = jnp.broadcast_to(piece(ref, 0, 2 * c, row, 1).astype(F32), (8, 128))
        b = jnp.broadcast_to(piece(ref, 0, 2 * c + 1, row, 1).astype(F32), (8, 128))
        a, b = jnp.where(flip, b, a), jnp.where(flip, a, b)
        first.append(jnp.where(lo, a, pltpu.roll(b, 64, 1)))
        second.append(jnp.where(lo, pltpu.roll(a, 64, 1), b))
    return jnp.concatenate(first, axis=1)[:1], jnp.concatenate(second, axis=1)[:1]


def cmul(a, b):
    return a[0] * b[0] - a[1] * b[1], a[0] * b[1] + a[1] * b[0]


def tensor_pos():
    return lax.axis_index("ty") * 2 + lax.axis_index("tc")


def fsdp_pos():
    return lax.axis_index("fz") * 2 + lax.axis_index("fx")


def pair_pos():
    return fsdp_pos() * 2 + lax.axis_index("ty")


def offsets_of(start_ref):
    return [start_ref[n : n + 1, :] for n in range(start_ref.shape[0])]


def starts_until(offsets, base, rows):
    at = (lax.broadcasted_iota(jnp.int32, (rows, 128), 0) + base).astype(F32)
    count = jnp.zeros((rows, 128), F32)
    for off in offsets:
        count = count + jnp.where((at >= off) & (off >= at[0:1]), 1.0, 0.0)
    return count


def no_start(offsets, base, rows):
    link = jnp.ones((1, 128), F32)
    first = (jnp.zeros((1, 128), jnp.int32) + base).astype(F32)
    for off in offsets:
        link = jnp.where((off >= first) & (off < first + rows), 0.0, link)
    return link


def expm1(x):
    series = x * (1 + x / 2 * (1 + x / 3 * (1 + x / 4 * (1 + x / 5 * (1 + x / 6 * (1 + x / 7))))))
    return jnp.where(jnp.abs(x) < 0.25, series, jnp.exp(x) - 1.0)


def discretize(decay_rate, lam_im, log_dt):
    step_size = jnp.exp(log_dt)
    lam_re = -decay_rate
    magnitude = jnp.exp(lam_re * step_size)
    phase = lam_im * step_size
    abar_re = magnitude * jnp.cos(phase)
    abar_im = magnitude * jnp.sin(phase)
    half_sin = jnp.sin(0.5 * phase)
    less_re = expm1(lam_re * step_size) * jnp.cos(phase) - 2.0 * half_sin * half_sin
    denom = lam_re * lam_re + lam_im * lam_im
    coef_re = (less_re * lam_re + abar_im * lam_im) / denom
    coef_im = (abar_im * lam_re - less_re * lam_im) / denom
    return abar_re, abar_im, coef_re, coef_im, step_size


def pack_kernel(*refs):
    *inputs, out_ref, square, four, glu_ref, halves, params, lengths, sems = refs
    seq_hbm, matrices, glu_hbm, features, states = inputs[0], inputs[1:5], inputs[5], inputs[6:10], inputs[10:13]
    units = pl.multiple_of(tensor_pos() * 128, 128)
    pairs = [(ref, four.at[k]) for k, ref in enumerate(matrices)]
    pairs += [(glu_hbm.at[:, pl.ds(units, 128)], glu_ref), (seq_hbm, lengths)]
    pairs += [(ref, halves.at[k]) for k, ref in enumerate(features)]
    pairs += [(ref, params.at[k]) for k, ref in enumerate(states)]
    copies = [pltpu.make_async_copy(source, target, sems.at[k]) for k, (source, target) in enumerate(pairs)]
    for copy in copies:
        copy.start()
    square[:, 96:128] = jnp.zeros((128, 32), F32)
    for copy in copies:
        copy.wait()
    vec = [
        jnp.concatenate([halves[0], halves[1]], axis=1).astype(F32),
        jnp.concatenate([halves[2], halves[3]], axis=1).astype(F32),
    ]
    for k in range(3):
        value = jnp.concatenate([params[k], jnp.zeros((1, 32), F32)], axis=1)
        for _ in range(3):
            part = value.astype(BF16).astype(F32)
            value = value - part
            vec.append(part)
    lane = lane_iota((1, 128))
    upper, lower, total = jnp.zeros((1, 128), jnp.int32), jnp.zeros((1, 128), jnp.int32), 0
    for n in range(lengths.shape[0]):
        upper = jnp.where(lane == n, total >> 8, upper)
        lower = jnp.where(lane == n, total & 255, lower)
        total = total + lengths[n]
    vec += [upper.astype(F32), lower.astype(F32)]
    vec.append(jnp.zeros((16 - len(vec), 128), F32))
    vec = jnp.concatenate(vec, axis=0).astype(BF16)
    pieces = []
    for k in (0, 2):
        square[0:64, 0:96] = four[k].astype(F32)
        square[64:128, 0:96] = four[k + 1].astype(F32)
        pieces.append(square[...].T[0:96].astype(BF16))
    packet = jnp.concatenate([pieces[0], vec, pieces[1], glu_ref[...]], axis=0)
    for z in range(GROUPS // 2):
        out_ref[z] = packet


def params_of(ref, vec_row):
    lane = lane_iota((8, 128))
    out = []
    for k, safe in enumerate((1.0, 0.0, 0.0)):
        rows = []
        for m in range(2):
            part = piece(ref, m, 0, vec_row, 16).astype(F32)
            rows.append((part[2 + 3 * k : 3 + 3 * k] + part[3 + 3 * k : 4 + 3 * k]) + part[4 + 3 * k : 5 + 3 * k])
        value = jnp.concatenate(rows + [jnp.full((6, 128), safe, F32)], axis=0)
        out.append(jnp.where(lane < 96, value, safe))
    return out


def carry_block(re_rows, im_rows, scratch):
    for m in range(2):
        y = lax.axis_index("ty") ^ m
        scratch[pl.ds(y, 1), :] = re_rows[m]
        scratch[pl.ds(2 + y, 1), :] = im_rows[m]


def standardize_kernel(x_ref, other_ref, xhat_ref, inv_ref):
    rows, width = x_ref.shape
    for ref, where, own in ((x_ref, own_rows(rows), True), (other_ref, other_rows(rows), False)):
        x = ref[...].astype(F32)
        centered = x - jnp.sum(x, axis=1, keepdims=True) / width
        inverse = lax.rsqrt(jnp.sum(centered * centered, axis=1, keepdims=True) / width + 1e-05)
        xhat_ref[where, :] = centered * inverse
        if own:
            inv_ref[...] = jnp.broadcast_to(inverse, (rows, 128))


def norm_kernel(xhat_ref, g_ref, normed_ref, feat_ref, start_ref):
    scale, bias = feature_rows(g_ref, VEC)
    feat_ref[0:1] = scale
    feat_ref[1:2], feat_ref[2:3] = feature_rows(g_ref, VEC + 1)
    normed = (xhat_ref[...] * scale + bias).astype(BF16)
    normed_ref[...] = normed
    upper, lower = (piece(g_ref, 0, 0, VEC + 11 + k, 1).astype(F32) for k in range(2))
    starts = upper * 256.0 + lower
    for n in range(start_ref.shape[0]):
        start_ref[n : n + 1, :] = jnp.broadcast_to(starts[:, n : n + 1], (1, 128))


def first_kernel(pairs, normed_ref, start_ref, g_ref, b_ref, v_ref, lane_ref, row_ref, send_ref, scratch):
    rows = normed_ref.shape[0]
    natural(lambda m, z, x: g_ref[lax.axis_index("fx") ^ x, m, z, 0:96, :], b_ref)
    v_ref[...] = dot(normed_ref[...], b_ref[...], NT)

    decay, lam, log_dt = params_of(g_ref, VEC)
    abar_re, abar_im, coef_re, coef_im, step_size = discretize(decay, lam, log_dt)
    power = (abar_re, abar_im)
    for _ in range(8):
        power = cmul(power, power)
    scratch[...] = jnp.zeros((8, 128), F32)
    carry_block([power[0][m : m + 1] for m in range(2)], [power[1][m : m + 1] for m in range(2)], scratch)
    for k, value in enumerate((decay, lam, step_size, abar_re, abar_im, coef_re, coef_im, scratch[...])):
        row_ref[k] = value
    for k, value in enumerate((abar_re, abar_im, coef_re, coef_im)):
        for m in range(2):
            lane_ref[k : k + 1, 128 * m : 128 * m + 128] = value[m : m + 1]

    count = starts_until(offsets_of(start_ref), pair_pos() * rows, rows)
    open_tail = jnp.where(count == count[rows - 1 : rows], 1.0, 0.0)
    last = ([], [])
    for m in range(2):
        eight, tail = eighth_powers((abar_re[m : m + 1], abar_im[m : m + 1]), lambda sub: 7 - sub)
        b = (coef_re[m : m + 1], coef_im[m : m + 1])
        acc = (jnp.zeros((8, 128), F32), jnp.zeros((8, 128), F32))
        for blk in range(rows // 8):
            here = slice(8 * blk, 8 * blk + 8)
            drive = cmul(b, (v_ref[here, part_lanes(0, m)], v_ref[here, part_lanes(1, m)]))
            moved = cmul(eight, acc)
            acc = (moved[0] + drive[0] * open_tail[here], moved[1] + drive[1] * open_tail[here])
        total = cmul(tail, acc)
        last[0].append(column_sum(total[0]))
        last[1].append(column_sum(total[1]))
    carry_block(last[0], last[1], scratch)
    packet = scratch[...]
    for d in range(pairs):
        send_ref[d] = packet[0:4]


def eighth_powers(a, exponent_of):
    exponent = exponent_of(lax.broadcasted_iota(jnp.int32, (8, 128), 0))
    a = (jnp.broadcast_to(a[0], (8, 128)), jnp.broadcast_to(a[1], (8, 128)))
    tile = (jnp.ones((8, 128), F32), jnp.zeros((8, 128), F32))
    for bit in range(4):
        if bit == 3:
            eight = a
        taken = (exponent & (1 << bit)) != 0
        more = cmul(tile, a)
        tile = (jnp.where(taken, more[0], tile[0]), jnp.where(taken, more[1], tile[1]))
        a = cmul(a, a)
    return eight, tile


def all_rows(row):
    return jnp.broadcast_to(row, (8, 128))


def scan(read, powers, carry, count, reverse, emit):
    groups = count.shape[0] // 8
    sub = lax.broadcasted_iota(jnp.int32, (8, 128), 0)
    steps, eights, tiles = [], [], []
    for a in powers:
        squared = cmul(a, a)
        steps.append((a, squared, cmul(squared, squared)))
        eight, tile = eighth_powers(a, (lambda sub: 8 - sub) if reverse else (lambda sub: sub + 1))
        eights.append(eight)
        tiles.append(tile)
    carry = [(all_rows(c[0]), all_rows(c[1])) for c in carry]
    edge = 0 if reverse else 7
    seen = all_rows(count[8 * groups - 1 :]) if reverse else jnp.zeros((8, 128), F32)
    for b in range(groups - 1, -1, -1) if reverse else range(groups):
        here = count[8 * b : 8 * b + 8]
        links = []
        for k in (1, 2, 4):
            other = pltpu.roll(here, 8 - k if reverse else k, 0)
            links.append(((sub < 8 - k) if reverse else (sub >= k)) & (other == here))
        came = here == seen
        last = all_rows(here[edge : edge + 1])
        through = last == seen
        seen = last
        for m in range(2):
            value = read(b, m)
            for k, link, a in zip((1, 2, 4), links, steps[m]):
                shift = 8 - k if reverse else k
                more = cmul(a, (pltpu.roll(value[0], shift, 0), pltpu.roll(value[1], shift, 0)))
                value = (value[0] + jnp.where(link, more[0], 0.0), value[1] + jnp.where(link, more[1], 0.0))
            more = cmul(tiles[m], carry[m])
            done = (value[0] + jnp.where(came, more[0], 0.0), value[1] + jnp.where(came, more[1], 0.0))
            more = cmul(eights[m], carry[m])
            carry[m] = (
                all_rows(value[0][edge : edge + 1]) + jnp.where(through, more[0], 0.0),
                all_rows(value[1][edge : edge + 1]) + jnp.where(through, more[1], 0.0),
            )
            emit(b, m, done)


def carried(recv_ref, row_ref, offsets, rows, reverse, scratch):
    pairs = recv_ref.shape[0]
    power = row_ref[7]
    pre, pim = power[0:2], power[2:4]
    if reverse:
        pim = -pim
    place = pair_pos()

    def turn(k, state):
        j = pairs - 1 - k if reverse else k
        link = no_start(offsets, j * rows, rows)
        got = recv_ref[j]
        new = cmul((pre * link, pim * link), state)
        return new[0] + got[0:2], new[1] + got[2:4]

    zero = jnp.zeros((2, 128), F32)
    out = lax.fori_loop(0, pairs - 1 - place if reverse else place, turn, (zero, zero))
    scratch[0:2, :] = out[0]
    scratch[2:4, :] = out[1]
    own = [lax.axis_index("ty") ^ m for m in range(2)]
    return [scratch[pl.ds(y, 1), :] for y in own], [scratch[pl.ds(2 + y, 1), :] for y in own]


def column_sum(value):
    return jnp.sum(value, axis=0, keepdims=True)


def states_kernel(
    recv_ref, start_ref, v_ref, lane_ref, row_ref, cw_ref, state_ref, twice_ref, enter_ref, c_ref, scratch
):
    rows = v_ref.shape[0]
    offsets = offsets_of(start_ref)
    count = starts_until(offsets, pair_pos() * rows, rows)
    enter = carried(recv_ref, row_ref, offsets, rows, False, scratch)
    for part in range(2):
        for m in range(2):
            enter_ref[0:1, part_lanes(part, m)] = enter[part][m]
    powers = [(lane_ref[0:1, 128 * m : 128 * m + 128], lane_ref[1:2, 128 * m : 128 * m + 128]) for m in range(2)]

    def read(b, m):
        here, lanes = slice(8 * b, 8 * b + 8), slice(128 * m, 128 * m + 128)
        return cmul((lane_ref[2:3, lanes], lane_ref[3:4, lanes]), (v_ref[here, part_lanes(0, m)], v_ref[here, part_lanes(1, m)]))

    def emit(b, m, value):
        for part in range(2):
            state_ref[8 * b : 8 * b + 8, part_lanes(part, m)] = value[part]

    scan(read, powers, [(enter[0][m], enter[1][m]) for m in range(2)], count, False, emit)
    twice_ref[:, 0:256] = state_ref[:, 0:256].astype(BF16) * 2
    twice_ref[:, 256:512] = state_ref[:, 256:512].astype(BF16) * -2
    natural(lambda m, z, x: cw_ref[lax.axis_index("fx") ^ x, m, z, 0:96, :], c_ref)


def readout_kernel(twice_ref, c_ref, own_ref, away_ref, scratch):
    rows = own_ref.shape[0]
    scratch[...] = dot(twice_ref[...], c_ref[...], NN)
    own_ref[...] = scratch[own_rows(rows), :]
    away_ref[...] = scratch[other_rows(rows), :]


def second_kernel(
    own_ref, got_ref, up_ref, normed_ref, feat_ref, cw_ref, othercw_ref,
    branch_ref, dmixed_ref, dlogit_ref, mine_ref, away_ref, gate_ref, all_ref,
):
    rows, width = up_ref.shape
    for core, ref in enumerate((cw_ref, othercw_ref)):
        for m in range(2):
            lanes = pl.ds(pl.multiple_of(slot_pos(m, core) * 128, 128), 128)
            for f in range(GROUPS):
                place = (f // 2) * 2 + (lax.axis_index("fx") ^ (f % 2))
                gate_ref[pl.ds(pl.multiple_of(place * 64, 64), 64), lanes] = piece(ref, m, f, 96, 64)
    skip, gate_bias = feat_ref[1:2], feat_ref[2:3]
    normed = normed_ref[own_rows(rows), :].astype(F32)
    mixed = (own_ref[...] + got_ref[...]) + skip * normed
    cdf = 0.5 * (1.0 + lax.erf(mixed * 0.7071067811865476))
    act_low = (mixed * cdf).astype(BF16)
    act = act_low.astype(F32)
    w_gate = gate_ref[...]
    logit = dot(act_low, w_gate, NN) + gate_bias
    gate = 1.0 / (1.0 + jnp.exp(-logit))
    branch_ref[...] = (act * gate).astype(BF16)
    up = up_ref[...].astype(F32)
    dlogit = (up * act * gate * (1.0 - gate)).astype(BF16)
    dlogit_ref[...] = dlogit
    all_ref[...] = dlogit
    d_act = dot(dlogit, w_gate, NT) + up * gate
    slope = cdf + mixed * jnp.exp(-0.5 * mixed * mixed) * 0.3989422804014327
    d_mixed = d_act * slope
    dmixed_ref[...] = d_mixed
    for core, ref in enumerate((mine_ref, away_ref)):
        ref[:, 0:width] = d_mixed.astype(BF16)
        ref[:, width : 2 * width] = act_low
        for m in range(2):
            lanes = pl.ds(pl.multiple_of(slot_pos(m, core) * 128, 128), 128)
            ref[:, 2 * width + 128 * m : 2 * width + 128 * m + 128] = all_ref[:, lanes]


def sums_kernel(x_ref, branch_ref, normed_ref, dmixed_ref, dlogit_ref, out_ref, part_ref):
    x = x_ref[...].astype(F32)
    branch = branch_ref[...].astype(F32)
    out_ref[...] = (x + branch).astype(BF16)
    skip = column_sum(dmixed_ref[...] * normed_ref[own_rows(x_ref.shape[0]), :].astype(F32))
    for k, value in enumerate((skip, column_sum(dlogit_ref[...].astype(F32)), column_sum(x * x), column_sum(branch * branch))):
        part_ref[k : k + 1, :] = value


def back_kernel(
    pairs, mine_ref, got_ref, twice_ref, start_ref, lane_ref, c_ref,
    dstate_ref, send_ref, stay_ref, leave_ref, dy_ref, dgate_ref, scratch, all_ref,
):
    rows, width = dy_ref.shape
    half = rows // 2
    dy_ref[own_rows(half), :] = mine_ref[:, 0:width]
    dy_ref[other_rows(half), :] = got_ref[:, 0:width]
    d_state = dot(dy_ref[...], c_ref[...], NT)
    dstate_ref[:, 0:256] = d_state[:, 0:256] * 2.0
    dstate_ref[:, 256:512] = d_state[:, 256:512] * -2.0
    count = starts_until(offsets_of(start_ref), pair_pos() * rows, rows)
    head = jnp.where(count == 0.0, 1.0, 0.0)
    first = ([], [])
    for m in range(2):
        lanes = slice(128 * m, 128 * m + 128)
        eight, tail = eighth_powers((lane_ref[0:1, lanes], -lane_ref[1:2, lanes]), lambda sub: sub + 1)
        acc = (jnp.zeros((8, 128), F32), jnp.zeros((8, 128), F32))
        for blk in range(rows // 8 - 1, -1, -1):
            here = slice(8 * blk, 8 * blk + 8)
            moved = cmul(eight, acc)
            acc = (
                moved[0] + dstate_ref[here, part_lanes(0, m)] * head[here],
                moved[1] + dstate_ref[here, part_lanes(1, m)] * head[here],
            )
        total = cmul(tail, acc)
        first[0].append(column_sum(total[0]))
        first[1].append(column_sum(total[1]))
    scratch[...] = jnp.zeros((8, 128), F32)
    carry_block(first[0], first[1], scratch)
    packet = scratch[...]
    for d in range(pairs):
        send_ref[d] = packet[0:4]
    d_c = dot(twice_ref[...], dy_ref[...], TN)
    act = slice(width, 2 * width)
    units = slice(2 * width, 2 * width + 256)
    d_gate = dot(mine_ref[:, act], mine_ref[:, units], TN) + dot(got_ref[:, act], got_ref[:, units], TN)
    dgate_ref[...] = d_gate.astype(BF16)
    for m in range(2):
        for z in range(GROUPS // 2):
            for x, packet in enumerate(packets(d_c, m, z)):
                j = lax.axis_index("fx") ^ x
                all_ref[j, m, z, 0:96, :] = packet.astype(BF16)
                all_ref[j, m, z, 96:160, :] = dgate_ref[128 * z + 64 * x : 128 * z + 64 * x + 64, 128 * m : 128 * m + 128]
    stay_ref[...] = all_ref[0]
    leave_ref[...] = all_ref[1]


def packed(vec):
    upper = vec.astype(BF16).astype(F32)
    return jnp.concatenate([upper, vec - upper], axis=0).astype(BF16)


def unpacked(packet):
    value = packet.astype(F32)
    return value[0:24] + value[24:48]


def third_kernel(
    recv_ref, start_ref, normed_ref, xhat_ref, v_ref, lane_ref, row_ref, feat_ref, state_ref, dstate_ref, enter_ref, dmixed_ref,
    part_ref, b_ref, stay_ref, y_ref, x_ref, xy_ref, dn_ref, dnaway_ref, scratch, dv_ref, all_ref, vec_ref,
):
    rows, width = xhat_ref.shape
    half = rows // 2
    offsets = offsets_of(start_ref)
    count = starts_until(offsets, pair_pos() * rows, rows)
    later = carried(recv_ref, row_ref, offsets, rows, True, scratch)
    sub = lax.broadcasted_iota(jnp.int32, (8, 128), 0)
    none = jnp.zeros((1, 128), F32)
    totals = [[jnp.zeros((8, 128), F32) for _ in range(4)] for _ in range(2)]
    powers = [(lane_ref[0:1, 128 * m : 128 * m + 128], -lane_ref[1:2, 128 * m : 128 * m + 128]) for m in range(2)]

    def read(b, m):
        value = [dstate_ref[8 * b : 8 * b + 8, part_lanes(part, m)] for part in range(2)]
        if b == rows // 8 - 1:
            value = [value[part] + jnp.where(sub == 7, later[part][m], 0.0) for part in range(2)]
        return tuple(value)

    def emit(b, m, adj):
        here, lanes = slice(8 * b, 8 * b + 8), slice(128 * m, 128 * m + 128)
        seen = count[8 * b - 1 : 8 * b] if b else none
        keep = count[here] == jnp.where(sub == 0, seen, pltpu.roll(count[here], 1, 0))
        prev = []
        for part in range(2):
            edge = state_ref[8 * b - 1 : 8 * b, part_lanes(part, m)] if b else enter_ref[0:1, part_lanes(part, m)]
            moved = jnp.where(sub == 0, edge, pltpu.roll(state_ref[here, part_lanes(part, m)], 1, 0))
            prev.append(jnp.where(keep, moved, 0.0))
        v = (v_ref[here, part_lanes(0, m)], v_ref[here, part_lanes(1, m)])
        for k, (p, q) in enumerate((prev, v)):
            totals[m][2 * k] = totals[m][2 * k] + (adj[0] * p + adj[1] * q)
            totals[m][2 * k + 1] = totals[m][2 * k + 1] + (adj[1] * p - adj[0] * q)
        dv = cmul((lane_ref[2:3, lanes], -lane_ref[3:4, lanes]), adj)
        for part in range(2):
            dvf_ref[here, part_lanes(part, m)] = dv[part]

    dvf_ref = all_ref
    scan(read, powers, [(none, none), (none, none)], count, True, emit)
    sums = [[column_sum(totals[m][k]) for m in range(2)] for k in range(4)]
    dv_ref[...] = dvf_ref[...].astype(BF16)
    dv = dv_ref[...]
    d_b = dot(dv, normed_ref[...], TN)
    flip = flipped()
    for m, (near, side) in enumerate(((stay_ref, x_ref), (y_ref, xy_ref))):
        for z in range(GROUPS // 2):
            even, odd = packets(d_b, m, z)
            here = slice(96 * z, 96 * z + 96)
            near[here, :] = jnp.where(flip, odd, even).astype(BF16)
            side[here, :] = jnp.where(flip, even, odd).astype(BF16)
    all_ref[...] = dot(dv, b_ref[...], NN)
    dnaway_ref[...] = all_ref[other_rows(half), :]
    own = all_ref[own_rows(half), :] + dmixed_ref[...] * feat_ref[1:2]
    dn_ref[...] = own
    all_ref[own_rows(half), :] = own
    d_normed = all_ref[...]
    vector = [column_sum(d_normed * xhat_ref[...]), column_sum(d_normed), part_ref[0:1, :], part_ref[1:2, :]]
    for k, value in enumerate(vector):
        for c in range(4):
            vec_ref[4 * k + c : 4 * k + c + 1, :] = value[:, 128 * c : 128 * c + 128]
    g = [jnp.concatenate(pair + [jnp.zeros((6, 128), F32)], axis=0) for pair in sums]
    decay, lam, step, abar_re, abar_im, coef_re, coef_im = (row_ref[k] for k in range(7))
    d_abar, d_coef = (g[0], g[1]), (g[2], g[3])
    denom = decay * decay + lam * lam
    numer = (step * abar_re - coef_re, step * abar_im - coef_im)
    ratio = cmul(numer, (-decay / denom, -lam / denom))
    to_lam_a = cmul((step * abar_re, -step * abar_im), d_abar)
    to_lam_c = cmul((ratio[0], -ratio[1]), d_coef)
    g_decay = -(to_lam_a[0] + to_lam_c[0])
    g_lam = to_lam_a[1] + to_lam_c[1]
    slope = cmul((-decay, lam), (abar_re, abar_im))
    g_step = (slope[0] * d_abar[0] + slope[1] * d_abar[1] + abar_re * d_coef[0] + abar_im * d_coef[1]) * step
    for k, value in enumerate((g_decay, g_lam, g_step)):
        for m in range(2):
            vec_ref[pl.ds(16 + 2 * k + (lax.axis_index("ty") ^ m), 1), :] = value[m : m + 1]
    folds = []
    for k in range(2):
        squares = part_ref[2 + k : 3 + k, :]
        total = (squares[:, 0:128] + squares[:, 128:256]) + (squares[:, 256:384] + squares[:, 384:512])
        total = jnp.broadcast_to(total, (8, 128))
        folds.append(total + pltpu.roll(total, 64, 1))
    vec_ref[22:23, :] = jnp.where(low_half((1, 128)), folds[0][:1], folds[1][:1])
    vec_ref[23:24, :] = jnp.zeros((1, 128), F32)
    vec = packed(vec_ref[...])
    for ref in (stay_ref, y_ref, x_ref, xy_ref):
        ref[384:432, :] = vec


def input_grad(dn_ref, got_ref, up_ref, xhat_ref, inv_ref, feat_ref, gin_ref):
    rows, width = up_ref.shape
    xhat = xhat_ref[own_rows(rows), :]
    d_xhat = (dn_ref[...] + got_ref[...]) * feat_ref[0:1]
    mean = jnp.sum(d_xhat, axis=1, keepdims=True) / width
    mean_hat = jnp.sum(d_xhat * xhat, axis=1, keepdims=True) / width
    gin_ref[...] = up_ref[...].astype(F32) + inv_ref[:, 0:1] * (d_xhat - mean - xhat * mean_hat)


def input_grad_kernel(*refs):
    input_grad(*refs)


def added(a, b):
    return (a.astype(F32) + b.astype(F32)).astype(BF16)


def middle_kernel(keep_ref, got_ref, stay_ref, leave_ref):
    stay_ref[...] = added(keep_ref[0], got_ref[0])
    leave_ref[...] = added(keep_ref[1], got_ref[1])


def plane_add_kernel(cw_ref, gotcw_ref, stay_ref, y_ref, x_ref, xy_ref, out_ref):
    def total(read):
        return (read(stay_ref) + read(y_ref)) + (read(x_ref) + read(xy_ref))

    vec = packed(total(lambda ref: unpacked(ref[384:432, :])))
    for z in range(GROUPS // 2):
        here = slice(96 * z, 96 * z + 96)
        out_ref[z, 0:96, :] = total(lambda ref, here=here: ref[here, :].astype(F32)).astype(BF16)
        out_ref[z, 96:256, :] = added(cw_ref[z], gotcw_ref[z])
        out_ref[z, 256:304, :] = vec


def vectors_kernel(got_ref, vec_ref):
    vec = unpacked(got_ref[0, 256:304, :])
    for z in range(1, GROUPS // 2):
        vec = vec + unpacked(got_ref[z, 256:304, :])
    vec_ref[...] = vec


def rows_to_lanes(rows):
    turned = [rows, pltpu.roll(rows, 96, 1), pltpu.roll(rows, 64, 1), pltpu.roll(rows, 32, 1)]
    lane = lane_iota((1, 128))
    return [
        jnp.where(lane < 96, rows[0:1], turned[1][1:2]),
        jnp.where(lane < 64, turned[1][1:2], turned[2][2:3]),
        jnp.where(lane < 32, turned[2][2:3], turned[3][3:4]),
    ]


def matrices_kernel(got_ref, dre_ref, dim_ref, ore_ref, oim_ref, glu_ref, square):
    def total(start, count):
        value = got_ref[0, start : start + count, :].astype(F32)
        for z in range(1, GROUPS // 2):
            value = value + got_ref[z, start : start + count, :].astype(F32)
        return value

    for start, first_ref, second_ref in ((0, dre_ref, dim_ref), (96, ore_ref, oim_ref)):
        square[0:96, :] = total(start, 96)
        square[96:128, :] = jnp.zeros((32, 128), F32)
        turned = square[...].T
        first_ref[...] = turned[0:64, 0:96]
        second_ref[...] = turned[64:128, 0:96]
    glu_ref[...] = total(192, 64)


def finish_kernel(
    count_all, own_ref, other_ref, dn_ref, got_ref, up_ref, xhat_ref, inv_ref, feat_ref,
    gin_ref, gbias_ref, scale_ref, bias_ref, skip_ref, decay_ref, lam_ref, step_ref, rms_ref, vec_ref,
):
    input_grad(dn_ref, got_ref, up_ref, xhat_ref, inv_ref, feat_ref, gin_ref)
    own, other = own_ref[...], other_ref[...]
    vec = own + other
    vec_ref[...] = vec
    first, second = jnp.where(lax.axis_index("tc") == 0, own, other), jnp.where(lax.axis_index("tc") == 0, other, own)
    for k, ref in enumerate((scale_ref, bias_ref, skip_ref)):
        for c in range(4):
            ref[:, 128 * c : 128 * c + 128] = vec[4 * k + c : 4 * k + c + 1]
    for k, ref in enumerate((decay_ref, lam_ref, step_ref)):
        at = 16 + 2 * k
        by_pos = [first[at : at + 1], second[at : at + 1], first[at + 1 : at + 2], second[at + 1 : at + 2]]
        for c, chunk in enumerate(rows_to_lanes(jnp.concatenate(by_pos + [jnp.zeros((4, 128), F32)], axis=0))):
            ref[128 * c : 128 * c + 128] = chunk.reshape(128)
    squares = vec[22:23]
    total = [jnp.sum(jnp.where(low_half((1, 128)) == low, squares, 0.0), axis=1, keepdims=True) for low in (True, False)]
    rms_ref[...] = jnp.sqrt(jnp.where(lane_iota((1, 2)) == 0, total[0], total[1]) / count_all)
    place = tensor_pos() * GROUPS + fsdp_pos()
    row = jnp.broadcast_to(vec_ref[pl.ds(12 + place // 8, 1), :], (8, 128))
    gbias_ref[...] = pltpu.roll(row, 128 - 16 * (place % 8), 1)[0:1, 0:16]


TAKES = {
    "pack": 1.5, "standardize": 0.4, "norm": 0.4, "first": 0.6, "states": 0.9, "readout": 0.4, "second": 0.7, "sums": 0.7, "back": 0.8,
    "third": 1.5, "input_grad": 0.5, "matrices": 0.5, "finish": 0.4,
}


def call(kernel, outs, args, scratch=(), specs=None, limit=24):
    name = getattr(kernel, "func", kernel).__name__.removesuffix("_kernel")
    return pl.pallas_call(
        kernel,
        out_shape=outs,
        in_specs=specs or [VM] * len(args),
        out_specs=jax.tree.map(lambda _: VM, outs),
        scratch_shapes=list(scratch),
        compiler_params=pltpu.CompilerParams(vmem_limit_bytes=limit << 20),
        cost_estimate=pl.CostEstimate(flops=0, transcendentals=0, bytes_accessed=int(TAKES.get(name, 0.1) * 3.6e6)),
        name=name,
    )(*args)


def tied(value, other):
    return lax.optimization_barrier((value, other))[0]


def swap(value, axis):
    return lax.ppermute(value, axis, [(0, 1), (1, 0)])


def across(value):
    return lax.ppermute(value, ("fx", "ty"), [(n, 3 - n) for n in range(4)])


def on_device(
    layer_in, grad_out, ln_scale, ln_bias, decay_rate, lam_im, log_dt, in_re, in_im, out_re, out_im, skip, glu_weight, glu_bias, seq_lengths
):
    rows, width = layer_in.shape
    fsdp = lax.axis_size(FSDP)
    pairs, pair = fsdp * 2, 2 * rows
    count_all = float(rows * pairs * 2 * width)
    fast = fsdp == GROUPS
    same_core = (*FSDP, "ty")
    if fast:
        row = lambda v: v.reshape(1, -1)
        sent = call(
            pack_kernel,
            sds((GROUPS // 2, 272, 128), BF16),
            (seq_lengths, in_re.T, in_im.T, out_re.T, out_im.T, glu_weight.T, row(ln_scale), row(ln_bias), row(skip), row(glu_bias),
             row(decay_rate), row(lam_im), row(log_dt)),
            [pltpu.VMEM((128, 128), F32), pltpu.VMEM((4, 64, 96), BF16), pltpu.VMEM((64, 128), BF16), pltpu.VMEM((4, 1, 64), BF16),
             pltpu.VMEM((3, 1, 96), F32), pltpu.SMEM(seq_lengths.shape, jnp.int32), pltpu.SemaphoreType.DMA((13,))],
            [HBM] * 13,
            60,
        )
        mine = lax.all_to_all(sent, "fz", 0, 0, tiled=True)
        own_b, own_cw = lax.optimization_barrier((mine[:, :112], mine[:, 112:]))
        plane_b = [own_b, swap(own_b, "ty"), swap(own_b, "fx"), across(own_b)]
        xhat, inverse = call(standardize_kernel, (sds((pair, width)), sds((rows, 128))), (layer_in, swap(layer_in, "tc")))
        plane_b, side_cw, xhat = lax.optimization_barrier((plane_b, swap(own_cw, "ty"), xhat))
        side_cw = jnp.stack([own_cw, side_cw])
        far_cw = swap(side_cw, "fx")
        g = jnp.stack(plane_b).reshape(2, 2, GROUPS // 2, 112, 128)
    else:
        xhat, inverse = call(standardize_kernel, (sds((pair, width)), sds((rows, 128))), (layer_in, swap(layer_in, "tc")))
        g, cw, other_cw = gathered(
            ln_scale, ln_bias, decay_rate, lam_im, log_dt, in_re, in_im, out_re, out_im, skip, glu_weight, glu_bias, seq_lengths
        )

    normed, feat, starts = call(
        norm_kernel,
        (sds((pair, width), BF16), sds((8, width)), sds((seq_lengths.shape[0], 128))),
        (xhat, g),
    )
    b_all, v, lane, row_prm, carry = call(
        functools.partial(first_kernel, pairs),
        (sds((512, width), BF16), sds((pair, 512)), sds((8, 256)), sds((8, 8, 128)), sds((pairs, 4, 128))),
        (normed, starts, g),
        [pltpu.VMEM((8, 128), F32)],
    )
    came = lax.all_to_all(carry, same_core, 0, 0, tiled=True)
    if fast:
        cw = jnp.stack(tied((side_cw, far_cw), came))
    state, twice, enter, c_all = call(
        states_kernel,
        (sds((pair, 512)), sds((pair, 512), BF16), sds((8, 512)), sds((512, width), BF16)),
        (came, starts, v, lane, row_prm, cw),
        [pltpu.VMEM((8, 128), F32)],
    )
    if fast:
        other_cw = swap(tied(cw, twice), "tc")
    own, away = call(
        readout_kernel, (sds((rows, width)), sds((rows, width))), (twice, c_all), [pltpu.VMEM((pair, width), F32)]
    )
    branch, d_mixed, dlogit, kept, away = call(
        second_kernel,
        (sds((rows, width), BF16), sds((rows, width)), sds((rows, width), BF16), *[sds((rows, 2 * width + 256), BF16)] * 2),
        (own, swap(away, "tc"), grad_out, normed, feat, cw, other_cw),
        [pltpu.VMEM((width, width), BF16), pltpu.VMEM((rows, width), BF16)],
    )
    got = swap(away, "tc")
    layer_out, part = call(
        sums_kernel, (sds((rows, width), BF16), sds((8, width))), (layer_in, branch, normed, d_mixed, dlogit)
    )
    got, part = lax.optimization_barrier((got, part))
    d_state, carry, stay_cw, leave_cw = call(
        functools.partial(back_kernel, pairs),
        (sds((pair, 512)), sds((pairs, 4, 128)), *[sds((2, GROUPS // 2, 160, 128), BF16)] * 2),
        (kept, got, twice, starts, lane, c_all),
        [pltpu.VMEM((pair, width), BF16), pltpu.VMEM((width, 256), BF16), pltpu.VMEM((8, 128), F32),
         pltpu.VMEM((2, 2, GROUPS // 2, 160, 128), BF16)],
    )
    if fast:
        far_cw = swap(leave_cw, "fx")
    came = lax.all_to_all(carry, same_core, 0, 0, tiled=True)
    if fast:
        came, far_cw, stay_cw = lax.optimization_barrier((came, far_cw, stay_cw))
        stay_cw, leave_cw = call(middle_kernel, [sds((GROUPS // 2, 160, 128), BF16)] * 2, (stay_cw, far_cw))
        far_cw = swap(leave_cw, "ty")
        came = tied(came, leave_cw)
    stay_b, y_b, x_b, xy_b, d_normed, away = call(
        third_kernel,
        (*[sds((432, 128), BF16)] * 4, sds((rows, width)), sds((rows, width))),
        (came, starts, normed, xhat, v, lane, row_prm, feat, state, d_state, enter, d_mixed, part, b_all),
        [pltpu.VMEM((8, 128), F32), pltpu.VMEM((pair, 512), BF16), pltpu.VMEM((pair, width), F32), pltpu.VMEM((24, 128), F32)],
    )
    if not fast:
        grad_in = call(
            input_grad_kernel, sds((rows, width)), (d_normed, swap(away, "tc"), grad_out, xhat, inverse, feat)
        )
        return reduced(layer_out, grad_in, stay_cw, leave_cw, (stay_b, y_b, x_b, xy_b), count_all, fsdp, width)
    xy_b = across(xy_b)
    x_b = swap(x_b, "fx")
    y_b = swap(y_b, "ty")
    sent = call(
        plane_add_kernel,
        sds((GROUPS // 2, 304, 128), BF16),
        (stay_cw, far_cw, stay_b, y_b, x_b, xy_b),
    )
    got = lax.all_to_all(sent, "fz", 0, 0, tiled=True)
    away = swap(tied(away, got), "tc")
    vec = call(vectors_kernel, sds((24, 128)), (got,))
    other = swap(vec, "tc")
    d_re, d_im, d_ore, d_oim, d_glu = call(
        matrices_kernel, (*[sds((64, 96))] * 4, sds((64, 128))), (got,), [pltpu.VMEM((128, 128), F32)]
    )
    grad_in, d_gbias, d_scale, d_bias, d_skip, g_decay, g_lam, g_step, rms = call(
        functools.partial(finish_kernel, count_all),
        (sds((rows, width)), sds((1, 16)), *[sds((1, 512))] * 3, *[sds((384,))] * 3, sds((1, 2))),
        (vec, other, d_normed, away, grad_out, xhat, inverse, feat),
        [pltpu.VMEM((24, 128), F32)],
    )
    flat = lambda value: value.reshape(-1)
    return (
        layer_out, grad_in, flat(d_scale), flat(d_bias), g_decay, g_lam, g_step, d_re.T, d_im.T, d_ore.T, d_oim.T,
        flat(d_skip), d_glu.T, flat(d_gbias), flat(rms),
    )


def gathered(ln_scale, ln_bias, decay_rate, lam_im, log_dt, in_re, in_im, out_re, out_im, skip, glu_weight, glu_bias, seq_lengths):
    tens = tensor_pos()
    full = lambda value, axis: lax.all_gather(value, FSDP, axis=axis, tiled=True)

    def pair(first, second):
        halves = jnp.stack([first.reshape(-1, GROUPS, 64), second.reshape(-1, GROUPS, 64)], axis=2)
        return halves.reshape(-1, GROUPS, 128).swapaxes(0, 1)

    gate = lax.dynamic_slice_in_dim(full(glu_weight, 1), tens * 128, 128, 0).T.reshape(GROUPS, 64, 128)
    vectors = [pair(full(ln_scale, 0)[None], full(ln_bias, 0)[None]), pair(full(skip, 0)[None], full(glu_bias, 0)[None])]
    for value in (decay_rate, lam_im, log_dt):
        value = jnp.pad(value, (0, 32))
        for _ in range(3):
            piece = lax.reduce_precision(value, 8, 7)
            value = value - piece
            vectors.append(jnp.broadcast_to(piece.astype(BF16)[None, None], (GROUPS, 1, 128)))
    starts = jnp.cumsum(seq_lengths) - seq_lengths
    for value in (starts >> 8, starts & 255):
        value = jnp.pad(value, (0, 128 - value.shape[0])).astype(BF16)
        vectors.append(jnp.broadcast_to(value[None, None], (GROUPS, 1, 128)))
    vectors.append(jnp.zeros((GROUPS, 3, 128), BF16))
    packet = jnp.concatenate(
        [pair(full(in_re, 1), full(in_im, 1)), *vectors, pair(full(out_re, 1), full(out_im, 1)), gate],
        axis=1,
    )
    everyone = lax.all_gather(packet, TENSOR, axis=0).reshape(2, 2, GROUPS // 2, 2, 272, 128)
    x, y, core = (lax.axis_index(axis) for axis in ("fx", "ty", "tc"))
    own_x = lambda value, axis: jnp.stack([lax.dynamic_index_in_dim(value, x ^ j, axis, keepdims=False) for j in range(2)])
    for i in range(2):
        both = lax.dynamic_index_in_dim(everyone, core ^ i, 1, keepdims=False)
        slots = [own_x(lax.dynamic_index_in_dim(both, y ^ m, 0, keepdims=False), 1) for m in range(2)]
        slots = jnp.stack(slots, axis=1)
        if i == 0:
            g, cw = slots[:, :, :, :112], slots[:, :, :, 112:]
    return g, cw, slots[:, :, :, 112:]


def reduced(layer_out, grad_in, stay_cw, leave_cw, plane_b, count_all, fsdp, width):
    tens = tensor_pos()
    x = lax.axis_index("fx")

    def canonical(slots):
        out = jnp.zeros((4, GROUPS, *slots[0].shape[2:]), F32)
        for m, slot in enumerate(slots):
            parts = [lax.dynamic_index_in_dim(slot.astype(F32), x ^ n, 1) for n in range(2)]
            block = jnp.concatenate(parts, axis=1).reshape(1, GROUPS, *slot.shape[2:])
            out = lax.dynamic_update_slice_in_dim(out, block, slot_pos(m, 0), 0)
        return out

    def natural(slots):
        halves = canonical(slots).reshape(4, GROUPS, -1, 2, 64).transpose(3, 0, 2, 1, 4)
        return halves[0].reshape(-1, width), halves[1].reshape(-1, width)

    def scattered(value):
        value = lax.psum_scatter(value, TENSOR, scatter_dimension=0, tiled=True)
        return lax.psum_scatter(value, FSDP, scatter_dimension=1, tiled=True)

    blocks = [value[:384].reshape(GROUPS // 2, 96, 128) for value in plane_b]
    d_re, d_im = natural([jnp.stack([blocks[m], blocks[2 + m]], axis=1) for m in range(2)])
    cw = jnp.stack([stay_cw, leave_cw]).transpose(1, 2, 0, 3, 4)
    d_ore, d_oim = natural([value[:, :, :96] for value in cw])
    d_glu = canonical([value[:, :, 96:] for value in cw]).reshape(4, width, 128).swapaxes(1, 2).reshape(-1, width)
    vec = unpacked(plane_b[0][384:432])
    by_pos = lax.dynamic_update_slice_in_dim(
        jnp.zeros((3, 2, 2, 96), F32), vec[16:22, :96].reshape(3, 2, 1, 96), lax.axis_index("tc"), 2
    )
    vec, by_pos = lax.psum((vec, by_pos), AXES)
    states = lambda k: by_pos[k].reshape(-1)
    own = width // (4 * fsdp)
    place = tens * fsdp + fsdp_pos()
    d_gbias = lax.dynamic_slice_in_dim(vec[12:16].reshape(-1), place * own, own, 0)
    rms = jnp.sqrt(jnp.sum(vec[22].reshape(2, 64), axis=1) / count_all)
    return (
        layer_out, grad_in, vec[0:4].reshape(-1), vec[4:8].reshape(-1), states(0), states(1), states(2), scattered(d_re), scattered(d_im),
        scattered(d_ore), scattered(d_oim), vec[8:12].reshape(-1), scattered(d_glu), d_gbias, rms,
    )


def solution(mesh):
    shape = (mesh.shape["fsdp"] // 2, 2, mesh.shape["tensor"] // 2, 2)
    split = Mesh(mesh.devices.reshape(shape), AXES)
    tokens, matrix = P(AXES, None), P(TENSOR, FSDP)
    return jax.shard_map(
        on_device,
        mesh=split,
        in_specs=(
            tokens, tokens, P(FSDP), P(FSDP), P(TENSOR), P(TENSOR), P(TENSOR), matrix, matrix, matrix, matrix,
            P(FSDP), P(None, FSDP), P(FSDP), P(),
        ),
        out_specs=(
            tokens, tokens, P(), P(), P(), P(), P(), matrix, matrix, matrix, matrix, P(), matrix, P((*TENSOR, *FSDP)), P(),
        ),
        check_vma=False,
    )
```

```python
import functools

import jax
import jax.numpy as jnp
from jax import lax
from jax.experimental import pallas as pl
from jax.experimental.pallas import tpu as pltpu
from jax.sharding import Mesh
from jax.sharding import PartitionSpec as P

F32 = jnp.float32
BF16 = jnp.bfloat16
FSDP = ("fz", "fx")
TENSOR = ("ty", "tc")
AXES = (*FSDP, *TENSOR)
HBM = pl.BlockSpec(memory_space=pltpu.HBM)
VM = pl.BlockSpec(memory_space=pltpu.VMEM)
SM = pl.BlockSpec(memory_space=pltpu.SMEM)

GROUPS = 8
VEC = 96


def sds(shape, dtype=F32):
    return jax.ShapeDtypeStruct(shape, dtype)


def low_half(shape):
    return lax.broadcasted_iota(jnp.int32, shape, len(shape) - 1) < 64


def lane_iota(shape):
    return lax.broadcasted_iota(jnp.int32, shape, len(shape) - 1)


def dot(a, b, dims):
    return lax.dot_general(a, b, (dims, ((), ())), preferred_element_type=F32)


NT = ((1,), (1,))
NN = ((1,), (0,))
TN = ((0,), (0,))


def flipped():
    return lax.axis_index("fx") == 1


def part_lanes(part, m):
    return slice(256 * part + 128 * m, 256 * part + 128 * m + 128)


def slot_pos(m, core):
    return (lax.axis_index("ty") ^ m) * 2 + (lax.axis_index("tc") ^ core)


def own_rows(rows):
    return pl.ds(pl.multiple_of(lax.axis_index("tc") * rows, rows), rows)


def other_rows(rows):
    return pl.ds(pl.multiple_of((1 - lax.axis_index("tc")) * rows, rows), rows)


def piece(ref, m, f, start, count):
    return ref[f % 2, m, f // 2, start : start + count, :]


def natural(get, ref):
    lo = low_half((96, 128))
    for m in range(2):
        for part in range(2):
            lanes = part_lanes(part, m)
            ref[lanes.start + 96 : lanes.stop, :] = jnp.zeros((32, 512), BF16)
        for z in range(GROUPS // 2):
            even, odd = get(m, z, 0).astype(F32), get(m, z, 1).astype(F32)
            here = slice(128 * z, 128 * z + 128)
            ref[128 * m : 128 * m + 96, here] = jnp.where(lo, even, pltpu.roll(odd, 64, 1)).astype(BF16)
            ref[256 + 128 * m : 256 + 128 * m + 96, here] = jnp.where(lo, pltpu.roll(even, 64, 1), odd).astype(BF16)


def packets(value, m, z):
    lo = low_half((96, 128))
    here = slice(128 * z, 128 * z + 128)
    re, im = value[128 * m : 128 * m + 96, here], value[256 + 128 * m : 256 + 128 * m + 96, here]
    return jnp.where(lo, re, pltpu.roll(im, 64, 1)), jnp.where(lo, pltpu.roll(re, 64, 1), im)


def feature_rows(ref, row):
    lo = low_half((8, 128))
    flip = flipped()
    first, second = [], []
    for c in range(GROUPS // 2):
        a = jnp.broadcast_to(piece(ref, 0, 2 * c, row, 1).astype(F32), (8, 128))
        b = jnp.broadcast_to(piece(ref, 0, 2 * c + 1, row, 1).astype(F32), (8, 128))
        a, b = jnp.where(flip, b, a), jnp.where(flip, a, b)
        first.append(jnp.where(lo, a, pltpu.roll(b, 64, 1)))
        second.append(jnp.where(lo, pltpu.roll(a, 64, 1), b))
    return jnp.concatenate(first, axis=1)[:1], jnp.concatenate(second, axis=1)[:1]


def cmul(a, b):
    return a[0] * b[0] - a[1] * b[1], a[0] * b[1] + a[1] * b[0]


def tensor_pos():
    return lax.axis_index("ty") * 2 + lax.axis_index("tc")


def fsdp_pos():
    return lax.axis_index("fz") * 2 + lax.axis_index("fx")


def pair_pos():
    return fsdp_pos() * 2 + lax.axis_index("ty")


def offsets_of(start_ref):
    return [start_ref[n : n + 1, :] for n in range(start_ref.shape[0])]


STEPS = 16


def in_tiles(ref, rows, value):
    for c in range(4):
        ref[c, rows, :] = value[:, 128 * c : 128 * c + 128]


def of_tiles(ref, rows):
    return jnp.concatenate([ref[c, rows, :] for c in range(4)], axis=1)


def interleaved(ref, b):
    groups = [of_tiles(ref, pl.ds((n // STEPS) * 128 + n % STEPS, 8, stride=STEPS)) for n in (b, b + 1)]
    return jnp.concatenate(groups, axis=0)


def in_order(source, target):
    for g in range(target.shape[0] // 8):
        h, s, i = g // STEPS, g % STEPS // 2, 8 * (g % 2)
        target[8 * g : 8 * g + 8, :] = of_tiles(source, pl.ds(128 * h + 8 * i + s, 8, stride=8))


def starts_until(offsets, base, rows):
    row = lax.broadcasted_iota(jnp.int32, (rows, 128), 0)
    token = (row & ~127) + (row & 7) * STEPS + ((row & 127) >> 3)
    at = (token + base).astype(F32)
    count = jnp.zeros((rows, 128), F32)
    for off in offsets:
        count = count + jnp.where((at >= off) & (off >= at[0:1]), 1.0, 0.0)
    return count


def no_start(offsets, base, rows):
    link = jnp.ones((1, 128), F32)
    first = (jnp.zeros((1, 128), jnp.int32) + base).astype(F32)
    for off in offsets:
        link = jnp.where((off >= first) & (off < first + rows), 0.0, link)
    return link


def expm1(x):
    series = x * (1 + x / 2 * (1 + x / 3 * (1 + x / 4 * (1 + x / 5 * (1 + x / 6 * (1 + x / 7))))))
    return jnp.where(jnp.abs(x) < 0.25, series, jnp.exp(x) - 1.0)


def discretize(decay_rate, lam_im, log_dt):
    step_size = jnp.exp(log_dt)
    lam_re = -decay_rate
    magnitude = jnp.exp(lam_re * step_size)
    phase = lam_im * step_size
    abar_re = magnitude * jnp.cos(phase)
    abar_im = magnitude * jnp.sin(phase)
    half_sin = jnp.sin(0.5 * phase)
    less_re = expm1(lam_re * step_size) * jnp.cos(phase) - 2.0 * half_sin * half_sin
    denom = lam_re * lam_re + lam_im * lam_im
    coef_re = (less_re * lam_re + abar_im * lam_im) / denom
    coef_im = (abar_im * lam_re - less_re * lam_im) / denom
    return abar_re, abar_im, coef_re, coef_im, step_size


def pack_kernel(*refs):
    *inputs, out_ref, start_ref, square, four, glu_ref, halves, params, lengths, sems = refs
    seq_hbm, matrices, glu_hbm, features, states = inputs[0], inputs[1:5], inputs[5], inputs[6:10], inputs[10:13]
    units = pl.multiple_of(tensor_pos() * 128, 128)
    pairs = [(ref, four.at[k]) for k, ref in enumerate(matrices)]
    pairs += [(glu_hbm.at[:, pl.ds(units, 128)], glu_ref), (seq_hbm, lengths)]
    pairs += [(ref, halves.at[k]) for k, ref in enumerate(features)]
    pairs += [(ref, params.at[k]) for k, ref in enumerate(states)]
    copies = [pltpu.make_async_copy(source, target, sems.at[k]) for k, (source, target) in enumerate(pairs)]
    for copy in copies:
        copy.start()
    square[:, 96:128] = jnp.zeros((128, 32), F32)
    for copy in copies:
        copy.wait()
    vec = [
        jnp.concatenate([halves[0], halves[1]], axis=1).astype(F32),
        jnp.concatenate([halves[2], halves[3]], axis=1).astype(F32),
    ]
    for k in range(3):
        value = jnp.concatenate([params[k], jnp.zeros((1, 32), F32)], axis=1)
        for _ in range(3):
            part = value.astype(BF16).astype(F32)
            value = value - part
            vec.append(part)
    total = 0
    for n in range(lengths.shape[0]):
        start_ref[n : n + 1, :] = jnp.full((1, 128), total, jnp.int32).astype(F32)
        total = total + lengths[n]
    vec.append(jnp.zeros((16 - len(vec), 128), F32))
    vec = jnp.concatenate(vec, axis=0).astype(BF16)
    pieces = []
    for k in (0, 2):
        square[0:64, 0:96] = four[k].astype(F32)
        square[64:128, 0:96] = four[k + 1].astype(F32)
        pieces.append(square[...].T[0:96].astype(BF16))
    packet = jnp.concatenate([pieces[0], vec, pieces[1], glu_ref[...]], axis=0)
    for z in range(GROUPS // 2):
        out_ref[z] = packet


def params_of(ref, vec_row):
    lane = lane_iota((8, 128))
    out = []
    for k, safe in enumerate((1.0, 0.0, 0.0)):
        rows = []
        for m in range(2):
            part = piece(ref, m, 0, vec_row, 16).astype(F32)
            rows.append((part[2 + 3 * k : 3 + 3 * k] + part[3 + 3 * k : 4 + 3 * k]) + part[4 + 3 * k : 5 + 3 * k])
        value = jnp.concatenate(rows + [jnp.full((6, 128), safe, F32)], axis=0)
        out.append(jnp.where(lane < 96, value, safe))
    return out


def carry_block(re_rows, im_rows, scratch):
    for m in range(2):
        y = lax.axis_index("ty") ^ m
        scratch[pl.ds(y, 1), :] = re_rows[m]
        scratch[pl.ds(2 + y, 1), :] = im_rows[m]


def standardize_kernel(x_ref, other_ref, up_ref, start_ref, xhat_ref, up_out_ref, inv_ref, count_ref, tiles, inverses):
    rows, width = x_ref.shape
    in_tiles(tiles, slice(0, rows), up_ref[...].astype(F32))
    for b in range(0, rows // 8, 2):
        up_out_ref[8 * b : 8 * b + 16, :] = interleaved(tiles, b)
    for ref, where, own in ((x_ref, own_rows(rows), True), (other_ref, other_rows(rows), False)):
        x = ref[...].astype(F32)
        centered = x - jnp.sum(x, axis=1, keepdims=True) / width
        inverse = lax.rsqrt(jnp.sum(centered * centered, axis=1, keepdims=True) / width + 1e-05)
        in_tiles(tiles, where, centered * inverse)
        if own:
            inverses[...] = jnp.broadcast_to(inverse, (rows, 128))
    for b in range(0, 2 * rows // 8, 2):
        xhat_ref[8 * b : 8 * b + 16, :] = interleaved(tiles, b)
    for b in range(rows // 8):
        inv_ref[8 * b : 8 * b + 8, :] = inverses[pl.ds(b, 8, stride=STEPS), :]
    count_ref[...] = starts_until(offsets_of(start_ref), pair_pos() * 2 * rows, 2 * rows)


def norm_kernel(xhat_ref, g_ref, normed_ref, feat_ref):
    scale, bias = feature_rows(g_ref, VEC)
    feat_ref[0:1] = scale
    feat_ref[1:2], feat_ref[2:3] = feature_rows(g_ref, VEC + 1)
    normed_ref[...] = (xhat_ref[...] * scale + bias).astype(BF16)


def first_kernel(pairs, normed_ref, count_ref, g_ref, b_ref, v_ref, lane_ref, row_ref, send_ref, scratch):
    rows = normed_ref.shape[0]
    natural(lambda m, z, x: g_ref[lax.axis_index("fx") ^ x, m, z, 0:96, :], b_ref)
    v_ref[...] = dot(normed_ref[...], b_ref[...], NT)

    decay, lam, log_dt = params_of(g_ref, VEC)
    abar_re, abar_im, coef_re, coef_im, step_size = discretize(decay, lam, log_dt)
    power = (abar_re, abar_im)
    for _ in range(8):
        power = cmul(power, power)
    scratch[...] = jnp.zeros((8, 128), F32)
    carry_block([power[0][m : m + 1] for m in range(2)], [power[1][m : m + 1] for m in range(2)], scratch)
    for k, value in enumerate((decay, lam, step_size, abar_re, abar_im, coef_re, coef_im, scratch[...])):
        row_ref[k] = value
    for k, value in enumerate((abar_re, abar_im, coef_re, coef_im)):
        for m in range(2):
            lane_ref[k : k + 1, 128 * m : 128 * m + 128] = value[m : m + 1]

    count = count_ref[...]
    open_tail = jnp.where(count == count[rows - 1 : rows], 1.0, 0.0)
    last = ([], [])
    for m in range(2):
        a = (all_rows(abar_re[m : m + 1]), all_rows(abar_im[m : m + 1]))
        b = (coef_re[m : m + 1], coef_im[m : m + 1])
        sixteen = squared(a, 4)
        tile = tile_powers(sixteen, lambda sub: 7 - sub)
        halves = []
        for h in range(2):
            acc = (jnp.zeros((8, 128), F32), jnp.zeros((8, 128), F32))
            for blk in range(STEPS * h, STEPS * h + STEPS):
                here = slice(8 * blk, 8 * blk + 8)
                drive = cmul(b, (v_ref[here, part_lanes(0, m)], v_ref[here, part_lanes(1, m)]))
                moved = cmul(a, acc)
                acc = (moved[0] + drive[0] * open_tail[here], moved[1] + drive[1] * open_tail[here])
            total = cmul(tile, acc)
            halves.append((column_sum(total[0]), column_sum(total[1])))
        moved = cmul(squared((sixteen[0][:1], sixteen[1][:1]), 3), halves[0])
        last[0].append(moved[0] + halves[1][0])
        last[1].append(moved[1] + halves[1][1])
    carry_block(last[0], last[1], scratch)
    packet = scratch[...]
    for d in range(pairs):
        send_ref[d] = packet[0:4]


def squared(a, times):
    for _ in range(times):
        a = cmul(a, a)
    return a


def tile_powers(a, exponent_of):
    exponent = exponent_of(lax.broadcasted_iota(jnp.int32, (8, 128), 0))
    tile = (jnp.ones((8, 128), F32), jnp.zeros((8, 128), F32))
    for bit in range(4):
        taken = (exponent & (1 << bit)) != 0
        more = cmul(tile, a)
        tile = (jnp.where(taken, more[0], tile[0]), jnp.where(taken, more[1], tile[1]))
        a = cmul(a, a)
    return tile


def all_rows(row):
    return jnp.broadcast_to(row, (8, 128))


def plus(value, link, more):
    return value[0] + jnp.where(link, more[0], 0.0), value[1] + jnp.where(link, more[1], 0.0)


def scan(read, powers, carry, count, reverse, emit):
    sub = lax.broadcasted_iota(jnp.int32, (8, 128), 0)
    order = range(STEPS - 1, -1, -1) if reverse else range(STEPS)
    end = 0 if reverse else 7
    back = lambda k: 8 - k if reverse else k
    carry = [(all_rows(c[0]), all_rows(c[1])) for c in carry]
    entries, ends, upto = [], [], []
    for a in powers:
        a = (all_rows(a[0]), all_rows(a[1]))
        power = [a]
        for _ in range(STEPS - 1):
            power.append(cmul(power[-1], a))
        upto.append(power)
        ends.append((power[-1], squared(power[-1], 1), squared(power[-1], 2)))
        entries.append(tile_powers(power[-1], (lambda sub: 8 - sub) if reverse else (lambda sub: sub + 1)))
    seen = jnp.zeros((8, 128), F32)
    for h in (1, 0) if reverse else (0, 1):
        counts = [count[8 * b : 8 * b + 8] for b in range(STEPS * h, STEPS * h + STEPS)]
        last = counts[order[-1]]
        near = jnp.where(sub == 7 - end, seen, pltpu.roll(last, back(1), 0))
        for m in range(2):
            values, before = {}, None
            for i in order:
                value = read(STEPS * h + i, m)
                if before is not None:
                    value = plus(value, counts[i] == counts[before], cmul(upto[m][0], values[before]))
                values[i], before = value, i
            tip = values[before]
            for k, power in zip((1, 2, 4), ends[m]):
                link = ((sub < 8 - k) if reverse else (sub >= k)) & (pltpu.roll(last, back(k), 0) == last)
                tip = plus(tip, link, cmul(power, (pltpu.roll(tip[0], back(k), 0), pltpu.roll(tip[1], back(k), 0))))
            tip = plus(tip, last == seen, cmul(entries[m], carry[m]))
            comes = tuple(jnp.where(sub == 7 - end, carry[m][p], pltpu.roll(tip[p], back(1), 0)) for p in range(2))
            for n, i in enumerate(order):
                emit(STEPS * h + i, m, plus(values[i], counts[i] == near, cmul(upto[m][n], comes)))
            carry[m] = (all_rows(tip[0][end : end + 1]), all_rows(tip[1][end : end + 1]))
        seen = all_rows(last[end : end + 1])


def carried(recv_ref, row_ref, offsets, rows, reverse, scratch):
    pairs = recv_ref.shape[0]
    power = row_ref[7]
    pre, pim = power[0:2], power[2:4]
    if reverse:
        pim = -pim
    place = pair_pos()

    zero = jnp.zeros((2, 128), F32)
    if pairs <= 32:
        first = lax.broadcasted_iota(jnp.int32, (pairs, 128), 0).astype(F32) * rows
        links = jnp.ones((pairs, 128), F32)
        for off in offsets:
            links = jnp.where((off >= first) & (off < first + rows), 0.0, links)
        out = (zero, zero)
        for j in range(pairs - 1, 0, -1) if reverse else range(pairs - 1):
            link = links[j : j + 1]
            got = recv_ref[j]
            new = cmul((pre * link, pim * link), out)
            reached = (j > place) if reverse else (j < place)
            out = (jnp.where(reached, new[0] + got[0:2], out[0]), jnp.where(reached, new[1] + got[2:4], out[1]))
    else:

        def turn(k, state):
            j = pairs - 1 - k if reverse else k
            link = no_start(offsets, j * rows, rows)
            got = recv_ref[j]
            new = cmul((pre * link, pim * link), state)
            return new[0] + got[0:2], new[1] + got[2:4]

        out = lax.fori_loop(0, pairs - 1 - place if reverse else place, turn, (zero, zero))
    scratch[0:2, :] = out[0]
    scratch[2:4, :] = out[1]
    own = [lax.axis_index("ty") ^ m for m in range(2)]
    return [scratch[pl.ds(y, 1), :] for y in own], [scratch[pl.ds(2 + y, 1), :] for y in own]


def column_sum(value):
    return jnp.sum(value, axis=0, keepdims=True)


def states_kernel(
    recv_ref, start_ref, count_ref, v_ref, lane_ref, row_ref, cw_ref, state_ref, twice_ref, enter_ref, c_ref, scratch
):
    rows = v_ref.shape[0]
    count = count_ref[...]
    enter = carried(recv_ref, row_ref, offsets_of(start_ref), rows, False, scratch)
    for part in range(2):
        for m in range(2):
            enter_ref[0:1, part_lanes(part, m)] = enter[part][m]
    powers = [(lane_ref[0:1, 128 * m : 128 * m + 128], lane_ref[1:2, 128 * m : 128 * m + 128]) for m in range(2)]

    def read(b, m):
        here, lanes = slice(8 * b, 8 * b + 8), slice(128 * m, 128 * m + 128)
        return cmul((lane_ref[2:3, lanes], lane_ref[3:4, lanes]), (v_ref[here, part_lanes(0, m)], v_ref[here, part_lanes(1, m)]))

    def emit(b, m, value):
        for part in range(2):
            state_ref[8 * b : 8 * b + 8, part_lanes(part, m)] = value[part]

    scan(read, powers, [(enter[0][m], enter[1][m]) for m in range(2)], count, False, emit)
    twice_ref[:, 0:256] = state_ref[:, 0:256].astype(BF16) * 2
    twice_ref[:, 256:512] = state_ref[:, 256:512].astype(BF16) * -2
    natural(lambda m, z, x: cw_ref[lax.axis_index("fx") ^ x, m, z, 0:96, :], c_ref)


def readout_kernel(twice_ref, c_ref, own_ref, away_ref, scratch):
    rows = own_ref.shape[0]
    scratch[...] = dot(twice_ref[...], c_ref[...], NN)
    own_ref[...] = scratch[own_rows(rows), :]
    away_ref[...] = scratch[other_rows(rows), :]


def second_kernel(
    own_ref, got_ref, up_ref, normed_ref, feat_ref, cw_ref, othercw_ref,
    branch_ref, dmixed_ref, dlogit_ref, mine_ref, away_ref, gate_ref, all_ref,
):
    rows, width = up_ref.shape
    for core, ref in enumerate((cw_ref, othercw_ref)):
        for m in range(2):
            lanes = pl.ds(pl.multiple_of(slot_pos(m, core) * 128, 128), 128)
            for f in range(GROUPS):
                place = (f // 2) * 2 + (lax.axis_index("fx") ^ (f % 2))
                gate_ref[pl.ds(pl.multiple_of(place * 64, 64), 64), lanes] = piece(ref, m, f, 96, 64)
    skip, gate_bias = feat_ref[1:2], feat_ref[2:3]
    normed = normed_ref[own_rows(rows), :].astype(F32)
    mixed = (own_ref[...] + got_ref[...]) + skip * normed
    cdf = 0.5 * (1.0 + lax.erf(mixed * 0.7071067811865476))
    act_low = (mixed * cdf).astype(BF16)
    act = act_low.astype(F32)
    w_gate = gate_ref[...]
    logit = dot(act_low, w_gate, NN) + gate_bias
    gate = 1.0 / (1.0 + jnp.exp(-logit))
    branch_ref[...] = (act * gate).astype(BF16)
    up = up_ref[...]
    dlogit = (up * act * gate * (1.0 - gate)).astype(BF16)
    dlogit_ref[...] = dlogit
    all_ref[...] = dlogit
    d_act = dot(dlogit, w_gate, NT) + up * gate
    slope = cdf + mixed * jnp.exp(-0.5 * mixed * mixed) * 0.3989422804014327
    d_mixed = d_act * slope
    dmixed_ref[...] = d_mixed
    for core, ref in enumerate((mine_ref, away_ref)):
        ref[:, 0:width] = d_mixed.astype(BF16)
        ref[:, width : 2 * width] = act_low
        for m in range(2):
            lanes = pl.ds(pl.multiple_of(slot_pos(m, core) * 128, 128), 128)
            ref[:, 2 * width + 128 * m : 2 * width + 128 * m + 128] = all_ref[:, lanes]


def sums_kernel(x_ref, branch_ref, normed_ref, dmixed_ref, dlogit_ref, out_ref, part_ref, tiles, ordered):
    x = x_ref[...].astype(F32)
    branch = branch_ref[...].astype(F32)
    in_tiles(tiles, slice(None), branch)
    in_order(tiles, ordered)
    out_ref[...] = (x + ordered[...]).astype(BF16)
    skip = column_sum(dmixed_ref[...] * normed_ref[own_rows(x_ref.shape[0]), :].astype(F32))
    for k, value in enumerate((skip, column_sum(dlogit_ref[...].astype(F32)), column_sum(x * x), column_sum(branch * branch))):
        part_ref[k : k + 1, :] = value


def back_kernel(
    pairs, mine_ref, got_ref, twice_ref, count_ref, lane_ref, c_ref,
    dstate_ref, send_ref, stay_ref, leave_ref, dy_ref, dgate_ref, scratch, all_ref,
):
    rows, width = dy_ref.shape
    half = rows // 2
    dy_ref[own_rows(half), :] = mine_ref[:, 0:width]
    dy_ref[other_rows(half), :] = got_ref[:, 0:width]
    d_state = dot(dy_ref[...], c_ref[...], NT)
    dstate_ref[:, 0:256] = d_state[:, 0:256] * 2.0
    dstate_ref[:, 256:512] = d_state[:, 256:512] * -2.0
    count = count_ref[...]
    head = jnp.where(count == 0.0, 1.0, 0.0)
    first = ([], [])
    for m in range(2):
        lanes = slice(128 * m, 128 * m + 128)
        a = (all_rows(lane_ref[0:1, lanes]), all_rows(-lane_ref[1:2, lanes]))
        sixteen = squared(a, 4)
        tile = tile_powers(sixteen, lambda sub: sub)
        halves = []
        for h in range(2):
            acc = (jnp.zeros((8, 128), F32), jnp.zeros((8, 128), F32))
            for blk in range(STEPS * h + STEPS - 1, STEPS * h - 1, -1):
                here = slice(8 * blk, 8 * blk + 8)
                moved = cmul(a, acc)
                acc = (
                    moved[0] + dstate_ref[here, part_lanes(0, m)] * head[here],
                    moved[1] + dstate_ref[here, part_lanes(1, m)] * head[here],
                )
            total = cmul(tile, acc)
            halves.append((column_sum(total[0]), column_sum(total[1])))
        moved = cmul(squared((sixteen[0][:1], sixteen[1][:1]), 3), halves[1])
        total = cmul((a[0][:1], a[1][:1]), (moved[0] + halves[0][0], moved[1] + halves[0][1]))
        first[0].append(total[0])
        first[1].append(total[1])
    scratch[...] = jnp.zeros((8, 128), F32)
    carry_block(first[0], first[1], scratch)
    packet = scratch[...]
    for d in range(pairs):
        send_ref[d] = packet[0:4]
    d_c = dot(twice_ref[...], dy_ref[...], TN)
    act = slice(width, 2 * width)
    units = slice(2 * width, 2 * width + 256)
    d_gate = dot(mine_ref[:, act], mine_ref[:, units], TN) + dot(got_ref[:, act], got_ref[:, units], TN)
    dgate_ref[...] = d_gate.astype(BF16)
    for m in range(2):
        for z in range(GROUPS // 2):
            for x, packet in enumerate(packets(d_c, m, z)):
                j = lax.axis_index("fx") ^ x
                all_ref[j, m, z, 0:96, :] = packet.astype(BF16)
                all_ref[j, m, z, 96:160, :] = dgate_ref[128 * z + 64 * x : 128 * z + 64 * x + 64, 128 * m : 128 * m + 128]
    stay_ref[...] = all_ref[0]
    leave_ref[...] = all_ref[1]


def packed(vec):
    upper = vec.astype(BF16).astype(F32)
    return jnp.concatenate([upper, vec - upper], axis=0).astype(BF16)


def unpacked(packet):
    value = packet.astype(F32)
    return value[0:24] + value[24:48]


def third_kernel(
    recv_ref, start_ref, count_ref, normed_ref, xhat_ref, v_ref, lane_ref, row_ref, feat_ref, state_ref, dstate_ref, enter_ref, dmixed_ref,
    part_ref, b_ref, stay_ref, y_ref, x_ref, xy_ref, dn_ref, dnaway_ref, scratch, dv_ref, all_ref, vec_ref,
):
    rows, width = normed_ref.shape
    half = rows // 2
    count = count_ref[...]
    later = carried(recv_ref, row_ref, offsets_of(start_ref), rows, True, scratch)
    sub = lax.broadcasted_iota(jnp.int32, (8, 128), 0)
    none = jnp.zeros((1, 128), F32)
    totals = [[jnp.zeros((8, 128), F32) for _ in range(4)] for _ in range(2)]
    powers = [(lane_ref[0:1, 128 * m : 128 * m + 128], -lane_ref[1:2, 128 * m : 128 * m + 128]) for m in range(2)]

    def read(b, m):
        value = [dstate_ref[8 * b : 8 * b + 8, part_lanes(part, m)] for part in range(2)]
        if b == rows // 8 - 1:
            value = [value[part] + jnp.where(sub == 7, later[part][m], 0.0) for part in range(2)]
        return tuple(value)

    def emit(b, m, adj):
        here, lanes = slice(8 * b, 8 * b + 8), slice(128 * m, 128 * m + 128)
        h, i = b // STEPS, b % STEPS
        if i:
            same = count[here] == count[8 * b - 8 : 8 * b]
            moved = [state_ref[8 * b - 8 : 8 * b, part_lanes(part, m)] for part in range(2)]
        else:
            end = slice(8 * (b + STEPS - 1), 8 * (b + STEPS))
            same = count[here] == jnp.where(sub == 0, count[127:128] if h else none, pltpu.roll(count[end], 1, 0))
            moved = []
            for part in range(2):
                edge = state_ref[127:128, part_lanes(part, m)] if h else enter_ref[0:1, part_lanes(part, m)]
                moved.append(jnp.where(sub == 0, edge, pltpu.roll(state_ref[end, part_lanes(part, m)], 1, 0)))
        prev = [jnp.where(same, part, 0.0) for part in moved]
        v = (v_ref[here, part_lanes(0, m)], v_ref[here, part_lanes(1, m)])
        for k, (p, q) in enumerate((prev, v)):
            totals[m][2 * k] = totals[m][2 * k] + (adj[0] * p + adj[1] * q)
            totals[m][2 * k + 1] = totals[m][2 * k + 1] + (adj[1] * p - adj[0] * q)
        dv = cmul((lane_ref[2:3, lanes], -lane_ref[3:4, lanes]), adj)
        for part in range(2):
            dvf_ref[here, part_lanes(part, m)] = dv[part]

    dvf_ref = all_ref
    scan(read, powers, [(none, none), (none, none)], count, True, emit)
    sums = [[column_sum(totals[m][k]) for m in range(2)] for k in range(4)]
    dv_ref[...] = dvf_ref[...].astype(BF16)
    dv = dv_ref[...]
    d_b = dot(dv, normed_ref[...], TN)
    flip = flipped()
    for m, (near, side) in enumerate(((stay_ref, x_ref), (y_ref, xy_ref))):
        for z in range(GROUPS // 2):
            even, odd = packets(d_b, m, z)
            here = slice(96 * z, 96 * z + 96)
            near[here, :] = jnp.where(flip, odd, even).astype(BF16)
            side[here, :] = jnp.where(flip, even, odd).astype(BF16)
    all_ref[...] = dot(dv, b_ref[...], NN)
    away = all_ref[other_rows(half), :]
    dnaway_ref[...] = away
    own = all_ref[own_rows(half), :] + dmixed_ref[...] * feat_ref[1:2]
    dn_ref[...] = own
    to_scale = column_sum(own * xhat_ref[own_rows(half), :]) + column_sum(away * xhat_ref[other_rows(half), :])
    vector = [to_scale, column_sum(own) + column_sum(away), part_ref[0:1, :], part_ref[1:2, :]]
    for k, value in enumerate(vector):
        for c in range(4):
            vec_ref[4 * k + c : 4 * k + c + 1, :] = value[:, 128 * c : 128 * c + 128]
    g = [jnp.concatenate(pair + [jnp.zeros((6, 128), F32)], axis=0) for pair in sums]
    decay, lam, step, abar_re, abar_im, coef_re, coef_im = (row_ref[k] for k in range(7))
    d_abar, d_coef = (g[0], g[1]), (g[2], g[3])
    denom = decay * decay + lam * lam
    numer = (step * abar_re - coef_re, step * abar_im - coef_im)
    ratio = cmul(numer, (-decay / denom, -lam / denom))
    to_lam_a = cmul((step * abar_re, -step * abar_im), d_abar)
    to_lam_c = cmul((ratio[0], -ratio[1]), d_coef)
    g_decay = -(to_lam_a[0] + to_lam_c[0])
    g_lam = to_lam_a[1] + to_lam_c[1]
    slope = cmul((-decay, lam), (abar_re, abar_im))
    g_step = (slope[0] * d_abar[0] + slope[1] * d_abar[1] + abar_re * d_coef[0] + abar_im * d_coef[1]) * step
    for k, value in enumerate((g_decay, g_lam, g_step)):
        for m in range(2):
            vec_ref[pl.ds(16 + 2 * k + (lax.axis_index("ty") ^ m), 1), :] = value[m : m + 1]
    folds = []
    for k in range(2):
        squares = part_ref[2 + k : 3 + k, :]
        total = (squares[:, 0:128] + squares[:, 128:256]) + (squares[:, 256:384] + squares[:, 384:512])
        total = jnp.broadcast_to(total, (8, 128))
        folds.append(total + pltpu.roll(total, 64, 1))
    vec_ref[22:23, :] = jnp.where(low_half((1, 128)), folds[0][:1], folds[1][:1])
    vec_ref[23:24, :] = jnp.zeros((1, 128), F32)
    vec = packed(vec_ref[...])
    for ref in (stay_ref, y_ref, x_ref, xy_ref):
        ref[384:432, :] = vec


def input_grad(dn_ref, got_ref, up_ref, xhat_ref, inv_ref, feat_ref, gin_ref, tiles):
    rows, width = up_ref.shape
    xhat = xhat_ref[own_rows(rows), :]
    d_xhat = (dn_ref[...] + got_ref[...]) * feat_ref[0:1]
    mean = jnp.sum(d_xhat, axis=1, keepdims=True) / width
    mean_hat = jnp.sum(d_xhat * xhat, axis=1, keepdims=True) / width
    in_tiles(tiles, slice(None), inv_ref[:, 0:1] * (d_xhat - mean - xhat * mean_hat))
    in_order(tiles, gin_ref)
    gin_ref[...] = gin_ref[...] + up_ref[...].astype(F32)


def input_grad_kernel(*refs):
    input_grad(*refs)


def added(a, b):
    return (a.astype(F32) + b.astype(F32)).astype(BF16)


def middle_kernel(keep_ref, got_ref, stay_ref, leave_ref):
    stay_ref[...] = added(keep_ref[0], got_ref[0])
    leave_ref[...] = added(keep_ref[1], got_ref[1])


def plane_add_kernel(cw_ref, gotcw_ref, stay_ref, y_ref, x_ref, xy_ref, out_ref):
    def total(read):
        return (read(stay_ref) + read(y_ref)) + (read(x_ref) + read(xy_ref))

    vec = packed(total(lambda ref: unpacked(ref[384:432, :])))
    for z in range(GROUPS // 2):
        here = slice(96 * z, 96 * z + 96)
        out_ref[z, 0:96, :] = total(lambda ref, here=here: ref[here, :].astype(F32)).astype(BF16)
        out_ref[z, 96:256, :] = added(cw_ref[z], gotcw_ref[z])
        out_ref[z, 256:304, :] = vec


def vectors_kernel(got_ref, vec_ref):
    vec = unpacked(got_ref[0, 256:304, :])
    for z in range(1, GROUPS // 2):
        vec = vec + unpacked(got_ref[z, 256:304, :])
    vec_ref[...] = vec


def rows_to_lanes(rows):
    turned = [rows, pltpu.roll(rows, 96, 1), pltpu.roll(rows, 64, 1), pltpu.roll(rows, 32, 1)]
    lane = lane_iota((1, 128))
    return [
        jnp.where(lane < 96, rows[0:1], turned[1][1:2]),
        jnp.where(lane < 64, turned[1][1:2], turned[2][2:3]),
        jnp.where(lane < 32, turned[2][2:3], turned[3][3:4]),
    ]


def matrices_kernel(got_ref, dre_ref, dim_ref, ore_ref, oim_ref, glu_ref, square):
    def total(start, count):
        value = got_ref[0, start : start + count, :].astype(F32)
        for z in range(1, GROUPS // 2):
            value = value + got_ref[z, start : start + count, :].astype(F32)
        return value

    for start, first_ref, second_ref in ((0, dre_ref, dim_ref), (96, ore_ref, oim_ref)):
        square[0:96, :] = total(start, 96)
        square[96:128, :] = jnp.zeros((32, 128), F32)
        turned = square[...].T
        first_ref[...] = turned[0:64, 0:96]
        second_ref[...] = turned[64:128, 0:96]
    glu_ref[...] = total(192, 64)


def finish_kernel(
    count_all, own_ref, other_ref, dn_ref, got_ref, up_ref, xhat_ref, inv_ref, feat_ref,
    gin_ref, gbias_ref, scale_ref, bias_ref, skip_ref, decay_ref, lam_ref, step_ref, rms_ref, vec_ref, tiles,
):
    input_grad(dn_ref, got_ref, up_ref, xhat_ref, inv_ref, feat_ref, gin_ref, tiles)
    own, other = own_ref[...], other_ref[...]
    vec = own + other
    vec_ref[...] = vec
    first, second = jnp.where(lax.axis_index("tc") == 0, own, other), jnp.where(lax.axis_index("tc") == 0, other, own)
    for k, ref in enumerate((scale_ref, bias_ref, skip_ref)):
        for c in range(4):
            ref[:, 128 * c : 128 * c + 128] = vec[4 * k + c : 4 * k + c + 1]
    for k, ref in enumerate((decay_ref, lam_ref, step_ref)):
        at = 16 + 2 * k
        by_pos = [first[at : at + 1], second[at : at + 1], first[at + 1 : at + 2], second[at + 1 : at + 2]]
        for c, chunk in enumerate(rows_to_lanes(jnp.concatenate(by_pos + [jnp.zeros((4, 128), F32)], axis=0))):
            ref[128 * c : 128 * c + 128] = chunk.reshape(128)
    squares = vec[22:23]
    total = [jnp.sum(jnp.where(low_half((1, 128)) == low, squares, 0.0), axis=1, keepdims=True) for low in (True, False)]
    rms_ref[...] = jnp.sqrt(jnp.where(lane_iota((1, 2)) == 0, total[0], total[1]) / count_all)
    place = tensor_pos() * GROUPS + fsdp_pos()
    row = jnp.broadcast_to(vec_ref[pl.ds(12 + place // 8, 1), :], (8, 128))
    gbias_ref[...] = pltpu.roll(row, 128 - 16 * (place % 8), 1)[0:1, 0:16]


TAKES = {
    "pack": 1.5, "standardize": 0.4, "norm": 0.4, "first": 0.6, "states": 0.9, "readout": 0.4, "second": 0.7, "sums": 0.7, "back": 0.8,
    "third": 1.5, "input_grad": 0.5, "matrices": 0.5, "finish": 0.4,
}


def call(kernel, outs, args, scratch=(), specs=None, limit=24):
    name = getattr(kernel, "func", kernel).__name__.removesuffix("_kernel")
    return pl.pallas_call(
        kernel,
        out_shape=outs,
        in_specs=specs or [VM] * len(args),
        out_specs=jax.tree.map(lambda _: VM, outs),
        scratch_shapes=list(scratch),
        compiler_params=pltpu.CompilerParams(vmem_limit_bytes=limit << 20),
        cost_estimate=pl.CostEstimate(flops=0, transcendentals=0, bytes_accessed=int(TAKES.get(name, 0.1) * 3.6e6)),
        name=name,
    )(*args)


def tied(value, other):
    return lax.optimization_barrier((value, other))[0]


def swap(value, axis):
    return lax.ppermute(value, axis, [(0, 1), (1, 0)])


def across(value):
    return lax.ppermute(value, ("fx", "ty"), [(n, 3 - n) for n in range(4)])


def standardized(layer_in, grad_out, starts):
    rows, width = layer_in.shape
    return call(
        standardize_kernel,
        (sds((2 * rows, width)), sds((rows, width)), sds((rows, 128)), sds((2 * rows, 128))),
        (layer_in, swap(layer_in, "tc"), grad_out, starts),
        [pltpu.VMEM((4, 2 * rows, 128), F32), pltpu.VMEM((rows, 128), F32)],
    )


def on_device(
    layer_in, grad_out, ln_scale, ln_bias, decay_rate, lam_im, log_dt, in_re, in_im, out_re, out_im, skip, glu_weight, glu_bias, seq_lengths
):
    rows, width = layer_in.shape
    fsdp = lax.axis_size(FSDP)
    pairs, pair = fsdp * 2, 2 * rows
    count_all = float(rows * pairs * 2 * width)
    fast = fsdp == GROUPS
    same_core = (*FSDP, "ty")
    if fast:
        row = lambda v: v.reshape(1, -1)
        sent, starts = call(
            pack_kernel,
            (sds((GROUPS // 2, 272, 128), BF16), sds((seq_lengths.shape[0], 128))),
            (seq_lengths, in_re.T, in_im.T, out_re.T, out_im.T, glu_weight.T, row(ln_scale), row(ln_bias), row(skip), row(glu_bias),
             row(decay_rate), row(lam_im), row(log_dt)),
            [pltpu.VMEM((128, 128), F32), pltpu.VMEM((4, 64, 96), BF16), pltpu.VMEM((64, 128), BF16), pltpu.VMEM((4, 1, 64), BF16),
             pltpu.VMEM((3, 1, 96), F32), pltpu.SMEM(seq_lengths.shape, jnp.int32), pltpu.SemaphoreType.DMA((13,))],
            [HBM] * 13,
            60,
        )
        mine = lax.all_to_all(sent, "fz", 0, 0, tiled=True)
        own_b, own_cw = lax.optimization_barrier((mine[:, :112], mine[:, 112:]))
        plane_b = [own_b, swap(own_b, "ty"), swap(own_b, "fx"), across(own_b)]
        xhat, up, inverse, count = standardized(layer_in, grad_out, starts)
        plane_b, side_cw, xhat = lax.optimization_barrier((plane_b, swap(own_cw, "ty"), xhat))
        side_cw = jnp.stack([own_cw, side_cw])
        far_cw = swap(side_cw, "fx")
        g = jnp.stack(plane_b).reshape(2, 2, GROUPS // 2, 112, 128)
    else:
        starts = jnp.broadcast_to((jnp.cumsum(seq_lengths) - seq_lengths).astype(F32)[:, None], (seq_lengths.shape[0], 128))
        xhat, up, inverse, count = standardized(layer_in, grad_out, starts)
        g, cw, other_cw = gathered(
            ln_scale, ln_bias, decay_rate, lam_im, log_dt, in_re, in_im, out_re, out_im, skip, glu_weight, glu_bias
        )

    normed, feat = call(norm_kernel, (sds((pair, width), BF16), sds((8, width))), (xhat, g))
    b_all, v, lane, row_prm, carry = call(
        functools.partial(first_kernel, pairs),
        (sds((512, width), BF16), sds((pair, 512)), sds((8, 256)), sds((8, 8, 128)), sds((pairs, 4, 128))),
        (normed, count, g),
        [pltpu.VMEM((8, 128), F32)],
    )
    came = lax.all_to_all(carry, same_core, 0, 0, tiled=True)
    if fast:
        cw = jnp.stack(tied((side_cw, far_cw), came))
    state, twice, enter, c_all = call(
        states_kernel,
        (sds((pair, 512)), sds((pair, 512), BF16), sds((8, 512)), sds((512, width), BF16)),
        (came, starts, count, v, lane, row_prm, cw),
        [pltpu.VMEM((8, 128), F32)],
    )
    if fast:
        other_cw = swap(tied(cw, twice), "tc")
    own, away = call(
        readout_kernel, (sds((rows, width)), sds((rows, width))), (twice, c_all), [pltpu.VMEM((pair, width), F32)]
    )
    branch, d_mixed, dlogit, kept, away = call(
        second_kernel,
        (sds((rows, width), BF16), sds((rows, width)), sds((rows, width), BF16), *[sds((rows, 2 * width + 256), BF16)] * 2),
        (own, swap(away, "tc"), up, normed, feat, cw, other_cw),
        [pltpu.VMEM((width, width), BF16), pltpu.VMEM((rows, width), BF16)],
    )
    got = swap(away, "tc")
    layer_out, part = call(
        sums_kernel,
        (sds((rows, width), BF16), sds((8, width))),
        (layer_in, branch, normed, d_mixed, dlogit),
        [pltpu.VMEM((4, rows, 128), F32), pltpu.VMEM((rows, width), F32)],
    )
    got, part = lax.optimization_barrier((got, part))
    d_state, carry, stay_cw, leave_cw = call(
        functools.partial(back_kernel, pairs),
        (sds((pair, 512)), sds((pairs, 4, 128)), *[sds((2, GROUPS // 2, 160, 128), BF16)] * 2),
        (kept, got, twice, count, lane, c_all),
        [pltpu.VMEM((pair, width), BF16), pltpu.VMEM((width, 256), BF16), pltpu.VMEM((8, 128), F32),
         pltpu.VMEM((2, 2, GROUPS // 2, 160, 128), BF16)],
    )
    if fast:
        far_cw = swap(leave_cw, "fx")
    came = lax.all_to_all(carry, same_core, 0, 0, tiled=True)
    if fast:
        came, far_cw, stay_cw = lax.optimization_barrier((came, far_cw, stay_cw))
        stay_cw, leave_cw = call(middle_kernel, [sds((GROUPS // 2, 160, 128), BF16)] * 2, (stay_cw, far_cw))
        far_cw = swap(leave_cw, "ty")
        came = tied(came, leave_cw)
    stay_b, y_b, x_b, xy_b, d_normed, away = call(
        third_kernel,
        (*[sds((432, 128), BF16)] * 4, sds((rows, width)), sds((rows, width))),
        (came, starts, count, normed, xhat, v, lane, row_prm, feat, state, d_state, enter, d_mixed, part, b_all),
        [pltpu.VMEM((8, 128), F32), pltpu.VMEM((pair, 512), BF16), pltpu.VMEM((pair, width), F32), pltpu.VMEM((24, 128), F32)],
    )
    if not fast:
        grad_in = call(
            input_grad_kernel,
            sds((rows, width)),
            (d_normed, swap(away, "tc"), grad_out, xhat, inverse, feat),
            [pltpu.VMEM((4, rows, 128), F32)],
        )
        return reduced(layer_out, grad_in, stay_cw, leave_cw, (stay_b, y_b, x_b, xy_b), count_all, fsdp, width)
    xy_b = across(xy_b)
    x_b = swap(x_b, "fx")
    y_b = swap(y_b, "ty")
    sent = call(
        plane_add_kernel,
        sds((GROUPS // 2, 304, 128), BF16),
        (stay_cw, far_cw, stay_b, y_b, x_b, xy_b),
    )
    got = lax.all_to_all(sent, "fz", 0, 0, tiled=True)
    away = swap(tied(away, got), "tc")
    vec = call(vectors_kernel, sds((24, 128)), (got,))
    other = swap(vec, "tc")
    d_re, d_im, d_ore, d_oim, d_glu = call(
        matrices_kernel, (*[sds((64, 96))] * 4, sds((64, 128))), (got,), [pltpu.VMEM((128, 128), F32)]
    )
    grad_in, d_gbias, d_scale, d_bias, d_skip, g_decay, g_lam, g_step, rms = call(
        functools.partial(finish_kernel, count_all),
        (sds((rows, width)), sds((1, 16)), *[sds((1, 512))] * 3, *[sds((384,))] * 3, sds((1, 2))),
        (vec, other, d_normed, away, grad_out, xhat, inverse, feat),
        [pltpu.VMEM((24, 128), F32), pltpu.VMEM((4, rows, 128), F32)],
    )
    flat = lambda value: value.reshape(-1)
    return (
        layer_out, grad_in, flat(d_scale), flat(d_bias), g_decay, g_lam, g_step, d_re.T, d_im.T, d_ore.T, d_oim.T,
        flat(d_skip), d_glu.T, flat(d_gbias), flat(rms),
    )


def gathered(ln_scale, ln_bias, decay_rate, lam_im, log_dt, in_re, in_im, out_re, out_im, skip, glu_weight, glu_bias):
    tens = tensor_pos()
    full = lambda value, axis: lax.all_gather(value, FSDP, axis=axis, tiled=True)

    def pair(first, second):
        halves = jnp.stack([first.reshape(-1, GROUPS, 64), second.reshape(-1, GROUPS, 64)], axis=2)
        return halves.reshape(-1, GROUPS, 128).swapaxes(0, 1)

    gate = lax.dynamic_slice_in_dim(full(glu_weight, 1), tens * 128, 128, 0).T.reshape(GROUPS, 64, 128)
    vectors = [pair(full(ln_scale, 0)[None], full(ln_bias, 0)[None]), pair(full(skip, 0)[None], full(glu_bias, 0)[None])]
    for value in (decay_rate, lam_im, log_dt):
        value = jnp.pad(value, (0, 32))
        for _ in range(3):
            piece = lax.reduce_precision(value, 8, 7)
            value = value - piece
            vectors.append(jnp.broadcast_to(piece.astype(BF16)[None, None], (GROUPS, 1, 128)))
    vectors.append(jnp.zeros((GROUPS, 5, 128), BF16))
    packet = jnp.concatenate(
        [pair(full(in_re, 1), full(in_im, 1)), *vectors, pair(full(out_re, 1), full(out_im, 1)), gate],
        axis=1,
    )
    everyone = lax.all_gather(packet, TENSOR, axis=0).reshape(2, 2, GROUPS // 2, 2, 272, 128)
    x, y, core = (lax.axis_index(axis) for axis in ("fx", "ty", "tc"))
    own_x = lambda value, axis: jnp.stack([lax.dynamic_index_in_dim(value, x ^ j, axis, keepdims=False) for j in range(2)])
    for i in range(2):
        both = lax.dynamic_index_in_dim(everyone, core ^ i, 1, keepdims=False)
        slots = [own_x(lax.dynamic_index_in_dim(both, y ^ m, 0, keepdims=False), 1) for m in range(2)]
        slots = jnp.stack(slots, axis=1)
        if i == 0:
            g, cw = slots[:, :, :, :112], slots[:, :, :, 112:]
    return g, cw, slots[:, :, :, 112:]


def reduced(layer_out, grad_in, stay_cw, leave_cw, plane_b, count_all, fsdp, width):
    tens = tensor_pos()
    x = lax.axis_index("fx")

    def canonical(slots):
        out = jnp.zeros((4, GROUPS, *slots[0].shape[2:]), F32)
        for m, slot in enumerate(slots):
            parts = [lax.dynamic_index_in_dim(slot.astype(F32), x ^ n, 1) for n in range(2)]
            block = jnp.concatenate(parts, axis=1).reshape(1, GROUPS, *slot.shape[2:])
            out = lax.dynamic_update_slice_in_dim(out, block, slot_pos(m, 0), 0)
        return out

    def natural(slots):
        halves = canonical(slots).reshape(4, GROUPS, -1, 2, 64).transpose(3, 0, 2, 1, 4)
        return halves[0].reshape(-1, width), halves[1].reshape(-1, width)

    def scattered(value):
        value = lax.psum_scatter(value, TENSOR, scatter_dimension=0, tiled=True)
        return lax.psum_scatter(value, FSDP, scatter_dimension=1, tiled=True)

    blocks = [value[:384].reshape(GROUPS // 2, 96, 128) for value in plane_b]
    d_re, d_im = natural([jnp.stack([blocks[m], blocks[2 + m]], axis=1) for m in range(2)])
    cw = jnp.stack([stay_cw, leave_cw]).transpose(1, 2, 0, 3, 4)
    d_ore, d_oim = natural([value[:, :, :96] for value in cw])
    d_glu = canonical([value[:, :, 96:] for value in cw]).reshape(4, width, 128).swapaxes(1, 2).reshape(-1, width)
    vec = unpacked(plane_b[0][384:432])
    by_pos = lax.dynamic_update_slice_in_dim(
        jnp.zeros((3, 2, 2, 96), F32), vec[16:22, :96].reshape(3, 2, 1, 96), lax.axis_index("tc"), 2
    )
    vec, by_pos = lax.psum((vec, by_pos), AXES)
    states = lambda k: by_pos[k].reshape(-1)
    own = width // (4 * fsdp)
    place = tens * fsdp + fsdp_pos()
    d_gbias = lax.dynamic_slice_in_dim(vec[12:16].reshape(-1), place * own, own, 0)
    rms = jnp.sqrt(jnp.sum(vec[22].reshape(2, 64), axis=1) / count_all)
    return (
        layer_out, grad_in, vec[0:4].reshape(-1), vec[4:8].reshape(-1), states(0), states(1), states(2), scattered(d_re), scattered(d_im),
        scattered(d_ore), scattered(d_oim), vec[8:12].reshape(-1), scattered(d_glu), d_gbias, rms,
    )


def solution(mesh):
    shape = (mesh.shape["fsdp"] // 2, 2, mesh.shape["tensor"] // 2, 2)
    split = Mesh(mesh.devices.reshape(shape), AXES)
    tokens, matrix = P(AXES, None), P(TENSOR, FSDP)
    return jax.shard_map(
        on_device,
        mesh=split,
        in_specs=(
            tokens, tokens, P(FSDP), P(FSDP), P(TENSOR), P(TENSOR), P(TENSOR), matrix, matrix, matrix, matrix,
            P(FSDP), P(None, FSDP), P(FSDP), P(),
        ),
        out_specs=(
            tokens, tokens, P(), P(), P(), P(), P(), matrix, matrix, matrix, matrix, P(), matrix, P((*TENSOR, *FSDP)), P(),
        ),
        check_vma=False,
    )
```

```python
import functools

import jax
import jax.numpy as jnp
from jax import lax
from jax.experimental import pallas as pl
from jax.experimental.pallas import tpu as pltpu
from jax.sharding import Mesh
from jax.sharding import PartitionSpec as P

F32 = jnp.float32
BF16 = jnp.bfloat16
FSDP = ("fz", "fx")
TENSOR = ("ty", "tc")
AXES = (*FSDP, *TENSOR)
HBM = pl.BlockSpec(memory_space=pltpu.HBM)
VM = pl.BlockSpec(memory_space=pltpu.VMEM)
SM = pl.BlockSpec(memory_space=pltpu.SMEM)

GROUPS = 8
VEC = 96


def sds(shape, dtype=F32):
    return jax.ShapeDtypeStruct(shape, dtype)


def low_half(shape):
    return lax.broadcasted_iota(jnp.int32, shape, len(shape) - 1) < 64


def lane_iota(shape):
    return lax.broadcasted_iota(jnp.int32, shape, len(shape) - 1)


def dot(a, b, dims):
    return lax.dot_general(a, b, (dims, ((), ())), preferred_element_type=F32)


NT = ((1,), (1,))
NN = ((1,), (0,))
TN = ((0,), (0,))


def flipped():
    return lax.axis_index("fx") == 1


def part_lanes(part, m):
    return slice(256 * part + 128 * m, 256 * part + 128 * m + 128)


def slot_pos(m, core):
    return (lax.axis_index("ty") ^ m) * 2 + (lax.axis_index("tc") ^ core)


def own_rows(rows):
    return pl.ds(pl.multiple_of(lax.axis_index("tc") * rows, rows), rows)


def other_rows(rows):
    return pl.ds(pl.multiple_of((1 - lax.axis_index("tc")) * rows, rows), rows)


def piece(ref, m, f, start, count):
    return ref[f % 2, m, f // 2, start : start + count, :]


def natural(get, ref):
    lo = low_half((96, 128))
    for m in range(2):
        for part in range(2):
            lanes = part_lanes(part, m)
            ref[lanes.start + 96 : lanes.stop, :] = jnp.zeros((32, 512), BF16)
        for z in range(GROUPS // 2):
            even, odd = get(m, z, 0).astype(F32), get(m, z, 1).astype(F32)
            here = slice(128 * z, 128 * z + 128)
            ref[128 * m : 128 * m + 96, here] = jnp.where(lo, even, pltpu.roll(odd, 64, 1)).astype(BF16)
            ref[256 + 128 * m : 256 + 128 * m + 96, here] = jnp.where(lo, pltpu.roll(even, 64, 1), odd).astype(BF16)


def packets(value, m, z):
    lo = low_half((96, 128))
    here = slice(128 * z, 128 * z + 128)
    re, im = value[128 * m : 128 * m + 96, here], value[256 + 128 * m : 256 + 128 * m + 96, here]
    return jnp.where(lo, re, pltpu.roll(im, 64, 1)), jnp.where(lo, pltpu.roll(re, 64, 1), im)


def feature_rows(ref, row):
    lo = low_half((8, 128))
    flip = flipped()
    first, second = [], []
    for c in range(GROUPS // 2):
        a = jnp.broadcast_to(piece(ref, 0, 2 * c, row, 1).astype(F32), (8, 128))
        b = jnp.broadcast_to(piece(ref, 0, 2 * c + 1, row, 1).astype(F32), (8, 128))
        a, b = jnp.where(flip, b, a), jnp.where(flip, a, b)
        first.append(jnp.where(lo, a, pltpu.roll(b, 64, 1)))
        second.append(jnp.where(lo, pltpu.roll(a, 64, 1), b))
    return jnp.concatenate(first, axis=1)[:1], jnp.concatenate(second, axis=1)[:1]


def cmul(a, b):
    return a[0] * b[0] - a[1] * b[1], a[0] * b[1] + a[1] * b[0]


def tensor_pos():
    return lax.axis_index("ty") * 2 + lax.axis_index("tc")


def fsdp_pos():
    return lax.axis_index("fz") * 2 + lax.axis_index("fx")


def pair_pos():
    return fsdp_pos() * 2 + lax.axis_index("ty")


def offsets_of(start_ref):
    return [start_ref[n : n + 1, :] for n in range(start_ref.shape[0])]


STEPS = 16


def in_tiles(ref, rows, value):
    for c in range(4):
        ref[c, rows, :] = value[:, 128 * c : 128 * c + 128]


def of_tiles(ref, rows):
    return jnp.concatenate([ref[c, rows, :] for c in range(4)], axis=1)


def interleaved(ref, b):
    groups = [of_tiles(ref, pl.ds((n // STEPS) * 128 + n % STEPS, 8, stride=STEPS)) for n in (b, b + 1)]
    return jnp.concatenate(groups, axis=0)


def in_order(source, target):
    for g in range(target.shape[0] // 8):
        h, s, i = g // STEPS, g % STEPS // 2, 8 * (g % 2)
        target[8 * g : 8 * g + 8, :] = of_tiles(source, pl.ds(128 * h + 8 * i + s, 8, stride=8))


def starts_until(offsets, base, rows):
    row = lax.broadcasted_iota(jnp.int32, (rows, 128), 0)
    token = (row & ~127) + (row & 7) * STEPS + ((row & 127) >> 3)
    at = (token + base).astype(F32)
    count = jnp.zeros((rows, 128), F32)
    for off in offsets:
        count = count + jnp.where((at >= off) & (off >= at[0:1]), 1.0, 0.0)
    return count


def no_start(offsets, base, rows):
    link = jnp.ones((1, 128), F32)
    first = (jnp.zeros((1, 128), jnp.int32) + base).astype(F32)
    for off in offsets:
        link = jnp.where((off >= first) & (off < first + rows), 0.0, link)
    return link


def expm1(x):
    series = x * (1 + x / 2 * (1 + x / 3 * (1 + x / 4 * (1 + x / 5 * (1 + x / 6 * (1 + x / 7))))))
    return jnp.where(jnp.abs(x) < 0.25, series, jnp.exp(x) - 1.0)


def discretize(decay_rate, lam_im, log_dt):
    step_size = jnp.exp(log_dt)
    lam_re = -decay_rate
    magnitude = jnp.exp(lam_re * step_size)
    phase = lam_im * step_size
    abar_re = magnitude * jnp.cos(phase)
    abar_im = magnitude * jnp.sin(phase)
    half_sin = jnp.sin(0.5 * phase)
    less_re = expm1(lam_re * step_size) * jnp.cos(phase) - 2.0 * half_sin * half_sin
    denom = lam_re * lam_re + lam_im * lam_im
    coef_re = (less_re * lam_re + abar_im * lam_im) / denom
    coef_im = (abar_im * lam_re - less_re * lam_im) / denom
    return abar_re, abar_im, coef_re, coef_im, step_size


def pack_kernel(*refs):
    *inputs, out_ref, start_ref, square, four, glu_ref, halves, params, lengths, sems = refs
    seq_hbm, matrices, glu_hbm, features, states = inputs[0], inputs[1:5], inputs[5], inputs[6:10], inputs[10:13]
    units = pl.multiple_of(tensor_pos() * 128, 128)
    pairs = [(ref, four.at[k]) for k, ref in enumerate(matrices)]
    pairs += [(glu_hbm.at[:, pl.ds(units, 128)], glu_ref), (seq_hbm, lengths)]
    pairs += [(ref, halves.at[k]) for k, ref in enumerate(features)]
    pairs += [(ref, params.at[k]) for k, ref in enumerate(states)]
    copies = [pltpu.make_async_copy(source, target, sems.at[k]) for k, (source, target) in enumerate(pairs)]
    for copy in copies:
        copy.start()
    square[:, 96:128] = jnp.zeros((128, 32), F32)
    for copy in copies:
        copy.wait()
    vec = [
        jnp.concatenate([halves[0], halves[1]], axis=1).astype(F32),
        jnp.concatenate([halves[2], halves[3]], axis=1).astype(F32),
    ]
    for k in range(3):
        value = jnp.concatenate([params[k], jnp.zeros((1, 32), F32)], axis=1)
        for _ in range(3):
            part = value.astype(BF16).astype(F32)
            value = value - part
            vec.append(part)
    total = 0
    for n in range(lengths.shape[0]):
        start_ref[n : n + 1, :] = jnp.full((1, 128), total, jnp.int32).astype(F32)
        total = total + lengths[n]
    vec.append(jnp.zeros((16 - len(vec), 128), F32))
    vec = jnp.concatenate(vec, axis=0).astype(BF16)
    pieces = []
    for k in (0, 2):
        square[0:64, 0:96] = four[k].astype(F32)
        square[64:128, 0:96] = four[k + 1].astype(F32)
        pieces.append(square[...].T[0:96].astype(BF16))
    packet = jnp.concatenate([pieces[0], vec, pieces[1], glu_ref[...]], axis=0)
    for z in range(GROUPS // 2):
        out_ref[z] = packet


def params_of(ref, vec_row):
    lane = lane_iota((8, 128))
    out = []
    for k, safe in enumerate((1.0, 0.0, 0.0)):
        rows = []
        for m in range(2):
            part = piece(ref, m, 0, vec_row, 16).astype(F32)
            rows.append((part[2 + 3 * k : 3 + 3 * k] + part[3 + 3 * k : 4 + 3 * k]) + part[4 + 3 * k : 5 + 3 * k])
        value = jnp.concatenate(rows + [jnp.full((6, 128), safe, F32)], axis=0)
        out.append(jnp.where(lane < 96, value, safe))
    return out


def carry_block(re_rows, im_rows, scratch):
    for m in range(2):
        y = lax.axis_index("ty") ^ m
        scratch[pl.ds(y, 1), :] = re_rows[m]
        scratch[pl.ds(2 + y, 1), :] = im_rows[m]


def standardize_kernel(x_ref, other_ref, up_ref, start_ref, xhat_ref, up_out_ref, inv_ref, count_ref, tiles, inverses):
    rows, width = x_ref.shape
    in_tiles(tiles, slice(0, rows), up_ref[...].astype(F32))
    for b in range(0, rows // 8, 2):
        up_out_ref[8 * b : 8 * b + 16, :] = interleaved(tiles, b)
    for ref, where, own in ((x_ref, own_rows(rows), True), (other_ref, other_rows(rows), False)):
        x = ref[...].astype(F32)
        centered = x - jnp.sum(x, axis=1, keepdims=True) / width
        inverse = lax.rsqrt(jnp.sum(centered * centered, axis=1, keepdims=True) / width + 1e-05)
        in_tiles(tiles, where, centered * inverse)
        if own:
            inverses[...] = jnp.broadcast_to(inverse, (rows, 128))
    for b in range(0, 2 * rows // 8, 2):
        xhat_ref[8 * b : 8 * b + 16, :] = interleaved(tiles, b)
    for b in range(rows // 8):
        inv_ref[8 * b : 8 * b + 8, :] = inverses[pl.ds(b, 8, stride=STEPS), :]
    count_ref[...] = starts_until(offsets_of(start_ref), pair_pos() * 2 * rows, 2 * rows)


def norm_kernel(xhat_ref, g_ref, normed_ref, feat_ref):
    scale, bias = feature_rows(g_ref, VEC)
    feat_ref[0:1] = scale
    feat_ref[1:2], feat_ref[2:3] = feature_rows(g_ref, VEC + 1)
    normed_ref[...] = (xhat_ref[...] * scale + bias).astype(BF16)


def first_kernel(pairs, normed_ref, count_ref, g_ref, b_ref, v_ref, lane_ref, row_ref, send_ref, scratch):
    rows = normed_ref.shape[0]
    natural(lambda m, z, x: g_ref[lax.axis_index("fx") ^ x, m, z, 0:96, :], b_ref)
    v_ref[...] = dot(normed_ref[...], b_ref[...], NT)

    decay, lam, log_dt = params_of(g_ref, VEC)
    abar_re, abar_im, coef_re, coef_im, step_size = discretize(decay, lam, log_dt)
    power = (abar_re, abar_im)
    for _ in range(8):
        power = cmul(power, power)
    scratch[...] = jnp.zeros((8, 128), F32)
    carry_block([power[0][m : m + 1] for m in range(2)], [power[1][m : m + 1] for m in range(2)], scratch)
    for k, value in enumerate((decay, lam, step_size, abar_re, abar_im, coef_re, coef_im, scratch[...])):
        row_ref[k] = value
    for k, value in enumerate((abar_re, abar_im, coef_re, coef_im)):
        for m in range(2):
            lane_ref[k : k + 1, 128 * m : 128 * m + 128] = value[m : m + 1]

    count = count_ref[...]
    open_tail = jnp.where(count == count[rows - 1 : rows], 1.0, 0.0)
    last = ([], [])
    for m in range(2):
        a = (all_rows(abar_re[m : m + 1]), all_rows(abar_im[m : m + 1]))
        b = (coef_re[m : m + 1], coef_im[m : m + 1])
        sixteen = squared(a, 4)
        tile = tile_powers(sixteen, lambda sub: 7 - sub)
        halves = []
        for h in range(2):
            acc = (jnp.zeros((8, 128), F32), jnp.zeros((8, 128), F32))
            for blk in range(STEPS * h, STEPS * h + STEPS):
                here = slice(8 * blk, 8 * blk + 8)
                drive = cmul(b, (v_ref[here, part_lanes(0, m)], v_ref[here, part_lanes(1, m)]))
                moved = cmul(a, acc)
                acc = (moved[0] + drive[0] * open_tail[here], moved[1] + drive[1] * open_tail[here])
            total = cmul(tile, acc)
            halves.append((column_sum(total[0]), column_sum(total[1])))
        moved = cmul(squared((sixteen[0][:1], sixteen[1][:1]), 3), halves[0])
        last[0].append(moved[0] + halves[1][0])
        last[1].append(moved[1] + halves[1][1])
    carry_block(last[0], last[1], scratch)
    packet = scratch[...]
    for d in range(pairs):
        send_ref[d] = packet[0:4]


def squared(a, times):
    for _ in range(times):
        a = cmul(a, a)
    return a


def tile_powers(a, exponent_of):
    exponent = exponent_of(lax.broadcasted_iota(jnp.int32, (8, 128), 0))
    tile = (jnp.ones((8, 128), F32), jnp.zeros((8, 128), F32))
    for bit in range(4):
        taken = (exponent & (1 << bit)) != 0
        more = cmul(tile, a)
        tile = (jnp.where(taken, more[0], tile[0]), jnp.where(taken, more[1], tile[1]))
        a = cmul(a, a)
    return tile


def all_rows(row):
    return jnp.broadcast_to(row, (8, 128))


def plus(value, link, more):
    return value[0] + jnp.where(link, more[0], 0.0), value[1] + jnp.where(link, more[1], 0.0)


def scan(read, powers, carry, count, reverse, emit):
    sub = lax.broadcasted_iota(jnp.int32, (8, 128), 0)
    order = range(STEPS - 1, -1, -1) if reverse else range(STEPS)
    end = 0 if reverse else 7
    back = lambda k: 8 - k if reverse else k
    carry = [(all_rows(c[0]), all_rows(c[1])) for c in carry]
    entries, ends, upto = [], [], []
    for a in powers:
        a = (all_rows(a[0]), all_rows(a[1]))
        power = [a]
        for _ in range(STEPS - 1):
            power.append(cmul(power[-1], a))
        upto.append(power)
        ends.append((power[-1], squared(power[-1], 1), squared(power[-1], 2)))
        entries.append(tile_powers(power[-1], (lambda sub: 8 - sub) if reverse else (lambda sub: sub + 1)))
    seen = jnp.zeros((8, 128), F32)
    for h in (1, 0) if reverse else (0, 1):
        counts = [count[8 * b : 8 * b + 8] for b in range(STEPS * h, STEPS * h + STEPS)]
        last = counts[order[-1]]
        near = jnp.where(sub == 7 - end, seen, pltpu.roll(last, back(1), 0))
        for m in range(2):
            values, before = {}, None
            for i in order:
                value = read(STEPS * h + i, m)
                if before is not None:
                    value = plus(value, counts[i] == counts[before], cmul(upto[m][0], values[before]))
                values[i], before = value, i
            tip = values[before]
            for k, power in zip((1, 2, 4), ends[m]):
                link = ((sub < 8 - k) if reverse else (sub >= k)) & (pltpu.roll(last, back(k), 0) == last)
                tip = plus(tip, link, cmul(power, (pltpu.roll(tip[0], back(k), 0), pltpu.roll(tip[1], back(k), 0))))
            tip = plus(tip, last == seen, cmul(entries[m], carry[m]))
            comes = tuple(jnp.where(sub == 7 - end, carry[m][p], pltpu.roll(tip[p], back(1), 0)) for p in range(2))
            for n, i in enumerate(order):
                emit(STEPS * h + i, m, plus(values[i], counts[i] == near, cmul(upto[m][n], comes)))
            carry[m] = (all_rows(tip[0][end : end + 1]), all_rows(tip[1][end : end + 1]))
        seen = all_rows(last[end : end + 1])


def carried(recv_ref, row_ref, offsets, rows, reverse, scratch):
    pairs = recv_ref.shape[0]
    power = row_ref[7]
    pre, pim = power[0:2], power[2:4]
    if reverse:
        pim = -pim
    place = pair_pos()

    zero = jnp.zeros((2, 128), F32)
    if pairs <= 32:
        first = lax.broadcasted_iota(jnp.int32, (pairs, 128), 0).astype(F32) * rows
        links = jnp.ones((pairs, 128), F32)
        for off in offsets:
            links = jnp.where((off >= first) & (off < first + rows), 0.0, links)
        out = (zero, zero)
        for j in range(pairs - 1, 0, -1) if reverse else range(pairs - 1):
            link = links[j : j + 1]
            got = recv_ref[j]
            new = cmul((pre * link, pim * link), out)
            reached = (j > place) if reverse else (j < place)
            out = (jnp.where(reached, new[0] + got[0:2], out[0]), jnp.where(reached, new[1] + got[2:4], out[1]))
    else:

        def turn(k, state):
            j = pairs - 1 - k if reverse else k
            link = no_start(offsets, j * rows, rows)
            got = recv_ref[j]
            new = cmul((pre * link, pim * link), state)
            return new[0] + got[0:2], new[1] + got[2:4]

        out = lax.fori_loop(0, pairs - 1 - place if reverse else place, turn, (zero, zero))
    scratch[0:2, :] = out[0]
    scratch[2:4, :] = out[1]
    own = [lax.axis_index("ty") ^ m for m in range(2)]
    return [scratch[pl.ds(y, 1), :] for y in own], [scratch[pl.ds(2 + y, 1), :] for y in own]


def column_sum(value):
    return jnp.sum(value, axis=0, keepdims=True)


def states_kernel(
    recv_ref, start_ref, count_ref, v_ref, lane_ref, row_ref, cw_ref, state_ref, twice_ref, enter_ref, c_ref, scratch
):
    rows = v_ref.shape[0]
    count = count_ref[...]
    enter = carried(recv_ref, row_ref, offsets_of(start_ref), rows, False, scratch)
    for part in range(2):
        for m in range(2):
            enter_ref[0:1, part_lanes(part, m)] = enter[part][m]
    powers = [(lane_ref[0:1, 128 * m : 128 * m + 128], lane_ref[1:2, 128 * m : 128 * m + 128]) for m in range(2)]

    def read(b, m):
        here, lanes = slice(8 * b, 8 * b + 8), slice(128 * m, 128 * m + 128)
        return cmul((lane_ref[2:3, lanes], lane_ref[3:4, lanes]), (v_ref[here, part_lanes(0, m)], v_ref[here, part_lanes(1, m)]))

    def emit(b, m, value):
        for part in range(2):
            state_ref[8 * b : 8 * b + 8, part_lanes(part, m)] = value[part]

    scan(read, powers, [(enter[0][m], enter[1][m]) for m in range(2)], count, False, emit)
    twice_ref[:, 0:256] = state_ref[:, 0:256].astype(BF16) * 2
    twice_ref[:, 256:512] = state_ref[:, 256:512].astype(BF16) * -2
    natural(lambda m, z, x: cw_ref[lax.axis_index("fx") ^ x, m, z, 0:96, :], c_ref)


def readout_kernel(core, twice_ref, c_ref, out_ref):
    where = (own_rows, other_rows)[core](out_ref.shape[0])
    out_ref[...] = dot(twice_ref[where, :], c_ref[...], NN)


def second_kernel(
    own_ref, got_ref, up_ref, normed_ref, feat_ref, cw_ref, othercw_ref,
    branch_ref, dmixed_ref, dlogit_ref, mine_ref, away_ref, gate_ref, all_ref,
):
    rows, width = up_ref.shape
    for core, ref in enumerate((cw_ref, othercw_ref)):
        for m in range(2):
            lanes = pl.ds(pl.multiple_of(slot_pos(m, core) * 128, 128), 128)
            for f in range(GROUPS):
                place = (f // 2) * 2 + (lax.axis_index("fx") ^ (f % 2))
                gate_ref[pl.ds(pl.multiple_of(place * 64, 64), 64), lanes] = piece(ref, m, f, 96 * (1 - core), 64)
    skip, gate_bias = feat_ref[1:2], feat_ref[2:3]
    normed = normed_ref[own_rows(rows), :].astype(F32)
    mixed = (own_ref[...] + got_ref[...]) + skip * normed
    cdf = 0.5 * (1.0 + lax.erf(mixed * 0.7071067811865476))
    act_low = (mixed * cdf).astype(BF16)
    act = act_low.astype(F32)
    w_gate = gate_ref[...]
    logit = dot(act_low, w_gate, NN) + gate_bias
    gate = 1.0 / (1.0 + jnp.exp(-logit))
    branch_ref[...] = (act * gate).astype(BF16)
    up = up_ref[...]
    dlogit = (up * act * gate * (1.0 - gate)).astype(BF16)
    dlogit_ref[...] = dlogit
    all_ref[...] = dlogit
    d_act = dot(dlogit, w_gate, NT) + up * gate
    slope = cdf + mixed * jnp.exp(-0.5 * mixed * mixed) * 0.3989422804014327
    d_mixed = d_act * slope
    dmixed_ref[...] = d_mixed
    for core, ref in enumerate((mine_ref, away_ref)):
        ref[:, 0:width] = d_mixed.astype(BF16)
        ref[:, width : 2 * width] = act_low
        for m in range(2):
            lanes = pl.ds(pl.multiple_of(slot_pos(m, core) * 128, 128), 128)
            ref[:, 2 * width + 128 * m : 2 * width + 128 * m + 128] = all_ref[:, lanes]


def sums_kernel(x_ref, branch_ref, normed_ref, dmixed_ref, dlogit_ref, out_ref, part_ref, tiles, ordered):
    x = x_ref[...].astype(F32)
    branch = branch_ref[...].astype(F32)
    in_tiles(tiles, slice(None), branch)
    in_order(tiles, ordered)
    out_ref[...] = (x + ordered[...]).astype(BF16)
    skip = column_sum(dmixed_ref[...] * normed_ref[own_rows(x_ref.shape[0]), :].astype(F32))
    for k, value in enumerate((skip, column_sum(dlogit_ref[...].astype(F32)), column_sum(x * x), column_sum(branch * branch))):
        part_ref[k : k + 1, :] = value


def back_kernel(
    pairs, mine_ref, got_ref, twice_ref, count_ref, lane_ref, c_ref,
    dstate_ref, send_ref, stay_ref, leave_ref, dy_ref, dgate_ref, scratch, all_ref,
):
    rows, width = dy_ref.shape
    half = rows // 2
    dy_ref[own_rows(half), :] = mine_ref[:, 0:width]
    dy_ref[other_rows(half), :] = got_ref[:, 0:width]
    d_state = dot(dy_ref[...], c_ref[...], NT)
    dstate_ref[:, 0:256] = d_state[:, 0:256] * 2.0
    dstate_ref[:, 256:512] = d_state[:, 256:512] * -2.0
    count = count_ref[...]
    head = jnp.where(count == 0.0, 1.0, 0.0)
    first = ([], [])
    for m in range(2):
        lanes = slice(128 * m, 128 * m + 128)
        a = (all_rows(lane_ref[0:1, lanes]), all_rows(-lane_ref[1:2, lanes]))
        sixteen = squared(a, 4)
        tile = tile_powers(sixteen, lambda sub: sub)
        halves = []
        for h in range(2):
            acc = (jnp.zeros((8, 128), F32), jnp.zeros((8, 128), F32))
            for blk in range(STEPS * h + STEPS - 1, STEPS * h - 1, -1):
                here = slice(8 * blk, 8 * blk + 8)
                moved = cmul(a, acc)
                acc = (
                    moved[0] + dstate_ref[here, part_lanes(0, m)] * head[here],
                    moved[1] + dstate_ref[here, part_lanes(1, m)] * head[here],
                )
            total = cmul(tile, acc)
            halves.append((column_sum(total[0]), column_sum(total[1])))
        moved = cmul(squared((sixteen[0][:1], sixteen[1][:1]), 3), halves[1])
        total = cmul((a[0][:1], a[1][:1]), (moved[0] + halves[0][0], moved[1] + halves[0][1]))
        first[0].append(total[0])
        first[1].append(total[1])
    scratch[...] = jnp.zeros((8, 128), F32)
    carry_block(first[0], first[1], scratch)
    packet = scratch[...]
    for d in range(pairs):
        send_ref[d] = packet[0:4]
    d_c = dot(twice_ref[...], dy_ref[...], TN)
    act = slice(width, 2 * width)
    units = slice(2 * width, 2 * width + 256)
    d_gate = dot(mine_ref[:, act], mine_ref[:, units], TN) + dot(got_ref[:, act], got_ref[:, units], TN)
    dgate_ref[...] = d_gate.astype(BF16)
    for m in range(2):
        for z in range(GROUPS // 2):
            for x, packet in enumerate(packets(d_c, m, z)):
                j = lax.axis_index("fx") ^ x
                all_ref[j, m, z, 0:96, :] = packet.astype(BF16)
                all_ref[j, m, z, 96:160, :] = dgate_ref[128 * z + 64 * x : 128 * z + 64 * x + 64, 128 * m : 128 * m + 128]
    stay_ref[...] = all_ref[0]
    leave_ref[...] = all_ref[1]


def packed(vec):
    upper = vec.astype(BF16).astype(F32)
    return jnp.concatenate([upper, vec - upper], axis=0).astype(BF16)


def unpacked(packet):
    value = packet.astype(F32)
    return value[0:24] + value[24:48]


def third_kernel(
    recv_ref, start_ref, count_ref, normed_ref, xhat_ref, v_ref, lane_ref, row_ref, feat_ref, state_ref, dstate_ref, enter_ref, dmixed_ref,
    part_ref, b_ref, stay_ref, y_ref, x_ref, xy_ref, dn_ref, dnaway_ref, scratch, dv_ref, all_ref, vec_ref,
):
    rows, width = normed_ref.shape
    half = rows // 2
    count = count_ref[...]
    later = carried(recv_ref, row_ref, offsets_of(start_ref), rows, True, scratch)
    sub = lax.broadcasted_iota(jnp.int32, (8, 128), 0)
    none = jnp.zeros((1, 128), F32)
    totals = [[jnp.zeros((8, 128), F32) for _ in range(4)] for _ in range(2)]
    powers = [(lane_ref[0:1, 128 * m : 128 * m + 128], -lane_ref[1:2, 128 * m : 128 * m + 128]) for m in range(2)]

    def read(b, m):
        value = [dstate_ref[8 * b : 8 * b + 8, part_lanes(part, m)] for part in range(2)]
        if b == rows // 8 - 1:
            value = [value[part] + jnp.where(sub == 7, later[part][m], 0.0) for part in range(2)]
        return tuple(value)

    def emit(b, m, adj):
        here, lanes = slice(8 * b, 8 * b + 8), slice(128 * m, 128 * m + 128)
        h, i = b // STEPS, b % STEPS
        if i:
            same = count[here] == count[8 * b - 8 : 8 * b]
            moved = [state_ref[8 * b - 8 : 8 * b, part_lanes(part, m)] for part in range(2)]
        else:
            end = slice(8 * (b + STEPS - 1), 8 * (b + STEPS))
            same = count[here] == jnp.where(sub == 0, count[127:128] if h else none, pltpu.roll(count[end], 1, 0))
            moved = []
            for part in range(2):
                edge = state_ref[127:128, part_lanes(part, m)] if h else enter_ref[0:1, part_lanes(part, m)]
                moved.append(jnp.where(sub == 0, edge, pltpu.roll(state_ref[end, part_lanes(part, m)], 1, 0)))
        prev = [jnp.where(same, part, 0.0) for part in moved]
        v = (v_ref[here, part_lanes(0, m)], v_ref[here, part_lanes(1, m)])
        for k, (p, q) in enumerate((prev, v)):
            totals[m][2 * k] = totals[m][2 * k] + (adj[0] * p + adj[1] * q)
            totals[m][2 * k + 1] = totals[m][2 * k + 1] + (adj[1] * p - adj[0] * q)
        dv = cmul((lane_ref[2:3, lanes], -lane_ref[3:4, lanes]), adj)
        for part in range(2):
            dvf_ref[here, part_lanes(part, m)] = dv[part]

    dvf_ref = all_ref
    scan(read, powers, [(none, none), (none, none)], count, True, emit)
    sums = [[column_sum(totals[m][k]) for m in range(2)] for k in range(4)]
    dv_ref[...] = dvf_ref[...].astype(BF16)
    dv = dv_ref[...]
    d_b = dot(dv, normed_ref[...], TN)
    flip = flipped()
    for m, (near, side) in enumerate(((stay_ref, x_ref), (y_ref, xy_ref))):
        for z in range(GROUPS // 2):
            even, odd = packets(d_b, m, z)
            here = slice(96 * z, 96 * z + 96)
            near[here, :] = jnp.where(flip, odd, even).astype(BF16)
            side[here, :] = jnp.where(flip, even, odd).astype(BF16)
    all_ref[...] = dot(dv, b_ref[...], NN)
    away = all_ref[other_rows(half), :]
    dnaway_ref[...] = away
    own = all_ref[own_rows(half), :] + dmixed_ref[...] * feat_ref[1:2]
    dn_ref[...] = own
    to_scale = column_sum(own * xhat_ref[own_rows(half), :]) + column_sum(away * xhat_ref[other_rows(half), :])
    vector = [to_scale, column_sum(own) + column_sum(away), part_ref[0:1, :], part_ref[1:2, :]]
    for k, value in enumerate(vector):
        for c in range(4):
            vec_ref[4 * k + c : 4 * k + c + 1, :] = value[:, 128 * c : 128 * c + 128]
    g = [jnp.concatenate(pair + [jnp.zeros((6, 128), F32)], axis=0) for pair in sums]
    decay, lam, step, abar_re, abar_im, coef_re, coef_im = (row_ref[k] for k in range(7))
    d_abar, d_coef = (g[0], g[1]), (g[2], g[3])
    denom = decay * decay + lam * lam
    numer = (step * abar_re - coef_re, step * abar_im - coef_im)
    ratio = cmul(numer, (-decay / denom, -lam / denom))
    to_lam_a = cmul((step * abar_re, -step * abar_im), d_abar)
    to_lam_c = cmul((ratio[0], -ratio[1]), d_coef)
    g_decay = -(to_lam_a[0] + to_lam_c[0])
    g_lam = to_lam_a[1] + to_lam_c[1]
    slope = cmul((-decay, lam), (abar_re, abar_im))
    g_step = (slope[0] * d_abar[0] + slope[1] * d_abar[1] + abar_re * d_coef[0] + abar_im * d_coef[1]) * step
    for k, value in enumerate((g_decay, g_lam, g_step)):
        for m in range(2):
            vec_ref[pl.ds(16 + 2 * k + (lax.axis_index("ty") ^ m), 1), :] = value[m : m + 1]
    folds = []
    for k in range(2):
        squares = part_ref[2 + k : 3 + k, :]
        total = (squares[:, 0:128] + squares[:, 128:256]) + (squares[:, 256:384] + squares[:, 384:512])
        total = jnp.broadcast_to(total, (8, 128))
        folds.append(total + pltpu.roll(total, 64, 1))
    vec_ref[22:23, :] = jnp.where(low_half((1, 128)), folds[0][:1], folds[1][:1])
    vec_ref[23:24, :] = jnp.zeros((1, 128), F32)
    vec = packed(vec_ref[...])
    for ref in (stay_ref, y_ref, x_ref, xy_ref):
        ref[384:432, :] = vec


def input_grad(dn_ref, got_ref, up_ref, xhat_ref, inv_ref, feat_ref, gin_ref, tiles):
    rows, width = up_ref.shape
    xhat = xhat_ref[own_rows(rows), :]
    d_xhat = (dn_ref[...] + got_ref[...]) * feat_ref[0:1]
    mean = jnp.sum(d_xhat, axis=1, keepdims=True) / width
    mean_hat = jnp.sum(d_xhat * xhat, axis=1, keepdims=True) / width
    in_tiles(tiles, slice(None), inv_ref[:, 0:1] * (d_xhat - mean - xhat * mean_hat))
    in_order(tiles, gin_ref)
    gin_ref[...] = gin_ref[...] + up_ref[...].astype(F32)


def input_grad_kernel(*refs):
    input_grad(*refs)


def added(a, b):
    return (a.astype(F32) + b.astype(F32)).astype(BF16)


def middle_kernel(keep_ref, got_ref, stay_ref, leave_ref):
    stay_ref[...] = added(keep_ref[0], got_ref[0])
    leave_ref[...] = added(keep_ref[1], got_ref[1])


def plane_add_kernel(cw_ref, gotcw_ref, stay_ref, y_ref, x_ref, xy_ref, out_ref):
    def total(read):
        return (read(stay_ref) + read(y_ref)) + (read(x_ref) + read(xy_ref))

    vec = packed(total(lambda ref: unpacked(ref[384:432, :])))
    for z in range(GROUPS // 2):
        here = slice(96 * z, 96 * z + 96)
        out_ref[z, 0:96, :] = total(lambda ref, here=here: ref[here, :].astype(F32)).astype(BF16)
        out_ref[z, 96:256, :] = added(cw_ref[z], gotcw_ref[z])
        out_ref[z, 256:304, :] = vec


def vectors_kernel(got_ref, vec_ref):
    vec = unpacked(got_ref[0, 256:304, :])
    for z in range(1, GROUPS // 2):
        vec = vec + unpacked(got_ref[z, 256:304, :])
    vec_ref[...] = vec


def rows_to_lanes(rows):
    turned = [rows, pltpu.roll(rows, 96, 1), pltpu.roll(rows, 64, 1), pltpu.roll(rows, 32, 1)]
    lane = lane_iota((1, 128))
    return [
        jnp.where(lane < 96, rows[0:1], turned[1][1:2]),
        jnp.where(lane < 64, turned[1][1:2], turned[2][2:3]),
        jnp.where(lane < 32, turned[2][2:3], turned[3][3:4]),
    ]


def matrices_kernel(got_ref, dre_ref, dim_ref, ore_ref, oim_ref, glu_ref, square):
    def total(start, count):
        value = got_ref[0, start : start + count, :].astype(F32)
        for z in range(1, GROUPS // 2):
            value = value + got_ref[z, start : start + count, :].astype(F32)
        return value

    for start, first_ref, second_ref in ((0, dre_ref, dim_ref), (96, ore_ref, oim_ref)):
        square[0:96, :] = total(start, 96)
        square[96:128, :] = jnp.zeros((32, 128), F32)
        turned = square[...].T
        first_ref[...] = turned[0:64, 0:96]
        second_ref[...] = turned[64:128, 0:96]
    glu_ref[...] = total(192, 64)


def finish_kernel(
    count_all, own_ref, other_ref, dn_ref, got_ref, up_ref, xhat_ref, inv_ref, feat_ref,
    gin_ref, gbias_ref, scale_ref, bias_ref, skip_ref, decay_ref, lam_ref, step_ref, rms_ref, vec_ref, tiles,
):
    input_grad(dn_ref, got_ref, up_ref, xhat_ref, inv_ref, feat_ref, gin_ref, tiles)
    own, other = own_ref[...], other_ref[...]
    vec = own + other
    vec_ref[...] = vec
    first, second = jnp.where(lax.axis_index("tc") == 0, own, other), jnp.where(lax.axis_index("tc") == 0, other, own)
    for k, ref in enumerate((scale_ref, bias_ref, skip_ref)):
        for c in range(4):
            ref[:, 128 * c : 128 * c + 128] = vec[4 * k + c : 4 * k + c + 1]
    for k, ref in enumerate((decay_ref, lam_ref, step_ref)):
        at = 16 + 2 * k
        by_pos = [first[at : at + 1], second[at : at + 1], first[at + 1 : at + 2], second[at + 1 : at + 2]]
        for c, chunk in enumerate(rows_to_lanes(jnp.concatenate(by_pos + [jnp.zeros((4, 128), F32)], axis=0))):
            ref[128 * c : 128 * c + 128] = chunk.reshape(128)
    squares = vec[22:23]
    total = [jnp.sum(jnp.where(low_half((1, 128)) == low, squares, 0.0), axis=1, keepdims=True) for low in (True, False)]
    rms_ref[...] = jnp.sqrt(jnp.where(lane_iota((1, 2)) == 0, total[0], total[1]) / count_all)
    place = tensor_pos() * GROUPS + fsdp_pos()
    row = jnp.broadcast_to(vec_ref[pl.ds(12 + place // 8, 1), :], (8, 128))
    gbias_ref[...] = pltpu.roll(row, 128 - 16 * (place % 8), 1)[0:1, 0:16]


TAKES = {
    "pack": 1.5, "standardize": 0.4, "norm": 0.4, "first": 0.6, "states": 0.9, "readout": 0.4, "second": 0.7, "sums": 0.7, "back": 0.8,
    "third": 1.5, "input_grad": 0.5, "matrices": 0.5, "finish": 0.4,
}


def call(kernel, outs, args, scratch=(), specs=None, limit=24):
    name = getattr(kernel, "func", kernel).__name__.removesuffix("_kernel")
    return pl.pallas_call(
        kernel,
        out_shape=outs,
        in_specs=specs or [VM] * len(args),
        out_specs=jax.tree.map(lambda _: VM, outs),
        scratch_shapes=list(scratch),
        compiler_params=pltpu.CompilerParams(vmem_limit_bytes=limit << 20),
        cost_estimate=pl.CostEstimate(flops=0, transcendentals=0, bytes_accessed=int(TAKES.get(name, 0.1) * 3.6e6)),
        name=name,
    )(*args)


def tied(value, other):
    return lax.optimization_barrier((value, other))[0]


def swap(value, axis):
    return lax.ppermute(value, axis, [(0, 1), (1, 0)])


def across(value):
    return lax.ppermute(value, ("fx", "ty"), [(n, 3 - n) for n in range(4)])


def standardized(layer_in, grad_out, starts):
    rows, width = layer_in.shape
    return call(
        standardize_kernel,
        (sds((2 * rows, width)), sds((rows, width)), sds((rows, 128)), sds((2 * rows, 128))),
        (layer_in, swap(layer_in, "tc"), grad_out, starts),
        [pltpu.VMEM((4, 2 * rows, 128), F32), pltpu.VMEM((rows, 128), F32)],
    )


def on_device(
    layer_in, grad_out, ln_scale, ln_bias, decay_rate, lam_im, log_dt, in_re, in_im, out_re, out_im, skip, glu_weight, glu_bias, seq_lengths
):
    rows, width = layer_in.shape
    fsdp = lax.axis_size(FSDP)
    pairs, pair = fsdp * 2, 2 * rows
    count_all = float(rows * pairs * 2 * width)
    fast = fsdp == GROUPS
    same_core = (*FSDP, "ty")
    if fast:
        row = lambda v: v.reshape(1, -1)
        sent, starts = call(
            pack_kernel,
            (sds((GROUPS // 2, 272, 128), BF16), sds((seq_lengths.shape[0], 128))),
            (seq_lengths, in_re.T, in_im.T, out_re.T, out_im.T, glu_weight.T, row(ln_scale), row(ln_bias), row(skip), row(glu_bias),
             row(decay_rate), row(lam_im), row(log_dt)),
            [pltpu.VMEM((128, 128), F32), pltpu.VMEM((4, 64, 96), BF16), pltpu.VMEM((64, 128), BF16), pltpu.VMEM((4, 1, 64), BF16),
             pltpu.VMEM((3, 1, 96), F32), pltpu.SMEM(seq_lengths.shape, jnp.int32), pltpu.SemaphoreType.DMA((13,))],
            [HBM] * 13,
            60,
        )
        mine = lax.all_to_all(sent, "fz", 0, 0, tiled=True)
        own_b, own_cw = lax.optimization_barrier((mine[:, :112], mine[:, 112:]))
        plane_b = [own_b, swap(own_b, "ty"), swap(own_b, "fx"), across(own_b)]
        xhat, up, inverse, count = standardized(layer_in, grad_out, starts)
        plane_b, side_cw, xhat = lax.optimization_barrier((plane_b, swap(own_cw, "ty"), xhat))
        side_cw = jnp.stack([own_cw, side_cw])
        far_cw = swap(side_cw, "fx")
        g = jnp.stack(plane_b).reshape(2, 2, GROUPS // 2, 112, 128)
    else:
        starts = jnp.broadcast_to((jnp.cumsum(seq_lengths) - seq_lengths).astype(F32)[:, None], (seq_lengths.shape[0], 128))
        xhat, up, inverse, count = standardized(layer_in, grad_out, starts)
        g, cw, other_cw = gathered(
            ln_scale, ln_bias, decay_rate, lam_im, log_dt, in_re, in_im, out_re, out_im, skip, glu_weight, glu_bias
        )

    normed, feat = call(norm_kernel, (sds((pair, width), BF16), sds((8, width))), (xhat, g))
    b_all, v, lane, row_prm, carry = call(
        functools.partial(first_kernel, pairs),
        (sds((512, width), BF16), sds((pair, 512)), sds((8, 256)), sds((8, 8, 128)), sds((pairs, 4, 128))),
        (normed, count, g),
        [pltpu.VMEM((8, 128), F32)],
    )
    came = lax.all_to_all(carry, same_core, 0, 0, tiled=True)
    if fast:
        cw = jnp.stack(tied((side_cw, far_cw), came))
    state, twice, enter, c_all = call(
        states_kernel,
        (sds((pair, 512)), sds((pair, 512), BF16), sds((8, 512)), sds((512, width), BF16)),
        (came, starts, count, v, lane, row_prm, cw),
        [pltpu.VMEM((8, 128), F32)],
    )
    if fast:
        other_cw = swap(cw[:, :, :, 96:], "tc")
    readout = lambda core: call(functools.partial(readout_kernel, core), sds((rows, width)), (twice, c_all))
    away, own = readout(1), readout(0)
    branch, d_mixed, dlogit, kept, away = call(
        second_kernel,
        (sds((rows, width), BF16), sds((rows, width)), sds((rows, width), BF16), *[sds((rows, 2 * width + 256), BF16)] * 2),
        (own, swap(away, "tc"), up, normed, feat, cw, other_cw),
        [pltpu.VMEM((width, width), BF16), pltpu.VMEM((rows, width), BF16)],
    )
    got = swap(away, "tc")
    layer_out, part = call(
        sums_kernel,
        (sds((rows, width), BF16), sds((8, width))),
        (layer_in, branch, normed, d_mixed, dlogit),
        [pltpu.VMEM((4, rows, 128), F32), pltpu.VMEM((rows, width), F32)],
    )
    got, part = lax.optimization_barrier((got, part))
    d_state, carry, stay_cw, leave_cw = call(
        functools.partial(back_kernel, pairs),
        (sds((pair, 512)), sds((pairs, 4, 128)), *[sds((2, GROUPS // 2, 160, 128), BF16)] * 2),
        (kept, got, twice, count, lane, c_all),
        [pltpu.VMEM((pair, width), BF16), pltpu.VMEM((width, 256), BF16), pltpu.VMEM((8, 128), F32),
         pltpu.VMEM((2, 2, GROUPS // 2, 160, 128), BF16)],
    )
    if fast:
        far_cw = swap(leave_cw, "fx")
    came = lax.all_to_all(carry, same_core, 0, 0, tiled=True)
    if fast:
        came, far_cw, stay_cw = lax.optimization_barrier((came, far_cw, stay_cw))
        stay_cw, leave_cw = call(middle_kernel, [sds((GROUPS // 2, 160, 128), BF16)] * 2, (stay_cw, far_cw))
        far_cw = swap(leave_cw, "ty")
        came = tied(came, leave_cw)
    stay_b, y_b, x_b, xy_b, d_normed, away = call(
        third_kernel,
        (*[sds((432, 128), BF16)] * 4, sds((rows, width)), sds((rows, width))),
        (came, starts, count, normed, xhat, v, lane, row_prm, feat, state, d_state, enter, d_mixed, part, b_all),
        [pltpu.VMEM((8, 128), F32), pltpu.VMEM((pair, 512), BF16), pltpu.VMEM((pair, width), F32), pltpu.VMEM((24, 128), F32)],
    )
    if not fast:
        grad_in = call(
            input_grad_kernel,
            sds((rows, width)),
            (d_normed, swap(away, "tc"), grad_out, xhat, inverse, feat),
            [pltpu.VMEM((4, rows, 128), F32)],
        )
        return reduced(layer_out, grad_in, stay_cw, leave_cw, (stay_b, y_b, x_b, xy_b), count_all, fsdp, width)
    xy_b = across(xy_b)
    x_b = swap(x_b, "fx")
    y_b = swap(y_b, "ty")
    sent = call(
        plane_add_kernel,
        sds((GROUPS // 2, 304, 128), BF16),
        (stay_cw, far_cw, stay_b, y_b, x_b, xy_b),
    )
    got = lax.all_to_all(sent, "fz", 0, 0, tiled=True)
    away = swap(tied(away, got), "tc")
    vec = call(vectors_kernel, sds((24, 128)), (got,))
    other = swap(vec, "tc")
    d_re, d_im, d_ore, d_oim, d_glu = call(
        matrices_kernel, (*[sds((64, 96))] * 4, sds((64, 128))), (got,), [pltpu.VMEM((128, 128), F32)]
    )
    grad_in, d_gbias, d_scale, d_bias, d_skip, g_decay, g_lam, g_step, rms = call(
        functools.partial(finish_kernel, count_all),
        (sds((rows, width)), sds((1, 16)), *[sds((1, 512))] * 3, *[sds((384,))] * 3, sds((1, 2))),
        (vec, other, d_normed, away, grad_out, xhat, inverse, feat),
        [pltpu.VMEM((24, 128), F32), pltpu.VMEM((4, rows, 128), F32)],
    )
    flat = lambda value: value.reshape(-1)
    return (
        layer_out, grad_in, flat(d_scale), flat(d_bias), g_decay, g_lam, g_step, d_re.T, d_im.T, d_ore.T, d_oim.T,
        flat(d_skip), d_glu.T, flat(d_gbias), flat(rms),
    )


def gathered(ln_scale, ln_bias, decay_rate, lam_im, log_dt, in_re, in_im, out_re, out_im, skip, glu_weight, glu_bias):
    tens = tensor_pos()
    full = lambda value, axis: lax.all_gather(value, FSDP, axis=axis, tiled=True)

    def pair(first, second):
        halves = jnp.stack([first.reshape(-1, GROUPS, 64), second.reshape(-1, GROUPS, 64)], axis=2)
        return halves.reshape(-1, GROUPS, 128).swapaxes(0, 1)

    gate = lax.dynamic_slice_in_dim(full(glu_weight, 1), tens * 128, 128, 0).T.reshape(GROUPS, 64, 128)
    vectors = [pair(full(ln_scale, 0)[None], full(ln_bias, 0)[None]), pair(full(skip, 0)[None], full(glu_bias, 0)[None])]
    for value in (decay_rate, lam_im, log_dt):
        value = jnp.pad(value, (0, 32))
        for _ in range(3):
            piece = lax.reduce_precision(value, 8, 7)
            value = value - piece
            vectors.append(jnp.broadcast_to(piece.astype(BF16)[None, None], (GROUPS, 1, 128)))
    vectors.append(jnp.zeros((GROUPS, 5, 128), BF16))
    packet = jnp.concatenate(
        [pair(full(in_re, 1), full(in_im, 1)), *vectors, pair(full(out_re, 1), full(out_im, 1)), gate],
        axis=1,
    )
    everyone = lax.all_gather(packet, TENSOR, axis=0).reshape(2, 2, GROUPS // 2, 2, 272, 128)
    x, y, core = (lax.axis_index(axis) for axis in ("fx", "ty", "tc"))
    own_x = lambda value, axis: jnp.stack([lax.dynamic_index_in_dim(value, x ^ j, axis, keepdims=False) for j in range(2)])
    for i in range(2):
        both = lax.dynamic_index_in_dim(everyone, core ^ i, 1, keepdims=False)
        slots = [own_x(lax.dynamic_index_in_dim(both, y ^ m, 0, keepdims=False), 1) for m in range(2)]
        slots = jnp.stack(slots, axis=1)
        if i == 0:
            g, cw = slots[:, :, :, :112], slots[:, :, :, 112:]
    return g, cw, slots[:, :, :, 208:]


def reduced(layer_out, grad_in, stay_cw, leave_cw, plane_b, count_all, fsdp, width):
    tens = tensor_pos()
    x = lax.axis_index("fx")

    def canonical(slots):
        out = jnp.zeros((4, GROUPS, *slots[0].shape[2:]), F32)
        for m, slot in enumerate(slots):
            parts = [lax.dynamic_index_in_dim(slot.astype(F32), x ^ n, 1) for n in range(2)]
            block = jnp.concatenate(parts, axis=1).reshape(1, GROUPS, *slot.shape[2:])
            out = lax.dynamic_update_slice_in_dim(out, block, slot_pos(m, 0), 0)
        return out

    def natural(slots):
        halves = canonical(slots).reshape(4, GROUPS, -1, 2, 64).transpose(3, 0, 2, 1, 4)
        return halves[0].reshape(-1, width), halves[1].reshape(-1, width)

    def scattered(value):
        value = lax.psum_scatter(value, TENSOR, scatter_dimension=0, tiled=True)
        return lax.psum_scatter(value, FSDP, scatter_dimension=1, tiled=True)

    blocks = [value[:384].reshape(GROUPS // 2, 96, 128) for value in plane_b]
    d_re, d_im = natural([jnp.stack([blocks[m], blocks[2 + m]], axis=1) for m in range(2)])
    cw = jnp.stack([stay_cw, leave_cw]).transpose(1, 2, 0, 3, 4)
    d_ore, d_oim = natural([value[:, :, :96] for value in cw])
    d_glu = canonical([value[:, :, 96:] for value in cw]).reshape(4, width, 128).swapaxes(1, 2).reshape(-1, width)
    vec = unpacked(plane_b[0][384:432])
    by_pos = lax.dynamic_update_slice_in_dim(
        jnp.zeros((3, 2, 2, 96), F32), vec[16:22, :96].reshape(3, 2, 1, 96), lax.axis_index("tc"), 2
    )
    vec, by_pos = lax.psum((vec, by_pos), AXES)
    states = lambda k: by_pos[k].reshape(-1)
    own = width // (4 * fsdp)
    place = tens * fsdp + fsdp_pos()
    d_gbias = lax.dynamic_slice_in_dim(vec[12:16].reshape(-1), place * own, own, 0)
    rms = jnp.sqrt(jnp.sum(vec[22].reshape(2, 64), axis=1) / count_all)
    return (
        layer_out, grad_in, vec[0:4].reshape(-1), vec[4:8].reshape(-1), states(0), states(1), states(2), scattered(d_re), scattered(d_im),
        scattered(d_ore), scattered(d_oim), vec[8:12].reshape(-1), scattered(d_glu), d_gbias, rms,
    )


def solution(mesh):
    shape = (mesh.shape["fsdp"] // 2, 2, mesh.shape["tensor"] // 2, 2)
    split = Mesh(mesh.devices.reshape(shape), AXES)
    tokens, matrix = P(AXES, None), P(TENSOR, FSDP)
    return jax.shard_map(
        on_device,
        mesh=split,
        in_specs=(
            tokens, tokens, P(FSDP), P(FSDP), P(TENSOR), P(TENSOR), P(TENSOR), matrix, matrix, matrix, matrix,
            P(FSDP), P(None, FSDP), P(FSDP), P(),
        ),
        out_specs=(
            tokens, tokens, P(), P(), P(), P(), P(), matrix, matrix, matrix, matrix, P(), matrix, P((*TENSOR, *FSDP)), P(),
        ),
        check_vma=False,
    )
```

```python
import functools

import jax
import jax.numpy as jnp
from jax import lax
from jax.experimental import pallas as pl
from jax.experimental.pallas import tpu as pltpu
from jax.sharding import Mesh
from jax.sharding import PartitionSpec as P

F32 = jnp.float32
BF16 = jnp.bfloat16
FSDP = ("fz", "fx")
TENSOR = ("ty", "tc")
AXES = (*FSDP, *TENSOR)
HBM = pl.BlockSpec(memory_space=pltpu.HBM)
VM = pl.BlockSpec(memory_space=pltpu.VMEM)
SM = pl.BlockSpec(memory_space=pltpu.SMEM)

GROUPS = 8
VEC = 96


def sds(shape, dtype=F32):
    return jax.ShapeDtypeStruct(shape, dtype)


def low_half(shape):
    return lax.broadcasted_iota(jnp.int32, shape, len(shape) - 1) < 64


def lane_iota(shape):
    return lax.broadcasted_iota(jnp.int32, shape, len(shape) - 1)


def dot(a, b, dims):
    return lax.dot_general(a, b, (dims, ((), ())), preferred_element_type=F32)


NT = ((1,), (1,))
NN = ((1,), (0,))
TN = ((0,), (0,))


def flipped():
    return lax.axis_index("fx") == 1


def part_lanes(part, m):
    return slice(256 * part + 128 * m, 256 * part + 128 * m + 128)


def slot_pos(m, core):
    return (lax.axis_index("ty") ^ m) * 2 + (lax.axis_index("tc") ^ core)


def own_rows(rows):
    return pl.ds(pl.multiple_of(lax.axis_index("tc") * rows, rows), rows)


def other_rows(rows):
    return pl.ds(pl.multiple_of((1 - lax.axis_index("tc")) * rows, rows), rows)


def piece(ref, m, f, start, count):
    return ref[f % 2, m, f // 2, start : start + count, :]


def natural(get, ref):
    lo = low_half((96, 128))
    for m in range(2):
        for part in range(2):
            lanes = part_lanes(part, m)
            ref[lanes.start + 96 : lanes.stop, :] = jnp.zeros((32, 512), BF16)
        for z in range(GROUPS // 2):
            even, odd = get(m, z, 0).astype(F32), get(m, z, 1).astype(F32)
            here = slice(128 * z, 128 * z + 128)
            ref[128 * m : 128 * m + 96, here] = jnp.where(lo, even, pltpu.roll(odd, 64, 1)).astype(BF16)
            ref[256 + 128 * m : 256 + 128 * m + 96, here] = jnp.where(lo, pltpu.roll(even, 64, 1), odd).astype(BF16)


def packets(value, m, z):
    lo = low_half((96, 128))
    here = slice(128 * z, 128 * z + 128)
    re, im = value[128 * m : 128 * m + 96, here], value[256 + 128 * m : 256 + 128 * m + 96, here]
    return jnp.where(lo, re, pltpu.roll(im, 64, 1)), jnp.where(lo, pltpu.roll(re, 64, 1), im)


def feature_rows(ref, row):
    lo = low_half((8, 128))
    flip = flipped()
    first, second = [], []
    for c in range(GROUPS // 2):
        a = jnp.broadcast_to(piece(ref, 0, 2 * c, row, 1).astype(F32), (8, 128))
        b = jnp.broadcast_to(piece(ref, 0, 2 * c + 1, row, 1).astype(F32), (8, 128))
        a, b = jnp.where(flip, b, a), jnp.where(flip, a, b)
        first.append(jnp.where(lo, a, pltpu.roll(b, 64, 1)))
        second.append(jnp.where(lo, pltpu.roll(a, 64, 1), b))
    return jnp.concatenate(first, axis=1)[:1], jnp.concatenate(second, axis=1)[:1]


def cmul(a, b):
    return a[0] * b[0] - a[1] * b[1], a[0] * b[1] + a[1] * b[0]


def tensor_pos():
    return lax.axis_index("ty") * 2 + lax.axis_index("tc")


def fsdp_pos():
    return lax.axis_index("fz") * 2 + lax.axis_index("fx")


def pair_pos():
    return fsdp_pos() * 2 + lax.axis_index("ty")


def offsets_of(start_ref):
    return [start_ref[n : n + 1, :] for n in range(start_ref.shape[0])]


STEPS = 16


def in_tiles(ref, rows, value):
    for c in range(4):
        ref[c, rows, :] = value[:, 128 * c : 128 * c + 128]


def of_tiles(ref, rows):
    return jnp.concatenate([ref[c, rows, :] for c in range(4)], axis=1)


def interleaved(ref, b):
    groups = [of_tiles(ref, pl.ds((n // STEPS) * 128 + n % STEPS, 8, stride=STEPS)) for n in (b, b + 1)]
    return jnp.concatenate(groups, axis=0)


def in_order(source, target):
    for g in range(target.shape[0] // 8):
        h, s, i = g // STEPS, g % STEPS // 2, 8 * (g % 2)
        target[8 * g : 8 * g + 8, :] = of_tiles(source, pl.ds(128 * h + 8 * i + s, 8, stride=8))


def starts_until(offsets, base, rows):
    row = lax.broadcasted_iota(jnp.int32, (rows, 128), 0)
    token = (row & ~127) + (row & 7) * STEPS + ((row & 127) >> 3)
    at = (token + base).astype(F32)
    count = jnp.zeros((rows, 128), F32)
    for off in offsets:
        count = count + jnp.where((at >= off) & (off >= at[0:1]), 1.0, 0.0)
    return count


def no_start(offsets, base, rows):
    link = jnp.ones((1, 128), F32)
    first = (jnp.zeros((1, 128), jnp.int32) + base).astype(F32)
    for off in offsets:
        link = jnp.where((off >= first) & (off < first + rows), 0.0, link)
    return link


def expm1(x):
    series = x * (1 + x / 2 * (1 + x / 3 * (1 + x / 4 * (1 + x / 5 * (1 + x / 6 * (1 + x / 7))))))
    return jnp.where(jnp.abs(x) < 0.25, series, jnp.exp(x) - 1.0)


def discretize(decay_rate, lam_im, log_dt):
    step_size = jnp.exp(log_dt)
    lam_re = -decay_rate
    magnitude = jnp.exp(lam_re * step_size)
    phase = lam_im * step_size
    abar_re = magnitude * jnp.cos(phase)
    abar_im = magnitude * jnp.sin(phase)
    half_sin = jnp.sin(0.5 * phase)
    less_re = expm1(lam_re * step_size) * jnp.cos(phase) - 2.0 * half_sin * half_sin
    denom = lam_re * lam_re + lam_im * lam_im
    coef_re = (less_re * lam_re + abar_im * lam_im) / denom
    coef_im = (abar_im * lam_re - less_re * lam_im) / denom
    return abar_re, abar_im, coef_re, coef_im, step_size


def pack_kernel(*refs):
    *inputs, out_ref, start_ref, square, four, glu_ref, halves, params, lengths, sems = refs
    seq_hbm, matrices, glu_hbm, features, states = inputs[0], inputs[1:5], inputs[5], inputs[6:10], inputs[10:13]
    units = pl.multiple_of(tensor_pos() * 128, 128)
    pairs = [(ref, four.at[k]) for k, ref in enumerate(matrices)]
    pairs += [(glu_hbm.at[:, pl.ds(units, 128)], glu_ref), (seq_hbm, lengths)]
    pairs += [(ref, halves.at[k]) for k, ref in enumerate(features)]
    pairs += [(ref, params.at[k]) for k, ref in enumerate(states)]
    copies = [pltpu.make_async_copy(source, target, sems.at[k]) for k, (source, target) in enumerate(pairs)]
    for copy in copies:
        copy.start()
    square[:, 96:128] = jnp.zeros((128, 32), F32)
    for copy in copies:
        copy.wait()
    vec = [
        jnp.concatenate([halves[0], halves[1]], axis=1).astype(F32),
        jnp.concatenate([halves[2], halves[3]], axis=1).astype(F32),
    ]
    for k in range(3):
        value = jnp.concatenate([params[k], jnp.zeros((1, 32), F32)], axis=1)
        for _ in range(3):
            part = value.astype(BF16).astype(F32)
            value = value - part
            vec.append(part)
    total = 0
    for n in range(lengths.shape[0]):
        start_ref[n : n + 1, :] = jnp.full((1, 128), total, jnp.int32).astype(F32)
        total = total + lengths[n]
    vec.append(jnp.zeros((16 - len(vec), 128), F32))
    vec = jnp.concatenate(vec, axis=0).astype(BF16)
    pieces = []
    for k in (0, 2):
        square[0:64, 0:96] = four[k].astype(F32)
        square[64:128, 0:96] = four[k + 1].astype(F32)
        pieces.append(square[...].T[0:96].astype(BF16))
    packet = jnp.concatenate([pieces[0], vec, pieces[1], glu_ref[...]], axis=0)
    for z in range(GROUPS // 2):
        out_ref[z] = packet


def params_of(ref, vec_row):
    lane = lane_iota((8, 128))
    out = []
    for k, safe in enumerate((1.0, 0.0, 0.0)):
        rows = []
        for m in range(2):
            part = piece(ref, m, 0, vec_row, 16).astype(F32)
            rows.append((part[2 + 3 * k : 3 + 3 * k] + part[3 + 3 * k : 4 + 3 * k]) + part[4 + 3 * k : 5 + 3 * k])
        value = jnp.concatenate(rows + [jnp.full((6, 128), safe, F32)], axis=0)
        out.append(jnp.where(lane < 96, value, safe))
    return out


def carry_block(re_rows, im_rows, scratch):
    for m in range(2):
        y = lax.axis_index("ty") ^ m
        scratch[pl.ds(y, 1), :] = re_rows[m]
        scratch[pl.ds(2 + y, 1), :] = im_rows[m]


def standardize_kernel(x_ref, other_ref, up_ref, start_ref, xhat_ref, up_out_ref, inv_ref, count_ref, tiles, inverses):
    rows, width = x_ref.shape
    in_tiles(tiles, slice(0, rows), up_ref[...].astype(F32))
    for b in range(0, rows // 8, 2):
        up_out_ref[8 * b : 8 * b + 16, :] = interleaved(tiles, b)
    for ref, where, own in ((x_ref, own_rows(rows), True), (other_ref, other_rows(rows), False)):
        x = ref[...].astype(F32)
        centered = x - jnp.sum(x, axis=1, keepdims=True) / width
        inverse = lax.rsqrt(jnp.sum(centered * centered, axis=1, keepdims=True) / width + 1e-05)
        in_tiles(tiles, where, centered * inverse)
        if own:
            inverses[...] = jnp.broadcast_to(inverse, (rows, 128))
    for b in range(0, 2 * rows // 8, 2):
        xhat_ref[8 * b : 8 * b + 16, :] = interleaved(tiles, b)
    for b in range(rows // 8):
        inv_ref[8 * b : 8 * b + 8, :] = inverses[pl.ds(b, 8, stride=STEPS), :]
    count_ref[...] = starts_until(offsets_of(start_ref), pair_pos() * 2 * rows, 2 * rows)


def norm_kernel(xhat_ref, g_ref, normed_ref, feat_ref):
    scale, bias = feature_rows(g_ref, VEC)
    feat_ref[0:1] = scale
    feat_ref[1:2], feat_ref[2:3] = feature_rows(g_ref, VEC + 1)
    normed_ref[...] = (xhat_ref[...] * scale + bias).astype(BF16)


def first_kernel(pairs, normed_ref, count_ref, g_ref, b_ref, v_ref, lane_ref, row_ref, send_ref, scratch):
    rows = normed_ref.shape[0]
    natural(lambda m, z, x: g_ref[lax.axis_index("fx") ^ x, m, z, 0:96, :], b_ref)
    v_ref[...] = dot(normed_ref[...], b_ref[...], NT)

    decay, lam, log_dt = params_of(g_ref, VEC)
    abar_re, abar_im, coef_re, coef_im, step_size = discretize(decay, lam, log_dt)
    power = (abar_re, abar_im)
    for _ in range(8):
        power = cmul(power, power)
    scratch[...] = jnp.zeros((8, 128), F32)
    carry_block([power[0][m : m + 1] for m in range(2)], [power[1][m : m + 1] for m in range(2)], scratch)
    for k, value in enumerate((decay, lam, step_size, abar_re, abar_im, coef_re, coef_im, scratch[...])):
        row_ref[k] = value
    for k, value in enumerate((abar_re, abar_im, coef_re, coef_im)):
        for m in range(2):
            lane_ref[k : k + 1, 128 * m : 128 * m + 128] = value[m : m + 1]

    count = count_ref[...]
    open_tail = jnp.where(count == count[rows - 1 : rows], 1.0, 0.0)
    last = ([], [])
    for m in range(2):
        a = (all_rows(abar_re[m : m + 1]), all_rows(abar_im[m : m + 1]))
        b = (coef_re[m : m + 1], coef_im[m : m + 1])
        sixteen = squared(a, 4)
        tile = tile_powers(sixteen, lambda sub: 7 - sub)
        halves = []
        for h in range(2):
            acc = (jnp.zeros((8, 128), F32), jnp.zeros((8, 128), F32))
            for blk in range(STEPS * h, STEPS * h + STEPS):
                here = slice(8 * blk, 8 * blk + 8)
                drive = cmul(b, (v_ref[here, part_lanes(0, m)], v_ref[here, part_lanes(1, m)]))
                moved = cmul(a, acc)
                acc = (moved[0] + drive[0] * open_tail[here], moved[1] + drive[1] * open_tail[here])
            total = cmul(tile, acc)
            halves.append((column_sum(total[0]), column_sum(total[1])))
        moved = cmul(squared((sixteen[0][:1], sixteen[1][:1]), 3), halves[0])
        last[0].append(moved[0] + halves[1][0])
        last[1].append(moved[1] + halves[1][1])
    carry_block(last[0], last[1], scratch)
    packet = scratch[...]
    for d in range(pairs):
        send_ref[d] = packet[0:4]


def squared(a, times):
    for _ in range(times):
        a = cmul(a, a)
    return a


def tile_powers(a, exponent_of):
    exponent = exponent_of(lax.broadcasted_iota(jnp.int32, (8, 128), 0))
    tile = (jnp.ones((8, 128), F32), jnp.zeros((8, 128), F32))
    for bit in range(4):
        taken = (exponent & (1 << bit)) != 0
        more = cmul(tile, a)
        tile = (jnp.where(taken, more[0], tile[0]), jnp.where(taken, more[1], tile[1]))
        a = cmul(a, a)
    return tile


def all_rows(row):
    return jnp.broadcast_to(row, (8, 128))


def plus(value, link, more):
    return value[0] + jnp.where(link, more[0], 0.0), value[1] + jnp.where(link, more[1], 0.0)


def scan(read, powers, carry, count, reverse, emit):
    sub = lax.broadcasted_iota(jnp.int32, (8, 128), 0)
    order = range(STEPS - 1, -1, -1) if reverse else range(STEPS)
    end = 0 if reverse else 7
    back = lambda k: 8 - k if reverse else k
    carry = [(all_rows(c[0]), all_rows(c[1])) for c in carry]
    entries, ends, upto = [], [], []
    for a in powers:
        a = (all_rows(a[0]), all_rows(a[1]))
        power = [a]
        for _ in range(STEPS - 1):
            power.append(cmul(power[-1], a))
        upto.append(power)
        ends.append((power[-1], squared(power[-1], 1), squared(power[-1], 2)))
        entries.append(tile_powers(power[-1], (lambda sub: 8 - sub) if reverse else (lambda sub: sub + 1)))
    seen = jnp.zeros((8, 128), F32)
    for h in (1, 0) if reverse else (0, 1):
        counts = [count[8 * b : 8 * b + 8] for b in range(STEPS * h, STEPS * h + STEPS)]
        last = counts[order[-1]]
        near = jnp.where(sub == 7 - end, seen, pltpu.roll(last, back(1), 0))
        for m in range(2):
            values, before = {}, None
            for i in order:
                value = read(STEPS * h + i, m)
                if before is not None:
                    value = plus(value, counts[i] == counts[before], cmul(upto[m][0], values[before]))
                values[i], before = value, i
            tip = values[before]
            for k, power in zip((1, 2, 4), ends[m]):
                link = ((sub < 8 - k) if reverse else (sub >= k)) & (pltpu.roll(last, back(k), 0) == last)
                tip = plus(tip, link, cmul(power, (pltpu.roll(tip[0], back(k), 0), pltpu.roll(tip[1], back(k), 0))))
            tip = plus(tip, last == seen, cmul(entries[m], carry[m]))
            comes = tuple(jnp.where(sub == 7 - end, carry[m][p], pltpu.roll(tip[p], back(1), 0)) for p in range(2))
            for n, i in enumerate(order):
                emit(STEPS * h + i, m, plus(values[i], counts[i] == near, cmul(upto[m][n], comes)))
            carry[m] = (all_rows(tip[0][end : end + 1]), all_rows(tip[1][end : end + 1]))
        seen = all_rows(last[end : end + 1])


def carried(recv_ref, row_ref, offsets, rows, reverse, scratch):
    pairs = recv_ref.shape[0]
    power = row_ref[7]
    pre, pim = power[0:2], power[2:4]
    if reverse:
        pim = -pim
    place = pair_pos()

    zero = jnp.zeros((2, 128), F32)
    if pairs <= 32:
        first = lax.broadcasted_iota(jnp.int32, (pairs, 128), 0).astype(F32) * rows
        links = jnp.ones((pairs, 128), F32)
        for off in offsets:
            links = jnp.where((off >= first) & (off < first + rows), 0.0, links)
        out = (zero, zero)
        for j in range(pairs - 1, 0, -1) if reverse else range(pairs - 1):
            link = links[j : j + 1]
            got = recv_ref[j]
            new = cmul((pre * link, pim * link), out)
            reached = (j > place) if reverse else (j < place)
            out = (jnp.where(reached, new[0] + got[0:2], out[0]), jnp.where(reached, new[1] + got[2:4], out[1]))
    else:

        def turn(k, state):
            j = pairs - 1 - k if reverse else k
            link = no_start(offsets, j * rows, rows)
            got = recv_ref[j]
            new = cmul((pre * link, pim * link), state)
            return new[0] + got[0:2], new[1] + got[2:4]

        out = lax.fori_loop(0, pairs - 1 - place if reverse else place, turn, (zero, zero))
    scratch[0:2, :] = out[0]
    scratch[2:4, :] = out[1]
    own = [lax.axis_index("ty") ^ m for m in range(2)]
    return [scratch[pl.ds(y, 1), :] for y in own], [scratch[pl.ds(2 + y, 1), :] for y in own]


def column_sum(value):
    return jnp.sum(value, axis=0, keepdims=True)


def states_kernel(
    recv_ref, start_ref, count_ref, v_ref, lane_ref, row_ref, cw_ref, state_ref, twice_ref, enter_ref, c_ref, scratch
):
    rows = v_ref.shape[0]
    count = count_ref[...]
    enter = carried(recv_ref, row_ref, offsets_of(start_ref), rows, False, scratch)
    for part in range(2):
        for m in range(2):
            enter_ref[0:1, part_lanes(part, m)] = enter[part][m]
    powers = [(lane_ref[0:1, 128 * m : 128 * m + 128], lane_ref[1:2, 128 * m : 128 * m + 128]) for m in range(2)]

    def read(b, m):
        here, lanes = slice(8 * b, 8 * b + 8), slice(128 * m, 128 * m + 128)
        return cmul((lane_ref[2:3, lanes], lane_ref[3:4, lanes]), (v_ref[here, part_lanes(0, m)], v_ref[here, part_lanes(1, m)]))

    def emit(b, m, value):
        for part in range(2):
            state_ref[8 * b : 8 * b + 8, part_lanes(part, m)] = value[part]

    scan(read, powers, [(enter[0][m], enter[1][m]) for m in range(2)], count, False, emit)
    twice_ref[:, 0:256] = state_ref[:, 0:256].astype(BF16) * 2
    twice_ref[:, 256:512] = state_ref[:, 256:512].astype(BF16) * -2
    natural(lambda m, z, x: cw_ref[lax.axis_index("fx") ^ x, m, z, 0:96, :], c_ref)


def readout_kernel(core, twice_ref, c_ref, out_ref):
    where = (own_rows, other_rows)[core](out_ref.shape[0])
    out_ref[...] = dot(twice_ref[where, :], c_ref[...], NN)


def second_kernel(
    own_ref, got_ref, up_ref, normed_ref, feat_ref, cw_ref, othercw_ref,
    branch_ref, dmixed_ref, dlogit_ref, mine_ref, away_ref, gate_ref, all_ref,
):
    rows, width = up_ref.shape
    for core, ref in enumerate((cw_ref, othercw_ref)):
        for m in range(2):
            lanes = pl.ds(pl.multiple_of(slot_pos(m, core) * 128, 128), 128)
            for f in range(GROUPS):
                place = (f // 2) * 2 + (lax.axis_index("fx") ^ (f % 2))
                gate_ref[pl.ds(pl.multiple_of(place * 64, 64), 64), lanes] = piece(ref, m, f, 96 * (1 - core), 64)
    skip, gate_bias = feat_ref[1:2], feat_ref[2:3]
    normed = normed_ref[own_rows(rows), :].astype(F32)
    mixed = (own_ref[...] + got_ref[...]) + skip * normed
    cdf = 0.5 * (1.0 + lax.erf(mixed * 0.7071067811865476))
    act_low = (mixed * cdf).astype(BF16)
    act = act_low.astype(F32)
    w_gate = gate_ref[...]
    logit = dot(act_low, w_gate, NN) + gate_bias
    gate = 1.0 / (1.0 + jnp.exp(-logit))
    branch_ref[...] = (act * gate).astype(BF16)
    up = up_ref[...]
    dlogit = (up * act * gate * (1.0 - gate)).astype(BF16)
    dlogit_ref[...] = dlogit
    all_ref[...] = dlogit
    d_act = dot(dlogit, w_gate, NT) + up * gate
    slope = cdf + mixed * jnp.exp(-0.5 * mixed * mixed) * 0.3989422804014327
    d_mixed = d_act * slope
    dmixed_ref[...] = d_mixed
    for core, ref in enumerate((mine_ref, away_ref)):
        ref[:, 0:width] = d_mixed.astype(BF16)
        ref[:, width : 2 * width] = act_low
        for m in range(2):
            lanes = pl.ds(pl.multiple_of(slot_pos(m, core) * 128, 128), 128)
            ref[:, 2 * width + 128 * m : 2 * width + 128 * m + 128] = all_ref[:, lanes]


def sums_kernel(x_ref, branch_ref, normed_ref, dmixed_ref, dlogit_ref, out_ref, part_ref, tiles, ordered):
    x = x_ref[...].astype(F32)
    branch = branch_ref[...].astype(F32)
    in_tiles(tiles, slice(None), branch)
    in_order(tiles, ordered)
    out_ref[...] = (x + ordered[...]).astype(BF16)
    skip = column_sum(dmixed_ref[...] * normed_ref[own_rows(x_ref.shape[0]), :].astype(F32))
    for k, value in enumerate((skip, column_sum(dlogit_ref[...].astype(F32)), column_sum(x * x), column_sum(branch * branch))):
        part_ref[k : k + 1, :] = value


def back_kernel(
    pairs, mine_ref, got_ref, twice_ref, count_ref, lane_ref, c_ref,
    dstate_ref, send_ref, stay_ref, leave_ref, dy_ref, dgate_ref, scratch, all_ref,
):
    rows, width = dy_ref.shape
    half = rows // 2
    dy_ref[own_rows(half), :] = mine_ref[:, 0:width]
    dy_ref[other_rows(half), :] = got_ref[:, 0:width]
    d_state = dot(dy_ref[...], c_ref[...], NT)
    dstate_ref[:, 0:256] = d_state[:, 0:256] * 2.0
    dstate_ref[:, 256:512] = d_state[:, 256:512] * -2.0
    count = count_ref[...]
    head = jnp.where(count == 0.0, 1.0, 0.0)
    first = ([], [])
    for m in range(2):
        lanes = slice(128 * m, 128 * m + 128)
        a = (all_rows(lane_ref[0:1, lanes]), all_rows(-lane_ref[1:2, lanes]))
        sixteen = squared(a, 4)
        tile = tile_powers(sixteen, lambda sub: sub)
        halves = []
        for h in range(2):
            acc = (jnp.zeros((8, 128), F32), jnp.zeros((8, 128), F32))
            for blk in range(STEPS * h + STEPS - 1, STEPS * h - 1, -1):
                here = slice(8 * blk, 8 * blk + 8)
                moved = cmul(a, acc)
                acc = (
                    moved[0] + dstate_ref[here, part_lanes(0, m)] * head[here],
                    moved[1] + dstate_ref[here, part_lanes(1, m)] * head[here],
                )
            total = cmul(tile, acc)
            halves.append((column_sum(total[0]), column_sum(total[1])))
        moved = cmul(squared((sixteen[0][:1], sixteen[1][:1]), 3), halves[1])
        total = cmul((a[0][:1], a[1][:1]), (moved[0] + halves[0][0], moved[1] + halves[0][1]))
        first[0].append(total[0])
        first[1].append(total[1])
    scratch[...] = jnp.zeros((8, 128), F32)
    carry_block(first[0], first[1], scratch)
    packet = scratch[...]
    for d in range(pairs):
        send_ref[d] = packet[0:4]
    d_c = dot(twice_ref[...], dy_ref[...], TN)
    act = slice(width, 2 * width)
    units = slice(2 * width, 2 * width + 256)
    d_gate = dot(mine_ref[:, act], mine_ref[:, units], TN) + dot(got_ref[:, act], got_ref[:, units], TN)
    dgate_ref[...] = d_gate.astype(BF16)
    for m in range(2):
        for z in range(GROUPS // 2):
            for x, packet in enumerate(packets(d_c, m, z)):
                j = lax.axis_index("fx") ^ x
                all_ref[j, m, z, 0:96, :] = packet.astype(BF16)
                all_ref[j, m, z, 96:160, :] = dgate_ref[128 * z + 64 * x : 128 * z + 64 * x + 64, 128 * m : 128 * m + 128]
    stay_ref[...] = all_ref[0]
    leave_ref[...] = all_ref[1]


def packed(vec):
    upper = vec.astype(BF16).astype(F32)
    return jnp.concatenate([upper, vec - upper], axis=0).astype(BF16)


def unpacked(packet):
    value = packet.astype(F32)
    return value[0:24] + value[24:48]


def third_kernel(
    recv_ref, start_ref, count_ref, normed_ref, xhat_ref, v_ref, lane_ref, row_ref, feat_ref, state_ref, dstate_ref, enter_ref, dmixed_ref,
    part_ref, b_ref, stay_ref, y_ref, x_ref, xy_ref, dn_ref, dnaway_ref, scratch, dv_ref, all_ref, vec_ref,
):
    rows, width = normed_ref.shape
    half = rows // 2
    count = count_ref[...]
    later = carried(recv_ref, row_ref, offsets_of(start_ref), rows, True, scratch)
    sub = lax.broadcasted_iota(jnp.int32, (8, 128), 0)
    none = jnp.zeros((1, 128), F32)
    totals = [[jnp.zeros((8, 128), F32) for _ in range(4)] for _ in range(2)]
    powers = [(lane_ref[0:1, 128 * m : 128 * m + 128], -lane_ref[1:2, 128 * m : 128 * m + 128]) for m in range(2)]

    def read(b, m):
        value = [dstate_ref[8 * b : 8 * b + 8, part_lanes(part, m)] for part in range(2)]
        if b == rows // 8 - 1:
            value = [value[part] + jnp.where(sub == 7, later[part][m], 0.0) for part in range(2)]
        return tuple(value)

    def emit(b, m, adj):
        here, lanes = slice(8 * b, 8 * b + 8), slice(128 * m, 128 * m + 128)
        h, i = b // STEPS, b % STEPS
        if i:
            same = count[here] == count[8 * b - 8 : 8 * b]
            moved = [state_ref[8 * b - 8 : 8 * b, part_lanes(part, m)] for part in range(2)]
        else:
            end = slice(8 * (b + STEPS - 1), 8 * (b + STEPS))
            same = count[here] == jnp.where(sub == 0, count[127:128] if h else none, pltpu.roll(count[end], 1, 0))
            moved = []
            for part in range(2):
                edge = state_ref[127:128, part_lanes(part, m)] if h else enter_ref[0:1, part_lanes(part, m)]
                moved.append(jnp.where(sub == 0, edge, pltpu.roll(state_ref[end, part_lanes(part, m)], 1, 0)))
        prev = [jnp.where(same, part, 0.0) for part in moved]
        v = (v_ref[here, part_lanes(0, m)], v_ref[here, part_lanes(1, m)])
        for k, (p, q) in enumerate((prev, v)):
            totals[m][2 * k] = totals[m][2 * k] + (adj[0] * p + adj[1] * q)
            totals[m][2 * k + 1] = totals[m][2 * k + 1] + (adj[1] * p - adj[0] * q)
        dv = cmul((lane_ref[2:3, lanes], -lane_ref[3:4, lanes]), adj)
        for part in range(2):
            dvf_ref[here, part_lanes(part, m)] = dv[part]

    dvf_ref = all_ref
    scan(read, powers, [(none, none), (none, none)], count, True, emit)
    sums = [[column_sum(totals[m][k]) for m in range(2)] for k in range(4)]
    dv_ref[...] = dvf_ref[...].astype(BF16)
    dv = dv_ref[...]
    d_b = dot(dv, normed_ref[...], TN)
    flip = flipped()
    for m, (near, side) in enumerate(((stay_ref, x_ref), (y_ref, xy_ref))):
        for z in range(GROUPS // 2):
            even, odd = packets(d_b, m, z)
            here = slice(96 * z, 96 * z + 96)
            near[here, :] = jnp.where(flip, odd, even).astype(BF16)
            side[here, :] = jnp.where(flip, even, odd).astype(BF16)
    all_ref[...] = dot(dv, b_ref[...], NN)
    away = all_ref[other_rows(half), :]
    dnaway_ref[...] = away.astype(BF16)
    own = all_ref[own_rows(half), :] + dmixed_ref[...] * feat_ref[1:2]
    dn_ref[...] = own
    to_scale = column_sum(own * xhat_ref[own_rows(half), :]) + column_sum(away * xhat_ref[other_rows(half), :])
    vector = [to_scale, column_sum(own) + column_sum(away), part_ref[0:1, :], part_ref[1:2, :]]
    for k, value in enumerate(vector):
        for c in range(4):
            vec_ref[4 * k + c : 4 * k + c + 1, :] = value[:, 128 * c : 128 * c + 128]
    g = [jnp.concatenate(pair + [jnp.zeros((6, 128), F32)], axis=0) for pair in sums]
    decay, lam, step, abar_re, abar_im, coef_re, coef_im = (row_ref[k] for k in range(7))
    d_abar, d_coef = (g[0], g[1]), (g[2], g[3])
    denom = decay * decay + lam * lam
    numer = (step * abar_re - coef_re, step * abar_im - coef_im)
    ratio = cmul(numer, (-decay / denom, -lam / denom))
    to_lam_a = cmul((step * abar_re, -step * abar_im), d_abar)
    to_lam_c = cmul((ratio[0], -ratio[1]), d_coef)
    g_decay = -(to_lam_a[0] + to_lam_c[0])
    g_lam = to_lam_a[1] + to_lam_c[1]
    slope = cmul((-decay, lam), (abar_re, abar_im))
    g_step = (slope[0] * d_abar[0] + slope[1] * d_abar[1] + abar_re * d_coef[0] + abar_im * d_coef[1]) * step
    for k, value in enumerate((g_decay, g_lam, g_step)):
        for m in range(2):
            vec_ref[pl.ds(16 + 2 * k + (lax.axis_index("ty") ^ m), 1), :] = value[m : m + 1]
    folds = []
    for k in range(2):
        squares = part_ref[2 + k : 3 + k, :]
        total = (squares[:, 0:128] + squares[:, 128:256]) + (squares[:, 256:384] + squares[:, 384:512])
        total = jnp.broadcast_to(total, (8, 128))
        folds.append(total + pltpu.roll(total, 64, 1))
    vec_ref[22:23, :] = jnp.where(low_half((1, 128)), folds[0][:1], folds[1][:1])
    vec_ref[23:24, :] = jnp.zeros((1, 128), F32)
    vec = packed(vec_ref[...])
    for ref in (stay_ref, y_ref, x_ref, xy_ref):
        ref[384:432, :] = vec


def input_grad(dn_ref, got_ref, up_ref, xhat_ref, inv_ref, feat_ref, gin_ref, tiles):
    rows, width = up_ref.shape
    xhat = xhat_ref[own_rows(rows), :]
    d_xhat = (dn_ref[...] + got_ref[...].astype(F32)) * feat_ref[0:1]
    mean = jnp.sum(d_xhat, axis=1, keepdims=True) / width
    mean_hat = jnp.sum(d_xhat * xhat, axis=1, keepdims=True) / width
    in_tiles(tiles, slice(None), inv_ref[:, 0:1] * (d_xhat - mean - xhat * mean_hat))
    in_order(tiles, gin_ref)
    gin_ref[...] = gin_ref[...] + up_ref[...].astype(F32)


def input_grad_kernel(*refs):
    input_grad(*refs)


def added(a, b):
    return (a.astype(F32) + b.astype(F32)).astype(BF16)


def middle_kernel(keep_ref, got_ref, stay_ref, leave_ref):
    stay_ref[...] = added(keep_ref[0], got_ref[0])
    leave_ref[...] = added(keep_ref[1], got_ref[1])


def plane_add_kernel(cw_ref, gotcw_ref, stay_ref, y_ref, x_ref, xy_ref, out_ref):
    def total(read):
        return (read(stay_ref) + read(y_ref)) + (read(x_ref) + read(xy_ref))

    vec = packed(total(lambda ref: unpacked(ref[384:432, :])))
    for z in range(GROUPS // 2):
        here = slice(96 * z, 96 * z + 96)
        out_ref[z, 0:96, :] = total(lambda ref, here=here: ref[here, :].astype(F32)).astype(BF16)
        out_ref[z, 96:256, :] = added(cw_ref[z], gotcw_ref[z])
        out_ref[z, 256:304, :] = vec


def vectors_kernel(got_ref, vec_ref):
    vec = unpacked(got_ref[0, 256:304, :])
    for z in range(1, GROUPS // 2):
        vec = vec + unpacked(got_ref[z, 256:304, :])
    vec_ref[...] = vec


def rows_to_lanes(rows):
    turned = [rows, pltpu.roll(rows, 96, 1), pltpu.roll(rows, 64, 1), pltpu.roll(rows, 32, 1)]
    lane = lane_iota((1, 128))
    return [
        jnp.where(lane < 96, rows[0:1], turned[1][1:2]),
        jnp.where(lane < 64, turned[1][1:2], turned[2][2:3]),
        jnp.where(lane < 32, turned[2][2:3], turned[3][3:4]),
    ]


def matrices_kernel(got_ref, dre_ref, dim_ref, ore_ref, oim_ref, glu_ref, square):
    def total(start, count):
        value = got_ref[0, start : start + count, :].astype(F32)
        for z in range(1, GROUPS // 2):
            value = value + got_ref[z, start : start + count, :].astype(F32)
        return value

    for start, first_ref, second_ref in ((0, dre_ref, dim_ref), (96, ore_ref, oim_ref)):
        square[0:96, :] = total(start, 96)
        square[96:128, :] = jnp.zeros((32, 128), F32)
        turned = square[...].T
        first_ref[...] = turned[0:64, 0:96]
        second_ref[...] = turned[64:128, 0:96]
    glu_ref[...] = total(192, 64)


def finish_kernel(
    count_all, own_ref, other_ref, dn_ref, got_ref, up_ref, xhat_ref, inv_ref, feat_ref,
    gin_ref, gbias_ref, scale_ref, bias_ref, skip_ref, decay_ref, lam_ref, step_ref, rms_ref, vec_ref, tiles,
):
    input_grad(dn_ref, got_ref, up_ref, xhat_ref, inv_ref, feat_ref, gin_ref, tiles)
    own, other = own_ref[...], other_ref[...]
    vec = own + other
    vec_ref[...] = vec
    first, second = jnp.where(lax.axis_index("tc") == 0, own, other), jnp.where(lax.axis_index("tc") == 0, other, own)
    for k, ref in enumerate((scale_ref, bias_ref, skip_ref)):
        for c in range(4):
            ref[:, 128 * c : 128 * c + 128] = vec[4 * k + c : 4 * k + c + 1]
    for k, ref in enumerate((decay_ref, lam_ref, step_ref)):
        at = 16 + 2 * k
        by_pos = [first[at : at + 1], second[at : at + 1], first[at + 1 : at + 2], second[at + 1 : at + 2]]
        for c, chunk in enumerate(rows_to_lanes(jnp.concatenate(by_pos + [jnp.zeros((4, 128), F32)], axis=0))):
            ref[128 * c : 128 * c + 128] = chunk.reshape(128)
    squares = vec[22:23]
    total = [jnp.sum(jnp.where(low_half((1, 128)) == low, squares, 0.0), axis=1, keepdims=True) for low in (True, False)]
    rms_ref[...] = jnp.sqrt(jnp.where(lane_iota((1, 2)) == 0, total[0], total[1]) / count_all)
    place = tensor_pos() * GROUPS + fsdp_pos()
    row = jnp.broadcast_to(vec_ref[pl.ds(12 + place // 8, 1), :], (8, 128))
    gbias_ref[...] = pltpu.roll(row, 128 - 16 * (place % 8), 1)[0:1, 0:16]


TAKES = {
    "pack": 1.5, "standardize": 0.4, "norm": 0.4, "first": 0.6, "states": 0.9, "readout": 0.4, "second": 0.7, "sums": 0.7, "back": 0.8,
    "third": 1.5, "input_grad": 0.5, "matrices": 0.5, "finish": 0.4,
}


def call(kernel, outs, args, scratch=(), specs=None, limit=24):
    name = getattr(kernel, "func", kernel).__name__.removesuffix("_kernel")
    return pl.pallas_call(
        kernel,
        out_shape=outs,
        in_specs=specs or [VM] * len(args),
        out_specs=jax.tree.map(lambda _: VM, outs),
        scratch_shapes=list(scratch),
        compiler_params=pltpu.CompilerParams(vmem_limit_bytes=limit << 20),
        cost_estimate=pl.CostEstimate(flops=0, transcendentals=0, bytes_accessed=int(TAKES.get(name, 0.1) * 3.6e6)),
        name=name,
    )(*args)


def tied(value, other):
    return lax.optimization_barrier((value, other))[0]


def swap(value, axis):
    return lax.ppermute(value, axis, [(0, 1), (1, 0)])


def across(value):
    return lax.ppermute(value, ("fx", "ty"), [(n, 3 - n) for n in range(4)])


def standardized(layer_in, grad_out, starts):
    rows, width = layer_in.shape
    return call(
        standardize_kernel,
        (sds((2 * rows, width)), sds((rows, width)), sds((rows, 128)), sds((2 * rows, 128))),
        (layer_in, swap(layer_in, "tc"), grad_out, starts),
        [pltpu.VMEM((4, 2 * rows, 128), F32), pltpu.VMEM((rows, 128), F32)],
    )


def on_device(
    layer_in, grad_out, ln_scale, ln_bias, decay_rate, lam_im, log_dt, in_re, in_im, out_re, out_im, skip, glu_weight, glu_bias, seq_lengths
):
    rows, width = layer_in.shape
    fsdp = lax.axis_size(FSDP)
    pairs, pair = fsdp * 2, 2 * rows
    count_all = float(rows * pairs * 2 * width)
    fast = fsdp == GROUPS
    same_core = (*FSDP, "ty")
    if fast:
        row = lambda v: v.reshape(1, -1)
        sent, starts = call(
            pack_kernel,
            (sds((GROUPS // 2, 272, 128), BF16), sds((seq_lengths.shape[0], 128))),
            (seq_lengths, in_re.T, in_im.T, out_re.T, out_im.T, glu_weight.T, row(ln_scale), row(ln_bias), row(skip), row(glu_bias),
             row(decay_rate), row(lam_im), row(log_dt)),
            [pltpu.VMEM((128, 128), F32), pltpu.VMEM((4, 64, 96), BF16), pltpu.VMEM((64, 128), BF16), pltpu.VMEM((4, 1, 64), BF16),
             pltpu.VMEM((3, 1, 96), F32), pltpu.SMEM(seq_lengths.shape, jnp.int32), pltpu.SemaphoreType.DMA((13,))],
            [HBM] * 13,
            60,
        )
        mine = lax.all_to_all(sent, "fz", 0, 0, tiled=True)
        own_b, own_cw = lax.optimization_barrier((mine[:, :112], mine[:, 112:]))
        plane_b = [own_b, swap(own_b, "ty"), swap(own_b, "fx"), across(own_b)]
        xhat, up, inverse, count = standardized(layer_in, grad_out, starts)
        plane_b, side_cw, xhat = lax.optimization_barrier((plane_b, swap(own_cw, "ty"), xhat))
        side_cw = jnp.stack([own_cw, side_cw])
        far_cw = swap(side_cw, "fx")
        g = jnp.stack(plane_b).reshape(2, 2, GROUPS // 2, 112, 128)
    else:
        starts = jnp.broadcast_to((jnp.cumsum(seq_lengths) - seq_lengths).astype(F32)[:, None], (seq_lengths.shape[0], 128))
        xhat, up, inverse, count = standardized(layer_in, grad_out, starts)
        g, cw, other_cw = gathered(
            ln_scale, ln_bias, decay_rate, lam_im, log_dt, in_re, in_im, out_re, out_im, skip, glu_weight, glu_bias
        )

    normed, feat = call(norm_kernel, (sds((pair, width), BF16), sds((8, width))), (xhat, g))
    b_all, v, lane, row_prm, carry = call(
        functools.partial(first_kernel, pairs),
        (sds((512, width), BF16), sds((pair, 512)), sds((8, 256)), sds((8, 8, 128)), sds((pairs, 4, 128))),
        (normed, count, g),
        [pltpu.VMEM((8, 128), F32)],
    )
    came = lax.all_to_all(carry, same_core, 0, 0, tiled=True)
    if fast:
        cw = jnp.stack(tied((side_cw, far_cw), came))
    state, twice, enter, c_all = call(
        states_kernel,
        (sds((pair, 512)), sds((pair, 512), BF16), sds((8, 512)), sds((512, width), BF16)),
        (came, starts, count, v, lane, row_prm, cw),
        [pltpu.VMEM((8, 128), F32)],
    )
    if fast:
        other_cw = swap(cw[:, :, :, 96:], "tc")
    readout = lambda core: call(functools.partial(readout_kernel, core), sds((rows, width)), (twice, c_all))
    away, own = readout(1), readout(0)
    branch, d_mixed, dlogit, kept, away = call(
        second_kernel,
        (sds((rows, width), BF16), sds((rows, width)), sds((rows, width), BF16), *[sds((rows, 2 * width + 256), BF16)] * 2),
        (own, swap(away, "tc"), up, normed, feat, cw, other_cw),
        [pltpu.VMEM((width, width), BF16), pltpu.VMEM((rows, width), BF16)],
    )
    got = swap(away, "tc")
    layer_out, part = call(
        sums_kernel,
        (sds((rows, width), BF16), sds((8, width))),
        (layer_in, branch, normed, d_mixed, dlogit),
        [pltpu.VMEM((4, rows, 128), F32), pltpu.VMEM((rows, width), F32)],
    )
    got, part = lax.optimization_barrier((got, part))
    d_state, carry, stay_cw, leave_cw = call(
        functools.partial(back_kernel, pairs),
        (sds((pair, 512)), sds((pairs, 4, 128)), *[sds((2, GROUPS // 2, 160, 128), BF16)] * 2),
        (kept, got, twice, count, lane, c_all),
        [pltpu.VMEM((pair, width), BF16), pltpu.VMEM((width, 256), BF16), pltpu.VMEM((8, 128), F32),
         pltpu.VMEM((2, 2, GROUPS // 2, 160, 128), BF16)],
    )
    if fast:
        far_cw = swap(leave_cw, "fx")
    came = lax.all_to_all(carry, same_core, 0, 0, tiled=True)
    if fast:
        came, far_cw, stay_cw = lax.optimization_barrier((came, far_cw, stay_cw))
        stay_cw, leave_cw = call(middle_kernel, [sds((GROUPS // 2, 160, 128), BF16)] * 2, (stay_cw, far_cw))
        far_cw = swap(leave_cw, "ty")
        came = tied(came, leave_cw)
    stay_b, y_b, x_b, xy_b, d_normed, away = call(
        third_kernel,
        (*[sds((432, 128), BF16)] * 4, sds((rows, width)), sds((rows, width), BF16)),
        (came, starts, count, normed, xhat, v, lane, row_prm, feat, state, d_state, enter, d_mixed, part, b_all),
        [pltpu.VMEM((8, 128), F32), pltpu.VMEM((pair, 512), BF16), pltpu.VMEM((pair, width), F32), pltpu.VMEM((24, 128), F32)],
    )
    if not fast:
        grad_in = call(
            input_grad_kernel,
            sds((rows, width)),
            (d_normed, swap(away, "tc"), grad_out, xhat, inverse, feat),
            [pltpu.VMEM((4, rows, 128), F32)],
        )
        return reduced(layer_out, grad_in, stay_cw, leave_cw, (stay_b, y_b, x_b, xy_b), count_all, fsdp, width)
    xy_b = across(xy_b)
    x_b = swap(x_b, "fx")
    y_b = swap(y_b, "ty")
    sent = call(
        plane_add_kernel,
        sds((GROUPS // 2, 304, 128), BF16),
        (stay_cw, far_cw, stay_b, y_b, x_b, xy_b),
    )
    got = lax.all_to_all(sent, "fz", 0, 0, tiled=True)
    away = swap(tied(away, got), "tc")
    vec = call(vectors_kernel, sds((24, 128)), (got,))
    other = swap(vec, "tc")
    d_re, d_im, d_ore, d_oim, d_glu = call(
        matrices_kernel, (*[sds((64, 96))] * 4, sds((64, 128))), (got,), [pltpu.VMEM((128, 128), F32)]
    )
    grad_in, d_gbias, d_scale, d_bias, d_skip, g_decay, g_lam, g_step, rms = call(
        functools.partial(finish_kernel, count_all),
        (sds((rows, width)), sds((1, 16)), *[sds((1, 512))] * 3, *[sds((384,))] * 3, sds((1, 2))),
        (vec, other, d_normed, away, grad_out, xhat, inverse, feat),
        [pltpu.VMEM((24, 128), F32), pltpu.VMEM((4, rows, 128), F32)],
    )
    flat = lambda value: value.reshape(-1)
    return (
        layer_out, grad_in, flat(d_scale), flat(d_bias), g_decay, g_lam, g_step, d_re.T, d_im.T, d_ore.T, d_oim.T,
        flat(d_skip), d_glu.T, flat(d_gbias), flat(rms),
    )


def gathered(ln_scale, ln_bias, decay_rate, lam_im, log_dt, in_re, in_im, out_re, out_im, skip, glu_weight, glu_bias):
    tens = tensor_pos()
    full = lambda value, axis: lax.all_gather(value, FSDP, axis=axis, tiled=True)

    def pair(first, second):
        halves = jnp.stack([first.reshape(-1, GROUPS, 64), second.reshape(-1, GROUPS, 64)], axis=2)
        return halves.reshape(-1, GROUPS, 128).swapaxes(0, 1)

    gate = lax.dynamic_slice_in_dim(full(glu_weight, 1), tens * 128, 128, 0).T.reshape(GROUPS, 64, 128)
    vectors = [pair(full(ln_scale, 0)[None], full(ln_bias, 0)[None]), pair(full(skip, 0)[None], full(glu_bias, 0)[None])]
    for value in (decay_rate, lam_im, log_dt):
        value = jnp.pad(value, (0, 32))
        for _ in range(3):
            piece = lax.reduce_precision(value, 8, 7)
            value = value - piece
            vectors.append(jnp.broadcast_to(piece.astype(BF16)[None, None], (GROUPS, 1, 128)))
    vectors.append(jnp.zeros((GROUPS, 5, 128), BF16))
    packet = jnp.concatenate(
        [pair(full(in_re, 1), full(in_im, 1)), *vectors, pair(full(out_re, 1), full(out_im, 1)), gate],
        axis=1,
    )
    everyone = lax.all_gather(packet, TENSOR, axis=0).reshape(2, 2, GROUPS // 2, 2, 272, 128)
    x, y, core = (lax.axis_index(axis) for axis in ("fx", "ty", "tc"))
    own_x = lambda value, axis: jnp.stack([lax.dynamic_index_in_dim(value, x ^ j, axis, keepdims=False) for j in range(2)])
    for i in range(2):
        both = lax.dynamic_index_in_dim(everyone, core ^ i, 1, keepdims=False)
        slots = [own_x(lax.dynamic_index_in_dim(both, y ^ m, 0, keepdims=False), 1) for m in range(2)]
        slots = jnp.stack(slots, axis=1)
        if i == 0:
            g, cw = slots[:, :, :, :112], slots[:, :, :, 112:]
    return g, cw, slots[:, :, :, 208:]


def reduced(layer_out, grad_in, stay_cw, leave_cw, plane_b, count_all, fsdp, width):
    tens = tensor_pos()
    x = lax.axis_index("fx")

    def canonical(slots):
        out = jnp.zeros((4, GROUPS, *slots[0].shape[2:]), F32)
        for m, slot in enumerate(slots):
            parts = [lax.dynamic_index_in_dim(slot.astype(F32), x ^ n, 1) for n in range(2)]
            block = jnp.concatenate(parts, axis=1).reshape(1, GROUPS, *slot.shape[2:])
            out = lax.dynamic_update_slice_in_dim(out, block, slot_pos(m, 0), 0)
        return out

    def natural(slots):
        halves = canonical(slots).reshape(4, GROUPS, -1, 2, 64).transpose(3, 0, 2, 1, 4)
        return halves[0].reshape(-1, width), halves[1].reshape(-1, width)

    def scattered(value):
        value = lax.psum_scatter(value, TENSOR, scatter_dimension=0, tiled=True)
        return lax.psum_scatter(value, FSDP, scatter_dimension=1, tiled=True)

    blocks = [value[:384].reshape(GROUPS // 2, 96, 128) for value in plane_b]
    d_re, d_im = natural([jnp.stack([blocks[m], blocks[2 + m]], axis=1) for m in range(2)])
    cw = jnp.stack([stay_cw, leave_cw]).transpose(1, 2, 0, 3, 4)
    d_ore, d_oim = natural([value[:, :, :96] for value in cw])
    d_glu = canonical([value[:, :, 96:] for value in cw]).reshape(4, width, 128).swapaxes(1, 2).reshape(-1, width)
    vec = unpacked(plane_b[0][384:432])
    by_pos = lax.dynamic_update_slice_in_dim(
        jnp.zeros((3, 2, 2, 96), F32), vec[16:22, :96].reshape(3, 2, 1, 96), lax.axis_index("tc"), 2
    )
    vec, by_pos = lax.psum((vec, by_pos), AXES)
    states = lambda k: by_pos[k].reshape(-1)
    own = width // (4 * fsdp)
    place = tens * fsdp + fsdp_pos()
    d_gbias = lax.dynamic_slice_in_dim(vec[12:16].reshape(-1), place * own, own, 0)
    rms = jnp.sqrt(jnp.sum(vec[22].reshape(2, 64), axis=1) / count_all)
    return (
        layer_out, grad_in, vec[0:4].reshape(-1), vec[4:8].reshape(-1), states(0), states(1), states(2), scattered(d_re), scattered(d_im),
        scattered(d_ore), scattered(d_oim), vec[8:12].reshape(-1), scattered(d_glu), d_gbias, rms,
    )


def solution(mesh):
    shape = (mesh.shape["fsdp"] // 2, 2, mesh.shape["tensor"] // 2, 2)
    split = Mesh(mesh.devices.reshape(shape), AXES)
    tokens, matrix = P(AXES, None), P(TENSOR, FSDP)
    return jax.shard_map(
        on_device,
        mesh=split,
        in_specs=(
            tokens, tokens, P(FSDP), P(FSDP), P(TENSOR), P(TENSOR), P(TENSOR), matrix, matrix, matrix, matrix,
            P(FSDP), P(None, FSDP), P(FSDP), P(),
        ),
        out_specs=(
            tokens, tokens, P(), P(), P(), P(), P(), matrix, matrix, matrix, matrix, P(), matrix, P((*TENSOR, *FSDP)), P(),
        ),
        check_vma=False,
    )
```

```python
import functools

import jax
import jax.numpy as jnp
from jax import lax
from jax.experimental import pallas as pl
from jax.experimental.pallas import tpu as pltpu
from jax.sharding import Mesh
from jax.sharding import PartitionSpec as P

F32 = jnp.float32
BF16 = jnp.bfloat16
FSDP = ("fz", "fx")
TENSOR = ("ty", "tc")
AXES = (*FSDP, *TENSOR)
HBM = pl.BlockSpec(memory_space=pltpu.HBM)
VM = pl.BlockSpec(memory_space=pltpu.VMEM)
SM = pl.BlockSpec(memory_space=pltpu.SMEM)

GROUPS = 8
VEC = 96


def sds(shape, dtype=F32):
    return jax.ShapeDtypeStruct(shape, dtype)


def low_half(shape):
    return lax.broadcasted_iota(jnp.int32, shape, len(shape) - 1) < 64


def lane_iota(shape):
    return lax.broadcasted_iota(jnp.int32, shape, len(shape) - 1)


def dot(a, b, dims):
    return lax.dot_general(a, b, (dims, ((), ())), preferred_element_type=F32)


NT = ((1,), (1,))
NN = ((1,), (0,))
TN = ((0,), (0,))


def flipped():
    return lax.axis_index("fx") == 1


def part_lanes(part, m):
    return slice(256 * part + 128 * m, 256 * part + 128 * m + 128)


def slot_pos(m, core):
    return (lax.axis_index("ty") ^ m) * 2 + (lax.axis_index("tc") ^ core)


def own_rows(rows):
    return pl.ds(pl.multiple_of(lax.axis_index("tc") * rows, rows), rows)


def other_rows(rows):
    return pl.ds(pl.multiple_of((1 - lax.axis_index("tc")) * rows, rows), rows)


def piece(ref, m, f, start, count):
    return ref[f % 2, m, f // 2, start : start + count, :]


def natural(get, ref):
    lo = low_half((96, 128))
    for m in range(2):
        for part in range(2):
            lanes = part_lanes(part, m)
            ref[lanes.start + 96 : lanes.stop, :] = jnp.zeros((32, 512), BF16)
        for z in range(GROUPS // 2):
            even, odd = get(m, z, 0).astype(F32), get(m, z, 1).astype(F32)
            here = slice(128 * z, 128 * z + 128)
            ref[128 * m : 128 * m + 96, here] = jnp.where(lo, even, pltpu.roll(odd, 64, 1)).astype(BF16)
            ref[256 + 128 * m : 256 + 128 * m + 96, here] = jnp.where(lo, pltpu.roll(even, 64, 1), odd).astype(BF16)


def packets(value, m, z):
    lo = low_half((96, 128))
    here = slice(128 * z, 128 * z + 128)
    re, im = value[128 * m : 128 * m + 96, here], value[256 + 128 * m : 256 + 128 * m + 96, here]
    return jnp.where(lo, re, pltpu.roll(im, 64, 1)), jnp.where(lo, pltpu.roll(re, 64, 1), im)


def feature_rows(ref, row):
    lo = low_half((8, 128))
    flip = flipped()
    first, second = [], []
    for c in range(GROUPS // 2):
        a = jnp.broadcast_to(piece(ref, 0, 2 * c, row, 1).astype(F32), (8, 128))
        b = jnp.broadcast_to(piece(ref, 0, 2 * c + 1, row, 1).astype(F32), (8, 128))
        a, b = jnp.where(flip, b, a), jnp.where(flip, a, b)
        first.append(jnp.where(lo, a, pltpu.roll(b, 64, 1)))
        second.append(jnp.where(lo, pltpu.roll(a, 64, 1), b))
    return jnp.concatenate(first, axis=1)[:1], jnp.concatenate(second, axis=1)[:1]


def cmul(a, b):
    return a[0] * b[0] - a[1] * b[1], a[0] * b[1] + a[1] * b[0]


def tensor_pos():
    return lax.axis_index("ty") * 2 + lax.axis_index("tc")


def fsdp_pos():
    return lax.axis_index("fz") * 2 + lax.axis_index("fx")


def pair_pos():
    return fsdp_pos() * 2 + lax.axis_index("ty")


def offsets_of(start_ref):
    return [start_ref[n : n + 1, :] for n in range(start_ref.shape[0])]


STEPS = 16


def in_tiles(ref, rows, value):
    for c in range(4):
        ref[c, rows, :] = value[:, 128 * c : 128 * c + 128]


def of_tiles(ref, rows):
    return jnp.concatenate([ref[c, rows, :] for c in range(4)], axis=1)


def interleaved(ref, b):
    groups = [of_tiles(ref, pl.ds((n // STEPS) * 128 + n % STEPS, 8, stride=STEPS)) for n in (b, b + 1)]
    return jnp.concatenate(groups, axis=0)


def in_order(source, target):
    for g in range(target.shape[0] // 8):
        h, s, i = g // STEPS, g % STEPS // 2, 8 * (g % 2)
        target[8 * g : 8 * g + 8, :] = of_tiles(source, pl.ds(128 * h + 8 * i + s, 8, stride=8))


def starts_until(offsets, base, rows):
    row = lax.broadcasted_iota(jnp.int32, (rows, 128), 0)
    token = (row & ~127) + (row & 7) * STEPS + ((row & 127) >> 3)
    at = (token + base).astype(F32)
    count = jnp.zeros((rows, 128), F32)
    for off in offsets:
        count = count + jnp.where((at >= off) & (off >= at[0:1]), 1.0, 0.0)
    return count


def no_start(offsets, base, rows):
    link = jnp.ones((1, 128), F32)
    first = (jnp.zeros((1, 128), jnp.int32) + base).astype(F32)
    for off in offsets:
        link = jnp.where((off >= first) & (off < first + rows), 0.0, link)
    return link


def expm1(x):
    series = x * (1 + x / 2 * (1 + x / 3 * (1 + x / 4 * (1 + x / 5 * (1 + x / 6 * (1 + x / 7))))))
    return jnp.where(jnp.abs(x) < 0.25, series, jnp.exp(x) - 1.0)


def discretize(decay_rate, lam_im, log_dt):
    step_size = jnp.exp(log_dt)
    lam_re = -decay_rate
    magnitude = jnp.exp(lam_re * step_size)
    phase = lam_im * step_size
    abar_re = magnitude * jnp.cos(phase)
    abar_im = magnitude * jnp.sin(phase)
    half_sin = jnp.sin(0.5 * phase)
    less_re = expm1(lam_re * step_size) * jnp.cos(phase) - 2.0 * half_sin * half_sin
    denom = lam_re * lam_re + lam_im * lam_im
    coef_re = (less_re * lam_re + abar_im * lam_im) / denom
    coef_im = (abar_im * lam_re - less_re * lam_im) / denom
    return abar_re, abar_im, coef_re, coef_im, step_size


def pack_kernel(*refs):
    *inputs, out_ref, start_ref, square, four, glu_ref, halves, params, lengths, sems = refs
    seq_hbm, matrices, glu_hbm, features, states = inputs[0], inputs[1:5], inputs[5], inputs[6:10], inputs[10:13]
    units = pl.multiple_of(tensor_pos() * 128, 128)
    pairs = [(ref, four.at[k]) for k, ref in enumerate(matrices)]
    pairs += [(glu_hbm.at[:, pl.ds(units, 128)], glu_ref), (seq_hbm, lengths)]
    pairs += [(ref, halves.at[k]) for k, ref in enumerate(features)]
    pairs += [(ref, params.at[k]) for k, ref in enumerate(states)]
    copies = [pltpu.make_async_copy(source, target, sems.at[k]) for k, (source, target) in enumerate(pairs)]
    for copy in copies:
        copy.start()
    square[:, 96:128] = jnp.zeros((128, 32), F32)
    for copy in copies:
        copy.wait()
    vec = [
        jnp.concatenate([halves[0], halves[1]], axis=1).astype(F32),
        jnp.concatenate([halves[2], halves[3]], axis=1).astype(F32),
    ]
    for k in range(3):
        value = jnp.concatenate([params[k], jnp.zeros((1, 32), F32)], axis=1)
        for _ in range(3):
            part = value.astype(BF16).astype(F32)
            value = value - part
            vec.append(part)
    total = 0
    for n in range(lengths.shape[0]):
        start_ref[n : n + 1, :] = jnp.full((1, 128), total, jnp.int32).astype(F32)
        total = total + lengths[n]
    vec.append(jnp.zeros((16 - len(vec), 128), F32))
    vec = jnp.concatenate(vec, axis=0).astype(BF16)
    pieces = []
    for k in (0, 2):
        square[0:64, 0:96] = four[k].astype(F32)
        square[64:128, 0:96] = four[k + 1].astype(F32)
        pieces.append(square[...].T[0:96].astype(BF16))
    packet = jnp.concatenate([pieces[0], vec, pieces[1], glu_ref[...]], axis=0)
    for z in range(GROUPS // 2):
        out_ref[z] = packet


def params_of(ref, vec_row):
    lane = lane_iota((8, 128))
    out = []
    for k, safe in enumerate((1.0, 0.0, 0.0)):
        rows = []
        for m in range(2):
            part = piece(ref, m, 0, vec_row, 16).astype(F32)
            rows.append((part[2 + 3 * k : 3 + 3 * k] + part[3 + 3 * k : 4 + 3 * k]) + part[4 + 3 * k : 5 + 3 * k])
        value = jnp.concatenate(rows + [jnp.full((6, 128), safe, F32)], axis=0)
        out.append(jnp.where(lane < 96, value, safe))
    return out


def carry_block(re_rows, im_rows, scratch):
    for m in range(2):
        y = lax.axis_index("ty") ^ m
        scratch[pl.ds(y, 1), :] = re_rows[m]
        scratch[pl.ds(2 + y, 1), :] = im_rows[m]


def standardize_kernel(x_ref, other_ref, up_ref, start_ref, xhat_ref, up_out_ref, inv_ref, count_ref, tiles, inverses):
    rows, width = x_ref.shape
    in_tiles(tiles, slice(0, rows), up_ref[...].astype(F32))
    for b in range(0, rows // 8, 2):
        up_out_ref[8 * b : 8 * b + 16, :] = interleaved(tiles, b)
    for ref, where, own in ((x_ref, own_rows(rows), True), (other_ref, other_rows(rows), False)):
        x = ref[...].astype(F32)
        centered = x - jnp.sum(x, axis=1, keepdims=True) / width
        inverse = lax.rsqrt(jnp.sum(centered * centered, axis=1, keepdims=True) / width + 1e-05)
        in_tiles(tiles, where, centered * inverse)
        if own:
            inverses[...] = jnp.broadcast_to(inverse, (rows, 128))
    for b in range(0, 2 * rows // 8, 2):
        xhat_ref[8 * b : 8 * b + 16, :] = interleaved(tiles, b)
    for b in range(rows // 8):
        inv_ref[8 * b : 8 * b + 8, :] = inverses[pl.ds(b, 8, stride=STEPS), :]
    count_ref[...] = starts_until(offsets_of(start_ref), pair_pos() * 2 * rows, 2 * rows)


def first_kernel(
    pairs, xhat_ref, count_ref, g_ref, normed_ref, feat_ref, b_ref, v_ref, lane_ref, row_ref, send_ref, scratch
):
    rows = normed_ref.shape[0]
    scale, bias = feature_rows(g_ref, VEC)
    feat_ref[0:1] = scale
    feat_ref[1:2], feat_ref[2:3] = feature_rows(g_ref, VEC + 1)
    normed_ref[...] = (xhat_ref[...] * scale + bias).astype(BF16)
    natural(lambda m, z, x: g_ref[lax.axis_index("fx") ^ x, m, z, 0:96, :], b_ref)
    v_ref[...] = dot(normed_ref[...], b_ref[...], NT)

    decay, lam, log_dt = params_of(g_ref, VEC)
    abar_re, abar_im, coef_re, coef_im, step_size = discretize(decay, lam, log_dt)
    power = (abar_re, abar_im)
    for _ in range(8):
        power = cmul(power, power)
    scratch[...] = jnp.zeros((8, 128), F32)
    carry_block([power[0][m : m + 1] for m in range(2)], [power[1][m : m + 1] for m in range(2)], scratch)
    for k, value in enumerate((decay, lam, step_size, abar_re, abar_im, coef_re, coef_im, scratch[...])):
        row_ref[k] = value
    for k, value in enumerate((abar_re, abar_im, coef_re, coef_im)):
        for m in range(2):
            lane_ref[k : k + 1, 128 * m : 128 * m + 128] = value[m : m + 1]

    count = count_ref[...]
    open_tail = jnp.where(count == count[rows - 1 : rows], 1.0, 0.0)
    last = ([], [])
    for m in range(2):
        a = (all_rows(abar_re[m : m + 1]), all_rows(abar_im[m : m + 1]))
        b = (coef_re[m : m + 1], coef_im[m : m + 1])
        sixteen = squared(a, 4)
        tile = tile_powers(sixteen, lambda sub: 7 - sub)
        halves = []
        for h in range(2):
            acc = (jnp.zeros((8, 128), F32), jnp.zeros((8, 128), F32))
            for blk in range(STEPS * h, STEPS * h + STEPS):
                here = slice(8 * blk, 8 * blk + 8)
                drive = cmul(b, (v_ref[here, part_lanes(0, m)], v_ref[here, part_lanes(1, m)]))
                moved = cmul(a, acc)
                acc = (moved[0] + drive[0] * open_tail[here], moved[1] + drive[1] * open_tail[here])
            total = cmul(tile, acc)
            halves.append((column_sum(total[0]), column_sum(total[1])))
        moved = cmul(squared((sixteen[0][:1], sixteen[1][:1]), 3), halves[0])
        last[0].append(moved[0] + halves[1][0])
        last[1].append(moved[1] + halves[1][1])
    carry_block(last[0], last[1], scratch)
    packet = scratch[...]
    for d in range(pairs):
        send_ref[d] = packet[0:4]


def squared(a, times):
    for _ in range(times):
        a = cmul(a, a)
    return a


def tile_powers(a, exponent_of):
    exponent = exponent_of(lax.broadcasted_iota(jnp.int32, (8, 128), 0))
    tile = (jnp.ones((8, 128), F32), jnp.zeros((8, 128), F32))
    for bit in range(4):
        taken = (exponent & (1 << bit)) != 0
        more = cmul(tile, a)
        tile = (jnp.where(taken, more[0], tile[0]), jnp.where(taken, more[1], tile[1]))
        a = cmul(a, a)
    return tile


def all_rows(row):
    return jnp.broadcast_to(row, (8, 128))


def plus(value, link, more):
    return value[0] + jnp.where(link, more[0], 0.0), value[1] + jnp.where(link, more[1], 0.0)


def scan(read, powers, carry, count, reverse, emit):
    sub = lax.broadcasted_iota(jnp.int32, (8, 128), 0)
    order = range(STEPS - 1, -1, -1) if reverse else range(STEPS)
    end = 0 if reverse else 7
    back = lambda k: 8 - k if reverse else k
    carry = [(all_rows(c[0]), all_rows(c[1])) for c in carry]
    entries, ends, upto = [], [], []
    for a in powers:
        a = (all_rows(a[0]), all_rows(a[1]))
        power = [a]
        for _ in range(STEPS - 1):
            power.append(cmul(power[-1], a))
        upto.append(power)
        ends.append((power[-1], squared(power[-1], 1), squared(power[-1], 2)))
        entries.append(tile_powers(power[-1], (lambda sub: 8 - sub) if reverse else (lambda sub: sub + 1)))
    seen = jnp.zeros((8, 128), F32)
    for h in (1, 0) if reverse else (0, 1):
        counts = [count[8 * b : 8 * b + 8] for b in range(STEPS * h, STEPS * h + STEPS)]
        last = counts[order[-1]]
        near = jnp.where(sub == 7 - end, seen, pltpu.roll(last, back(1), 0))
        for m in range(2):
            values, before = {}, None
            for i in order:
                value = read(STEPS * h + i, m)
                if before is not None:
                    value = plus(value, counts[i] == counts[before], cmul(upto[m][0], values[before]))
                values[i], before = value, i
            tip = values[before]
            for k, power in zip((1, 2, 4), ends[m]):
                link = ((sub < 8 - k) if reverse else (sub >= k)) & (pltpu.roll(last, back(k), 0) == last)
                tip = plus(tip, link, cmul(power, (pltpu.roll(tip[0], back(k), 0), pltpu.roll(tip[1], back(k), 0))))
            tip = plus(tip, last == seen, cmul(entries[m], carry[m]))
            comes = tuple(jnp.where(sub == 7 - end, carry[m][p], pltpu.roll(tip[p], back(1), 0)) for p in range(2))
            for n, i in enumerate(order):
                emit(STEPS * h + i, m, plus(values[i], counts[i] == near, cmul(upto[m][n], comes)))
            carry[m] = (all_rows(tip[0][end : end + 1]), all_rows(tip[1][end : end + 1]))
        seen = all_rows(last[end : end + 1])


def carried(recv_ref, row_ref, offsets, rows, reverse, scratch):
    pairs = recv_ref.shape[0]
    power = row_ref[7]
    pre, pim = power[0:2], power[2:4]
    if reverse:
        pim = -pim
    place = pair_pos()

    zero = jnp.zeros((2, 128), F32)
    if pairs <= 32:
        first = lax.broadcasted_iota(jnp.int32, (pairs, 128), 0).astype(F32) * rows
        links = jnp.ones((pairs, 128), F32)
        for off in offsets:
            links = jnp.where((off >= first) & (off < first + rows), 0.0, links)
        out = (zero, zero)
        for j in range(pairs - 1, 0, -1) if reverse else range(pairs - 1):
            link = links[j : j + 1]
            got = recv_ref[j]
            new = cmul((pre * link, pim * link), out)
            reached = (j > place) if reverse else (j < place)
            out = (jnp.where(reached, new[0] + got[0:2], out[0]), jnp.where(reached, new[1] + got[2:4], out[1]))
    else:

        def turn(k, state):
            j = pairs - 1 - k if reverse else k
            link = no_start(offsets, j * rows, rows)
            got = recv_ref[j]
            new = cmul((pre * link, pim * link), state)
            return new[0] + got[0:2], new[1] + got[2:4]

        out = lax.fori_loop(0, pairs - 1 - place if reverse else place, turn, (zero, zero))
    scratch[0:2, :] = out[0]
    scratch[2:4, :] = out[1]
    own = [lax.axis_index("ty") ^ m for m in range(2)]
    return [scratch[pl.ds(y, 1), :] for y in own], [scratch[pl.ds(2 + y, 1), :] for y in own]


def column_sum(value):
    return jnp.sum(value, axis=0, keepdims=True)


def states_kernel(
    recv_ref, start_ref, count_ref, v_ref, lane_ref, row_ref, cw_ref, state_ref, twice_ref, enter_ref, c_ref, scratch
):
    rows = v_ref.shape[0]
    count = count_ref[...]
    enter = carried(recv_ref, row_ref, offsets_of(start_ref), rows, False, scratch)
    for part in range(2):
        for m in range(2):
            enter_ref[0:1, part_lanes(part, m)] = enter[part][m]
    powers = [(lane_ref[0:1, 128 * m : 128 * m + 128], lane_ref[1:2, 128 * m : 128 * m + 128]) for m in range(2)]

    def read(b, m):
        here, lanes = slice(8 * b, 8 * b + 8), slice(128 * m, 128 * m + 128)
        return cmul((lane_ref[2:3, lanes], lane_ref[3:4, lanes]), (v_ref[here, part_lanes(0, m)], v_ref[here, part_lanes(1, m)]))

    def emit(b, m, value):
        for part in range(2):
            state_ref[8 * b : 8 * b + 8, part_lanes(part, m)] = value[part]

    scan(read, powers, [(enter[0][m], enter[1][m]) for m in range(2)], count, False, emit)
    twice_ref[:, 0:256] = state_ref[:, 0:256].astype(BF16) * 2
    twice_ref[:, 256:512] = state_ref[:, 256:512].astype(BF16) * -2
    natural(lambda m, z, x: cw_ref[lax.axis_index("fx") ^ x, m, z, 0:96, :], c_ref)


def readout_kernel(core, twice_ref, c_ref, out_ref):
    where = (own_rows, other_rows)[core](out_ref.shape[0])
    out_ref[...] = dot(twice_ref[where, :], c_ref[...], NN)


def second_kernel(
    own_ref, got_ref, up_ref, normed_ref, feat_ref, cw_ref, othercw_ref,
    branch_ref, dmixed_ref, dlogit_ref, mine_ref, away_ref, gate_ref, all_ref,
):
    rows, width = up_ref.shape
    for core, ref in enumerate((cw_ref, othercw_ref)):
        for m in range(2):
            lanes = pl.ds(pl.multiple_of(slot_pos(m, core) * 128, 128), 128)
            for f in range(GROUPS):
                place = (f // 2) * 2 + (lax.axis_index("fx") ^ (f % 2))
                gate_ref[pl.ds(pl.multiple_of(place * 64, 64), 64), lanes] = piece(ref, m, f, 96 * (1 - core), 64)
    skip, gate_bias = feat_ref[1:2], feat_ref[2:3]
    normed = normed_ref[own_rows(rows), :].astype(F32)
    mixed = (own_ref[...] + got_ref[...]) + skip * normed
    cdf = 0.5 * (1.0 + lax.erf(mixed * 0.7071067811865476))
    act_low = (mixed * cdf).astype(BF16)
    act = act_low.astype(F32)
    w_gate = gate_ref[...]
    logit = dot(act_low, w_gate, NN) + gate_bias
    gate = 1.0 / (1.0 + jnp.exp(-logit))
    branch_ref[...] = (act * gate).astype(BF16)
    up = up_ref[...]
    dlogit = (up * act * gate * (1.0 - gate)).astype(BF16)
    dlogit_ref[...] = dlogit
    all_ref[...] = dlogit
    d_act = dot(dlogit, w_gate, NT) + up * gate
    slope = cdf + mixed * jnp.exp(-0.5 * mixed * mixed) * 0.3989422804014327
    d_mixed = d_act * slope
    dmixed_ref[...] = d_mixed
    for core, ref in enumerate((mine_ref, away_ref)):
        ref[:, 0:width] = d_mixed.astype(BF16)
        ref[:, width : 2 * width] = act_low
        for m in range(2):
            lanes = pl.ds(pl.multiple_of(slot_pos(m, core) * 128, 128), 128)
            ref[:, 2 * width + 128 * m : 2 * width + 128 * m + 128] = all_ref[:, lanes]


def sums_kernel(x_ref, branch_ref, normed_ref, dmixed_ref, dlogit_ref, out_ref, part_ref, tiles, ordered):
    x = x_ref[...].astype(F32)
    branch = branch_ref[...].astype(F32)
    in_tiles(tiles, slice(None), branch)
    in_order(tiles, ordered)
    out_ref[...] = (x + ordered[...]).astype(BF16)
    skip = column_sum(dmixed_ref[...] * normed_ref[own_rows(x_ref.shape[0]), :].astype(F32))
    for k, value in enumerate((skip, column_sum(dlogit_ref[...].astype(F32)), column_sum(x * x), column_sum(branch * branch))):
        part_ref[k : k + 1, :] = value


def back_kernel(
    pairs, mine_ref, got_ref, twice_ref, count_ref, lane_ref, c_ref,
    dstate_ref, send_ref, stay_ref, leave_ref, dy_ref, dgate_ref, scratch, all_ref,
):
    rows, width = dy_ref.shape
    half = rows // 2
    dy_ref[own_rows(half), :] = mine_ref[:, 0:width]
    dy_ref[other_rows(half), :] = got_ref[:, 0:width]
    d_state = dot(dy_ref[...], c_ref[...], NT)
    dstate_ref[:, 0:256] = d_state[:, 0:256] * 2.0
    dstate_ref[:, 256:512] = d_state[:, 256:512] * -2.0
    count = count_ref[...]
    head = jnp.where(count == 0.0, 1.0, 0.0)
    first = ([], [])
    for m in range(2):
        lanes = slice(128 * m, 128 * m + 128)
        a = (all_rows(lane_ref[0:1, lanes]), all_rows(-lane_ref[1:2, lanes]))
        sixteen = squared(a, 4)
        tile = tile_powers(sixteen, lambda sub: sub)
        halves = []
        for h in range(2):
            acc = (jnp.zeros((8, 128), F32), jnp.zeros((8, 128), F32))
            for blk in range(STEPS * h + STEPS - 1, STEPS * h - 1, -1):
                here = slice(8 * blk, 8 * blk + 8)
                moved = cmul(a, acc)
                acc = (
                    moved[0] + dstate_ref[here, part_lanes(0, m)] * head[here],
                    moved[1] + dstate_ref[here, part_lanes(1, m)] * head[here],
                )
            total = cmul(tile, acc)
            halves.append((column_sum(total[0]), column_sum(total[1])))
        moved = cmul(squared((sixteen[0][:1], sixteen[1][:1]), 3), halves[1])
        total = cmul((a[0][:1], a[1][:1]), (moved[0] + halves[0][0], moved[1] + halves[0][1]))
        first[0].append(total[0])
        first[1].append(total[1])
    scratch[...] = jnp.zeros((8, 128), F32)
    carry_block(first[0], first[1], scratch)
    packet = scratch[...]
    for d in range(pairs):
        send_ref[d] = packet[0:4]
    d_c = dot(twice_ref[...], dy_ref[...], TN)
    act = slice(width, 2 * width)
    units = slice(2 * width, 2 * width + 256)
    d_gate = dot(mine_ref[:, act], mine_ref[:, units], TN) + dot(got_ref[:, act], got_ref[:, units], TN)
    dgate_ref[...] = d_gate.astype(BF16)
    for m in range(2):
        for z in range(GROUPS // 2):
            for x, packet in enumerate(packets(d_c, m, z)):
                j = lax.axis_index("fx") ^ x
                all_ref[j, m, z, 0:96, :] = packet.astype(BF16)
                all_ref[j, m, z, 96:160, :] = dgate_ref[128 * z + 64 * x : 128 * z + 64 * x + 64, 128 * m : 128 * m + 128]
    stay_ref[...] = all_ref[0]
    leave_ref[...] = all_ref[1]


def packed(vec):
    upper = vec.astype(BF16).astype(F32)
    return jnp.concatenate([upper, vec - upper], axis=0).astype(BF16)


def unpacked(packet):
    value = packet.astype(F32)
    return value[0:24] + value[24:48]


def third_kernel(
    recv_ref, start_ref, count_ref, normed_ref, xhat_ref, v_ref, lane_ref, row_ref, feat_ref, state_ref, dstate_ref, enter_ref, dmixed_ref,
    part_ref, b_ref, stay_ref, y_ref, x_ref, xy_ref, dn_ref, dnaway_ref, scratch, dv_ref, all_ref, vec_ref,
):
    rows, width = normed_ref.shape
    half = rows // 2
    count = count_ref[...]
    later = carried(recv_ref, row_ref, offsets_of(start_ref), rows, True, scratch)
    sub = lax.broadcasted_iota(jnp.int32, (8, 128), 0)
    none = jnp.zeros((1, 128), F32)
    totals = [[jnp.zeros((8, 128), F32) for _ in range(4)] for _ in range(2)]
    powers = [(lane_ref[0:1, 128 * m : 128 * m + 128], -lane_ref[1:2, 128 * m : 128 * m + 128]) for m in range(2)]

    def read(b, m):
        value = [dstate_ref[8 * b : 8 * b + 8, part_lanes(part, m)] for part in range(2)]
        if b == rows // 8 - 1:
            value = [value[part] + jnp.where(sub == 7, later[part][m], 0.0) for part in range(2)]
        return tuple(value)

    def emit(b, m, adj):
        here, lanes = slice(8 * b, 8 * b + 8), slice(128 * m, 128 * m + 128)
        h, i = b // STEPS, b % STEPS
        if i:
            same = count[here] == count[8 * b - 8 : 8 * b]
            moved = [state_ref[8 * b - 8 : 8 * b, part_lanes(part, m)] for part in range(2)]
        else:
            end = slice(8 * (b + STEPS - 1), 8 * (b + STEPS))
            same = count[here] == jnp.where(sub == 0, count[127:128] if h else none, pltpu.roll(count[end], 1, 0))
            moved = []
            for part in range(2):
                edge = state_ref[127:128, part_lanes(part, m)] if h else enter_ref[0:1, part_lanes(part, m)]
                moved.append(jnp.where(sub == 0, edge, pltpu.roll(state_ref[end, part_lanes(part, m)], 1, 0)))
        prev = [jnp.where(same, part, 0.0) for part in moved]
        v = (v_ref[here, part_lanes(0, m)], v_ref[here, part_lanes(1, m)])
        for k, (p, q) in enumerate((prev, v)):
            totals[m][2 * k] = totals[m][2 * k] + (adj[0] * p + adj[1] * q)
            totals[m][2 * k + 1] = totals[m][2 * k + 1] + (adj[1] * p - adj[0] * q)
        dv = cmul((lane_ref[2:3, lanes], -lane_ref[3:4, lanes]), adj)
        for part in range(2):
            dvf_ref[here, part_lanes(part, m)] = dv[part]

    dvf_ref = all_ref
    scan(read, powers, [(none, none), (none, none)], count, True, emit)
    sums = [[column_sum(totals[m][k]) for m in range(2)] for k in range(4)]
    dv_ref[...] = dvf_ref[...].astype(BF16)
    dv = dv_ref[...]
    d_b = dot(dv, normed_ref[...], TN)
    flip = flipped()
    for m, (near, side) in enumerate(((stay_ref, x_ref), (y_ref, xy_ref))):
        for z in range(GROUPS // 2):
            even, odd = packets(d_b, m, z)
            here = slice(96 * z, 96 * z + 96)
            near[here, :] = jnp.where(flip, odd, even).astype(BF16)
            side[here, :] = jnp.where(flip, even, odd).astype(BF16)
    all_ref[...] = dot(dv, b_ref[...], NN)
    away = all_ref[other_rows(half), :]
    dnaway_ref[...] = away.astype(BF16)
    own = all_ref[own_rows(half), :] + dmixed_ref[...] * feat_ref[1:2]
    dn_ref[...] = own
    to_scale = column_sum(own * xhat_ref[own_rows(half), :]) + column_sum(away * xhat_ref[other_rows(half), :])
    vector = [to_scale, column_sum(own) + column_sum(away), part_ref[0:1, :], part_ref[1:2, :]]
    for k, value in enumerate(vector):
        for c in range(4):
            vec_ref[4 * k + c : 4 * k + c + 1, :] = value[:, 128 * c : 128 * c + 128]
    g = [jnp.concatenate(pair + [jnp.zeros((6, 128), F32)], axis=0) for pair in sums]
    decay, lam, step, abar_re, abar_im, coef_re, coef_im = (row_ref[k] for k in range(7))
    d_abar, d_coef = (g[0], g[1]), (g[2], g[3])
    denom = decay * decay + lam * lam
    numer = (step * abar_re - coef_re, step * abar_im - coef_im)
    ratio = cmul(numer, (-decay / denom, -lam / denom))
    to_lam_a = cmul((step * abar_re, -step * abar_im), d_abar)
    to_lam_c = cmul((ratio[0], -ratio[1]), d_coef)
    g_decay = -(to_lam_a[0] + to_lam_c[0])
    g_lam = to_lam_a[1] + to_lam_c[1]
    slope = cmul((-decay, lam), (abar_re, abar_im))
    g_step = (slope[0] * d_abar[0] + slope[1] * d_abar[1] + abar_re * d_coef[0] + abar_im * d_coef[1]) * step
    for k, value in enumerate((g_decay, g_lam, g_step)):
        for m in range(2):
            vec_ref[pl.ds(16 + 2 * k + (lax.axis_index("ty") ^ m), 1), :] = value[m : m + 1]
    folds = []
    for k in range(2):
        squares = part_ref[2 + k : 3 + k, :]
        total = (squares[:, 0:128] + squares[:, 128:256]) + (squares[:, 256:384] + squares[:, 384:512])
        total = jnp.broadcast_to(total, (8, 128))
        folds.append(total + pltpu.roll(total, 64, 1))
    vec_ref[22:23, :] = jnp.where(low_half((1, 128)), folds[0][:1], folds[1][:1])
    vec_ref[23:24, :] = jnp.zeros((1, 128), F32)
    vec = packed(vec_ref[...])
    for ref in (stay_ref, y_ref, x_ref, xy_ref):
        ref[384:432, :] = vec


def input_grad(dn_ref, got_ref, up_ref, xhat_ref, inv_ref, feat_ref, gin_ref, tiles):
    rows, width = up_ref.shape
    xhat = xhat_ref[own_rows(rows), :]
    d_xhat = (dn_ref[...] + got_ref[...].astype(F32)) * feat_ref[0:1]
    mean = jnp.sum(d_xhat, axis=1, keepdims=True) / width
    mean_hat = jnp.sum(d_xhat * xhat, axis=1, keepdims=True) / width
    in_tiles(tiles, slice(None), inv_ref[:, 0:1] * (d_xhat - mean - xhat * mean_hat))
    in_order(tiles, gin_ref)
    gin_ref[...] = gin_ref[...] + up_ref[...].astype(F32)


def input_grad_kernel(*refs):
    input_grad(*refs)


def added(a, b):
    return (a.astype(F32) + b.astype(F32)).astype(BF16)


def middle_kernel(keep_ref, got_ref, stay_ref, leave_ref):
    stay_ref[...] = added(keep_ref[0], got_ref[0])
    leave_ref[...] = added(keep_ref[1], got_ref[1])


def plane_add_kernel(cw_ref, gotcw_ref, stay_ref, y_ref, x_ref, xy_ref, out_ref):
    def total(read):
        return (read(stay_ref) + read(y_ref)) + (read(x_ref) + read(xy_ref))

    vec = packed(total(lambda ref: unpacked(ref[384:432, :])))
    for z in range(GROUPS // 2):
        here = slice(96 * z, 96 * z + 96)
        out_ref[z, 0:96, :] = total(lambda ref, here=here: ref[here, :].astype(F32)).astype(BF16)
        out_ref[z, 96:256, :] = added(cw_ref[z], gotcw_ref[z])
        out_ref[z, 256:304, :] = vec


def vectors_kernel(got_ref, vec_ref):
    vec = unpacked(got_ref[0, 256:304, :])
    for z in range(1, GROUPS // 2):
        vec = vec + unpacked(got_ref[z, 256:304, :])
    vec_ref[...] = vec


def rows_to_lanes(rows):
    turned = [rows, pltpu.roll(rows, 96, 1), pltpu.roll(rows, 64, 1), pltpu.roll(rows, 32, 1)]
    lane = lane_iota((1, 128))
    return [
        jnp.where(lane < 96, rows[0:1], turned[1][1:2]),
        jnp.where(lane < 64, turned[1][1:2], turned[2][2:3]),
        jnp.where(lane < 32, turned[2][2:3], turned[3][3:4]),
    ]


def matrices_kernel(got_ref, dre_ref, dim_ref, ore_ref, oim_ref, glu_ref, square):
    def total(start, count):
        value = got_ref[0, start : start + count, :].astype(F32)
        for z in range(1, GROUPS // 2):
            value = value + got_ref[z, start : start + count, :].astype(F32)
        return value

    for start, first_ref, second_ref in ((0, dre_ref, dim_ref), (96, ore_ref, oim_ref)):
        square[0:96, :] = total(start, 96)
        square[96:128, :] = jnp.zeros((32, 128), F32)
        turned = square[...].T
        first_ref[...] = turned[0:64, 0:96]
        second_ref[...] = turned[64:128, 0:96]
    glu_ref[...] = total(192, 64)


def finish_kernel(
    count_all, own_ref, other_ref, dn_ref, got_ref, up_ref, xhat_ref, inv_ref, feat_ref,
    gin_ref, gbias_ref, scale_ref, bias_ref, skip_ref, decay_ref, lam_ref, step_ref, rms_ref, vec_ref, tiles,
):
    input_grad(dn_ref, got_ref, up_ref, xhat_ref, inv_ref, feat_ref, gin_ref, tiles)
    own, other = own_ref[...], other_ref[...]
    vec = own + other
    vec_ref[...] = vec
    first, second = jnp.where(lax.axis_index("tc") == 0, own, other), jnp.where(lax.axis_index("tc") == 0, other, own)
    for k, ref in enumerate((scale_ref, bias_ref, skip_ref)):
        for c in range(4):
            ref[:, 128 * c : 128 * c + 128] = vec[4 * k + c : 4 * k + c + 1]
    for k, ref in enumerate((decay_ref, lam_ref, step_ref)):
        at = 16 + 2 * k
        by_pos = [first[at : at + 1], second[at : at + 1], first[at + 1 : at + 2], second[at + 1 : at + 2]]
        for c, chunk in enumerate(rows_to_lanes(jnp.concatenate(by_pos + [jnp.zeros((4, 128), F32)], axis=0))):
            ref[128 * c : 128 * c + 128] = chunk.reshape(128)
    squares = vec[22:23]
    total = [jnp.sum(jnp.where(low_half((1, 128)) == low, squares, 0.0), axis=1, keepdims=True) for low in (True, False)]
    rms_ref[...] = jnp.sqrt(jnp.where(lane_iota((1, 2)) == 0, total[0], total[1]) / count_all)
    place = tensor_pos() * GROUPS + fsdp_pos()
    row = jnp.broadcast_to(vec_ref[pl.ds(12 + place // 8, 1), :], (8, 128))
    gbias_ref[...] = pltpu.roll(row, 128 - 16 * (place % 8), 1)[0:1, 0:16]


TAKES = {
    "pack": 1.5, "standardize": 0.4, "norm": 0.4, "first": 0.6, "states": 0.9, "readout": 0.4, "second": 0.7, "sums": 0.7, "back": 0.8,
    "third": 1.5, "input_grad": 0.5, "matrices": 0.5, "finish": 0.4,
}


def call(kernel, outs, args, scratch=(), specs=None, limit=24):
    name = getattr(kernel, "func", kernel).__name__.removesuffix("_kernel")
    return pl.pallas_call(
        kernel,
        out_shape=outs,
        in_specs=specs or [VM] * len(args),
        out_specs=jax.tree.map(lambda _: VM, outs),
        scratch_shapes=list(scratch),
        compiler_params=pltpu.CompilerParams(vmem_limit_bytes=limit << 20),
        cost_estimate=pl.CostEstimate(flops=0, transcendentals=0, bytes_accessed=int(TAKES.get(name, 0.1) * 3.6e6)),
        name=name,
    )(*args)


def tied(value, other):
    return lax.optimization_barrier((value, other))[0]


def swap(value, axis):
    return lax.ppermute(value, axis, [(0, 1), (1, 0)])


def across(value):
    return lax.ppermute(value, ("fx", "ty"), [(n, 3 - n) for n in range(4)])


def standardized(layer_in, grad_out, starts):
    rows, width = layer_in.shape
    return call(
        standardize_kernel,
        (sds((2 * rows, width)), sds((rows, width)), sds((rows, 128)), sds((2 * rows, 128))),
        (layer_in, swap(layer_in, "tc"), grad_out, starts),
        [pltpu.VMEM((4, 2 * rows, 128), F32), pltpu.VMEM((rows, 128), F32)],
    )


def on_device(
    layer_in, grad_out, ln_scale, ln_bias, decay_rate, lam_im, log_dt, in_re, in_im, out_re, out_im, skip, glu_weight, glu_bias, seq_lengths
):
    rows, width = layer_in.shape
    fsdp = lax.axis_size(FSDP)
    pairs, pair = fsdp * 2, 2 * rows
    count_all = float(rows * pairs * 2 * width)
    fast = fsdp == GROUPS
    same_core = (*FSDP, "ty")
    if fast:
        row = lambda v: v.reshape(1, -1)
        sent, starts = call(
            pack_kernel,
            (sds((GROUPS // 2, 272, 128), BF16), sds((seq_lengths.shape[0], 128))),
            (seq_lengths, in_re.T, in_im.T, out_re.T, out_im.T, glu_weight.T, row(ln_scale), row(ln_bias), row(skip), row(glu_bias),
             row(decay_rate), row(lam_im), row(log_dt)),
            [pltpu.VMEM((128, 128), F32), pltpu.VMEM((4, 64, 96), BF16), pltpu.VMEM((64, 128), BF16), pltpu.VMEM((4, 1, 64), BF16),
             pltpu.VMEM((3, 1, 96), F32), pltpu.SMEM(seq_lengths.shape, jnp.int32), pltpu.SemaphoreType.DMA((13,))],
            [HBM] * 13,
            60,
        )
        mine = lax.all_to_all(sent, "fz", 0, 0, tiled=True)
        own_b, own_cw = lax.optimization_barrier((mine[:, :112], mine[:, 112:]))
        plane_b = [own_b, swap(own_b, "ty"), swap(own_b, "fx"), across(own_b)]
        xhat, up, inverse, count = standardized(layer_in, grad_out, starts)
        plane_b, side_cw, xhat = lax.optimization_barrier((plane_b, swap(own_cw, "ty"), xhat))
        side_cw = jnp.stack([own_cw, side_cw])
        far_cw = swap(side_cw, "fx")
        g = jnp.stack(plane_b).reshape(2, 2, GROUPS // 2, 112, 128)
    else:
        starts = jnp.broadcast_to((jnp.cumsum(seq_lengths) - seq_lengths).astype(F32)[:, None], (seq_lengths.shape[0], 128))
        xhat, up, inverse, count = standardized(layer_in, grad_out, starts)
        g, cw, other_cw = gathered(
            ln_scale, ln_bias, decay_rate, lam_im, log_dt, in_re, in_im, out_re, out_im, skip, glu_weight, glu_bias
        )

    normed, feat, b_all, v, lane, row_prm, carry = call(
        functools.partial(first_kernel, pairs),
        (sds((pair, width), BF16), sds((8, width)), sds((512, width), BF16), sds((pair, 512)), sds((8, 256)), sds((8, 8, 128)), sds((pairs, 4, 128))),
        (xhat, count, g),
        [pltpu.VMEM((8, 128), F32)],
    )
    came = lax.all_to_all(carry, same_core, 0, 0, tiled=True)
    if fast:
        cw = jnp.stack(tied((side_cw, far_cw), came))
    state, twice, enter, c_all = call(
        states_kernel,
        (sds((pair, 512)), sds((pair, 512), BF16), sds((8, 512)), sds((512, width), BF16)),
        (came, starts, count, v, lane, row_prm, cw),
        [pltpu.VMEM((8, 128), F32)],
    )
    if fast:
        other_cw = swap(cw[:, :, :, 96:], "tc")
    readout = lambda core: call(functools.partial(readout_kernel, core), sds((rows, width)), (twice, c_all))
    away, own = readout(1), readout(0)
    branch, d_mixed, dlogit, kept, away = call(
        second_kernel,
        (sds((rows, width), BF16), sds((rows, width)), sds((rows, width), BF16), *[sds((rows, 2 * width + 256), BF16)] * 2),
        (own, swap(away, "tc"), up, normed, feat, cw, other_cw),
        [pltpu.VMEM((width, width), BF16), pltpu.VMEM((rows, width), BF16)],
    )
    got = swap(away, "tc")
    layer_out, part = call(
        sums_kernel,
        (sds((rows, width), BF16), sds((8, width))),
        (layer_in, branch, normed, d_mixed, dlogit),
        [pltpu.VMEM((4, rows, 128), F32), pltpu.VMEM((rows, width), F32)],
    )
    got, part = lax.optimization_barrier((got, part))
    d_state, carry, stay_cw, leave_cw = call(
        functools.partial(back_kernel, pairs),
        (sds((pair, 512)), sds((pairs, 4, 128)), *[sds((2, GROUPS // 2, 160, 128), BF16)] * 2),
        (kept, got, twice, count, lane, c_all),
        [pltpu.VMEM((pair, width), BF16), pltpu.VMEM((width, 256), BF16), pltpu.VMEM((8, 128), F32),
         pltpu.VMEM((2, 2, GROUPS // 2, 160, 128), BF16)],
    )
    if fast:
        far_cw = swap(leave_cw, "fx")
    came = lax.all_to_all(carry, same_core, 0, 0, tiled=True)
    if fast:
        came, far_cw, stay_cw = lax.optimization_barrier((came, far_cw, stay_cw))
        stay_cw, leave_cw = call(middle_kernel, [sds((GROUPS // 2, 160, 128), BF16)] * 2, (stay_cw, far_cw))
        far_cw = swap(leave_cw, "ty")
        came = tied(came, leave_cw)
    stay_b, y_b, x_b, xy_b, d_normed, away = call(
        third_kernel,
        (*[sds((432, 128), BF16)] * 4, sds((rows, width)), sds((rows, width), BF16)),
        (came, starts, count, normed, xhat, v, lane, row_prm, feat, state, d_state, enter, d_mixed, part, b_all),
        [pltpu.VMEM((8, 128), F32), pltpu.VMEM((pair, 512), BF16), pltpu.VMEM((pair, width), F32), pltpu.VMEM((24, 128), F32)],
    )
    if not fast:
        grad_in = call(
            input_grad_kernel,
            sds((rows, width)),
            (d_normed, swap(away, "tc"), grad_out, xhat, inverse, feat),
            [pltpu.VMEM((4, rows, 128), F32)],
        )
        return reduced(layer_out, grad_in, stay_cw, leave_cw, (stay_b, y_b, x_b, xy_b), count_all, fsdp, width)
    xy_b = across(xy_b)
    x_b = swap(x_b, "fx")
    y_b = swap(y_b, "ty")
    sent = call(
        plane_add_kernel,
        sds((GROUPS // 2, 304, 128), BF16),
        (stay_cw, far_cw, stay_b, y_b, x_b, xy_b),
    )
    got = lax.all_to_all(sent, "fz", 0, 0, tiled=True)
    away = swap(tied(away, got), "tc")
    vec = call(vectors_kernel, sds((24, 128)), (got,))
    other = swap(vec, "tc")
    d_re, d_im, d_ore, d_oim, d_glu = call(
        matrices_kernel, (*[sds((64, 96))] * 4, sds((64, 128))), (got,), [pltpu.VMEM((128, 128), F32)]
    )
    grad_in, d_gbias, d_scale, d_bias, d_skip, g_decay, g_lam, g_step, rms = call(
        functools.partial(finish_kernel, count_all),
        (sds((rows, width)), sds((1, 16)), *[sds((1, 512))] * 3, *[sds((384,))] * 3, sds((1, 2))),
        (vec, other, d_normed, away, grad_out, xhat, inverse, feat),
        [pltpu.VMEM((24, 128), F32), pltpu.VMEM((4, rows, 128), F32)],
    )
    flat = lambda value: value.reshape(-1)
    return (
        layer_out, grad_in, flat(d_scale), flat(d_bias), g_decay, g_lam, g_step, d_re.T, d_im.T, d_ore.T, d_oim.T,
        flat(d_skip), d_glu.T, flat(d_gbias), flat(rms),
    )


def gathered(ln_scale, ln_bias, decay_rate, lam_im, log_dt, in_re, in_im, out_re, out_im, skip, glu_weight, glu_bias):
    tens = tensor_pos()
    full = lambda value, axis: lax.all_gather(value, FSDP, axis=axis, tiled=True)

    def pair(first, second):
        halves = jnp.stack([first.reshape(-1, GROUPS, 64), second.reshape(-1, GROUPS, 64)], axis=2)
        return halves.reshape(-1, GROUPS, 128).swapaxes(0, 1)

    gate = lax.dynamic_slice_in_dim(full(glu_weight, 1), tens * 128, 128, 0).T.reshape(GROUPS, 64, 128)
    vectors = [pair(full(ln_scale, 0)[None], full(ln_bias, 0)[None]), pair(full(skip, 0)[None], full(glu_bias, 0)[None])]
    for value in (decay_rate, lam_im, log_dt):
        value = jnp.pad(value, (0, 32))
        for _ in range(3):
            piece = lax.reduce_precision(value, 8, 7)
            value = value - piece
            vectors.append(jnp.broadcast_to(piece.astype(BF16)[None, None], (GROUPS, 1, 128)))
    vectors.append(jnp.zeros((GROUPS, 5, 128), BF16))
    packet = jnp.concatenate(
        [pair(full(in_re, 1), full(in_im, 1)), *vectors, pair(full(out_re, 1), full(out_im, 1)), gate],
        axis=1,
    )
    everyone = lax.all_gather(packet, TENSOR, axis=0).reshape(2, 2, GROUPS // 2, 2, 272, 128)
    x, y, core = (lax.axis_index(axis) for axis in ("fx", "ty", "tc"))
    own_x = lambda value, axis: jnp.stack([lax.dynamic_index_in_dim(value, x ^ j, axis, keepdims=False) for j in range(2)])
    for i in range(2):
        both = lax.dynamic_index_in_dim(everyone, core ^ i, 1, keepdims=False)
        slots = [own_x(lax.dynamic_index_in_dim(both, y ^ m, 0, keepdims=False), 1) for m in range(2)]
        slots = jnp.stack(slots, axis=1)
        if i == 0:
            g, cw = slots[:, :, :, :112], slots[:, :, :, 112:]
    return g, cw, slots[:, :, :, 208:]


def reduced(layer_out, grad_in, stay_cw, leave_cw, plane_b, count_all, fsdp, width):
    tens = tensor_pos()
    x = lax.axis_index("fx")

    def canonical(slots):
        out = jnp.zeros((4, GROUPS, *slots[0].shape[2:]), F32)
        for m, slot in enumerate(slots):
            parts = [lax.dynamic_index_in_dim(slot.astype(F32), x ^ n, 1) for n in range(2)]
            block = jnp.concatenate(parts, axis=1).reshape(1, GROUPS, *slot.shape[2:])
            out = lax.dynamic_update_slice_in_dim(out, block, slot_pos(m, 0), 0)
        return out

    def natural(slots):
        halves = canonical(slots).reshape(4, GROUPS, -1, 2, 64).transpose(3, 0, 2, 1, 4)
        return halves[0].reshape(-1, width), halves[1].reshape(-1, width)

    def scattered(value):
        value = lax.psum_scatter(value, TENSOR, scatter_dimension=0, tiled=True)
        return lax.psum_scatter(value, FSDP, scatter_dimension=1, tiled=True)

    blocks = [value[:384].reshape(GROUPS // 2, 96, 128) for value in plane_b]
    d_re, d_im = natural([jnp.stack([blocks[m], blocks[2 + m]], axis=1) for m in range(2)])
    cw = jnp.stack([stay_cw, leave_cw]).transpose(1, 2, 0, 3, 4)
    d_ore, d_oim = natural([value[:, :, :96] for value in cw])
    d_glu = canonical([value[:, :, 96:] for value in cw]).reshape(4, width, 128).swapaxes(1, 2).reshape(-1, width)
    vec = unpacked(plane_b[0][384:432])
    by_pos = lax.dynamic_update_slice_in_dim(
        jnp.zeros((3, 2, 2, 96), F32), vec[16:22, :96].reshape(3, 2, 1, 96), lax.axis_index("tc"), 2
    )
    vec, by_pos = lax.psum((vec, by_pos), AXES)
    states = lambda k: by_pos[k].reshape(-1)
    own = width // (4 * fsdp)
    place = tens * fsdp + fsdp_pos()
    d_gbias = lax.dynamic_slice_in_dim(vec[12:16].reshape(-1), place * own, own, 0)
    rms = jnp.sqrt(jnp.sum(vec[22].reshape(2, 64), axis=1) / count_all)
    return (
        layer_out, grad_in, vec[0:4].reshape(-1), vec[4:8].reshape(-1), states(0), states(1), states(2), scattered(d_re), scattered(d_im),
        scattered(d_ore), scattered(d_oim), vec[8:12].reshape(-1), scattered(d_glu), d_gbias, rms,
    )


def solution(mesh):
    shape = (mesh.shape["fsdp"] // 2, 2, mesh.shape["tensor"] // 2, 2)
    split = Mesh(mesh.devices.reshape(shape), AXES)
    tokens, matrix = P(AXES, None), P(TENSOR, FSDP)
    return jax.shard_map(
        on_device,
        mesh=split,
        in_specs=(
            tokens, tokens, P(FSDP), P(FSDP), P(TENSOR), P(TENSOR), P(TENSOR), matrix, matrix, matrix, matrix,
            P(FSDP), P(None, FSDP), P(FSDP), P(),
        ),
        out_specs=(
            tokens, tokens, P(), P(), P(), P(), P(), matrix, matrix, matrix, matrix, P(), matrix, P((*TENSOR, *FSDP)), P(),
        ),
        check_vma=False,
    )
```

```python
import functools

import jax
import jax.numpy as jnp
from jax import lax
from jax.experimental import pallas as pl
from jax.experimental.pallas import tpu as pltpu
from jax.sharding import Mesh
from jax.sharding import PartitionSpec as P

F32 = jnp.float32
BF16 = jnp.bfloat16
FSDP = ("fz", "fx")
TENSOR = ("ty", "tc")
AXES = (*FSDP, *TENSOR)
HBM = pl.BlockSpec(memory_space=pltpu.HBM)
VM = pl.BlockSpec(memory_space=pltpu.VMEM)
SM = pl.BlockSpec(memory_space=pltpu.SMEM)

GROUPS = 8
VEC = 96


def sds(shape, dtype=F32):
    return jax.ShapeDtypeStruct(shape, dtype)


def low_half(shape):
    return lax.broadcasted_iota(jnp.int32, shape, len(shape) - 1) < 64


def lane_iota(shape):
    return lax.broadcasted_iota(jnp.int32, shape, len(shape) - 1)


def dot(a, b, dims):
    return lax.dot_general(a, b, (dims, ((), ())), preferred_element_type=F32)


NT = ((1,), (1,))
NN = ((1,), (0,))
TN = ((0,), (0,))


def flipped():
    return lax.axis_index("fx") == 1


def part_lanes(part, m):
    return slice(256 * part + 128 * m, 256 * part + 128 * m + 128)


def slot_pos(m, core):
    return (lax.axis_index("ty") ^ m) * 2 + (lax.axis_index("tc") ^ core)


def own_rows(rows):
    return pl.ds(pl.multiple_of(lax.axis_index("tc") * rows, rows), rows)


def other_rows(rows):
    return pl.ds(pl.multiple_of((1 - lax.axis_index("tc")) * rows, rows), rows)


def piece(ref, m, f, start, count):
    return ref[f % 2, m, f // 2, start : start + count, :]


def natural(get, ref):
    lo = low_half((96, 128))
    for m in range(2):
        for part in range(2):
            lanes = part_lanes(part, m)
            ref[lanes.start + 96 : lanes.stop, :] = jnp.zeros((32, 512), BF16)
        for z in range(GROUPS // 2):
            even, odd = get(m, z, 0).astype(F32), get(m, z, 1).astype(F32)
            here = slice(128 * z, 128 * z + 128)
            ref[128 * m : 128 * m + 96, here] = jnp.where(lo, even, pltpu.roll(odd, 64, 1)).astype(BF16)
            ref[256 + 128 * m : 256 + 128 * m + 96, here] = jnp.where(lo, pltpu.roll(even, 64, 1), odd).astype(BF16)


def packets(value, m, z):
    lo = low_half((96, 128))
    here = slice(128 * z, 128 * z + 128)
    re, im = value[128 * m : 128 * m + 96, here], value[256 + 128 * m : 256 + 128 * m + 96, here]
    return jnp.where(lo, re, pltpu.roll(im, 64, 1)), jnp.where(lo, pltpu.roll(re, 64, 1), im)


def feature_rows(ref, row):
    lo = low_half((8, 128))
    flip = flipped()
    first, second = [], []
    for c in range(GROUPS // 2):
        a = jnp.broadcast_to(piece(ref, 0, 2 * c, row, 1).astype(F32), (8, 128))
        b = jnp.broadcast_to(piece(ref, 0, 2 * c + 1, row, 1).astype(F32), (8, 128))
        a, b = jnp.where(flip, b, a), jnp.where(flip, a, b)
        first.append(jnp.where(lo, a, pltpu.roll(b, 64, 1)))
        second.append(jnp.where(lo, pltpu.roll(a, 64, 1), b))
    return jnp.concatenate(first, axis=1)[:1], jnp.concatenate(second, axis=1)[:1]


def cmul(a, b):
    return a[0] * b[0] - a[1] * b[1], a[0] * b[1] + a[1] * b[0]


def tensor_pos():
    return lax.axis_index("ty") * 2 + lax.axis_index("tc")


def fsdp_pos():
    return lax.axis_index("fz") * 2 + lax.axis_index("fx")


def pair_pos():
    return fsdp_pos() * 2 + lax.axis_index("ty")


def offsets_of(start_ref):
    return [start_ref[n : n + 1, :] for n in range(start_ref.shape[0])]


STEPS = 16


def in_tiles(ref, rows, value):
    for c in range(4):
        ref[c, rows, :] = value[:, 128 * c : 128 * c + 128]


def of_tiles(ref, rows):
    return jnp.concatenate([ref[c, rows, :] for c in range(4)], axis=1)


def interleaved(ref, b):
    groups = [of_tiles(ref, pl.ds((n // STEPS) * 128 + n % STEPS, 8, stride=STEPS)) for n in (b, b + 1)]
    return jnp.concatenate(groups, axis=0)


def in_order(source, target):
    for g in range(target.shape[0] // 8):
        h, s, i = g // STEPS, g % STEPS // 2, 8 * (g % 2)
        target[8 * g : 8 * g + 8, :] = of_tiles(source, pl.ds(128 * h + 8 * i + s, 8, stride=8))


def starts_until(offsets, base, rows):
    row = lax.broadcasted_iota(jnp.int32, (rows, 128), 0)
    token = (row & ~127) + (row & 7) * STEPS + ((row & 127) >> 3)
    at = (token + base).astype(F32)
    count = jnp.zeros((rows, 128), F32)
    for off in offsets:
        count = count + jnp.where((at >= off) & (off >= at[0:1]), 1.0, 0.0)
    return count


def no_start(offsets, base, rows):
    link = jnp.ones((1, 128), F32)
    first = (jnp.zeros((1, 128), jnp.int32) + base).astype(F32)
    for off in offsets:
        link = jnp.where((off >= first) & (off < first + rows), 0.0, link)
    return link


def expm1(x):
    series = x * (1 + x / 2 * (1 + x / 3 * (1 + x / 4 * (1 + x / 5 * (1 + x / 6 * (1 + x / 7))))))
    return jnp.where(jnp.abs(x) < 0.25, series, jnp.exp(x) - 1.0)


def discretize(decay_rate, lam_im, log_dt):
    step_size = jnp.exp(log_dt)
    lam_re = -decay_rate
    magnitude = jnp.exp(lam_re * step_size)
    phase = lam_im * step_size
    abar_re = magnitude * jnp.cos(phase)
    abar_im = magnitude * jnp.sin(phase)
    half_sin = jnp.sin(0.5 * phase)
    less_re = expm1(lam_re * step_size) * jnp.cos(phase) - 2.0 * half_sin * half_sin
    denom = lam_re * lam_re + lam_im * lam_im
    coef_re = (less_re * lam_re + abar_im * lam_im) / denom
    coef_im = (abar_im * lam_re - less_re * lam_im) / denom
    return abar_re, abar_im, coef_re, coef_im, step_size


def pack_kernel(*refs):
    *inputs, out_ref, start_ref, square, four, glu_ref, halves, params, lengths, sems = refs
    seq_hbm, matrices, glu_hbm, features, states = inputs[0], inputs[1:5], inputs[5], inputs[6:10], inputs[10:13]
    units = pl.multiple_of(tensor_pos() * 128, 128)
    pairs = [(ref, four.at[k]) for k, ref in enumerate(matrices)]
    pairs += [(glu_hbm.at[:, pl.ds(units, 128)], glu_ref), (seq_hbm, lengths)]
    pairs += [(ref, halves.at[k]) for k, ref in enumerate(features)]
    pairs += [(ref, params.at[k]) for k, ref in enumerate(states)]
    copies = [pltpu.make_async_copy(source, target, sems.at[k]) for k, (source, target) in enumerate(pairs)]
    for copy in copies:
        copy.start()
    square[:, 96:128] = jnp.zeros((128, 32), F32)
    for copy in copies:
        copy.wait()
    vec = [
        jnp.concatenate([halves[0], halves[1]], axis=1).astype(F32),
        jnp.concatenate([halves[2], halves[3]], axis=1).astype(F32),
    ]
    for k in range(3):
        value = jnp.concatenate([params[k], jnp.zeros((1, 32), F32)], axis=1)
        for _ in range(3):
            part = value.astype(BF16).astype(F32)
            value = value - part
            vec.append(part)
    total = 0
    for n in range(lengths.shape[0]):
        start_ref[n : n + 1, :] = jnp.full((1, 128), total, jnp.int32).astype(F32)
        total = total + lengths[n]
    vec.append(jnp.zeros((16 - len(vec), 128), F32))
    vec = jnp.concatenate(vec, axis=0).astype(BF16)
    pieces = []
    for k in (0, 2):
        square[0:64, 0:96] = four[k].astype(F32)
        square[64:128, 0:96] = four[k + 1].astype(F32)
        pieces.append(square[...].T[0:96].astype(BF16))
    packet = jnp.concatenate([pieces[0], vec, pieces[1], glu_ref[...]], axis=0)
    for z in range(GROUPS // 2):
        out_ref[z] = packet


def params_of(ref, vec_row):
    lane = lane_iota((8, 128))
    out = []
    for k, safe in enumerate((1.0, 0.0, 0.0)):
        rows = []
        for m in range(2):
            part = piece(ref, m, 0, vec_row, 16).astype(F32)
            rows.append((part[2 + 3 * k : 3 + 3 * k] + part[3 + 3 * k : 4 + 3 * k]) + part[4 + 3 * k : 5 + 3 * k])
        value = jnp.concatenate(rows + [jnp.full((6, 128), safe, F32)], axis=0)
        out.append(jnp.where(lane < 96, value, safe))
    return out


def carry_block(re_rows, im_rows, scratch):
    for m in range(2):
        y = lax.axis_index("ty") ^ m
        scratch[pl.ds(y, 1), :] = re_rows[m]
        scratch[pl.ds(2 + y, 1), :] = im_rows[m]


def standardize_kernel(x_ref, other_ref, up_ref, start_ref, xhat_ref, up_out_ref, inv_ref, count_ref, tiles, inverses):
    rows, width = x_ref.shape
    in_tiles(tiles, slice(0, rows), up_ref[...].astype(F32))
    for b in range(0, rows // 8, 2):
        up_out_ref[8 * b : 8 * b + 16, :] = interleaved(tiles, b)
    for ref, where, own in ((x_ref, own_rows(rows), True), (other_ref, other_rows(rows), False)):
        x = ref[...].astype(F32)
        centered = x - jnp.sum(x, axis=1, keepdims=True) / width
        inverse = lax.rsqrt(jnp.sum(centered * centered, axis=1, keepdims=True) / width + 1e-05)
        in_tiles(tiles, where, centered * inverse)
        if own:
            inverses[...] = jnp.broadcast_to(inverse, (rows, 128))
    for b in range(0, 2 * rows // 8, 2):
        xhat_ref[8 * b : 8 * b + 16, :] = interleaved(tiles, b)
    for b in range(rows // 8):
        inv_ref[8 * b : 8 * b + 8, :] = inverses[pl.ds(b, 8, stride=STEPS), :]
    count_ref[...] = starts_until(offsets_of(start_ref), pair_pos() * 2 * rows, 2 * rows)


def first_kernel(
    pairs, xhat_ref, count_ref, g_ref, normed_ref, feat_ref, b_ref, v_ref, lane_ref, row_ref, send_ref, scratch
):
    rows = normed_ref.shape[0]
    scale, bias = feature_rows(g_ref, VEC)
    feat_ref[0:1] = scale
    feat_ref[1:2], feat_ref[2:3] = feature_rows(g_ref, VEC + 1)
    normed_ref[...] = (xhat_ref[...] * scale + bias).astype(BF16)
    natural(lambda m, z, x: g_ref[lax.axis_index("fx") ^ x, m, z, 0:96, :], b_ref)
    v_ref[...] = dot(normed_ref[...], b_ref[...], NT)

    decay, lam, log_dt = params_of(g_ref, VEC)
    abar_re, abar_im, coef_re, coef_im, step_size = discretize(decay, lam, log_dt)
    power = (abar_re, abar_im)
    for _ in range(8):
        power = cmul(power, power)
    scratch[...] = jnp.zeros((8, 128), F32)
    carry_block([power[0][m : m + 1] for m in range(2)], [power[1][m : m + 1] for m in range(2)], scratch)
    for k, value in enumerate((decay, lam, step_size, abar_re, abar_im, coef_re, coef_im, scratch[...])):
        row_ref[k] = value
    for k, value in enumerate((abar_re, abar_im, coef_re, coef_im)):
        for m in range(2):
            lane_ref[k : k + 1, 128 * m : 128 * m + 128] = value[m : m + 1]

    count = count_ref[...]
    open_tail = jnp.where(count == count[rows - 1 : rows], 1.0, 0.0)
    last = ([], [])
    for m in range(2):
        a = (all_rows(abar_re[m : m + 1]), all_rows(abar_im[m : m + 1]))
        b = (coef_re[m : m + 1], coef_im[m : m + 1])
        sixteen = squared(a, 4)
        tile = tile_powers(sixteen, lambda sub: 7 - sub)
        halves = []
        for h in range(2):
            acc = (jnp.zeros((8, 128), F32), jnp.zeros((8, 128), F32))
            for blk in range(STEPS * h, STEPS * h + STEPS):
                here = slice(8 * blk, 8 * blk + 8)
                drive = cmul(b, (v_ref[here, part_lanes(0, m)], v_ref[here, part_lanes(1, m)]))
                moved = cmul(a, acc)
                acc = (moved[0] + drive[0] * open_tail[here], moved[1] + drive[1] * open_tail[here])
            total = cmul(tile, acc)
            halves.append((column_sum(total[0]), column_sum(total[1])))
        moved = cmul(squared((sixteen[0][:1], sixteen[1][:1]), 3), halves[0])
        last[0].append(moved[0] + halves[1][0])
        last[1].append(moved[1] + halves[1][1])
    carry_block(last[0], last[1], scratch)
    packet = scratch[...]
    for d in range(pairs):
        send_ref[d] = packet[0:4]


def squared(a, times):
    for _ in range(times):
        a = cmul(a, a)
    return a


def tile_powers(a, exponent_of):
    exponent = exponent_of(lax.broadcasted_iota(jnp.int32, (8, 128), 0))
    tile = (jnp.ones((8, 128), F32), jnp.zeros((8, 128), F32))
    for bit in range(4):
        taken = (exponent & (1 << bit)) != 0
        more = cmul(tile, a)
        tile = (jnp.where(taken, more[0], tile[0]), jnp.where(taken, more[1], tile[1]))
        a = cmul(a, a)
    return tile


def all_rows(row):
    return jnp.broadcast_to(row, (8, 128))


def plus(value, link, more):
    return value[0] + jnp.where(link, more[0], 0.0), value[1] + jnp.where(link, more[1], 0.0)


def scan(read, powers, carry, count, reverse, emit):
    sub = lax.broadcasted_iota(jnp.int32, (8, 128), 0)
    order = range(STEPS - 1, -1, -1) if reverse else range(STEPS)
    end = 0 if reverse else 7
    back = lambda k: 8 - k if reverse else k
    carry = [(all_rows(c[0]), all_rows(c[1])) for c in carry]
    entries, ends, upto = [], [], []
    for a in powers:
        a = (all_rows(a[0]), all_rows(a[1]))
        power = [a]
        for _ in range(STEPS - 1):
            power.append(cmul(power[-1], a))
        upto.append(power)
        ends.append((power[-1], squared(power[-1], 1), squared(power[-1], 2)))
        entries.append(tile_powers(power[-1], (lambda sub: 8 - sub) if reverse else (lambda sub: sub + 1)))
    seen = jnp.zeros((8, 128), F32)
    for h in (1, 0) if reverse else (0, 1):
        counts = [count[8 * b : 8 * b + 8] for b in range(STEPS * h, STEPS * h + STEPS)]
        last = counts[order[-1]]
        near = jnp.where(sub == 7 - end, seen, pltpu.roll(last, back(1), 0))
        for m in range(2):
            values, before = {}, None
            for i in order:
                value = read(STEPS * h + i, m)
                if before is not None:
                    value = plus(value, counts[i] == counts[before], cmul(upto[m][0], values[before]))
                values[i], before = value, i
            tip = values[before]
            for k, power in zip((1, 2, 4), ends[m]):
                link = ((sub < 8 - k) if reverse else (sub >= k)) & (pltpu.roll(last, back(k), 0) == last)
                tip = plus(tip, link, cmul(power, (pltpu.roll(tip[0], back(k), 0), pltpu.roll(tip[1], back(k), 0))))
            tip = plus(tip, last == seen, cmul(entries[m], carry[m]))
            comes = tuple(jnp.where(sub == 7 - end, carry[m][p], pltpu.roll(tip[p], back(1), 0)) for p in range(2))
            for n, i in enumerate(order):
                emit(STEPS * h + i, m, plus(values[i], counts[i] == near, cmul(upto[m][n], comes)))
            carry[m] = (all_rows(tip[0][end : end + 1]), all_rows(tip[1][end : end + 1]))
        seen = all_rows(last[end : end + 1])


def carried(recv_ref, row_ref, offsets, rows, reverse, scratch):
    pairs = recv_ref.shape[0]
    power = row_ref[7]
    pre, pim = power[0:2], power[2:4]
    if reverse:
        pim = -pim
    place = pair_pos()

    zero = jnp.zeros((2, 128), F32)
    if pairs <= 32:
        first = lax.broadcasted_iota(jnp.int32, (pairs, 128), 0).astype(F32) * rows
        links = jnp.ones((pairs, 128), F32)
        for off in offsets:
            links = jnp.where((off >= first) & (off < first + rows), 0.0, links)
        out = (zero, zero)
        for j in range(pairs - 1, 0, -1) if reverse else range(pairs - 1):
            link = links[j : j + 1]
            got = recv_ref[j]
            new = cmul((pre * link, pim * link), out)
            reached = (j > place) if reverse else (j < place)
            out = (jnp.where(reached, new[0] + got[0:2], out[0]), jnp.where(reached, new[1] + got[2:4], out[1]))
    else:

        def turn(k, state):
            j = pairs - 1 - k if reverse else k
            link = no_start(offsets, j * rows, rows)
            got = recv_ref[j]
            new = cmul((pre * link, pim * link), state)
            return new[0] + got[0:2], new[1] + got[2:4]

        out = lax.fori_loop(0, pairs - 1 - place if reverse else place, turn, (zero, zero))
    scratch[0:2, :] = out[0]
    scratch[2:4, :] = out[1]
    own = [lax.axis_index("ty") ^ m for m in range(2)]
    return [scratch[pl.ds(y, 1), :] for y in own], [scratch[pl.ds(2 + y, 1), :] for y in own]


def column_sum(value):
    return jnp.sum(value, axis=0, keepdims=True)


def states_kernel(
    recv_ref, start_ref, count_ref, v_ref, lane_ref, row_ref, cw_ref, state_ref, twice_ref, enter_ref, c_ref, away_ref, scratch
):
    rows = v_ref.shape[0]
    count = count_ref[...]
    enter = carried(recv_ref, row_ref, offsets_of(start_ref), rows, False, scratch)
    for part in range(2):
        for m in range(2):
            enter_ref[0:1, part_lanes(part, m)] = enter[part][m]
    powers = [(lane_ref[0:1, 128 * m : 128 * m + 128], lane_ref[1:2, 128 * m : 128 * m + 128]) for m in range(2)]

    def read(b, m):
        here, lanes = slice(8 * b, 8 * b + 8), slice(128 * m, 128 * m + 128)
        return cmul((lane_ref[2:3, lanes], lane_ref[3:4, lanes]), (v_ref[here, part_lanes(0, m)], v_ref[here, part_lanes(1, m)]))

    def emit(b, m, value):
        for part in range(2):
            state_ref[8 * b : 8 * b + 8, part_lanes(part, m)] = value[part]

    scan(read, powers, [(enter[0][m], enter[1][m]) for m in range(2)], count, False, emit)
    twice_ref[:, 0:256] = state_ref[:, 0:256].astype(BF16) * 2
    twice_ref[:, 256:512] = state_ref[:, 256:512].astype(BF16) * -2
    natural(lambda m, z, x: cw_ref[lax.axis_index("fx") ^ x, m, z, 0:96, :], c_ref)
    away_ref[...] = dot(twice_ref[other_rows(rows // 2), :], c_ref[...], NN)


def readout_kernel(twice_ref, c_ref, out_ref):
    out_ref[...] = dot(twice_ref[own_rows(out_ref.shape[0]), :], c_ref[...], NN)


def second_kernel(
    own_ref, got_ref, up_ref, normed_ref, feat_ref, cw_ref, othercw_ref,
    branch_ref, dmixed_ref, dlogit_ref, mine_ref, away_ref, gate_ref, all_ref,
):
    rows, width = up_ref.shape
    for core, ref in enumerate((cw_ref, othercw_ref)):
        for m in range(2):
            lanes = pl.ds(pl.multiple_of(slot_pos(m, core) * 128, 128), 128)
            for f in range(GROUPS):
                place = (f // 2) * 2 + (lax.axis_index("fx") ^ (f % 2))
                gate_ref[pl.ds(pl.multiple_of(place * 64, 64), 64), lanes] = piece(ref, m, f, 96 * (1 - core), 64)
    skip, gate_bias = feat_ref[1:2], feat_ref[2:3]
    normed = normed_ref[own_rows(rows), :].astype(F32)
    mixed = (own_ref[...] + got_ref[...]) + skip * normed
    cdf = 0.5 * (1.0 + lax.erf(mixed * 0.7071067811865476))
    act_low = (mixed * cdf).astype(BF16)
    act = act_low.astype(F32)
    w_gate = gate_ref[...]
    logit = dot(act_low, w_gate, NN) + gate_bias
    gate = 1.0 / (1.0 + jnp.exp(-logit))
    branch_ref[...] = (act * gate).astype(BF16)
    up = up_ref[...]
    dlogit = (up * act * gate * (1.0 - gate)).astype(BF16)
    dlogit_ref[...] = dlogit
    all_ref[...] = dlogit
    d_act = dot(dlogit, w_gate, NT) + up * gate
    slope = cdf + mixed * jnp.exp(-0.5 * mixed * mixed) * 0.3989422804014327
    d_mixed = d_act * slope
    dmixed_ref[...] = d_mixed
    for core, ref in enumerate((mine_ref, away_ref)):
        ref[:, 0:width] = d_mixed.astype(BF16)
        ref[:, width : 2 * width] = act_low
        for m in range(2):
            lanes = pl.ds(pl.multiple_of(slot_pos(m, core) * 128, 128), 128)
            ref[:, 2 * width + 128 * m : 2 * width + 128 * m + 128] = all_ref[:, lanes]


def sums_kernel(x_ref, branch_ref, normed_ref, dmixed_ref, dlogit_ref, out_ref, part_ref, tiles, ordered):
    x = x_ref[...].astype(F32)
    branch = branch_ref[...].astype(F32)
    in_tiles(tiles, slice(None), branch)
    in_order(tiles, ordered)
    out_ref[...] = (x + ordered[...]).astype(BF16)
    skip = column_sum(dmixed_ref[...] * normed_ref[own_rows(x_ref.shape[0]), :].astype(F32))
    for k, value in enumerate((skip, column_sum(dlogit_ref[...].astype(F32)), column_sum(x * x), column_sum(branch * branch))):
        part_ref[k : k + 1, :] = value


def back_kernel(
    pairs, mine_ref, got_ref, twice_ref, count_ref, lane_ref, c_ref,
    dstate_ref, send_ref, stay_ref, leave_ref, dy_ref, dgate_ref, scratch, all_ref,
):
    rows, width = dy_ref.shape
    half = rows // 2
    dy_ref[own_rows(half), :] = mine_ref[:, 0:width]
    dy_ref[other_rows(half), :] = got_ref[:, 0:width]
    d_state = dot(dy_ref[...], c_ref[...], NT)
    dstate_ref[:, 0:256] = d_state[:, 0:256] * 2.0
    dstate_ref[:, 256:512] = d_state[:, 256:512] * -2.0
    count = count_ref[...]
    head = jnp.where(count == 0.0, 1.0, 0.0)
    first = ([], [])
    for m in range(2):
        lanes = slice(128 * m, 128 * m + 128)
        a = (all_rows(lane_ref[0:1, lanes]), all_rows(-lane_ref[1:2, lanes]))
        sixteen = squared(a, 4)
        tile = tile_powers(sixteen, lambda sub: sub)
        halves = []
        for h in range(2):
            acc = (jnp.zeros((8, 128), F32), jnp.zeros((8, 128), F32))
            for blk in range(STEPS * h + STEPS - 1, STEPS * h - 1, -1):
                here = slice(8 * blk, 8 * blk + 8)
                moved = cmul(a, acc)
                acc = (
                    moved[0] + dstate_ref[here, part_lanes(0, m)] * head[here],
                    moved[1] + dstate_ref[here, part_lanes(1, m)] * head[here],
                )
            total = cmul(tile, acc)
            halves.append((column_sum(total[0]), column_sum(total[1])))
        moved = cmul(squared((sixteen[0][:1], sixteen[1][:1]), 3), halves[1])
        total = cmul((a[0][:1], a[1][:1]), (moved[0] + halves[0][0], moved[1] + halves[0][1]))
        first[0].append(total[0])
        first[1].append(total[1])
    scratch[...] = jnp.zeros((8, 128), F32)
    carry_block(first[0], first[1], scratch)
    packet = scratch[...]
    for d in range(pairs):
        send_ref[d] = packet[0:4]
    d_c = dot(twice_ref[...], dy_ref[...], TN)
    act = slice(width, 2 * width)
    units = slice(2 * width, 2 * width + 256)
    d_gate = dot(mine_ref[:, act], mine_ref[:, units], TN) + dot(got_ref[:, act], got_ref[:, units], TN)
    dgate_ref[...] = d_gate.astype(BF16)
    for m in range(2):
        for z in range(GROUPS // 2):
            for x, packet in enumerate(packets(d_c, m, z)):
                j = lax.axis_index("fx") ^ x
                all_ref[j, m, z, 0:96, :] = packet.astype(BF16)
                all_ref[j, m, z, 96:160, :] = dgate_ref[128 * z + 64 * x : 128 * z + 64 * x + 64, 128 * m : 128 * m + 128]
    stay_ref[...] = all_ref[0]
    leave_ref[...] = all_ref[1]


def packed(vec):
    upper = vec.astype(BF16).astype(F32)
    return jnp.concatenate([upper, vec - upper], axis=0).astype(BF16)


def unpacked(packet):
    value = packet.astype(F32)
    return value[0:24] + value[24:48]


def third_kernel(
    recv_ref, start_ref, count_ref, normed_ref, xhat_ref, v_ref, lane_ref, row_ref, feat_ref, state_ref, dstate_ref, enter_ref, dmixed_ref,
    part_ref, b_ref, stay_ref, y_ref, x_ref, xy_ref, dn_ref, dnaway_ref, scratch, dv_ref, all_ref, vec_ref,
):
    rows, width = normed_ref.shape
    half = rows // 2
    count = count_ref[...]
    later = carried(recv_ref, row_ref, offsets_of(start_ref), rows, True, scratch)
    sub = lax.broadcasted_iota(jnp.int32, (8, 128), 0)
    none = jnp.zeros((1, 128), F32)
    totals = [[jnp.zeros((8, 128), F32) for _ in range(4)] for _ in range(2)]
    powers = [(lane_ref[0:1, 128 * m : 128 * m + 128], -lane_ref[1:2, 128 * m : 128 * m + 128]) for m in range(2)]

    def read(b, m):
        value = [dstate_ref[8 * b : 8 * b + 8, part_lanes(part, m)] for part in range(2)]
        if b == rows // 8 - 1:
            value = [value[part] + jnp.where(sub == 7, later[part][m], 0.0) for part in range(2)]
        return tuple(value)

    def emit(b, m, adj):
        here, lanes = slice(8 * b, 8 * b + 8), slice(128 * m, 128 * m + 128)
        h, i = b // STEPS, b % STEPS
        if i:
            same = count[here] == count[8 * b - 8 : 8 * b]
            moved = [state_ref[8 * b - 8 : 8 * b, part_lanes(part, m)] for part in range(2)]
        else:
            end = slice(8 * (b + STEPS - 1), 8 * (b + STEPS))
            same = count[here] == jnp.where(sub == 0, count[127:128] if h else none, pltpu.roll(count[end], 1, 0))
            moved = []
            for part in range(2):
                edge = state_ref[127:128, part_lanes(part, m)] if h else enter_ref[0:1, part_lanes(part, m)]
                moved.append(jnp.where(sub == 0, edge, pltpu.roll(state_ref[end, part_lanes(part, m)], 1, 0)))
        prev = [jnp.where(same, part, 0.0) for part in moved]
        v = (v_ref[here, part_lanes(0, m)], v_ref[here, part_lanes(1, m)])
        for k, (p, q) in enumerate((prev, v)):
            totals[m][2 * k] = totals[m][2 * k] + (adj[0] * p + adj[1] * q)
            totals[m][2 * k + 1] = totals[m][2 * k + 1] + (adj[1] * p - adj[0] * q)
        dv = cmul((lane_ref[2:3, lanes], -lane_ref[3:4, lanes]), adj)
        for part in range(2):
            dvf_ref[here, part_lanes(part, m)] = dv[part]

    dvf_ref = all_ref
    scan(read, powers, [(none, none), (none, none)], count, True, emit)
    sums = [[column_sum(totals[m][k]) for m in range(2)] for k in range(4)]
    dv_ref[...] = dvf_ref[...].astype(BF16)
    dv = dv_ref[...]
    d_b = dot(dv, normed_ref[...], TN)
    flip = flipped()
    for m, (near, side) in enumerate(((stay_ref, x_ref), (y_ref, xy_ref))):
        for z in range(GROUPS // 2):
            even, odd = packets(d_b, m, z)
            here = slice(96 * z, 96 * z + 96)
            near[here, :] = jnp.where(flip, odd, even).astype(BF16)
            side[here, :] = jnp.where(flip, even, odd).astype(BF16)
    all_ref[...] = dot(dv, b_ref[...], NN)
    away = all_ref[other_rows(half), :]
    dnaway_ref[...] = away.astype(BF16)
    own = all_ref[own_rows(half), :] + dmixed_ref[...] * feat_ref[1:2]
    dn_ref[...] = own
    to_scale = column_sum(own * xhat_ref[own_rows(half), :]) + column_sum(away * xhat_ref[other_rows(half), :])
    vector = [to_scale, column_sum(own) + column_sum(away), part_ref[0:1, :], part_ref[1:2, :]]
    for k, value in enumerate(vector):
        for c in range(4):
            vec_ref[4 * k + c : 4 * k + c + 1, :] = value[:, 128 * c : 128 * c + 128]
    g = [jnp.concatenate(pair + [jnp.zeros((6, 128), F32)], axis=0) for pair in sums]
    decay, lam, step, abar_re, abar_im, coef_re, coef_im = (row_ref[k] for k in range(7))
    d_abar, d_coef = (g[0], g[1]), (g[2], g[3])
    denom = decay * decay + lam * lam
    numer = (step * abar_re - coef_re, step * abar_im - coef_im)
    ratio = cmul(numer, (-decay / denom, -lam / denom))
    to_lam_a = cmul((step * abar_re, -step * abar_im), d_abar)
    to_lam_c = cmul((ratio[0], -ratio[1]), d_coef)
    g_decay = -(to_lam_a[0] + to_lam_c[0])
    g_lam = to_lam_a[1] + to_lam_c[1]
    slope = cmul((-decay, lam), (abar_re, abar_im))
    g_step = (slope[0] * d_abar[0] + slope[1] * d_abar[1] + abar_re * d_coef[0] + abar_im * d_coef[1]) * step
    for k, value in enumerate((g_decay, g_lam, g_step)):
        for m in range(2):
            vec_ref[pl.ds(16 + 2 * k + (lax.axis_index("ty") ^ m), 1), :] = value[m : m + 1]
    folds = []
    for k in range(2):
        squares = part_ref[2 + k : 3 + k, :]
        total = (squares[:, 0:128] + squares[:, 128:256]) + (squares[:, 256:384] + squares[:, 384:512])
        total = jnp.broadcast_to(total, (8, 128))
        folds.append(total + pltpu.roll(total, 64, 1))
    vec_ref[22:23, :] = jnp.where(low_half((1, 128)), folds[0][:1], folds[1][:1])
    vec_ref[23:24, :] = jnp.zeros((1, 128), F32)
    vec = packed(vec_ref[...])
    for ref in (stay_ref, y_ref, x_ref, xy_ref):
        ref[384:432, :] = vec


def input_grad(dn_ref, got_ref, up_ref, xhat_ref, inv_ref, feat_ref, gin_ref, tiles):
    rows, width = up_ref.shape
    xhat = xhat_ref[own_rows(rows), :]
    d_xhat = (dn_ref[...] + got_ref[...].astype(F32)) * feat_ref[0:1]
    mean = jnp.sum(d_xhat, axis=1, keepdims=True) / width
    mean_hat = jnp.sum(d_xhat * xhat, axis=1, keepdims=True) / width
    in_tiles(tiles, slice(None), inv_ref[:, 0:1] * (d_xhat - mean - xhat * mean_hat))
    in_order(tiles, gin_ref)
    gin_ref[...] = gin_ref[...] + up_ref[...].astype(F32)


def input_grad_kernel(*refs):
    input_grad(*refs)


def added(a, b):
    return (a.astype(F32) + b.astype(F32)).astype(BF16)


def middle_kernel(keep_ref, got_ref, stay_ref, leave_ref):
    stay_ref[...] = added(keep_ref[0], got_ref[0])
    leave_ref[...] = added(keep_ref[1], got_ref[1])


def plane_add_kernel(cw_ref, gotcw_ref, stay_ref, y_ref, x_ref, xy_ref, out_ref):
    def total(read):
        return (read(stay_ref) + read(y_ref)) + (read(x_ref) + read(xy_ref))

    vec = packed(total(lambda ref: unpacked(ref[384:432, :])))
    for z in range(GROUPS // 2):
        here = slice(96 * z, 96 * z + 96)
        out_ref[z, 0:96, :] = total(lambda ref, here=here: ref[here, :].astype(F32)).astype(BF16)
        out_ref[z, 96:256, :] = added(cw_ref[z], gotcw_ref[z])
        out_ref[z, 256:304, :] = vec


def vectors_kernel(got_ref, vec_ref):
    vec = unpacked(got_ref[0, 256:304, :])
    for z in range(1, GROUPS // 2):
        vec = vec + unpacked(got_ref[z, 256:304, :])
    vec_ref[...] = vec


def rows_to_lanes(rows):
    turned = [rows, pltpu.roll(rows, 96, 1), pltpu.roll(rows, 64, 1), pltpu.roll(rows, 32, 1)]
    lane = lane_iota((1, 128))
    return [
        jnp.where(lane < 96, rows[0:1], turned[1][1:2]),
        jnp.where(lane < 64, turned[1][1:2], turned[2][2:3]),
        jnp.where(lane < 32, turned[2][2:3], turned[3][3:4]),
    ]


def matrices_kernel(got_ref, dre_ref, dim_ref, ore_ref, oim_ref, glu_ref, square):
    def total(start, count):
        value = got_ref[0, start : start + count, :].astype(F32)
        for z in range(1, GROUPS // 2):
            value = value + got_ref[z, start : start + count, :].astype(F32)
        return value

    for start, first_ref, second_ref in ((0, dre_ref, dim_ref), (96, ore_ref, oim_ref)):
        square[0:96, :] = total(start, 96)
        square[96:128, :] = jnp.zeros((32, 128), F32)
        turned = square[...].T
        first_ref[...] = turned[0:64, 0:96]
        second_ref[...] = turned[64:128, 0:96]
    glu_ref[...] = total(192, 64)


def finish_kernel(
    count_all, own_ref, other_ref, dn_ref, got_ref, up_ref, xhat_ref, inv_ref, feat_ref,
    gin_ref, gbias_ref, scale_ref, bias_ref, skip_ref, decay_ref, lam_ref, step_ref, rms_ref, vec_ref, tiles,
):
    input_grad(dn_ref, got_ref, up_ref, xhat_ref, inv_ref, feat_ref, gin_ref, tiles)
    own, other = own_ref[...], other_ref[...]
    vec = own + other
    vec_ref[...] = vec
    first, second = jnp.where(lax.axis_index("tc") == 0, own, other), jnp.where(lax.axis_index("tc") == 0, other, own)
    for k, ref in enumerate((scale_ref, bias_ref, skip_ref)):
        for c in range(4):
            ref[:, 128 * c : 128 * c + 128] = vec[4 * k + c : 4 * k + c + 1]
    for k, ref in enumerate((decay_ref, lam_ref, step_ref)):
        at = 16 + 2 * k
        by_pos = [first[at : at + 1], second[at : at + 1], first[at + 1 : at + 2], second[at + 1 : at + 2]]
        for c, chunk in enumerate(rows_to_lanes(jnp.concatenate(by_pos + [jnp.zeros((4, 128), F32)], axis=0))):
            ref[128 * c : 128 * c + 128] = chunk.reshape(128)
    squares = vec[22:23]
    total = [jnp.sum(jnp.where(low_half((1, 128)) == low, squares, 0.0), axis=1, keepdims=True) for low in (True, False)]
    rms_ref[...] = jnp.sqrt(jnp.where(lane_iota((1, 2)) == 0, total[0], total[1]) / count_all)
    place = tensor_pos() * GROUPS + fsdp_pos()
    row = jnp.broadcast_to(vec_ref[pl.ds(12 + place // 8, 1), :], (8, 128))
    gbias_ref[...] = pltpu.roll(row, 128 - 16 * (place % 8), 1)[0:1, 0:16]


TAKES = {
    "pack": 1.5, "standardize": 0.4, "norm": 0.4, "first": 0.6, "states": 0.9, "readout": 0.4, "second": 0.7, "sums": 0.7, "back": 0.8,
    "third": 1.5, "input_grad": 0.5, "matrices": 0.5, "finish": 0.4,
}


def call(kernel, outs, args, scratch=(), specs=None, limit=24):
    name = getattr(kernel, "func", kernel).__name__.removesuffix("_kernel")
    return pl.pallas_call(
        kernel,
        out_shape=outs,
        in_specs=specs or [VM] * len(args),
        out_specs=jax.tree.map(lambda _: VM, outs),
        scratch_shapes=list(scratch),
        compiler_params=pltpu.CompilerParams(vmem_limit_bytes=limit << 20),
        cost_estimate=pl.CostEstimate(flops=0, transcendentals=0, bytes_accessed=int(TAKES.get(name, 0.1) * 3.6e6)),
        name=name,
    )(*args)


def tied(value, other):
    return lax.optimization_barrier((value, other))[0]


def swap(value, axis):
    return lax.ppermute(value, axis, [(0, 1), (1, 0)])


def across(value):
    return lax.ppermute(value, ("fx", "ty"), [(n, 3 - n) for n in range(4)])


def standardized(layer_in, grad_out, starts):
    rows, width = layer_in.shape
    return call(
        standardize_kernel,
        (sds((2 * rows, width)), sds((rows, width)), sds((rows, 128)), sds((2 * rows, 128))),
        (layer_in, swap(layer_in, "tc"), grad_out, starts),
        [pltpu.VMEM((4, 2 * rows, 128), F32), pltpu.VMEM((rows, 128), F32)],
    )


def on_device(
    layer_in, grad_out, ln_scale, ln_bias, decay_rate, lam_im, log_dt, in_re, in_im, out_re, out_im, skip, glu_weight, glu_bias, seq_lengths
):
    rows, width = layer_in.shape
    fsdp = lax.axis_size(FSDP)
    pairs, pair = fsdp * 2, 2 * rows
    count_all = float(rows * pairs * 2 * width)
    fast = fsdp == GROUPS
    same_core = (*FSDP, "ty")
    if fast:
        row = lambda v: v.reshape(1, -1)
        sent, starts = call(
            pack_kernel,
            (sds((GROUPS // 2, 272, 128), BF16), sds((seq_lengths.shape[0], 128))),
            (seq_lengths, in_re.T, in_im.T, out_re.T, out_im.T, glu_weight.T, row(ln_scale), row(ln_bias), row(skip), row(glu_bias),
             row(decay_rate), row(lam_im), row(log_dt)),
            [pltpu.VMEM((128, 128), F32), pltpu.VMEM((4, 64, 96), BF16), pltpu.VMEM((64, 128), BF16), pltpu.VMEM((4, 1, 64), BF16),
             pltpu.VMEM((3, 1, 96), F32), pltpu.SMEM(seq_lengths.shape, jnp.int32), pltpu.SemaphoreType.DMA((13,))],
            [HBM] * 13,
            60,
        )
        mine = lax.all_to_all(sent, "fz", 0, 0, tiled=True)
        own_b, own_cw = lax.optimization_barrier((mine[:, :112], mine[:, 112:]))
        plane_b = [own_b, swap(own_b, "ty"), swap(own_b, "fx"), across(own_b)]
        xhat, up, inverse, count = standardized(layer_in, grad_out, starts)
        plane_b, side_cw, xhat = lax.optimization_barrier((plane_b, swap(own_cw, "ty"), xhat))
        side_cw = jnp.stack([own_cw, side_cw])
        far_cw = swap(side_cw, "fx")
        g = jnp.stack(plane_b).reshape(2, 2, GROUPS // 2, 112, 128)
    else:
        starts = jnp.broadcast_to((jnp.cumsum(seq_lengths) - seq_lengths).astype(F32)[:, None], (seq_lengths.shape[0], 128))
        xhat, up, inverse, count = standardized(layer_in, grad_out, starts)
        g, cw, other_cw = gathered(
            ln_scale, ln_bias, decay_rate, lam_im, log_dt, in_re, in_im, out_re, out_im, skip, glu_weight, glu_bias
        )

    normed, feat, b_all, v, lane, row_prm, carry = call(
        functools.partial(first_kernel, pairs),
        (sds((pair, width), BF16), sds((8, width)), sds((512, width), BF16), sds((pair, 512)), sds((8, 256)), sds((8, 8, 128)), sds((pairs, 4, 128))),
        (xhat, count, g),
        [pltpu.VMEM((8, 128), F32)],
    )
    came = lax.all_to_all(carry, same_core, 0, 0, tiled=True)
    if fast:
        cw = jnp.stack(tied((side_cw, far_cw), came))
    state, twice, enter, c_all, away = call(
        states_kernel,
        (sds((pair, 512)), sds((pair, 512), BF16), sds((8, 512)), sds((512, width), BF16), sds((rows, width))),
        (came, starts, count, v, lane, row_prm, cw),
        [pltpu.VMEM((8, 128), F32)],
    )
    if fast:
        other_cw = swap(cw[:, :, :, 96:], "tc")
    own = call(readout_kernel, sds((rows, width)), (twice, c_all))
    branch, d_mixed, dlogit, kept, away = call(
        second_kernel,
        (sds((rows, width), BF16), sds((rows, width)), sds((rows, width), BF16), *[sds((rows, 2 * width + 256), BF16)] * 2),
        (own, swap(away, "tc"), up, normed, feat, cw, other_cw),
        [pltpu.VMEM((width, width), BF16), pltpu.VMEM((rows, width), BF16)],
    )
    got = swap(away, "tc")
    layer_out, part = call(
        sums_kernel,
        (sds((rows, width), BF16), sds((8, width))),
        (layer_in, branch, normed, d_mixed, dlogit),
        [pltpu.VMEM((4, rows, 128), F32), pltpu.VMEM((rows, width), F32)],
    )
    got, part = lax.optimization_barrier((got, part))
    d_state, carry, stay_cw, leave_cw = call(
        functools.partial(back_kernel, pairs),
        (sds((pair, 512)), sds((pairs, 4, 128)), *[sds((2, GROUPS // 2, 160, 128), BF16)] * 2),
        (kept, got, twice, count, lane, c_all),
        [pltpu.VMEM((pair, width), BF16), pltpu.VMEM((width, 256), BF16), pltpu.VMEM((8, 128), F32),
         pltpu.VMEM((2, 2, GROUPS // 2, 160, 128), BF16)],
    )
    if fast:
        far_cw = swap(leave_cw, "fx")
    came = lax.all_to_all(carry, same_core, 0, 0, tiled=True)
    if fast:
        came, far_cw, stay_cw = lax.optimization_barrier((came, far_cw, stay_cw))
        stay_cw, leave_cw = call(middle_kernel, [sds((GROUPS // 2, 160, 128), BF16)] * 2, (stay_cw, far_cw))
        far_cw = swap(leave_cw, "ty")
        came = tied(came, leave_cw)
    stay_b, y_b, x_b, xy_b, d_normed, away = call(
        third_kernel,
        (*[sds((432, 128), BF16)] * 4, sds((rows, width)), sds((rows, width), BF16)),
        (came, starts, count, normed, xhat, v, lane, row_prm, feat, state, d_state, enter, d_mixed, part, b_all),
        [pltpu.VMEM((8, 128), F32), pltpu.VMEM((pair, 512), BF16), pltpu.VMEM((pair, width), F32), pltpu.VMEM((24, 128), F32)],
    )
    if not fast:
        grad_in = call(
            input_grad_kernel,
            sds((rows, width)),
            (d_normed, swap(away, "tc"), grad_out, xhat, inverse, feat),
            [pltpu.VMEM((4, rows, 128), F32)],
        )
        return reduced(layer_out, grad_in, stay_cw, leave_cw, (stay_b, y_b, x_b, xy_b), count_all, fsdp, width)
    xy_b = across(xy_b)
    x_b = swap(x_b, "fx")
    y_b = swap(y_b, "ty")
    sent = call(
        plane_add_kernel,
        sds((GROUPS // 2, 304, 128), BF16),
        (stay_cw, far_cw, stay_b, y_b, x_b, xy_b),
    )
    got = lax.all_to_all(sent, "fz", 0, 0, tiled=True)
    away = swap(tied(away, got), "tc")
    vec = call(vectors_kernel, sds((24, 128)), (got,))
    other = swap(vec, "tc")
    d_re, d_im, d_ore, d_oim, d_glu = call(
        matrices_kernel, (*[sds((64, 96))] * 4, sds((64, 128))), (got,), [pltpu.VMEM((128, 128), F32)]
    )
    grad_in, d_gbias, d_scale, d_bias, d_skip, g_decay, g_lam, g_step, rms = call(
        functools.partial(finish_kernel, count_all),
        (sds((rows, width)), sds((1, 16)), *[sds((1, 512))] * 3, *[sds((384,))] * 3, sds((1, 2))),
        (vec, other, d_normed, away, grad_out, xhat, inverse, feat),
        [pltpu.VMEM((24, 128), F32), pltpu.VMEM((4, rows, 128), F32)],
    )
    flat = lambda value: value.reshape(-1)
    return (
        layer_out, grad_in, flat(d_scale), flat(d_bias), g_decay, g_lam, g_step, d_re.T, d_im.T, d_ore.T, d_oim.T,
        flat(d_skip), d_glu.T, flat(d_gbias), flat(rms),
    )


def gathered(ln_scale, ln_bias, decay_rate, lam_im, log_dt, in_re, in_im, out_re, out_im, skip, glu_weight, glu_bias):
    tens = tensor_pos()
    full = lambda value, axis: lax.all_gather(value, FSDP, axis=axis, tiled=True)

    def pair(first, second):
        halves = jnp.stack([first.reshape(-1, GROUPS, 64), second.reshape(-1, GROUPS, 64)], axis=2)
        return halves.reshape(-1, GROUPS, 128).swapaxes(0, 1)

    gate = lax.dynamic_slice_in_dim(full(glu_weight, 1), tens * 128, 128, 0).T.reshape(GROUPS, 64, 128)
    vectors = [pair(full(ln_scale, 0)[None], full(ln_bias, 0)[None]), pair(full(skip, 0)[None], full(glu_bias, 0)[None])]
    for value in (decay_rate, lam_im, log_dt):
        value = jnp.pad(value, (0, 32))
        for _ in range(3):
            piece = lax.reduce_precision(value, 8, 7)
            value = value - piece
            vectors.append(jnp.broadcast_to(piece.astype(BF16)[None, None], (GROUPS, 1, 128)))
    vectors.append(jnp.zeros((GROUPS, 5, 128), BF16))
    packet = jnp.concatenate(
        [pair(full(in_re, 1), full(in_im, 1)), *vectors, pair(full(out_re, 1), full(out_im, 1)), gate],
        axis=1,
    )
    everyone = lax.all_gather(packet, TENSOR, axis=0).reshape(2, 2, GROUPS // 2, 2, 272, 128)
    x, y, core = (lax.axis_index(axis) for axis in ("fx", "ty", "tc"))
    own_x = lambda value, axis: jnp.stack([lax.dynamic_index_in_dim(value, x ^ j, axis, keepdims=False) for j in range(2)])
    for i in range(2):
        both = lax.dynamic_index_in_dim(everyone, core ^ i, 1, keepdims=False)
        slots = [own_x(lax.dynamic_index_in_dim(both, y ^ m, 0, keepdims=False), 1) for m in range(2)]
        slots = jnp.stack(slots, axis=1)
        if i == 0:
            g, cw = slots[:, :, :, :112], slots[:, :, :, 112:]
    return g, cw, slots[:, :, :, 208:]


def reduced(layer_out, grad_in, stay_cw, leave_cw, plane_b, count_all, fsdp, width):
    tens = tensor_pos()
    x = lax.axis_index("fx")

    def canonical(slots):
        out = jnp.zeros((4, GROUPS, *slots[0].shape[2:]), F32)
        for m, slot in enumerate(slots):
            parts = [lax.dynamic_index_in_dim(slot.astype(F32), x ^ n, 1) for n in range(2)]
            block = jnp.concatenate(parts, axis=1).reshape(1, GROUPS, *slot.shape[2:])
            out = lax.dynamic_update_slice_in_dim(out, block, slot_pos(m, 0), 0)
        return out

    def natural(slots):
        halves = canonical(slots).reshape(4, GROUPS, -1, 2, 64).transpose(3, 0, 2, 1, 4)
        return halves[0].reshape(-1, width), halves[1].reshape(-1, width)

    def scattered(value):
        value = lax.psum_scatter(value, TENSOR, scatter_dimension=0, tiled=True)
        return lax.psum_scatter(value, FSDP, scatter_dimension=1, tiled=True)

    blocks = [value[:384].reshape(GROUPS // 2, 96, 128) for value in plane_b]
    d_re, d_im = natural([jnp.stack([blocks[m], blocks[2 + m]], axis=1) for m in range(2)])
    cw = jnp.stack([stay_cw, leave_cw]).transpose(1, 2, 0, 3, 4)
    d_ore, d_oim = natural([value[:, :, :96] for value in cw])
    d_glu = canonical([value[:, :, 96:] for value in cw]).reshape(4, width, 128).swapaxes(1, 2).reshape(-1, width)
    vec = unpacked(plane_b[0][384:432])
    by_pos = lax.dynamic_update_slice_in_dim(
        jnp.zeros((3, 2, 2, 96), F32), vec[16:22, :96].reshape(3, 2, 1, 96), lax.axis_index("tc"), 2
    )
    vec, by_pos = lax.psum((vec, by_pos), AXES)
    states = lambda k: by_pos[k].reshape(-1)
    own = width // (4 * fsdp)
    place = tens * fsdp + fsdp_pos()
    d_gbias = lax.dynamic_slice_in_dim(vec[12:16].reshape(-1), place * own, own, 0)
    rms = jnp.sqrt(jnp.sum(vec[22].reshape(2, 64), axis=1) / count_all)
    return (
        layer_out, grad_in, vec[0:4].reshape(-1), vec[4:8].reshape(-1), states(0), states(1), states(2), scattered(d_re), scattered(d_im),
        scattered(d_ore), scattered(d_oim), vec[8:12].reshape(-1), scattered(d_glu), d_gbias, rms,
    )


def solution(mesh):
    shape = (mesh.shape["fsdp"] // 2, 2, mesh.shape["tensor"] // 2, 2)
    split = Mesh(mesh.devices.reshape(shape), AXES)
    tokens, matrix = P(AXES, None), P(TENSOR, FSDP)
    return jax.shard_map(
        on_device,
        mesh=split,
        in_specs=(
            tokens, tokens, P(FSDP), P(FSDP), P(TENSOR), P(TENSOR), P(TENSOR), matrix, matrix, matrix, matrix,
            P(FSDP), P(None, FSDP), P(FSDP), P(),
        ),
        out_specs=(
            tokens, tokens, P(), P(), P(), P(), P(), matrix, matrix, matrix, matrix, P(), matrix, P((*TENSOR, *FSDP)), P(),
        ),
        check_vma=False,
    )
```
